32 devices in a mesh: expert: 8 (over z, x), tensor: 4 (over y, core).
Axes of the slice: x: 2, y: 2, z: 4, core: 2. Of those that a mesh axis runs over, the one named last changes fastest.
Arguments:
- tokens: bfloat16 [20480, 1024], P(('expert', 'tensor')), may hold values from -6 to 6
- cotangent: bfloat16 [20480, 1024], P(('expert', 'tensor')), may hold values from -6 to 6
- routes: int32 [20480, 1], P('expert'), may hold values from 0 to 7; in each aligned block of 640 rows (0 to 639, 640 to 1279, ...) at most 112 rows name the same one
- parents: int32 [8, 13], P('expert'), may hold values from 0 to 4, as said below
- ln_attn: float32 [1024], replicated, may hold values from 0.5 to 1.5
- w_qkv: bfloat16 [3, 1024, 1024], P(None, None, 'tensor'), may hold values from -0.1875 to 0.1875
- w_out: bfloat16 [1024, 1024], P('tensor'), may hold values from -3 to 3
- ln_mlp: float32 [1024], replicated, may hold values from 0.5 to 1.5
- w_up: bfloat16 [1024, 4096], P(None, 'tensor'), may hold values from -0.1875 to 0.1875
- w_down: bfloat16 [4096, 1024], P('tensor'), may hold values from -0.09375 to 0.09375
- w_router: bfloat16 [1024, 8], replicated, may hold values from -0.09375 to 0.09375
- w_mix: bfloat16 [1024, 2], replicated, may hold values from -0.1875 to 0.1875
- ex_up: bfloat16 [8, 1024, 4096], P('expert', None, 'tensor'), may hold values from -0.1875 to 0.1875
- ex_down: bfloat16 [8, 4096, 1024], P('expert', 'tensor')
Outputs:
- out: bfloat16 [20480, 1024], P(('expert', 'tensor'))
- grad_tokens: float32 [20480, 1024], P(('expert', 'tensor'))
- grad_ln_attn: float32 [1024], replicated
- grad_qkv: float32 [3, 1024, 1024], P(None, 'expert', 'tensor')
- grad_w_out: float32 [1024, 1024], P('tensor', 'expert')
- grad_ln_mlp: float32 [1024], P('expert')
- grad_up: float32 [1024, 4096], P('expert', 'tensor')
- grad_down: float32 [4096, 1024], P('tensor', 'expert')
- grad_router: float32 [1024, 8], P('expert')
- grad_mix: float32 [1024, 2], P('expert')
- grad_ex_up: float32 [8, 1024, 4096], P('expert', None, 'tensor')
- grad_ex_down: float32 [8, 4096, 1024], P('expert', 'tensor')
The draws below stay inside these ranges and needn't reach their ends.
Inputs may be any that keep to these rules, and one draw needn't show every extreme that they name: `routes`: in each aligned block of 640 rows (the rows of one device), no expert is named by more than 112 rows, a bound that some block reaches. `parents`: entry j of a row is the parent segment of segment j. Entries 0 to 4 are 0 (the trunk and the four branches hang on the trunk); entries 5 to 12 (the leaves) name each branch 1 to 4 exactly twice.
All inputs are finite; a program needn't handle non-finite values.
Results may differ from the reference program's by a relative error of at most 0.017.
Values may be sent and summed in bfloat16 or wider, within the bound.
No kernel may reach another device: no remote copies, remote signals or barrier semaphores. Data moves between devices by JAX's collectives and lax.ppermute only.
A program may use at most 320 MiB of HBM per device.

```python
import math
import jax
import jax.numpy as jnp
import numpy as np
from jax import lax

D = 1024
HEADS = 16
HEAD_DIM = 64
FF = 4096
TRUNK = 1024
SEG = 128
SEGS = 13
QBLK = 512
EXPERTS = 8
TREE_LEN = 2560
TOK_DEV = 640
TOKENS = 20480
TREES_ALL = 8
CAP = 112


def draw_parents(key, part):
    subkeys = jax.random.split(key, TREES_ALL)
    orders = jax.vmap(lambda subkey: jax.random.permutation(subkey, SEGS - 5))(subkeys)
    leaves = (1 + orders // 2).astype(jnp.int32)
    leading = jnp.zeros((TREES_ALL, 5), dtype=jnp.int32)
    return jnp.concatenate([leading, leaves], axis=1)


def draw_ex_down(key, part):
    spread = 2.0 * EXPERTS / math.sqrt(FF)
    base = jax.random.truncated_normal(jax.random.fold_in(key, 7), -6.0, 6.0, (EXPERTS, FF, D), jnp.float32)
    return (base * spread).astype(jnp.bfloat16)


def levels(key, dims, cuts, smallest, top_value):
    level, own = 1.0, jax.random.fold_in(key, 6)
    for dim, parts in cuts:
        draws = jnp.exp(jax.random.uniform(jax.random.fold_in(own, dim), (parts,), jnp.float32, smallest / len(cuts), top_value / len(cuts)))
        level = level * jnp.repeat(draws, dims[dim] // parts).reshape([-1 if axis == dim else 1 for axis in range(len(dims))])
    return level


def deal_out(rng, own, number, rows, count, top, limit, skew):
    ranking = jax.random.permutation(rng, count)
    packed, common = shares(count, rows * top, limit, skew, True), shares(count, rows * top, limit, skew, False)
    places = jnp.arange(count)

    def named(lengths, turn):
        used = int((lengths > 0).sum())
        fixed = max(1, used // 4)
        moved = fixed + (places - fixed + turn * (used - fixed)) % max(1, count - fixed)
        return jnp.zeros((count,), jnp.int32).at[ranking[jnp.where(places < fixed, places, moved)]].set(jnp.asarray(lengths, jnp.int32))

    lengths = jnp.where(number % 4 == 0, named(packed, number // 4), named(common, number - number // 4 - 1))
    mixed = jax.random.permutation(jax.random.fold_in(own, 3), count)
    source_of, taker = mixed[0:count // 2 * 2:2], mixed[1:count // 2 * 2:2]
    room = jnp.minimum(lengths[source_of] - 1, limit - lengths[taker]) // 2
    room = jnp.where((source_of == ranking[0]) | (taker == ranking[0]) | (lengths[taker] == 0), 0, jnp.maximum(room, 0))
    moved = jax.random.randint(jax.random.fold_in(own, 4), (count // 2,), 0, 1 << 20) % (room + 1)
    lengths = lengths.at[source_of].add(-moved).at[taker].add(moved)
    members = jnp.searchsorted(jnp.cumsum(lengths), jnp.arange(rows * top), side="right").astype(jnp.int32)
    listing = members.reshape(top, rows).T
    listing = listing[jax.random.permutation(jax.random.fold_in(own, 1), rows)]
    turn = jax.random.randint(jax.random.fold_in(own, 2), (rows, 1), 0, top)
    return jnp.take_along_axis(listing, (jnp.arange(top)[None, :] + turn) % top, axis=1)


def shares(amount, total, reach, slope, full):
    weights = [(1 << 20) // math.isqrt(grade ** slope) + 1 for grade in range(1, amount + 1)]
    largest = reach if full else min(reach, max(-(-total // amount), total * weights[0] // sum(weights)))
    least = 1 if total - largest >= amount - 1 else 0
    counts, spare = [largest] + [least] * (amount - 1), total - largest - least * (amount - 1)
    while spare > 0:
        movable = [i for i in range(1, amount) if counts[i] < largest] or [i for i in range(1, amount) if counts[i] < reach]
        mass, remaining = sum([weights[i] for i in movable]), spare
        for i in movable:
            more = min(reach - counts[i], max(1, remaining * weights[i] // mass), spare)
            counts[i] = counts[i] + more
            spare = spare - more
    return np.array(counts)


def bell_draw(own_key, extent, scale, most, shards=(), held_as=jnp.bfloat16):
    values = jax.random.normal(own_key, extent, jnp.float32) * scale
    if len(shards) > 0:
        values = levels(own_key, extent, shards, -0.22, 0.18) * values
    return jnp.clip(values, min=-most, max=most).astype(held_as)


def setup_inputs(seed: int = 0) -> dict:
    key_of = jax.random.split(jax.random.key(seed), 15)
    tokens = bell_draw(key_of[0], (TOKENS, D), 1.0, 6.0, ((0, 32),))
    cotangent = bell_draw(key_of[1], (TOKENS, D), 1.0, 6.0, ((0, 32),))
    routes_keys = jax.random.split(jax.random.fold_in(key_of[2], 1), TOKENS // TOK_DEV)
    routes_turns = jax.random.permutation(jax.random.fold_in(key_of[2], 3), TOKENS // TOK_DEV)
    routes = jax.vmap(lambda own, number: deal_out(jax.random.fold_in(key_of[2], 2), own, number, TOK_DEV, EXPERTS, 1, CAP, 2))(routes_keys, routes_turns).reshape((TOKENS, 1))
    parents = draw_parents(jax.random.fold_in(key_of[14], 71), 0)
    ln_attn = jnp.clip(1.0 + 0.1 * jax.random.normal(key_of[4], (D,), jnp.float32), 0.5, 1.5)
    w_qkv = bell_draw(key_of[5], (3, D, D), D ** -0.5, 0.1875, ((2, 4),))
    w_out = bell_draw(key_of[6], (D, D), (max(4, D // 256)) ** -0.5, 3.0, ((0, 4),))
    ln_mlp = jnp.clip(1.0 + 0.1 * jax.random.normal(key_of[7], (D,), jnp.float32), 0.5, 1.5)
    w_up = bell_draw(key_of[8], (D, FF), D ** -0.5, 0.1875, ((1, 4),))
    w_down = bell_draw(key_of[9], (FF, D), FF ** -0.5, 0.09375, ((0, 4),))
    w_router = bell_draw(key_of[10], (D, EXPERTS), (4 * D) ** -0.5, 0.09375)
    w_mix = bell_draw(key_of[11], (D, 2), D ** -0.5, 0.1875)
    ex_up = bell_draw(key_of[12], (EXPERTS, D, FF), D ** -0.5, 0.1875, ((0, 8), (2, 4)))
    ex_down = draw_ex_down(jax.random.fold_in(key_of[14], 71), 0)
    return dict(tokens=tokens, cotangent=cotangent, routes=routes, parents=parents, ln_attn=ln_attn, w_qkv=w_qkv, w_out=w_out, ln_mlp=ln_mlp, w_up=w_up, w_down=w_down, w_router=w_router, w_mix=w_mix, ex_up=ex_up, ex_down=ex_down)


@jax.custom_vjp
def low(v):
    return lax.optimization_barrier(v.astype(jnp.bfloat16)).astype(jnp.float32)

@jax.custom_vjp
def low_back(v):
    return v

def low_keep(v):
    return (low(v), None)

def low_pass(kept, grad):
    return (grad,)

def back_keep(v):
    return (v, None)

def back_low(kept, grad):
    return (low(grad),)
low.defvjp(low_keep, low_pass)
low_back.defvjp(back_keep, back_low)
EPSILON = 1e-05
NEGATIVE_FILL = -1e+30
PRECISE = lax.Precision.HIGHEST

def both_round(values):
    return low(low_back(values))

def layer_norm(values, gain_vec):
    row_mean = lax.optimization_barrier(jnp.mean(values, axis=-1, keepdims=True))
    centred = values - row_mean
    row_var = lax.optimization_barrier(jnp.mean(centred * centred, axis=-1, keepdims=True))
    return centred * lax.rsqrt(row_var + EPSILON) * gain_vec

def gelu_exact(values):
    return jax.nn.gelu(values, approximate=False)

def segment_of(position):
    return jnp.where(position < TRUNK, 0, 1 + (position - TRUNK) // SEG)

def path_mask(parents_row, query_pos, key_pos):
    seg_ids = jnp.arange(SEGS, dtype=jnp.int32)
    query_seg = segment_of(query_pos)
    key_seg = segment_of(key_pos)
    parent_seg = lax.optimization_barrier(jnp.sum(jnp.where(query_seg[:, None] == seg_ids[None, :], parents_row[None, :], 0), axis=1))
    grand_seg = lax.optimization_barrier(jnp.sum(jnp.where(parent_seg[:, None] == seg_ids[None, :], parents_row[None, :], 0), axis=1))
    on_path = (key_seg[None, :] == query_seg[:, None]) | (key_seg[None, :] == parent_seg[:, None]) | (key_seg[None, :] == grand_seg[:, None])
    return on_path & (key_pos[None, :] <= query_pos[:, None])

def tree_attention(inputs):
    queries, key_rows, values, parents_row = inputs
    blocked = queries.reshape(TREE_LEN // QBLK, QBLK, HEADS, HEAD_DIM)
    starts = jnp.arange(TREE_LEN // QBLK, dtype=jnp.int32) * QBLK

    def one_block(block_pair):
        block_rows, first_row = block_pair
        allowed = path_mask(parents_row, first_row + jnp.arange(QBLK, dtype=jnp.int32), jnp.arange(TREE_LEN, dtype=jnp.int32))
        scores = low_back(jnp.einsum('qhd,khd->hqk', block_rows, key_rows, precision=PRECISE) * HEAD_DIM ** (-0.5))
        scores = jnp.where(allowed[None], scores, NEGATIVE_FILL)
        weights = jax.nn.softmax(scores, axis=-1)
        return jnp.einsum('hqk,khd->qhd', low(weights), values, precision=PRECISE)
    outputs = lax.map(jax.checkpoint(one_block), (blocked, starts))
    return outputs.reshape(TREE_LEN, HEADS, HEAD_DIM)

def forward(tokens, ln_attn, w_qkv, w_out, ln_mlp, w_up, w_down, w_router, w_mix, ex_up, ex_down, routes, parents):
    normed_one = low(layer_norm(tokens, ln_attn))
    qkv_rows = both_round(jnp.einsum('td,sdc->stc', normed_one, w_qkv, precision=PRECISE))
    shaped = qkv_rows.reshape(3, TREES_ALL, TREE_LEN, HEADS, HEAD_DIM)
    attended = lax.map(tree_attention, (shaped[0], shaped[1], shaped[2], parents))
    attended = both_round(attended.reshape(TOKENS, D))
    branch = low_back(jnp.dot(attended, w_out, precision=PRECISE))
    residual = tokens + branch
    normed_two = low(layer_norm(residual, ln_mlp))
    pre_dense = low_back(jnp.dot(normed_two, w_up, precision=PRECISE))
    dense = low_back(jnp.dot(low(gelu_exact(pre_dense)), w_down, precision=PRECISE))
    router_probs = jax.nn.softmax(low_back(jnp.dot(normed_two, w_router, precision=PRECISE)), axis=-1)
    expert_ids = routes[:, 0]
    chosen = expert_ids[:, None] == jnp.arange(EXPERTS, dtype=jnp.int32)[None, :]
    gate_prob = lax.optimization_barrier(jnp.sum(jnp.where(chosen, router_probs, 0.0), axis=1))
    mix_coef = jax.nn.softmax(low_back(jnp.dot(normed_two, w_mix, precision=PRECISE)), axis=-1)
    block_count = TOKENS // TOK_DEV
    counted = chosen.astype(jnp.int32).reshape(block_count, TOK_DEV, EXPERTS)
    position = (jnp.cumsum(counted, axis=1) - 1).reshape(TOKENS, EXPERTS)
    slot_index = lax.optimization_barrier(jnp.sum(jnp.where(chosen, position, 0), axis=1)).astype(jnp.int32)
    block_ids = (jnp.arange(TOKENS, dtype=jnp.int32) // TOK_DEV).astype(jnp.int32)
    dispatched = jnp.zeros((EXPERTS, block_count, CAP, D), dtype=normed_two.dtype)
    dispatched = dispatched.at[expert_ids, block_ids, slot_index].set(normed_two)
    expert_pre = low_back(jnp.einsum('ebcd,edf->ebcf', dispatched, ex_up, precision=PRECISE))
    expert_out = low_back(jnp.einsum('ebcf,efd->ebcd', low(gelu_exact(expert_pre)), ex_down, precision=PRECISE))
    expert_rows = expert_out[expert_ids, block_ids, slot_index]
    mixed = mix_coef[:, 0:1] * dense + (mix_coef[:, 1] * gate_prob)[:, None] * expert_rows
    return residual + mixed

def reference(tokens, cotangent, routes, parents, ln_attn, w_qkv, w_out, ln_mlp, w_up, w_down, w_router, w_mix, ex_up, ex_down):
    floats = [array.astype(jnp.float32) for array in (tokens, ln_attn, w_qkv, w_out, ln_mlp, w_up, w_down, w_router, w_mix, ex_up, ex_down)]

    def closed(*params):
        return forward(*params, routes, parents)
    result, pullback = jax.vjp(closed, *floats)
    gradients = pullback(cotangent.astype(jnp.float32))
    return (result.astype(jnp.bfloat16), gradients[0], gradients[1], gradients[2], gradients[3], gradients[4], gradients[5], gradients[6], gradients[7], gradients[8], gradients[9], gradients[10])
```

```python
import functools

import jax
import jax.numpy as jnp
from jax import lax
from jax.experimental import pallas as pl
from jax.experimental.pallas import tpu as pltpu
from jax.sharding import PartitionSpec as P

HEAD_DIM = 64
TRUNK = 1024
SEG = 128
SEGS = 13
TREE_LEN = 2560
BRANCHES = 4
FAMILY = 3 * SEG
QROWS = 256
PAIR = 2 * HEAD_DIM
NEGATIVE_FILL = -1e30
F32 = jnp.float32
BF16 = jnp.bfloat16
EPSILON = 1e-05


def norm_parts(values):
    row_mean = jnp.mean(values, axis=-1, keepdims=True)
    centred = values - row_mean
    row_var = jnp.mean(centred * centred, axis=-1, keepdims=True)
    inverse = lax.rsqrt(row_var + EPSILON)
    return (centred * inverse, inverse)


def norm_back(grad_normed, gain_vec, scaled, inverse):
    grad_scaled = grad_normed * gain_vec
    first_mean = jnp.mean(grad_scaled, axis=-1, keepdims=True)
    second = jnp.mean(grad_scaled * scaled, axis=-1, keepdims=True)
    return inverse * (grad_scaled - first_mean - scaled * second)


def gelu_exact(values):
    return jax.nn.gelu(values, approximate=False)


def gelu_slope(values):
    return (
        0.5 * (1.0 + lax.erf(values * 0.7071067811865476))
        + values * jnp.exp(-0.5 * values * values) * 0.3989422804014327
    )


def dot_nn(a, b):
    return lax.dot_general(a, b, (((1,), (0,)), ((), ())), preferred_element_type=F32)


def dot_nt(a, b):
    return lax.dot_general(a, b, (((1,), (1,)), ((), ())), preferred_element_type=F32)


def head_lanes(rows, head):
    lane = lax.broadcasted_iota(jnp.int32, rows.shape, 1)
    return jnp.where(lane // HEAD_DIM == head, rows, jnp.zeros_like(rows))


def causal(scores):
    key = lax.broadcasted_iota(jnp.int32, scores.shape, 0)
    query = lax.broadcasted_iota(jnp.int32, scores.shape, 1)
    return jnp.where(key <= query, scores, NEGATIVE_FILL)


def family_rows(leaves_ref, branch):
    def start(segment):
        return pl.multiple_of(TRUNK + (segment - 1) * SEG, SEG)

    return [start(branch + 1), start(leaves_ref[2 * branch]), start(leaves_ref[2 * branch + 1])]


def transpose_into(target_ref, source_ref, part):
    for first in range(0, TREE_LEN, 512):
        piece = source_ref[part, pl.ds(first, 512), :].astype(F32)
        target_ref[:, pl.ds(first, 512)] = piece.T.astype(BF16)


def widen(piece, first, width, fill):
    parts = []
    if first:
        parts.append(jnp.full((piece.shape[0], first), fill, piece.dtype))
    parts.append(piece)
    rest = width - first - piece.shape[1]
    if rest:
        parts.append(jnp.full((piece.shape[0], rest), fill, piece.dtype))
    return parts[0] if len(parts) == 1 else jnp.concatenate(parts, axis=1)


def trunk_groups(block):
    first = block * QROWS
    groups = [(0, first, 0, QROWS, None)] if first else []
    return groups + [(first, QROWS, 0, QROWS, "causal")]


def family_groups(starts):
    return [
        (0, TRUNK, 0, FAMILY, None),
        (starts[0], SEG, 0, FAMILY, "branch"),
        (starts[1], SEG, SEG, 2 * SEG, "causal"),
        (starts[2], SEG, 2 * SEG, FAMILY, "causal"),
    ]


def masked_scores(keys, queries, rule):
    scores = dot_nt(keys, queries)
    if rule == "causal":
        return causal(scores)
    if rule == "branch":
        return jnp.concatenate([causal(scores[:, :SEG]), scores[:, SEG:]], axis=1)
    return scores


def forward_block(qkv_ref, values_t_ref, queries, groups):
    width = queries.shape[0]
    outs, logs = [], []
    for head in range(2):
        own = head_lanes(queries, head)
        all_scores = [
            masked_scores(qkv_ref[1, pl.ds(start, size), :], own[first:last], rule)
            for start, size, first, last, rule in groups
        ]
        top = functools.reduce(
            jnp.maximum,
            [
                widen(jnp.max(s, axis=0, keepdims=True), first, width, NEGATIVE_FILL)
                for s, (_, _, first, last, _) in zip(all_scores, groups)
            ],
        )
        total, output = None, None
        for s, (start, size, first, last, _) in zip(all_scores, groups):
            weights = jnp.exp(s - top[:, first:last])
            part = widen(jnp.sum(weights, axis=0, keepdims=True), first, width, 0.0)
            values_t = values_t_ref[pl.ds(head * HEAD_DIM, HEAD_DIM), pl.ds(start, size)]
            mixed = widen(dot_nn(values_t, weights.astype(BF16)), first, width, 0.0)
            total = part if total is None else total + part
            output = mixed if output is None else output + mixed
        outs.append(output / total)
        logs.append(top + jnp.log(total))
    return jnp.concatenate(outs, axis=0).T.astype(BF16), jnp.concatenate(logs, axis=0)


def scaled_queries(qkv_ref, starts, size):
    rows = [qkv_ref[0, pl.ds(start, size), :] for start in starts]
    rows = rows[0] if len(rows) == 1 else jnp.concatenate(rows, axis=0)
    return rows * jnp.asarray(HEAD_DIM ** (-0.5), BF16)


def forward_kernel(leaves_ref, qkv_ref, out_ref, trunk_log_ref, family_log_ref, values_t_ref):
    transpose_into(values_t_ref, qkv_ref, 2)
    for block in range(TRUNK // QROWS):
        first = block * QROWS
        queries = scaled_queries(qkv_ref, [first], QROWS)
        out, logs = forward_block(qkv_ref, values_t_ref, queries, trunk_groups(block))
        out_ref[pl.ds(first, QROWS), :] = out
        trunk_log_ref[0, :, pl.ds(first, QROWS)] = logs

    def one_family(branch, carry):
        starts = family_rows(leaves_ref, branch)
        queries = scaled_queries(qkv_ref, starts, SEG)
        out, logs = forward_block(qkv_ref, values_t_ref, queries, family_groups(starts))
        for place, start in enumerate(starts):
            out_ref[pl.ds(start, SEG), :] = out[place * SEG : (place + 1) * SEG]
        family_log_ref[0, branch] = logs
        return carry

    lax.fori_loop(0, BRANCHES, one_family, 0)


def attention_forward(leaves, qkv_rows):
    width = qkv_rows.shape[2]
    pairs = width // PAIR
    return pl.pallas_call(
        forward_kernel,
        grid_spec=pltpu.PrefetchScalarGridSpec(
            num_scalar_prefetch=1,
            grid=(pairs,),
            in_specs=[pl.BlockSpec((3, TREE_LEN, PAIR), lambda p, leaves: (0, 0, p))],
            out_specs=[
                pl.BlockSpec((TREE_LEN, PAIR), lambda p, leaves: (0, p)),
                pl.BlockSpec((1, 2, TRUNK), lambda p, leaves: (p, 0, 0)),
                pl.BlockSpec((1, BRANCHES, 2, FAMILY), lambda p, leaves: (p, 0, 0, 0)),
            ],
            scratch_shapes=[pltpu.VMEM((PAIR, TREE_LEN), BF16)],
        ),
        out_shape=[
            jax.ShapeDtypeStruct((TREE_LEN, width), BF16),
            jax.ShapeDtypeStruct((pairs, 2, TRUNK), F32),
            jax.ShapeDtypeStruct((pairs, BRANCHES, 2, FAMILY), F32),
        ],
        name="tree_attention",
    )(leaves, qkv_rows)


def backward_block(qkv_ref, keys_t_ref, queries, grads, outs, logs, groups):
    products = grads.astype(F32) * outs.astype(F32)
    products_t = products.T
    key_ds = [[] for _ in groups]
    value_ws = [[] for _ in groups]
    own_q, own_g, query_grads = [], [], []
    for head in range(2):
        own = head_lanes(queries, head)
        own_grads = head_lanes(grads, head)
        own_q.append(own)
        own_g.append(own_grads)
        inner = jnp.sum(
            products_t[head * HEAD_DIM : (head + 1) * HEAD_DIM], axis=0, keepdims=True
        )
        log = logs[head : head + 1]
        query_grad = None
        for place, (start, size, first, last, rule) in enumerate(groups):
            scores = masked_scores(qkv_ref[1, pl.ds(start, size), :], own[first:last], rule)
            weights = jnp.exp(scores - log[:, first:last])
            grad_weights = dot_nt(qkv_ref[2, pl.ds(start, size), :], own_grads[first:last])
            grad_scores = (weights * (grad_weights - inner[:, first:last])).astype(BF16)
            keys_t = keys_t_ref[pl.ds(head * HEAD_DIM, HEAD_DIM), pl.ds(start, size)]
            part = widen(dot_nn(keys_t, grad_scores), first, queries.shape[0], 0.0)
            query_grad = part if query_grad is None else query_grad + part
            key_ds[place].append(grad_scores)
            value_ws[place].append(weights.astype(BF16))
        query_grads.append(query_grad)
    grad_query = (jnp.concatenate(query_grads, axis=0) * HEAD_DIM ** (-0.5)).T.astype(BF16)
    key_grads, value_grads = [], []
    for place, (start, size, first, last, rule) in enumerate(groups):
        stacked_q = jnp.concatenate([own_q[0][first:last], own_q[1][first:last]], axis=0)
        stacked_g = jnp.concatenate([own_g[0][first:last], own_g[1][first:last]], axis=0)
        key_grads.append(dot_nn(jnp.concatenate(key_ds[place], axis=1), stacked_q))
        value_grads.append(dot_nn(jnp.concatenate(value_ws[place], axis=1), stacked_g))
    return grad_query, key_grads, value_grads


def backward_kernel(
    leaves_ref,
    qkv_ref,
    grads_ref,
    outs_ref,
    trunk_log_ref,
    family_log_ref,
    result_ref,
    keys_t_ref,
    trunk_keys_ref,
    trunk_values_ref,
):
    transpose_into(keys_t_ref, qkv_ref, 1)
    trunk_keys_ref[...] = jnp.zeros_like(trunk_keys_ref)
    trunk_values_ref[...] = jnp.zeros_like(trunk_values_ref)
    for block in range(TRUNK // QROWS):
        first = block * QROWS
        rows = pl.ds(first, QROWS)
        groups = trunk_groups(block)
        grad_query, key_grads, value_grads = backward_block(
            qkv_ref,
            keys_t_ref,
            scaled_queries(qkv_ref, [first], QROWS),
            grads_ref[rows, :],
            outs_ref[rows, :],
            trunk_log_ref[0, :, rows],
            groups,
        )
        result_ref[0, rows, :] = grad_query
        for (start, size, _, _, _), key_grad, value_grad in zip(groups, key_grads, value_grads):
            trunk_keys_ref[pl.ds(start, size), :] += key_grad
            trunk_values_ref[pl.ds(start, size), :] += value_grad

    def one_family(branch, carry):
        starts = family_rows(leaves_ref, branch)
        groups = family_groups(starts)
        grad_query, key_grads, value_grads = backward_block(
            qkv_ref,
            keys_t_ref,
            scaled_queries(qkv_ref, starts, SEG),
            jnp.concatenate([grads_ref[pl.ds(start, SEG), :] for start in starts], axis=0),
            jnp.concatenate([outs_ref[pl.ds(start, SEG), :] for start in starts], axis=0),
            family_log_ref[0, branch],
            groups,
        )
        trunk_keys_ref[...] += key_grads[0]
        trunk_values_ref[...] += value_grads[0]
        for place, start in enumerate(starts):
            rows = pl.ds(start, SEG)
            result_ref[0, rows, :] = grad_query[place * SEG : (place + 1) * SEG]
            result_ref[1, rows, :] = key_grads[1 + place].astype(BF16)
            result_ref[2, rows, :] = value_grads[1 + place].astype(BF16)
        return carry

    lax.fori_loop(0, BRANCHES, one_family, 0)
    result_ref[1, pl.ds(0, TRUNK), :] = trunk_keys_ref[...].astype(BF16)
    result_ref[2, pl.ds(0, TRUNK), :] = trunk_values_ref[...].astype(BF16)


def attention_backward(leaves, qkv_rows, grads, outs, trunk_log, family_log):
    width = qkv_rows.shape[2]
    pairs = width // PAIR
    whole = pl.BlockSpec((3, TREE_LEN, PAIR), lambda p, leaves: (0, 0, p))
    rows = pl.BlockSpec((TREE_LEN, PAIR), lambda p, leaves: (0, p))
    return pl.pallas_call(
        backward_kernel,
        grid_spec=pltpu.PrefetchScalarGridSpec(
            num_scalar_prefetch=1,
            grid=(pairs,),
            in_specs=[
                whole,
                rows,
                rows,
                pl.BlockSpec((1, 2, TRUNK), lambda p, leaves: (p, 0, 0)),
                pl.BlockSpec((1, BRANCHES, 2, FAMILY), lambda p, leaves: (p, 0, 0, 0)),
            ],
            out_specs=whole,
            scratch_shapes=[
                pltpu.VMEM((PAIR, TREE_LEN), BF16),
                pltpu.VMEM((TRUNK, PAIR), F32),
                pltpu.VMEM((TRUNK, PAIR), F32),
            ],
        ),
        out_shape=jax.ShapeDtypeStruct(qkv_rows.shape, BF16),
        name="tree_attention_back",
    )(leaves, qkv_rows, grads, outs, trunk_log, family_log)


def leaf_order(parents_row):
    first_leaf = BRANCHES + 1
    leaf_parents = parents_row[first_leaf:]
    segments = first_leaf + jnp.arange(leaf_parents.shape[0], dtype=jnp.int32)
    same = leaf_parents[:, None] == leaf_parents[None, :]
    later = segments[None, :] < segments[:, None]
    place = 2 * (leaf_parents - 1) + jnp.sum(jnp.where(same & later, 1, 0), axis=1)
    slots = jnp.arange(2 * BRANCHES, dtype=jnp.int32)
    return jnp.sum(jnp.where(slots[:, None] == place[None, :], segments[None, :], 0), axis=1)


def to_owners(values, expert_ids, quarter, slot_index, experts, quarters, capacity):
    width = values.shape[1]
    outgoing = jnp.zeros((experts, quarters, capacity, width), jnp.bfloat16)
    outgoing = outgoing.at[expert_ids, quarter, slot_index].set(values)
    return lax.all_to_all(outgoing, "expert", split_axis=0, concat_axis=0, tiled=True)


def to_sources(parts):
    return lax.all_to_all(
        parts.astype(jnp.bfloat16), "expert", split_axis=0, concat_axis=0, tiled=True
    ).astype(parts.dtype)


def per_device(
    tokens,
    cotangent,
    routes,
    parents,
    ln_attn,
    w_qkv,
    w_out,
    ln_mlp,
    w_up,
    w_down,
    w_router,
    w_mix,
    ex_up,
    ex_down,
):
    tok_dev = tokens.shape[0]
    model_width = tokens.shape[1]
    quarters = lax.axis_size("tensor")
    own_start = lax.axis_index("tensor") * tok_dev
    group_rows = tok_dev * quarters
    experts = w_router.shape[1]
    capacity = max(2, tok_dev * 7 // (5 * experts))
    gathered = lax.all_gather(tokens, "tensor", axis=0, tiled=True)
    scaled_one, inverse_one = norm_parts(gathered.astype(jnp.float32))
    normed_one = (scaled_one * ln_attn).astype(jnp.bfloat16)
    qkv_rows = jnp.einsum(
        "td,sdc->stc", normed_one, w_qkv, preferred_element_type=jnp.float32
    ).astype(jnp.bfloat16)

    leaves = leaf_order(parents[0])
    attended, trunk_log, family_log = attention_forward(leaves, qkv_rows)
    residual = tokens.astype(jnp.float32) + lax.psum_scatter(
        jnp.dot(attended, w_out, preferred_element_type=jnp.float32),
        "tensor",
        scatter_dimension=0,
        tiled=True,
    )
    residual_all = lax.all_gather(residual, "tensor", axis=0, tiled=True)
    scaled_two, inverse_two = norm_parts(residual_all)
    normed_two = (scaled_two * ln_mlp).astype(jnp.bfloat16)
    pre_dense = jnp.dot(normed_two, w_up, preferred_element_type=jnp.float32)
    active = gelu_exact(pre_dense).astype(jnp.bfloat16)
    dense_part = jnp.dot(active, w_down, preferred_element_type=jnp.float32)
    router_probs = jax.nn.softmax(
        jnp.dot(normed_two, w_router, preferred_element_type=jnp.float32), axis=-1
    )
    expert_ids = routes[:, 0]
    chosen = expert_ids[:, None] == jnp.arange(experts, dtype=jnp.int32)[None, :]
    gate_prob = jnp.sum(jnp.where(chosen, router_probs, 0.0), axis=1)
    mix_coef = jax.nn.softmax(
        jnp.dot(normed_two, w_mix, preferred_element_type=jnp.float32), axis=-1
    )
    counted = chosen.astype(jnp.int32).reshape(quarters, tok_dev, experts)
    position = (jnp.cumsum(counted, axis=1) - 1).reshape(group_rows, experts)
    slot_index = jnp.sum(jnp.where(chosen, position, 0), axis=1)
    quarter = jnp.arange(group_rows, dtype=jnp.int32) // tok_dev
    arrived = to_owners(normed_two, expert_ids, quarter, slot_index, experts, quarters, capacity)
    flat_rows = arrived.reshape(-1, model_width)
    expert_pre = jnp.dot(flat_rows, ex_up[0], preferred_element_type=jnp.float32)
    expert_active = gelu_exact(expert_pre).astype(jnp.bfloat16)
    expert_part = jnp.dot(expert_active, ex_down[0], preferred_element_type=jnp.float32).reshape(
        arrived.shape
    )
    returned = to_sources(expert_part)
    expert_weight = mix_coef[:, 1] * gate_prob
    expert_rows = returned[expert_ids, quarter, slot_index]
    extra_term = 0.0
    dense_coef = mix_coef[:, 0]
    mixed = (
        lax.psum_scatter(
            (dense_coef[:, None] * dense_part + expert_weight[:, None] * expert_rows).astype(
                jnp.bfloat16
            ),
            "tensor",
            scatter_dimension=0,
            tiled=True,
        ).astype(jnp.float32)
        + extra_term
    )
    out = (residual + mixed).astype(jnp.bfloat16)
    grad_all = lax.all_gather(cotangent, "tensor", axis=0, tiled=True).astype(jnp.float32)
    grad_dense = (mix_coef[:, 0:1] * grad_all).astype(jnp.bfloat16)
    grad_down = jnp.einsum("gf,gd->fd", active, grad_dense, preferred_element_type=jnp.float32)
    grad_active = jnp.einsum("gd,fd->gf", grad_dense, w_down, preferred_element_type=jnp.float32)
    grad_pre = (grad_active * gelu_slope(pre_dense)).astype(jnp.bfloat16)
    grad_up = jnp.einsum("gd,gf->df", normed_two, grad_pre, preferred_element_type=jnp.float32)
    grad_normed_two = jnp.einsum("gf,df->gd", grad_pre, w_up, preferred_element_type=jnp.float32)
    dense_dot = jnp.sum(grad_all * dense_part, axis=1)
    grad_expert = (expert_weight[:, None] * grad_all).astype(jnp.bfloat16)
    arrived_grad = to_owners(
        grad_expert, expert_ids, quarter, slot_index, experts, quarters, capacity
    )
    flat_grad = arrived_grad.reshape(-1, model_width)
    grad_ex_down = jnp.einsum(
        "rf,rd->fd", expert_active, flat_grad, preferred_element_type=jnp.float32
    )[None]
    grad_ex_active = jnp.einsum(
        "rd,fd->rf", flat_grad, ex_down[0], preferred_element_type=jnp.float32
    )
    grad_ex_pre = (grad_ex_active * gelu_slope(expert_pre)).astype(jnp.bfloat16)
    grad_ex_up = jnp.einsum(
        "rd,rf->df", flat_rows, grad_ex_pre, preferred_element_type=jnp.float32
    )[None]
    grad_ex_rows = jnp.einsum(
        "rf,df->rd", grad_ex_pre, ex_up[0], preferred_element_type=jnp.float32
    ).reshape(arrived.shape)
    grad_back = to_sources(grad_ex_rows)
    grad_normed_two = grad_normed_two + grad_back[expert_ids, quarter, slot_index]
    expert_dot = jnp.sum(grad_all * expert_rows, axis=1)
    row_dots = jnp.stack([dense_dot, expert_dot], axis=1)
    grad_normed_two, row_dots = (
        lax.psum(grad_normed_two.astype(jnp.bfloat16), "tensor").astype(jnp.float32),
        lax.psum(row_dots.astype(jnp.bfloat16), "tensor").astype(jnp.float32),
    )
    mix_grad = jnp.stack([row_dots[:, 0], gate_prob * row_dots[:, 1]], axis=1)
    grad_mix_logits = (
        mix_coef * (mix_grad - jnp.sum(mix_coef * mix_grad, axis=1, keepdims=True))
    ).astype(jnp.bfloat16)
    grad_gate = mix_coef[:, 1] * row_dots[:, 1]
    grad_router_logits = (
        router_probs
        * (jnp.where(chosen, grad_gate[:, None], 0.0) - (gate_prob * grad_gate)[:, None])
    ).astype(jnp.bfloat16)
    grad_normed_two = grad_normed_two + jnp.einsum(
        "ge,de->gd", grad_router_logits, w_router, preferred_element_type=jnp.float32
    )
    grad_normed_two = grad_normed_two + jnp.einsum(
        "gm,dm->gd", grad_mix_logits, w_mix, preferred_element_type=jnp.float32
    )
    grad_router = jnp.einsum(
        "gd,ge->de", normed_two, grad_router_logits, preferred_element_type=jnp.float32
    )
    grad_mix = jnp.einsum(
        "gd,gm->dm", normed_two, grad_mix_logits, preferred_element_type=jnp.float32
    )
    grad_ln_mlp = jnp.sum(grad_normed_two * scaled_two, axis=0)
    grad_residual = grad_all + norm_back(grad_normed_two, ln_mlp, scaled_two, inverse_two)
    grad_branch = grad_residual.astype(jnp.bfloat16)
    grad_w_out = jnp.einsum("gc,gd->cd", attended, grad_branch, preferred_element_type=jnp.float32)
    grad_attended = jnp.einsum(
        "gd,cd->gc", grad_branch, w_out, preferred_element_type=jnp.float32
    ).astype(jnp.bfloat16)

    grad_qkv_rows = attention_backward(
        leaves, qkv_rows, grad_attended, attended, trunk_log, family_log
    )
    grad_w_qkv = jnp.einsum(
        "gd,sgc->sdc", normed_one, grad_qkv_rows, preferred_element_type=jnp.float32
    )
    grad_normed_one = jnp.einsum(
        "sgc,sdc->gd", grad_qkv_rows, w_qkv, preferred_element_type=jnp.float32
    )
    part_gain = jnp.sum(grad_normed_one * scaled_one, axis=0)
    grad_normed_own = lax.psum_scatter(
        grad_normed_one.astype(jnp.bfloat16), "tensor", scatter_dimension=0, tiled=True
    ).astype(jnp.float32)
    own_scaled = lax.dynamic_slice_in_dim(scaled_one, own_start, tok_dev, 0)
    own_inverse = lax.dynamic_slice_in_dim(inverse_one, own_start, tok_dev, 0)
    own_residual_grad = lax.dynamic_slice_in_dim(grad_residual, own_start, tok_dev, 0)
    grad_tokens = own_residual_grad + norm_back(grad_normed_own, ln_attn, own_scaled, own_inverse)
    summed_grads = (
        lax.psum_scatter(grad_w_qkv, "expert", scatter_dimension=1, tiled=True),
        lax.psum_scatter(grad_w_out, "expert", scatter_dimension=1, tiled=True),
        lax.psum_scatter(grad_ln_mlp, "expert", scatter_dimension=0, tiled=True),
        lax.psum_scatter(grad_up, "expert", scatter_dimension=0, tiled=True),
        lax.psum_scatter(grad_down, "expert", scatter_dimension=1, tiled=True),
        lax.psum_scatter(grad_router, "expert", scatter_dimension=0, tiled=True),
        lax.psum_scatter(grad_mix, "expert", scatter_dimension=0, tiled=True),
    )
    grad_ln_attn = lax.psum(part_gain, ("expert", "tensor"))
    return (
        out,
        grad_tokens,
        grad_ln_attn,
        summed_grads[0],
        summed_grads[1],
        summed_grads[2],
        summed_grads[3],
        summed_grads[4],
        summed_grads[5],
        summed_grads[6],
        grad_ex_up,
        grad_ex_down,
    )


def solution(mesh):
    return jax.shard_map(
        per_device,
        mesh=mesh,
        in_specs=(
            P(("expert", "tensor"), None),
            P(("expert", "tensor"), None),
            P("expert", None),
            P("expert", None),
            P(),
            P(None, None, "tensor"),
            P("tensor", None),
            P(),
            P(None, "tensor"),
            P("tensor", None),
            P(),
            P(),
            P("expert", None, "tensor"),
            P("expert", "tensor", None),
        ),
        out_specs=(
            P(("expert", "tensor"), None),
            P(("expert", "tensor"), None),
            P(),
            P(None, "expert", "tensor"),
            P("tensor", "expert"),
            P("expert"),
            P("expert", "tensor"),
            P("tensor", "expert"),
            P("expert", None),
            P("expert", None),
            P("expert", None, "tensor"),
            P("expert", "tensor", None),
        ),
        check_vma=False,
    )
```

```python
import functools

import jax
import jax.numpy as jnp
from jax import lax
from jax.experimental import pallas as pl
from jax.experimental.pallas import tpu as pltpu
from jax.sharding import PartitionSpec as P

HEAD_DIM = 64
TRUNK = 1024
SEG = 128
SEGS = 13
TREE_LEN = 2560
BRANCHES = 4
FAMILY = 3 * SEG
QROWS = 256
PAIR = 2 * HEAD_DIM
NEGATIVE_FILL = -1e30
F32 = jnp.float32
BF16 = jnp.bfloat16
EPSILON = 1e-05


def dot_nn(a, b):
    return lax.dot_general(a, b, (((1,), (0,)), ((), ())), preferred_element_type=F32)


def dot_nt(a, b):
    return lax.dot_general(a, b, (((1,), (1,)), ((), ())), preferred_element_type=F32)


def head_lanes(rows, head):
    lane = lax.broadcasted_iota(jnp.int32, rows.shape, 1)
    return jnp.where(lane // HEAD_DIM == head, rows, jnp.zeros_like(rows))


def causal(scores):
    key = lax.broadcasted_iota(jnp.int32, scores.shape, 0)
    query = lax.broadcasted_iota(jnp.int32, scores.shape, 1)
    return jnp.where(key <= query, scores, NEGATIVE_FILL)


def family_rows(leaves_ref, branch):
    def start(segment):
        return pl.multiple_of(TRUNK + (segment - 1) * SEG, SEG)

    return [start(branch + 1), start(leaves_ref[2 * branch]), start(leaves_ref[2 * branch + 1])]


def transpose_into(target_ref, source_ref, part):
    for first in range(0, TREE_LEN, 512):
        piece = source_ref[part, pl.ds(first, 512), :].astype(F32)
        target_ref[:, pl.ds(first, 512)] = piece.T.astype(BF16)


def widen(piece, first, width, fill):
    parts = []
    if first:
        parts.append(jnp.full((piece.shape[0], first), fill, piece.dtype))
    parts.append(piece)
    rest = width - first - piece.shape[1]
    if rest:
        parts.append(jnp.full((piece.shape[0], rest), fill, piece.dtype))
    return parts[0] if len(parts) == 1 else jnp.concatenate(parts, axis=1)


def trunk_groups(block):
    first = block * QROWS
    groups = [(0, first, 0, QROWS, None)] if first else []
    return groups + [(first, QROWS, 0, QROWS, "causal")]


def family_groups(starts):
    return [
        (0, TRUNK, 0, FAMILY, None),
        (starts[0], SEG, 0, FAMILY, "branch"),
        (starts[1], SEG, SEG, 2 * SEG, "causal"),
        (starts[2], SEG, 2 * SEG, FAMILY, "causal"),
    ]


def masked_scores(keys, queries, rule):
    scores = dot_nt(keys, queries)
    if rule == "causal":
        return causal(scores)
    if rule == "branch":
        return jnp.concatenate([causal(scores[:, :SEG]), scores[:, SEG:]], axis=1)
    return scores


def forward_block(qkv_ref, values_t_ref, queries, groups):
    width = queries.shape[0]
    outs, logs = [], []
    for head in range(2):
        own = head_lanes(queries, head)
        all_scores = [
            masked_scores(qkv_ref[1, pl.ds(start, size), :], own[first:last], rule)
            for start, size, first, last, rule in groups
        ]
        top = functools.reduce(
            jnp.maximum,
            [
                widen(jnp.max(s, axis=0, keepdims=True), first, width, NEGATIVE_FILL)
                for s, (_, _, first, last, _) in zip(all_scores, groups)
            ],
        )
        total, output = None, None
        for s, (start, size, first, last, _) in zip(all_scores, groups):
            weights = jnp.exp(s - top[:, first:last])
            part = widen(jnp.sum(weights, axis=0, keepdims=True), first, width, 0.0)
            values_t = values_t_ref[pl.ds(head * HEAD_DIM, HEAD_DIM), pl.ds(start, size)]
            mixed = widen(dot_nn(values_t, weights.astype(BF16)), first, width, 0.0)
            total = part if total is None else total + part
            output = mixed if output is None else output + mixed
        outs.append(output / total)
        logs.append(top + jnp.log(total))
    return jnp.concatenate(outs, axis=0).T.astype(BF16), jnp.concatenate(logs, axis=0)


def scaled_queries(qkv_ref, starts, size):
    rows = [qkv_ref[0, pl.ds(start, size), :] for start in starts]
    rows = rows[0] if len(rows) == 1 else jnp.concatenate(rows, axis=0)
    return rows * jnp.asarray(HEAD_DIM ** (-0.5), BF16)


def forward_kernel(leaves_ref, qkv_ref, out_ref, trunk_log_ref, family_log_ref, values_t_ref):
    transpose_into(values_t_ref, qkv_ref, 2)
    for block in range(TRUNK // QROWS):
        first = block * QROWS
        queries = scaled_queries(qkv_ref, [first], QROWS)
        out, logs = forward_block(qkv_ref, values_t_ref, queries, trunk_groups(block))
        out_ref[pl.ds(first, QROWS), :] = out
        trunk_log_ref[0, :, pl.ds(first, QROWS)] = logs

    def one_family(branch, carry):
        starts = family_rows(leaves_ref, branch)
        queries = scaled_queries(qkv_ref, starts, SEG)
        out, logs = forward_block(qkv_ref, values_t_ref, queries, family_groups(starts))
        for place, start in enumerate(starts):
            out_ref[pl.ds(start, SEG), :] = out[place * SEG : (place + 1) * SEG]
        family_log_ref[0, branch] = logs
        return carry

    lax.fori_loop(0, BRANCHES, one_family, 0)


def attention_forward(leaves, qkv_rows):
    width = qkv_rows.shape[2]
    pairs = width // PAIR
    return pl.pallas_call(
        forward_kernel,
        grid_spec=pltpu.PrefetchScalarGridSpec(
            num_scalar_prefetch=1,
            grid=(pairs,),
            in_specs=[pl.BlockSpec((3, TREE_LEN, PAIR), lambda p, leaves: (0, 0, p))],
            out_specs=[
                pl.BlockSpec((TREE_LEN, PAIR), lambda p, leaves: (0, p)),
                pl.BlockSpec((1, 2, TRUNK), lambda p, leaves: (p, 0, 0)),
                pl.BlockSpec((1, BRANCHES, 2, FAMILY), lambda p, leaves: (p, 0, 0, 0)),
            ],
            scratch_shapes=[pltpu.VMEM((PAIR, TREE_LEN), BF16)],
        ),
        out_shape=[
            jax.ShapeDtypeStruct((TREE_LEN, width), BF16),
            jax.ShapeDtypeStruct((pairs, 2, TRUNK), F32),
            jax.ShapeDtypeStruct((pairs, BRANCHES, 2, FAMILY), F32),
        ],
        name="tree_attention",
    )(leaves, qkv_rows)


def backward_block(qkv_ref, keys_t_ref, queries, grads, outs, logs, groups):
    products = grads.astype(F32) * outs.astype(F32)
    products_t = products.T
    key_ds = [[] for _ in groups]
    value_ws = [[] for _ in groups]
    own_q, own_g, query_grads = [], [], []
    for head in range(2):
        own = head_lanes(queries, head)
        own_grads = head_lanes(grads, head)
        own_q.append(own)
        own_g.append(own_grads)
        inner = jnp.sum(
            products_t[head * HEAD_DIM : (head + 1) * HEAD_DIM], axis=0, keepdims=True
        )
        log = logs[head : head + 1]
        query_grad = None
        for place, (start, size, first, last, rule) in enumerate(groups):
            scores = masked_scores(qkv_ref[1, pl.ds(start, size), :], own[first:last], rule)
            weights = jnp.exp(scores - log[:, first:last])
            grad_weights = dot_nt(qkv_ref[2, pl.ds(start, size), :], own_grads[first:last])
            grad_scores = (weights * (grad_weights - inner[:, first:last])).astype(BF16)
            keys_t = keys_t_ref[pl.ds(head * HEAD_DIM, HEAD_DIM), pl.ds(start, size)]
            part = widen(dot_nn(keys_t, grad_scores), first, queries.shape[0], 0.0)
            query_grad = part if query_grad is None else query_grad + part
            key_ds[place].append(grad_scores)
            value_ws[place].append(weights.astype(BF16))
        query_grads.append(query_grad)
    grad_query = (jnp.concatenate(query_grads, axis=0) * HEAD_DIM ** (-0.5)).T.astype(BF16)
    key_grads, value_grads = [], []
    for place, (start, size, first, last, rule) in enumerate(groups):
        stacked_q = jnp.concatenate([own_q[0][first:last], own_q[1][first:last]], axis=0)
        stacked_g = jnp.concatenate([own_g[0][first:last], own_g[1][first:last]], axis=0)
        key_grads.append(dot_nn(jnp.concatenate(key_ds[place], axis=1), stacked_q))
        value_grads.append(dot_nn(jnp.concatenate(value_ws[place], axis=1), stacked_g))
    return grad_query, key_grads, value_grads


def backward_kernel(
    leaves_ref,
    qkv_ref,
    grads_ref,
    outs_ref,
    trunk_log_ref,
    family_log_ref,
    result_ref,
    keys_t_ref,
    trunk_keys_ref,
    trunk_values_ref,
):
    transpose_into(keys_t_ref, qkv_ref, 1)
    trunk_keys_ref[...] = jnp.zeros_like(trunk_keys_ref)
    trunk_values_ref[...] = jnp.zeros_like(trunk_values_ref)
    for block in range(TRUNK // QROWS):
        first = block * QROWS
        rows = pl.ds(first, QROWS)
        groups = trunk_groups(block)
        grad_query, key_grads, value_grads = backward_block(
            qkv_ref,
            keys_t_ref,
            scaled_queries(qkv_ref, [first], QROWS),
            grads_ref[rows, :],
            outs_ref[rows, :],
            trunk_log_ref[0, :, rows],
            groups,
        )
        result_ref[0, rows, :] = grad_query
        for (start, size, _, _, _), key_grad, value_grad in zip(groups, key_grads, value_grads):
            trunk_keys_ref[pl.ds(start, size), :] += key_grad
            trunk_values_ref[pl.ds(start, size), :] += value_grad

    def one_family(branch, carry):
        starts = family_rows(leaves_ref, branch)
        groups = family_groups(starts)
        grad_query, key_grads, value_grads = backward_block(
            qkv_ref,
            keys_t_ref,
            scaled_queries(qkv_ref, starts, SEG),
            jnp.concatenate([grads_ref[pl.ds(start, SEG), :] for start in starts], axis=0),
            jnp.concatenate([outs_ref[pl.ds(start, SEG), :] for start in starts], axis=0),
            family_log_ref[0, branch],
            groups,
        )
        trunk_keys_ref[...] += key_grads[0]
        trunk_values_ref[...] += value_grads[0]
        for place, start in enumerate(starts):
            rows = pl.ds(start, SEG)
            result_ref[0, rows, :] = grad_query[place * SEG : (place + 1) * SEG]
            result_ref[1, rows, :] = key_grads[1 + place].astype(BF16)
            result_ref[2, rows, :] = value_grads[1 + place].astype(BF16)
        return carry

    lax.fori_loop(0, BRANCHES, one_family, 0)
    result_ref[1, pl.ds(0, TRUNK), :] = trunk_keys_ref[...].astype(BF16)
    result_ref[2, pl.ds(0, TRUNK), :] = trunk_values_ref[...].astype(BF16)


def attention_backward(leaves, qkv_rows, grads, outs, trunk_log, family_log):
    width = qkv_rows.shape[2]
    pairs = width // PAIR
    whole = pl.BlockSpec((3, TREE_LEN, PAIR), lambda p, leaves: (0, 0, p))
    rows = pl.BlockSpec((TREE_LEN, PAIR), lambda p, leaves: (0, p))
    return pl.pallas_call(
        backward_kernel,
        grid_spec=pltpu.PrefetchScalarGridSpec(
            num_scalar_prefetch=1,
            grid=(pairs,),
            in_specs=[
                whole,
                rows,
                rows,
                pl.BlockSpec((1, 2, TRUNK), lambda p, leaves: (p, 0, 0)),
                pl.BlockSpec((1, BRANCHES, 2, FAMILY), lambda p, leaves: (p, 0, 0, 0)),
            ],
            out_specs=whole,
            scratch_shapes=[
                pltpu.VMEM((PAIR, TREE_LEN), BF16),
                pltpu.VMEM((TRUNK, PAIR), F32),
                pltpu.VMEM((TRUNK, PAIR), F32),
            ],
        ),
        out_shape=jax.ShapeDtypeStruct(qkv_rows.shape, BF16),
        name="tree_attention_back",
    )(leaves, qkv_rows, grads, outs, trunk_log, family_log)


def leaf_order(parents_row):
    first_leaf = BRANCHES + 1
    leaf_parents = parents_row[first_leaf:]
    segments = first_leaf + jnp.arange(leaf_parents.shape[0], dtype=jnp.int32)
    same = leaf_parents[:, None] == leaf_parents[None, :]
    later = segments[None, :] < segments[:, None]
    place = 2 * (leaf_parents - 1) + jnp.sum(jnp.where(same & later, 1, 0), axis=1)
    slots = jnp.arange(2 * BRANCHES, dtype=jnp.int32)
    return jnp.sum(jnp.where(slots[:, None] == place[None, :], segments[None, :], 0), axis=1)


def gates(logits, experts, expert):
    lane = lax.broadcasted_iota(jnp.int32, logits.shape, 1)
    first, second = logits[:, experts : experts + 1], logits[:, experts + 1 : experts + 2]
    top = jnp.maximum(first, second)
    first, second = jnp.exp(first - top), jnp.exp(second - top)
    total = first + second
    first, second = first / total, second / total
    if expert is None:
        return lane, first, second, None, None
    routed = jnp.where(lane < experts, logits, NEGATIVE_FILL)
    raised = jnp.exp(routed - jnp.max(routed, axis=1, keepdims=True))
    probs = raised / jnp.sum(raised, axis=1, keepdims=True)
    gate = jnp.sum(jnp.where(lane == expert, probs, 0.0), axis=1, keepdims=True)
    return lane, first, second, probs, gate


def feed_kernel(experts, routed, expert_ref, xa_ref, xb_ref, ga_ref, gb_ref, head_ref, up_ref, down_ref,
                out_ref, back_ref, active_ref, pre_ref, grad_ref, head_grad_ref):
    step = pl.program_id(0)
    early = step < pl.num_programs(0) // 2
    rows = jnp.where(early, xa_ref[...], xb_ref[...])
    grads = jnp.where(early, ga_ref[...], gb_ref[...]).astype(F32)
    logits = dot_nn(rows, head_ref[...])
    expert = expert_ref[0] if routed else None
    lane, first, second, probs, gate = gates(logits, experts, expert)
    coef = second * gate if routed else first
    weighted = (coef * grads).astype(BF16)
    grad_ref[...] = weighted
    pre = dot_nn(rows, up_ref[...])
    grad_active = dot_nt(weighted, down_ref[...])
    cumulative = 0.5 + 0.5 * lax.erf(pre * 0.7071067811865476)
    slope = cumulative + pre * jnp.exp(-0.5 * pre * pre) * 0.3989422804014327
    active = (pre * cumulative).astype(BF16)
    active_ref[...] = active
    grad_pre = (grad_active * slope).astype(BF16)
    pre_ref[...] = grad_pre
    out = dot_nn(active, down_ref[...])
    out_ref[...] = (coef * out).astype(BF16)
    inner = jnp.sum(grads * out, axis=1, keepdims=True)
    swing = first * second * inner
    if routed:
        swing = -gate * swing
    grad_logits = jnp.where(lane == experts, swing, jnp.where(lane == experts + 1, -swing, 0.0))
    if routed:
        picked = jnp.where(lane == expert, 1.0, 0.0) - gate
        grad_logits = grad_logits + jnp.where(lane < experts, probs * picked * (second * inner), 0.0)
    back = dot_nt(grad_pre, up_ref[...]) + dot_nt(grad_logits.astype(BF16), head_ref[...])
    back_ref[...] = back.astype(BF16)

    @pl.when(step == 0)
    def _():
        head_grad_ref[...] = jnp.zeros_like(head_grad_ref)

    head_grad_ref[...] += dot_nn(grad_logits.T.astype(BF16), rows)


def feed(xa, xb, ga, gb, head, up, down, experts, expert, size):
    total = 2 * xa.shape[0]
    width, hidden = up.shape
    steps = total // size
    half = steps // 2
    lanes = head.shape[1]
    routed = expert is not None
    pick = jnp.reshape(expert, (1,)) if routed else jnp.zeros((1,), jnp.int32)
    early = pl.BlockSpec((size, width), lambda i, pick: (jnp.minimum(i, half - 1), 0))
    late = pl.BlockSpec((size, width), lambda i, pick: (jnp.maximum(i - half, 0), 0))

    def held(shape):
        return pl.BlockSpec(shape, lambda i, pick: (0, 0), pipeline_mode=pl.Buffered(1))

    wide = pl.BlockSpec((size, width), lambda i, pick: (i, 0))
    deep = pl.BlockSpec((size, hidden), lambda i, pick: (i, 0))
    return pl.pallas_call(
        functools.partial(feed_kernel, experts, routed),
        grid_spec=pltpu.PrefetchScalarGridSpec(
            num_scalar_prefetch=1,
            grid=(steps,),
            in_specs=[early, late, early, late, held((width, lanes)), held((width, hidden)), held((hidden, width))],
            out_specs=[wide, wide, deep, deep, wide, pl.BlockSpec((lanes, width), lambda i, pick: (0, 0))],
        ),
        out_shape=[
            jax.ShapeDtypeStruct((total, width), BF16),
            jax.ShapeDtypeStruct((total, width), BF16),
            jax.ShapeDtypeStruct((total, hidden), BF16),
            jax.ShapeDtypeStruct((total, hidden), BF16),
            jax.ShapeDtypeStruct((total, width), BF16),
            jax.ShapeDtypeStruct((lanes, width), F32),
        ],
        compiler_params=pltpu.CompilerParams(vmem_limit_bytes=60 * 1024 * 1024),
        name="feed_routed" if routed else "feed_dense",
    )(pick, xa, xb, ga, gb, head, up, down)


LANES = 128
DIRECT = 8


def norm_parts(values):
    row_mean = jnp.mean(values, axis=-1, keepdims=True)
    centred = values - row_mean
    row_var = jnp.mean(centred * centred, axis=-1, keepdims=True)
    inverse = lax.rsqrt(row_var + EPSILON)
    return (centred * inverse, inverse)


def norm_back(grad_normed, gain_vec, scaled, inverse):
    grad_scaled = grad_normed * gain_vec
    first_mean = jnp.mean(grad_scaled, axis=-1, keepdims=True)
    second = jnp.mean(grad_scaled * scaled, axis=-1, keepdims=True)
    return inverse * (grad_scaled - first_mean - scaled * second)


def from_side(values):
    return lax.ppermute(values, "tensor", [(i, i ^ 1) for i in range(4)])


def from_far(values):
    return lax.ppermute(values, "tensor", [(i, i ^ 2) for i in range(4)])


def both_halves(own):
    near = jnp.concatenate([own, from_far(own)], axis=0)
    return near, from_side(near)


def sum_to_owner(values):
    half = values.shape[0] // 2
    quarter = half // 2
    near = values[:half].astype(F32) + from_side(values[half:]).astype(F32)
    return near[:quarter] + from_far(near[quarter:].astype(BF16)).astype(F32)


def own_core(values, axis, flip):
    core = lax.axis_index("tensor") % 2
    return lax.dynamic_index_in_dim(values, 1 - core if flip else core, axis, keepdims=False)


def sum_tree_to_owner(partial):
    sent = partial(True).astype(BF16)
    near = partial(False) + from_side(sent).astype(F32)
    near = near.reshape(2, -1, near.shape[1])
    place = lax.axis_index("tensor") // 2
    kept = lax.dynamic_index_in_dim(near, place, 0, keepdims=False)
    far = lax.dynamic_index_in_dim(near, 1 - place, 0, keepdims=False)
    return kept + from_far(far.astype(BF16)).astype(F32)


def exchange(blocks, back):
    count = lax.axis_size("expert")
    if count > DIRECT:
        return lax.all_to_all(blocks, "expert", split_axis=0, concat_axis=0, tiled=True)
    arrived = [blocks[0]]
    for step in range(1, count):
        pairs = [(i, (i - step if back else i + step) % count) for i in range(count)]
        arrived.append(lax.ppermute(blocks[step], "expert", pairs))
    return jnp.stack(arrived)


def slots_of(expert_ids, experts, capacity):
    rows = expert_ids.shape[0]
    chosen = expert_ids[:, None] == jnp.arange(experts, dtype=jnp.int32)[None, :]
    at = jnp.arange(rows, dtype=jnp.int32)
    before = (at[None, :] < at[:, None]).astype(BF16)
    earlier = jnp.dot(before, chosen.astype(BF16), preferred_element_type=F32)
    slot = jnp.sum(jnp.where(chosen, earlier, 0.0), axis=1).astype(jnp.int32)
    first = lax.axis_index("expert") if experts <= DIRECT else 0
    place = ((expert_ids - first) % experts) * capacity + slot
    places = jnp.arange(experts * capacity, dtype=jnp.int32)
    return (places[:, None] == place[None, :]).astype(BF16)


def per_device(
    tokens,
    cotangent,
    routes,
    parents,
    ln_attn,
    w_qkv,
    w_out,
    ln_mlp,
    w_up,
    w_down,
    w_router,
    w_mix,
    ex_up,
    ex_down,
):
    tok_dev, width = tokens.shape
    mine = lax.axis_index("tensor")
    experts = w_router.shape[1]
    capacity = max(2, tok_dev * 7 // (5 * experts))
    heads_width = w_qkv.shape[2]
    leaves = leaf_order(parents[0])

    scaled_one, inverse_one = norm_parts(tokens.astype(F32))
    normed_own = (scaled_one * ln_attn).astype(BF16)
    normed_one = lax.all_gather(normed_own, "tensor", axis=0, tiled=True)

    quarter_ids = routes[:, 0].reshape(4, tok_dev)
    own_slots = slots_of(
        lax.dynamic_index_in_dim(quarter_ids, mine, 0, keepdims=False), experts, capacity
    )
    far_slots = slots_of(
        lax.dynamic_index_in_dim(quarter_ids, mine ^ 2, 0, keepdims=False), experts, capacity
    )

    def dispatch(slots, rows):
        placed = jnp.dot(slots, rows, preferred_element_type=F32).astype(BF16)
        return exchange(placed.reshape(experts, capacity, width), False).reshape(-1, width)

    grads_near, grads_side = both_halves(dispatch(own_slots, cotangent))

    qkv_rows = jnp.einsum("td,sdc->stc", normed_one, w_qkv, preferred_element_type=F32).astype(BF16)
    attended, trunk_log, family_log = attention_forward(leaves, qkv_rows)
    attended_view = attended.reshape(2, 2, tok_dev, heads_width)

    def branch_part(flip):
        rows = own_core(attended_view, 1, flip).reshape(2 * tok_dev, heads_width)
        return jnp.dot(rows, w_out, preferred_element_type=F32)

    residual = tokens.astype(F32) + sum_tree_to_owner(branch_part)
    cotangent_near, cotangent_side = both_halves(cotangent)

    scaled_two, inverse_two = norm_parts(residual)
    normed_two = (scaled_two * ln_mlp).astype(BF16)
    own_arrived = dispatch(own_slots, normed_two)
    normed_far = from_far(normed_two)
    near_arrived = jnp.concatenate([own_arrived, dispatch(far_slots, normed_far)], axis=0)
    side_arrived = from_side(near_arrived)
    normed_near = jnp.concatenate([normed_two, normed_far], axis=0)
    normed_side = from_side(normed_near)

    lanes = -(-(experts + 2) // LANES) * LANES
    head = jnp.concatenate(
        [w_router, w_mix, jnp.zeros((width, lanes - experts - 2), BF16)], axis=1
    )
    dense_out, dense_back, dense_active, dense_pre, dense_grad, dense_head = feed(
        normed_near, normed_side, cotangent_near, cotangent_side, head, w_up, w_down, experts, None, tok_dev * 2 // 5
    )
    expert = lax.axis_index("expert").astype(jnp.int32)
    expert_out, expert_back, expert_active, expert_pre, expert_grad, expert_head = feed(
        near_arrived, side_arrived, grads_near, grads_side, head, ex_up[0], ex_down[0], experts, expert,
        near_arrived.shape[0] // 7,
    )

    def returned(partial):
        rows = sum_to_owner(partial).astype(BF16).reshape(experts, capacity, width)
        rows = exchange(rows, True).reshape(-1, width)
        return lax.dot_general(own_slots, rows, (((0,), (0,)), ((), ())), preferred_element_type=F32)

    grad_normed_two = sum_to_owner(dense_back) + returned(expert_back)

    normed_rows = jnp.concatenate([normed_near, normed_side], axis=0)
    grad_up = jnp.einsum("gd,gf->df", normed_rows, dense_pre, preferred_element_type=F32)
    grad_down = jnp.einsum("gd,gf->df", dense_grad, dense_active, preferred_element_type=F32)
    dense_grads = lax.psum_scatter(
        jnp.concatenate([grad_up.astype(BF16), grad_down.astype(BF16)], axis=1),
        "expert",
        scatter_dimension=0,
        tiled=True,
    ).astype(F32)
    expert_rows = jnp.concatenate([near_arrived, side_arrived], axis=0)
    grad_ex_up = jnp.einsum("gd,gf->df", expert_rows, expert_pre, preferred_element_type=F32)[None]
    grad_ex_down = jnp.einsum("gf,gd->fd", expert_active, expert_grad, preferred_element_type=F32)[None]

    gain_two = jnp.sum(grad_normed_two * scaled_two, axis=0)
    grad_residual = cotangent.astype(F32) + norm_back(grad_normed_two, ln_mlp, scaled_two, inverse_two)
    branch_near, branch_side = both_halves(grad_residual.astype(BF16))
    grad_branch = jnp.concatenate([branch_near, branch_side], axis=0)
    small = lax.psum(
        jnp.concatenate([(dense_head + expert_head)[: experts + 2], gain_two[None]], axis=0), "tensor"
    )

    offsets = jnp.arange(4, dtype=jnp.int32) ^ mine
    place_of = (offsets % 2) * 2 + offsets // 2
    grad_attended = jnp.einsum("gd,cd->gc", grad_branch, w_out, preferred_element_type=F32)
    grad_attended = grad_attended.astype(BF16).reshape(4, tok_dev, heads_width)
    grad_attended = jnp.take(grad_attended, place_of, axis=0).reshape(4 * tok_dev, heads_width)
    quarter_at = jnp.asarray([0, 2, 1, 3], jnp.int32) ^ mine
    attended_rows = jnp.take(
        attended.reshape(4, tok_dev, heads_width), quarter_at, axis=0
    ).reshape(4 * tok_dev, heads_width)
    grad_w_out = jnp.einsum("gd,gc->dc", grad_branch, attended_rows, preferred_element_type=F32)

    grad_attended, small = lax.optimization_barrier((grad_attended, small))
    grad_qkv_rows = attention_backward(
        leaves, qkv_rows, grad_attended, attended, trunk_log, family_log
    )
    grad_view = grad_qkv_rows.reshape(3, 2, 2, tok_dev, heads_width)

    def normed_part(flip):
        rows = own_core(grad_view, 2, flip).reshape(3, 2 * tok_dev, heads_width)
        return jnp.einsum("sgc,sdc->gd", rows, w_qkv, preferred_element_type=F32)

    grad_normed_one = sum_tree_to_owner(normed_part)
    grad_w_qkv = jnp.einsum("gd,sgc->dsc", normed_one, grad_qkv_rows, preferred_element_type=F32)
    small_columns = -(-small.shape[0] // LANES) * LANES
    small_block = jnp.pad(small, ((0, small_columns - small.shape[0]), (0, 0))).T
    last_grads = lax.psum_scatter(
        jnp.concatenate(
            [
                grad_w_qkv.reshape(width, 3 * heads_width).astype(BF16),
                grad_w_out.astype(BF16),
                small_block.astype(BF16),
            ],
            axis=1,
        ),
        "expert",
        scatter_dimension=0,
        tiled=True,
    ).astype(F32)
    grad_ln_attn = lax.psum(
        lax.psum(jnp.sum(grad_normed_one * scaled_one, axis=0), "tensor"), "expert"
    )
    grad_tokens = grad_residual + norm_back(grad_normed_one, ln_attn, scaled_one, inverse_one)
    out = (residual + sum_to_owner(dense_out) + returned(expert_out)).astype(BF16)

    hidden = w_up.shape[1]
    strip = last_grads.shape[0]
    after_qkv = 3 * heads_width
    after_out = after_qkv + heads_width
    return (
        out,
        grad_tokens,
        grad_ln_attn,
        last_grads[:, :after_qkv].reshape(strip, 3, heads_width).transpose(1, 0, 2),
        last_grads[:, after_qkv:after_out].T,
        last_grads[:, after_out + experts + 2],
        dense_grads[:, :hidden],
        dense_grads[:, hidden:].T,
        last_grads[:, after_out : after_out + experts],
        last_grads[:, after_out + experts : after_out + experts + 2],
        grad_ex_up,
        grad_ex_down,
    )


def solution(mesh):
    return jax.shard_map(
        per_device,
        mesh=mesh,
        in_specs=(
            P(("expert", "tensor"), None),
            P(("expert", "tensor"), None),
            P("expert", None),
            P("expert", None),
            P(),
            P(None, None, "tensor"),
            P("tensor", None),
            P(),
            P(None, "tensor"),
            P("tensor", None),
            P(),
            P(),
            P("expert", None, "tensor"),
            P("expert", "tensor", None),
        ),
        out_specs=(
            P(("expert", "tensor"), None),
            P(("expert", "tensor"), None),
            P(),
            P(None, "expert", "tensor"),
            P("tensor", "expert"),
            P("expert"),
            P("expert", "tensor"),
            P("tensor", "expert"),
            P("expert", None),
            P("expert", None),
            P("expert", None, "tensor"),
            P("expert", "tensor", None),
        ),
        check_vma=False,
    )
```

```python
import functools

import jax
import jax.numpy as jnp
from jax import lax
from jax.experimental import pallas as pl
from jax.experimental.pallas import tpu as pltpu
from jax.sharding import PartitionSpec as P

HEAD_DIM = 64
TRUNK = 1024
SEG = 128
SEGS = 13
TREE_LEN = 2560
BRANCHES = 4
FAMILY = 3 * SEG
QROWS = 256
PAIR = 2 * HEAD_DIM
NEGATIVE_FILL = -1e30
F32 = jnp.float32
BF16 = jnp.bfloat16
EPSILON = 1e-05


def dot_nn(a, b):
    return lax.dot_general(a, b, (((1,), (0,)), ((), ())), preferred_element_type=F32)


def dot_nt(a, b):
    return lax.dot_general(a, b, (((1,), (1,)), ((), ())), preferred_element_type=F32)


def head_lanes(rows, head):
    lane = lax.broadcasted_iota(jnp.int32, rows.shape, 1)
    return jnp.where(lane // HEAD_DIM == head, rows, jnp.zeros_like(rows))


def causal(scores):
    key = lax.broadcasted_iota(jnp.int32, scores.shape, 0)
    query = lax.broadcasted_iota(jnp.int32, scores.shape, 1)
    return jnp.where(key <= query, scores, NEGATIVE_FILL)


def family_rows(leaves_ref, branch):
    def start(segment):
        return pl.multiple_of(TRUNK + (segment - 1) * SEG, SEG)

    return [start(branch + 1), start(leaves_ref[2 * branch]), start(leaves_ref[2 * branch + 1])]


def transpose_into(target_ref, source_ref, part):
    for first in range(0, TREE_LEN, 512):
        piece = source_ref[part, pl.ds(first, 512), :].astype(F32)
        target_ref[:, pl.ds(first, 512)] = piece.T.astype(BF16)


def widen(piece, first, width, fill):
    parts = []
    if first:
        parts.append(jnp.full((piece.shape[0], first), fill, piece.dtype))
    parts.append(piece)
    rest = width - first - piece.shape[1]
    if rest:
        parts.append(jnp.full((piece.shape[0], rest), fill, piece.dtype))
    return parts[0] if len(parts) == 1 else jnp.concatenate(parts, axis=1)


def trunk_groups(block):
    first = block * QROWS
    groups = [(0, first, 0, QROWS, None)] if first else []
    return groups + [(first, QROWS, 0, QROWS, "causal")]


def family_groups(starts):
    return [
        (0, TRUNK, 0, FAMILY, None),
        (starts[0], SEG, 0, FAMILY, "branch"),
        (starts[1], SEG, SEG, 2 * SEG, "causal"),
        (starts[2], SEG, 2 * SEG, FAMILY, "causal"),
    ]


def masked_scores(keys, queries, rule):
    scores = dot_nt(keys, queries)
    if rule == "causal":
        return causal(scores)
    if rule == "branch":
        return jnp.concatenate([causal(scores[:, :SEG]), scores[:, SEG:]], axis=1)
    return scores


def forward_block(qkv_ref, values_t_ref, queries, groups):
    width = queries.shape[0]
    outs, logs = [], []
    for head in range(2):
        own = head_lanes(queries, head)
        all_scores = [
            masked_scores(qkv_ref[1, pl.ds(start, size), :], own[first:last], rule)
            for start, size, first, last, rule in groups
        ]
        top = functools.reduce(
            jnp.maximum,
            [
                widen(jnp.max(s, axis=0, keepdims=True), first, width, NEGATIVE_FILL)
                for s, (_, _, first, last, _) in zip(all_scores, groups)
            ],
        )
        total, output = None, None
        for s, (start, size, first, last, _) in zip(all_scores, groups):
            weights = jnp.exp(s - top[:, first:last])
            part = widen(jnp.sum(weights, axis=0, keepdims=True), first, width, 0.0)
            values_t = values_t_ref[pl.ds(head * HEAD_DIM, HEAD_DIM), pl.ds(start, size)]
            mixed = widen(dot_nn(values_t, weights.astype(BF16)), first, width, 0.0)
            total = part if total is None else total + part
            output = mixed if output is None else output + mixed
        outs.append(output / total)
        logs.append(top + jnp.log(total))
    return jnp.concatenate(outs, axis=0).T.astype(BF16), jnp.concatenate(logs, axis=0)


def scaled_queries(qkv_ref, starts, size):
    rows = [qkv_ref[0, pl.ds(start, size), :] for start in starts]
    rows = rows[0] if len(rows) == 1 else jnp.concatenate(rows, axis=0)
    return rows * jnp.asarray(HEAD_DIM ** (-0.5), BF16)


def quarter_rows(leaves_ref, offset):
    quarter = TREE_LEN // 4
    return pl.ds(pl.multiple_of((leaves_ref[2 * BRANCHES] ^ offset) * quarter, quarter), quarter)


def forward_kernel(
    leaves_ref,
    near_ref,
    far_ref,
    near_out_ref,
    far_out_ref,
    trunk_log_ref,
    family_log_ref,
    qkv_ref,
    out_ref,
    values_t_ref,
):
    for offset in range(4):
        half_ref = near_ref if offset < 2 else far_ref
        qkv_ref[:, quarter_rows(leaves_ref, offset), :] = half_ref[:, offset % 2]
    transpose_into(values_t_ref, qkv_ref, 2)
    for block in range(TRUNK // QROWS):
        first = block * QROWS
        queries = scaled_queries(qkv_ref, [first], QROWS)
        out, logs = forward_block(qkv_ref, values_t_ref, queries, trunk_groups(block))
        out_ref[pl.ds(first, QROWS), :] = out
        trunk_log_ref[0, :, pl.ds(first, QROWS)] = logs

    def one_family(branch, carry):
        starts = family_rows(leaves_ref, branch)
        queries = scaled_queries(qkv_ref, starts, SEG)
        out, logs = forward_block(qkv_ref, values_t_ref, queries, family_groups(starts))
        for place, start in enumerate(starts):
            out_ref[pl.ds(start, SEG), :] = out[place * SEG : (place + 1) * SEG]
        family_log_ref[0, branch] = logs
        return carry

    lax.fori_loop(0, BRANCHES, one_family, 0)
    for offset in range(4):
        half_ref = near_out_ref if offset < 2 else far_out_ref
        half_ref[offset % 2] = out_ref[quarter_rows(leaves_ref, offset), :]


def halves_spec(parts):
    quarter = TREE_LEN // 4
    if parts == 1:
        return pl.BlockSpec((2, quarter, PAIR), lambda p, leaves: (0, 0, p))
    return pl.BlockSpec((parts, 2, quarter, PAIR), lambda p, leaves: (0, 0, 0, p))


def attention_cost(products):
    visited = TRUNK * (TRUNK + QROWS) // 2 + BRANCHES * FAMILY * (TRUNK + SEG)
    return pl.CostEstimate(
        flops=2 * products * 4 * visited * 2 * PAIR,
        transcendentals=4 * visited,
        bytes_accessed=8 * TREE_LEN * 4 * HEAD_DIM * 2,
    )


def attention_forward(leaves, near, far):
    width = near.shape[3]
    quarter = TREE_LEN // 4
    pairs = width // PAIR
    return pl.pallas_call(
        forward_kernel,
        grid_spec=pltpu.PrefetchScalarGridSpec(
            num_scalar_prefetch=1,
            grid=(pairs,),
            in_specs=[halves_spec(3), halves_spec(3)],
            out_specs=[
                halves_spec(1),
                halves_spec(1),
                pl.BlockSpec((1, 2, TRUNK), lambda p, leaves: (p, 0, 0)),
                pl.BlockSpec((1, BRANCHES, 2, FAMILY), lambda p, leaves: (p, 0, 0, 0)),
            ],
            scratch_shapes=[
                pltpu.VMEM((3, TREE_LEN, PAIR), BF16),
                pltpu.VMEM((TREE_LEN, PAIR), BF16),
                pltpu.VMEM((PAIR, TREE_LEN), BF16),
            ],
        ),
        out_shape=[
            jax.ShapeDtypeStruct((2, quarter, width), BF16),
            jax.ShapeDtypeStruct((2, quarter, width), BF16),
            jax.ShapeDtypeStruct((pairs, 2, TRUNK), F32),
            jax.ShapeDtypeStruct((pairs, BRANCHES, 2, FAMILY), F32),
        ],
        cost_estimate=attention_cost(2),
        name="tree_attention",
    )(leaves, near, far)


def backward_block(qkv_ref, keys_t_ref, queries, grads, outs, logs, groups):
    products = grads.astype(F32) * outs.astype(F32)
    products_t = products.T
    key_ds = [[] for _ in groups]
    value_ws = [[] for _ in groups]
    own_q, own_g, query_grads = [], [], []
    for head in range(2):
        own = head_lanes(queries, head)
        own_grads = head_lanes(grads, head)
        own_q.append(own)
        own_g.append(own_grads)
        inner = jnp.sum(
            products_t[head * HEAD_DIM : (head + 1) * HEAD_DIM], axis=0, keepdims=True
        )
        log = logs[head : head + 1]
        query_grad = None
        for place, (start, size, first, last, rule) in enumerate(groups):
            scores = masked_scores(qkv_ref[1, pl.ds(start, size), :], own[first:last], rule)
            weights = jnp.exp(scores - log[:, first:last])
            grad_weights = dot_nt(qkv_ref[2, pl.ds(start, size), :], own_grads[first:last])
            grad_scores = (weights * (grad_weights - inner[:, first:last])).astype(BF16)
            keys_t = keys_t_ref[pl.ds(head * HEAD_DIM, HEAD_DIM), pl.ds(start, size)]
            part = widen(dot_nn(keys_t, grad_scores), first, queries.shape[0], 0.0)
            query_grad = part if query_grad is None else query_grad + part
            key_ds[place].append(grad_scores)
            value_ws[place].append(weights.astype(BF16))
        query_grads.append(query_grad)
    grad_query = (jnp.concatenate(query_grads, axis=0) * HEAD_DIM ** (-0.5)).T.astype(BF16)
    key_grads, value_grads = [], []
    for place, (start, size, first, last, rule) in enumerate(groups):
        stacked_q = jnp.concatenate([own_q[0][first:last], own_q[1][first:last]], axis=0)
        stacked_g = jnp.concatenate([own_g[0][first:last], own_g[1][first:last]], axis=0)
        key_grads.append(dot_nn(jnp.concatenate(key_ds[place], axis=1), stacked_q))
        value_grads.append(dot_nn(jnp.concatenate(value_ws[place], axis=1), stacked_g))
    return grad_query, key_grads, value_grads


def backward_kernel(
    leaves_ref,
    near_ref,
    far_ref,
    near_grads_ref,
    far_grads_ref,
    near_outs_ref,
    far_outs_ref,
    trunk_log_ref,
    family_log_ref,
    near_result_ref,
    far_result_ref,
    qkv_ref,
    grads_ref,
    outs_ref,
    result_ref,
    keys_t_ref,
    trunk_keys_ref,
    trunk_values_ref,
):
    for offset in range(4):
        rows = quarter_rows(leaves_ref, offset)
        at = offset % 2
        qkv_ref[:, rows, :] = (near_ref if offset < 2 else far_ref)[:, at]
        grads_ref[rows, :] = (near_grads_ref if offset < 2 else far_grads_ref)[at]
        outs_ref[rows, :] = (near_outs_ref if offset < 2 else far_outs_ref)[at]
    transpose_into(keys_t_ref, qkv_ref, 1)
    trunk_keys_ref[...] = jnp.zeros_like(trunk_keys_ref)
    trunk_values_ref[...] = jnp.zeros_like(trunk_values_ref)
    for block in range(TRUNK // QROWS):
        first = block * QROWS
        rows = pl.ds(first, QROWS)
        groups = trunk_groups(block)
        grad_query, key_grads, value_grads = backward_block(
            qkv_ref,
            keys_t_ref,
            scaled_queries(qkv_ref, [first], QROWS),
            grads_ref[rows, :],
            outs_ref[rows, :],
            trunk_log_ref[0, :, rows],
            groups,
        )
        result_ref[0, rows, :] = grad_query
        for (start, size, _, _, _), key_grad, value_grad in zip(groups, key_grads, value_grads):
            trunk_keys_ref[pl.ds(start, size), :] += key_grad
            trunk_values_ref[pl.ds(start, size), :] += value_grad

    def one_family(branch, carry):
        starts = family_rows(leaves_ref, branch)
        groups = family_groups(starts)
        grad_query, key_grads, value_grads = backward_block(
            qkv_ref,
            keys_t_ref,
            scaled_queries(qkv_ref, starts, SEG),
            jnp.concatenate([grads_ref[pl.ds(start, SEG), :] for start in starts], axis=0),
            jnp.concatenate([outs_ref[pl.ds(start, SEG), :] for start in starts], axis=0),
            family_log_ref[0, branch],
            groups,
        )
        trunk_keys_ref[...] += key_grads[0]
        trunk_values_ref[...] += value_grads[0]
        for place, start in enumerate(starts):
            rows = pl.ds(start, SEG)
            result_ref[0, rows, :] = grad_query[place * SEG : (place + 1) * SEG]
            result_ref[1, rows, :] = key_grads[1 + place].astype(BF16)
            result_ref[2, rows, :] = value_grads[1 + place].astype(BF16)
        return carry

    lax.fori_loop(0, BRANCHES, one_family, 0)
    result_ref[1, pl.ds(0, TRUNK), :] = trunk_keys_ref[...].astype(BF16)
    result_ref[2, pl.ds(0, TRUNK), :] = trunk_values_ref[...].astype(BF16)
    for offset in range(4):
        half_ref = near_result_ref if offset < 2 else far_result_ref
        half_ref[:, offset % 2] = result_ref[:, quarter_rows(leaves_ref, offset), :]


def attention_backward(leaves, near, far, near_grads, far_grads, near_outs, far_outs, logs):
    pairs = near.shape[3] // PAIR
    return pl.pallas_call(
        backward_kernel,
        grid_spec=pltpu.PrefetchScalarGridSpec(
            num_scalar_prefetch=1,
            grid=(pairs,),
            in_specs=[
                halves_spec(3),
                halves_spec(3),
                halves_spec(1),
                halves_spec(1),
                halves_spec(1),
                halves_spec(1),
                pl.BlockSpec((1, 2, TRUNK), lambda p, leaves: (p, 0, 0)),
                pl.BlockSpec((1, BRANCHES, 2, FAMILY), lambda p, leaves: (p, 0, 0, 0)),
            ],
            out_specs=[halves_spec(3), halves_spec(3)],
            scratch_shapes=[
                pltpu.VMEM((3, TREE_LEN, PAIR), BF16),
                pltpu.VMEM((TREE_LEN, PAIR), BF16),
                pltpu.VMEM((TREE_LEN, PAIR), BF16),
                pltpu.VMEM((3, TREE_LEN, PAIR), BF16),
                pltpu.VMEM((PAIR, TREE_LEN), BF16),
                pltpu.VMEM((TRUNK, PAIR), F32),
                pltpu.VMEM((TRUNK, PAIR), F32),
            ],
        ),
        out_shape=[jax.ShapeDtypeStruct(near.shape, BF16), jax.ShapeDtypeStruct(far.shape, BF16)],
        cost_estimate=attention_cost(5),
        name="tree_attention_back",
    )(leaves, near, far, near_grads, far_grads, near_outs, far_outs, *logs)


def leaf_order(parents_row):
    first_leaf = BRANCHES + 1
    leaf_parents = parents_row[first_leaf:]
    segments = first_leaf + jnp.arange(leaf_parents.shape[0], dtype=jnp.int32)
    same = leaf_parents[:, None] == leaf_parents[None, :]
    later = segments[None, :] < segments[:, None]
    place = 2 * (leaf_parents - 1) + jnp.sum(jnp.where(same & later, 1, 0), axis=1)
    slots = jnp.arange(2 * BRANCHES, dtype=jnp.int32)
    return jnp.sum(jnp.where(slots[:, None] == place[None, :], segments[None, :], 0), axis=1)


def gates(logits, experts, expert):
    lane = lax.broadcasted_iota(jnp.int32, logits.shape, 1)
    first, second = logits[:, experts : experts + 1], logits[:, experts + 1 : experts + 2]
    top = jnp.maximum(first, second)
    first, second = jnp.exp(first - top), jnp.exp(second - top)
    total = first + second
    first, second = first / total, second / total
    if expert is None:
        return lane, first, second, None, None
    routed = jnp.where(lane < experts, logits, NEGATIVE_FILL)
    raised = jnp.exp(routed - jnp.max(routed, axis=1, keepdims=True))
    probs = raised / jnp.sum(raised, axis=1, keepdims=True)
    gate = jnp.sum(jnp.where(lane == expert, probs, 0.0), axis=1, keepdims=True)
    return lane, first, second, probs, gate


def feed_kernel(
    experts,
    routed,
    expert_ref,
    own_ref,
    side_ref,
    own_grads_ref,
    side_grads_ref,
    head_ref,
    up_ref,
    down_ref,
    own_out_ref,
    side_out_ref,
    own_back_ref,
    side_back_ref,
    active_ref,
    pre_ref,
    grad_ref,
    head_grad_ref,
):
    step = pl.program_id(0)
    early = step < pl.num_programs(0) // 2
    rows = jnp.where(early, own_ref[...], side_ref[...])
    grads = jnp.where(early, own_grads_ref[...], side_grads_ref[...]).astype(F32)
    logits = dot_nn(rows, head_ref[...])
    expert = expert_ref[0] if routed else None
    lane, first, second, probs, gate = gates(logits, experts, expert)
    coef = second * gate if routed else first
    weighted = (coef * grads).astype(BF16)
    grad_ref[...] = weighted
    pre = dot_nn(rows, up_ref[...])
    grad_active = dot_nt(weighted, down_ref[...])
    cumulative = 0.5 + 0.5 * lax.erf(pre * 0.7071067811865476)
    slope = cumulative + pre * jnp.exp(-0.5 * pre * pre) * 0.3989422804014327
    active = (pre * cumulative).astype(BF16)
    active_ref[...] = active
    grad_pre = (grad_active * slope).astype(BF16)
    pre_ref[...] = grad_pre
    out = dot_nn(active, down_ref[...])
    out_rows = (coef * out).astype(BF16)
    inner = jnp.sum(grads * out, axis=1, keepdims=True)
    swing = first * second * inner
    if routed:
        swing = -gate * swing
    grad_logits = jnp.where(lane == experts, swing, jnp.where(lane == experts + 1, -swing, 0.0))
    if routed:
        picked = jnp.where(lane == expert, 1.0, 0.0) - gate
        grad_logits = grad_logits + jnp.where(
            lane < experts, probs * picked * (second * inner), 0.0
        )
    back = dot_nt(grad_pre, up_ref[...]) + dot_nt(grad_logits.astype(BF16), head_ref[...])
    back_rows = back.astype(BF16)

    @pl.when(early)
    def _():
        own_out_ref[...] = out_rows
        own_back_ref[...] = back_rows

    @pl.when(jnp.logical_not(early))
    def _():
        side_out_ref[...] = out_rows
        side_back_ref[...] = back_rows

    @pl.when(step == 0)
    def _():
        head_grad_ref[...] = jnp.zeros_like(head_grad_ref)

    head_grad_ref[...] += dot_nn(grad_logits.T.astype(BF16), rows)


def feed(own, side, own_grads, side_grads, head, up, down, experts, expert, size):
    count = own.shape[0]
    width, hidden = up.shape
    half = count // size
    lanes = head.shape[1]
    routed = expert is not None
    pick = jnp.reshape(expert, (1,)) if routed else jnp.zeros((1,), jnp.int32)
    early = pl.BlockSpec((size, width), lambda i, pick: (jnp.minimum(i, half - 1), 0))
    late = pl.BlockSpec((size, width), lambda i, pick: (jnp.maximum(i - half, 0), 0))

    def held(shape):
        return pl.BlockSpec(shape, lambda i, pick: (0, 0), pipeline_mode=pl.Buffered(1))

    wide = pl.BlockSpec((size, width), lambda i, pick: (i, 0))
    deep = pl.BlockSpec((size, hidden), lambda i, pick: (i, 0))
    quarter = jax.ShapeDtypeStruct((count, width), BF16)
    return pl.pallas_call(
        functools.partial(feed_kernel, experts, routed),
        grid_spec=pltpu.PrefetchScalarGridSpec(
            num_scalar_prefetch=1,
            grid=(2 * half,),
            in_specs=[
                early,
                late,
                early,
                late,
                held((width, lanes)),
                held((width, hidden)),
                held((hidden, width)),
            ],
            out_specs=[
                early,
                late,
                early,
                late,
                deep,
                deep,
                wide,
                pl.BlockSpec((lanes, width), lambda i, pick: (0, 0)),
            ],
        ),
        out_shape=[
            quarter,
            quarter,
            quarter,
            quarter,
            jax.ShapeDtypeStruct((2 * count, hidden), BF16),
            jax.ShapeDtypeStruct((2 * count, hidden), BF16),
            jax.ShapeDtypeStruct((2 * count, width), BF16),
            jax.ShapeDtypeStruct((lanes, width), F32),
        ],
        cost_estimate=pl.CostEstimate(
            flops=16 * count * width * hidden,
            transcendentals=4 * count * hidden,
            bytes_accessed=2 * (8 * count * width + 4 * count * hidden + 2 * width * hidden),
        ),
        compiler_params=pltpu.CompilerParams(vmem_limit_bytes=60 * 1024 * 1024),
        name="feed_routed" if routed else "feed_dense",
    )(pick, own, side, own_grads, side_grads, head, up, down)


LANES = 128
DENSE_ROWS = 320
EXPERT_ROWS = 448


def norm_parts(values):
    row_mean = jnp.mean(values, axis=-1, keepdims=True)
    centred = values - row_mean
    row_var = jnp.mean(centred * centred, axis=-1, keepdims=True)
    inverse = lax.rsqrt(row_var + EPSILON)
    return (centred * inverse, inverse)


def norm_back(grad_normed, gain_vec, scaled, inverse):
    grad_scaled = grad_normed * gain_vec
    first_mean = jnp.mean(grad_scaled, axis=-1, keepdims=True)
    second = jnp.mean(grad_scaled * scaled, axis=-1, keepdims=True)
    return inverse * (grad_scaled - first_mean - scaled * second)


def after(value, *others):
    return lax.optimization_barrier((value, *others))[0]


def from_side(values):
    return lax.ppermute(values, "tensor", [(i, i ^ 1) for i in range(4)])


def from_far(values):
    return lax.ppermute(values, "tensor", [(i, i ^ 2) for i in range(4)])


def plus_side(own, side):
    return own.astype(F32) + from_side(side.astype(BF16)).astype(F32)


def sum_over(values, axis):
    count, step = lax.axis_size(axis), 1
    while step < count:
        pairs = [(i, i ^ step) for i in range(count)]
        values = values + lax.ppermute(values, axis, pairs)
        step *= 2
    return values


def exchange(blocks):
    return lax.all_to_all(blocks, "expert", split_axis=0, concat_axis=0, tiled=True)


def scatter_sum(strips):
    strips = strips.astype(BF16)
    return lax.psum_scatter(strips, "expert", scatter_dimension=0, tiled=True).astype(F32)


def slots_of(expert_ids, experts, capacity):
    rows = expert_ids.shape[0]
    chosen = expert_ids[:, None] == jnp.arange(experts, dtype=jnp.int32)[None, :]
    at = jnp.arange(rows, dtype=jnp.int32)
    before = (at[None, :] < at[:, None]).astype(BF16)
    earlier = jnp.dot(before, chosen.astype(BF16), preferred_element_type=F32)
    slot = jnp.sum(jnp.where(chosen, earlier, 0.0), axis=1).astype(jnp.int32)
    place = expert_ids * capacity + slot
    places = jnp.arange(experts * capacity, dtype=jnp.int32)
    return (places[:, None] == place[None, :]).astype(BF16)


def per_device(
    tokens,
    cotangent,
    routes,
    parents,
    ln_attn,
    w_qkv,
    w_out,
    ln_mlp,
    w_up,
    w_down,
    w_router,
    w_mix,
    ex_up,
    ex_down,
):
    tok_dev, width = tokens.shape
    mine = lax.axis_index("tensor")
    experts = w_router.shape[1]
    capacity = max(2, tok_dev * 7 // (5 * experts))
    heads_width = w_qkv.shape[2]
    hidden = w_up.shape[1]
    leaves = jnp.concatenate([leaf_order(parents[0]), mine.astype(jnp.int32)[None]])

    scaled_one, inverse_one = norm_parts(tokens.astype(F32))
    normed_own = (scaled_one * ln_attn).astype(BF16)
    normed_far = from_far(normed_own)
    near_one = jnp.concatenate([normed_own, from_side(normed_own)], axis=0)
    far_one = jnp.concatenate([normed_far, from_side(normed_far)], axis=0)

    quarter_ids = routes[:, 0].reshape(4, tok_dev)

    def slots_at(offset):
        ids = lax.dynamic_index_in_dim(quarter_ids, mine ^ offset, 0, keepdims=False)
        return slots_of(ids, experts, capacity)

    own_slots, far_slots = slots_at(0), slots_at(2)

    def dispatch(slots, rows):
        placed = jnp.dot(slots, rows, preferred_element_type=F32).astype(BF16)
        return exchange(placed.reshape(experts, capacity, width)).reshape(-1, width)

    own_grads = dispatch(own_slots, cotangent)
    cotangent_side = from_side(cotangent)

    def project(rows):
        qkv = jnp.einsum("td,sdc->stc", rows, w_qkv, preferred_element_type=F32)
        return qkv.astype(BF16).reshape(3, 2, tok_dev, heads_width)

    near_qkv, far_qkv = project(near_one), project(far_one)
    cotangent_far = from_far(after(cotangent, normed_far))
    near_out, far_out, *logs = attention_forward(leaves, near_qkv, far_qkv)
    far_out, own_grads, cotangent_far, cotangent_side = lax.optimization_barrier(
        (far_out, own_grads, cotangent_far, cotangent_side)
    )

    def branch_part(rows):
        return jnp.dot(rows, w_out, preferred_element_type=F32)

    far_sum = plus_side(branch_part(far_out[0]), branch_part(far_out[1])).astype(BF16)
    branch = plus_side(branch_part(near_out[0]), branch_part(near_out[1]))
    branch_far = from_far(far_sum)
    side_grads = from_side(own_grads)
    cotangent_corner = from_side(cotangent_far)
    branch_far, side_grads, cotangent_corner = lax.optimization_barrier(
        (branch_far, side_grads, cotangent_corner)
    )
    residual = tokens.astype(F32) + (branch + branch_far.astype(F32))

    scaled_two, inverse_two = norm_parts(residual)
    normed_two = (scaled_two * ln_mlp).astype(BF16)
    normed_two_far = from_far(normed_two)
    normed_two_side = from_side(normed_two)
    normed_two_corner = from_side(normed_two_far)
    own_rows = dispatch(own_slots, normed_two)
    far_rows = from_far(own_rows)
    far_grads = dispatch(far_slots, after(cotangent_far, own_rows))

    lanes = -(-(experts + 2) // LANES) * LANES
    head = jnp.concatenate(
        [w_router, w_mix, jnp.zeros((width, lanes - experts - 2), BF16)], axis=1
    )

    def dense(own, side, own_cotangent, side_cotangent):
        return feed(
            own, side, own_cotangent, side_cotangent, head, w_up, w_down, experts, None, DENSE_ROWS
        )

    near_dense = dense(normed_two, normed_two_side, cotangent, cotangent_side)
    far_dense = dense(
        after(normed_two_far, near_dense[2]), normed_two_corner, cotangent_far, cotangent_corner
    )

    def weight_grads(near_left, far_left, near_right, far_right):
        product = functools.partial(jnp.einsum, "gd,gf->df", preferred_element_type=F32)
        return product(near_left, near_right) + product(far_left, far_right)

    near_two = jnp.concatenate([normed_two, normed_two_side], axis=0)
    far_two = jnp.concatenate([normed_two_far, normed_two_corner], axis=0)
    grad_up = weight_grads(near_two, far_two, near_dense[5], far_dense[5])
    grad_down = weight_grads(near_dense[6], far_dense[6], near_dense[4], far_dense[4])
    dense_grads = jnp.concatenate([grad_up.astype(BF16), grad_down.astype(BF16)], axis=1)

    expert = lax.axis_index("expert").astype(jnp.int32)

    def routed(own, side, own_cotangent, side_cotangent):
        return feed(
            own,
            side,
            own_cotangent,
            side_cotangent,
            head,
            ex_up[0],
            ex_down[0],
            experts,
            expert,
            EXPERT_ROWS,
        )

    far_rows, dense_grads = lax.optimization_barrier((far_rows, dense_grads))
    dense_grads = scatter_sum(dense_grads)
    corner_rows = from_side(far_rows)
    far_expert = routed(far_rows, corner_rows, far_grads, from_side(far_grads))
    side_rows = from_side(own_rows)
    near_expert = routed(after(own_rows, far_expert[2]), side_rows, own_grads, side_grads)

    def chip_sum(parts, place, *others):
        return plus_side(parts[place], after(parts[place + 1], *others))

    def returned(rows):
        rows = rows.astype(BF16).reshape(experts, capacity, width)
        rows = exchange(rows).reshape(-1, width)
        return lax.dot_general(
            own_slots, rows, (((0,), (0,)), ((), ())), preferred_element_type=F32
        )

    dense_back = chip_sum(near_dense, 2) + from_far(chip_sum(far_dense, 2).astype(BF16)).astype(F32)
    far_back = chip_sum(far_expert, 2).astype(BF16)
    expert_back = chip_sum(near_expert, 2) + from_far(far_back).astype(F32)
    grad_normed_two = dense_back + returned(expert_back)
    far_dense_out = chip_sum(far_dense, 0, far_back).astype(BF16)
    far_expert_out = chip_sum(far_expert, 0, far_back).astype(BF16)
    dense_out = chip_sum(near_dense, 0, far_back) + from_far(far_dense_out).astype(F32)
    expert_out = chip_sum(near_expert, 0, expert_back) + from_far(far_expert_out).astype(F32)
    expert_out = returned(after(expert_out, grad_normed_two))

    near_tokens = jnp.concatenate([own_rows, side_rows], axis=0)
    far_tokens = jnp.concatenate([far_rows, corner_rows], axis=0)
    grad_ex_up = weight_grads(near_tokens, far_tokens, near_expert[5], far_expert[5])[None]
    grad_ex_down = weight_grads(near_expert[4], far_expert[4], near_expert[6], far_expert[6])[None]

    gain_two = jnp.sum(grad_normed_two * scaled_two, axis=0)
    grad_residual = cotangent.astype(F32) + norm_back(
        grad_normed_two, ln_mlp, scaled_two, inverse_two
    )
    grad_branch = grad_residual.astype(BF16)
    grad_branch_far = from_far(grad_branch)
    near_branch = jnp.concatenate([grad_branch, from_side(grad_branch)], axis=0)
    far_branch = jnp.concatenate([grad_branch_far, from_side(grad_branch_far)], axis=0)
    head_grads = near_dense[7] + far_dense[7] + near_expert[7] + far_expert[7]
    small = jnp.concatenate([head_grads[: experts + 2], gain_two[None]], axis=0)
    small = sum_over(small, "tensor")

    def into_heads(rows):
        grads = jnp.einsum("gd,cd->gc", rows, w_out, preferred_element_type=F32)
        return grads.astype(BF16).reshape(2, tok_dev, heads_width)

    near_heads, far_heads = into_heads(near_branch), into_heads(far_branch)
    near_heads, grad_ex_up, grad_ex_down, small, dense_grads = lax.optimization_barrier(
        (near_heads, grad_ex_up, grad_ex_down, small, dense_grads)
    )
    near_result, far_result = attention_backward(
        leaves, near_qkv, far_qkv, near_heads, far_heads, near_out, far_out, logs
    )
    far_result, expert_out = lax.optimization_barrier((far_result, expert_out))
    out = (residual + dense_out + expert_out).astype(BF16)

    def normed_part(grads):
        return jnp.einsum("sgc,sdc->gd", grads, w_qkv, preferred_element_type=F32)

    far_sum = plus_side(normed_part(far_result[:, 0]), normed_part(far_result[:, 1])).astype(BF16)
    grad_normed_one = plus_side(normed_part(near_result[:, 0]), normed_part(near_result[:, 1]))
    grad_normed_one = grad_normed_one + from_far(far_sum).astype(F32)

    near_result = near_result.reshape(3, 2 * tok_dev, heads_width)
    far_result = far_result.reshape(3, 2 * tok_dev, heads_width)
    grad_w_qkv = jnp.einsum(
        "gd,sgc->dsc", near_one, near_result, preferred_element_type=F32
    ) + jnp.einsum("gd,sgc->dsc", far_one, far_result, preferred_element_type=F32)
    flat = (2 * tok_dev, heads_width)
    grad_w_out = weight_grads(near_branch, far_branch, near_out.reshape(flat), far_out.reshape(flat))
    small_columns = -(-small.shape[0] // LANES) * LANES
    small_block = jnp.pad(small, ((0, small_columns - small.shape[0]), (0, 0))).T
    last_grads = scatter_sum(
        jnp.concatenate(
            [
                grad_w_qkv.reshape(width, 3 * heads_width).astype(BF16),
                grad_w_out.astype(BF16),
                small_block.astype(BF16),
            ],
            axis=1,
        )
    )
    gain_one = jnp.sum(grad_normed_one * scaled_one, axis=0, keepdims=True)
    grad_ln_attn = sum_over(sum_over(gain_one, "tensor"), "expert")[0]
    grad_tokens = grad_residual + norm_back(grad_normed_one, ln_attn, scaled_one, inverse_one)

    strip = last_grads.shape[0]
    after_qkv = 3 * heads_width
    after_out = after_qkv + heads_width
    return (
        out,
        grad_tokens,
        grad_ln_attn,
        last_grads[:, :after_qkv].reshape(strip, 3, heads_width).transpose(1, 0, 2),
        last_grads[:, after_qkv:after_out].T,
        last_grads[:, after_out + experts + 2],
        dense_grads[:, :hidden],
        dense_grads[:, hidden:].T,
        last_grads[:, after_out : after_out + experts],
        last_grads[:, after_out + experts : after_out + experts + 2],
        grad_ex_up,
        grad_ex_down,
    )


def solution(mesh):
    return jax.shard_map(
        per_device,
        mesh=mesh,
        in_specs=(
            P(("expert", "tensor"), None),
            P(("expert", "tensor"), None),
            P("expert", None),
            P("expert", None),
            P(),
            P(None, None, "tensor"),
            P("tensor", None),
            P(),
            P(None, "tensor"),
            P("tensor", None),
            P(),
            P(),
            P("expert", None, "tensor"),
            P("expert", "tensor", None),
        ),
        out_specs=(
            P(("expert", "tensor"), None),
            P(("expert", "tensor"), None),
            P(),
            P(None, "expert", "tensor"),
            P("tensor", "expert"),
            P("expert"),
            P("expert", "tensor"),
            P("tensor", "expert"),
            P("expert", None),
            P("expert", None),
            P("expert", None, "tensor"),
            P("expert", "tensor", None),
        ),
        check_vma=False,
    )
```

```python
import functools

import jax
import jax.numpy as jnp
from jax import lax
from jax.experimental import pallas as pl
from jax.experimental.layout import Layout, with_layout_constraint
from jax.experimental.pallas import tpu as pltpu
from jax.sharding import PartitionSpec as P

HEAD_DIM = 64
TRUNK = 1024
SEG = 128
SEGS = 13
TREE_LEN = 2560
BRANCHES = 4
FAMILY = 3 * SEG
QROWS = 256
COVER = 8
PAIR = 2 * HEAD_DIM
NEGATIVE_FILL = -1e30
F32 = jnp.float32
BF16 = jnp.bfloat16
EPSILON = 1e-05


def dot_nn(a, b):
    return lax.dot_general(a, b, (((1,), (0,)), ((), ())), preferred_element_type=F32)


def dot_nt(a, b):
    return lax.dot_general(a, b, (((1,), (1,)), ((), ())), preferred_element_type=F32)


def head_lanes(rows, head):
    lane = lax.broadcasted_iota(jnp.int32, rows.shape, 1)
    return jnp.where(lane // HEAD_DIM == head, rows, jnp.zeros_like(rows))


def causal(scores):
    key = lax.broadcasted_iota(jnp.int32, scores.shape, 0)
    query = lax.broadcasted_iota(jnp.int32, scores.shape, 1)
    return jnp.where(key <= query, scores, NEGATIVE_FILL)


def family_rows(leaves_ref, branch):
    def start(segment):
        return pl.multiple_of(TRUNK + (segment - 1) * SEG, SEG)

    return [start(branch + 1), start(leaves_ref[2 * branch]), start(leaves_ref[2 * branch + 1])]


def transpose_into(target_ref, source_ref, part):
    for first in range(0, TREE_LEN, 512):
        piece = source_ref[part, pl.ds(first, 512), :].astype(F32)
        target_ref[:, pl.ds(first, 512)] = piece.T.astype(BF16)


def widen(piece, first, width, fill):
    parts = []
    if first:
        parts.append(jnp.full((piece.shape[0], first), fill, piece.dtype))
    parts.append(piece)
    rest = width - first - piece.shape[1]
    if rest:
        parts.append(jnp.full((piece.shape[0], rest), fill, piece.dtype))
    return parts[0] if len(parts) == 1 else jnp.concatenate(parts, axis=1)


def trunk_groups(block):
    first = block * QROWS
    groups = [(0, first, 0, QROWS, None)] if first else []
    return groups + [(first, QROWS, 0, QROWS, "causal")]


def family_groups(starts):
    return [
        (0, TRUNK, 0, FAMILY, None),
        (starts[0], SEG, 0, FAMILY, "branch"),
        (starts[1], SEG, SEG, 2 * SEG, "causal"),
        (starts[2], SEG, 2 * SEG, FAMILY, "causal"),
    ]


def masked_scores(keys, queries, rule):
    scores = dot_nt(keys, queries)
    if rule == "causal":
        return causal(scores)
    if rule == "branch":
        return jnp.concatenate([causal(scores[:, :SEG]), scores[:, SEG:]], axis=1)
    return scores


def forward_block(qkv_ref, values_t_ref, queries, groups):
    width = queries.shape[0]
    outs, logs = [], []
    for head in range(2):
        own = head_lanes(queries, head)
        all_scores = [
            masked_scores(qkv_ref[1, pl.ds(start, size), :], own[first:last], rule)
            for start, size, first, last, rule in groups
        ]
        top = functools.reduce(
            jnp.maximum,
            [
                widen(jnp.max(s, axis=0, keepdims=True), first, width, NEGATIVE_FILL)
                for s, (_, _, first, last, _) in zip(all_scores, groups)
            ],
        )
        total, output = None, None
        for s, (start, size, first, last, _) in zip(all_scores, groups):
            weights = jnp.exp(s - top[:, first:last])
            part = widen(jnp.sum(weights, axis=0, keepdims=True), first, width, 0.0)
            values_t = values_t_ref[pl.ds(head * HEAD_DIM, HEAD_DIM), pl.ds(start, size)]
            mixed = widen(dot_nn(values_t, weights.astype(BF16)), first, width, 0.0)
            total = part if total is None else total + part
            output = mixed if output is None else output + mixed
        outs.append(output / total)
        logs.append(top + jnp.log(total))
    return jnp.concatenate(outs, axis=0).T.astype(BF16), jnp.concatenate(logs, axis=0)


def scaled_queries(qkv_ref, starts, size):
    rows = [qkv_ref[0, pl.ds(start, size), :] for start in starts]
    rows = rows[0] if len(rows) == 1 else jnp.concatenate(rows, axis=0)
    return rows * jnp.asarray(HEAD_DIM ** (-0.5), BF16)


def quarter_rows(leaves_ref, offset):
    quarter = TREE_LEN // 4
    return pl.ds(pl.multiple_of((leaves_ref[2 * BRANCHES] ^ offset) * quarter, quarter), quarter)


def forward_kernel(
    leaves_ref,
    near_ref,
    far_ref,
    near_out_ref,
    far_out_ref,
    trunk_log_ref,
    family_log_ref,
    qkv_ref,
    out_ref,
    values_t_ref,
):
    for offset in range(4):
        half_ref = near_ref if offset < 2 else far_ref
        qkv_ref[:, quarter_rows(leaves_ref, offset), :] = half_ref[:, offset % 2]
    transpose_into(values_t_ref, qkv_ref, 2)
    for block in range(TRUNK // QROWS):
        first = block * QROWS
        queries = scaled_queries(qkv_ref, [first], QROWS)
        out, logs = forward_block(qkv_ref, values_t_ref, queries, trunk_groups(block))
        out_ref[pl.ds(first, QROWS), :] = out
        trunk_log_ref[0, :, pl.ds(first, QROWS)] = logs

    def one_family(branch, carry):
        starts = family_rows(leaves_ref, branch)
        queries = scaled_queries(qkv_ref, starts, SEG)
        out, logs = forward_block(qkv_ref, values_t_ref, queries, family_groups(starts))
        for place, start in enumerate(starts):
            out_ref[pl.ds(start, SEG), :] = out[place * SEG : (place + 1) * SEG]
        family_log_ref[0, branch] = logs
        return carry

    lax.fori_loop(0, BRANCHES, one_family, 0)
    for offset in range(4):
        half_ref = near_out_ref if offset < 2 else far_out_ref
        half_ref[offset % 2] = out_ref[quarter_rows(leaves_ref, offset), :]


def halves_spec(parts):
    quarter = TREE_LEN // 4
    if parts == 1:
        return pl.BlockSpec((2, quarter, PAIR), lambda p, leaves: (0, 0, p))
    return pl.BlockSpec((parts, 2, quarter, PAIR), lambda p, leaves: (0, 0, 0, p))


def attention_cost(products):
    visited = (TRUNK * (TRUNK + QROWS) // 2 + BRANCHES * FAMILY * (TRUNK + SEG)) // COVER
    return pl.CostEstimate(
        flops=2 * products * 4 * visited * 2 * PAIR,
        transcendentals=4 * visited,
        bytes_accessed=8 * TREE_LEN * 4 * HEAD_DIM * 2 // COVER,
    )


def attention_forward(leaves, near, far):
    width = near.shape[3]
    quarter = TREE_LEN // 4
    pairs = width // PAIR
    return pl.pallas_call(
        forward_kernel,
        grid_spec=pltpu.PrefetchScalarGridSpec(
            num_scalar_prefetch=1,
            grid=(pairs,),
            in_specs=[halves_spec(3), halves_spec(3)],
            out_specs=[
                halves_spec(1),
                halves_spec(1),
                pl.BlockSpec((1, 2, TRUNK), lambda p, leaves: (p, 0, 0)),
                pl.BlockSpec((1, BRANCHES, 2, FAMILY), lambda p, leaves: (p, 0, 0, 0)),
            ],
            scratch_shapes=[
                pltpu.VMEM((3, TREE_LEN, PAIR), BF16),
                pltpu.VMEM((TREE_LEN, PAIR), BF16),
                pltpu.VMEM((PAIR, TREE_LEN), BF16),
            ],
        ),
        out_shape=[
            jax.ShapeDtypeStruct((2, quarter, width), BF16),
            jax.ShapeDtypeStruct((2, quarter, width), BF16),
            jax.ShapeDtypeStruct((pairs, 2, TRUNK), F32),
            jax.ShapeDtypeStruct((pairs, BRANCHES, 2, FAMILY), F32),
        ],
        cost_estimate=attention_cost(2),
        name="tree_attention",
    )(leaves, near, far)


def backward_block(qkv_ref, keys_t_ref, queries, grads, outs, logs, groups):
    products = grads.astype(F32) * outs.astype(F32)
    products_t = products.T
    key_ds = [[] for _ in groups]
    value_ws = [[] for _ in groups]
    own_q, own_g, query_grads = [], [], []
    for head in range(2):
        own = head_lanes(queries, head)
        own_grads = head_lanes(grads, head)
        own_q.append(own)
        own_g.append(own_grads)
        inner = jnp.sum(
            products_t[head * HEAD_DIM : (head + 1) * HEAD_DIM], axis=0, keepdims=True
        )
        log = logs[head : head + 1]
        query_grad = None
        for place, (start, size, first, last, rule) in enumerate(groups):
            scores = masked_scores(qkv_ref[1, pl.ds(start, size), :], own[first:last], rule)
            weights = jnp.exp(scores - log[:, first:last])
            grad_weights = dot_nt(qkv_ref[2, pl.ds(start, size), :], own_grads[first:last])
            grad_scores = (weights * (grad_weights - inner[:, first:last])).astype(BF16)
            keys_t = keys_t_ref[pl.ds(head * HEAD_DIM, HEAD_DIM), pl.ds(start, size)]
            part = widen(dot_nn(keys_t, grad_scores), first, queries.shape[0], 0.0)
            query_grad = part if query_grad is None else query_grad + part
            key_ds[place].append(grad_scores)
            value_ws[place].append(weights.astype(BF16))
        query_grads.append(query_grad)
    grad_query = (jnp.concatenate(query_grads, axis=0) * HEAD_DIM ** (-0.5)).T.astype(BF16)
    key_grads, value_grads = [], []
    for place, (start, size, first, last, rule) in enumerate(groups):
        stacked_q = jnp.concatenate([own_q[0][first:last], own_q[1][first:last]], axis=0)
        stacked_g = jnp.concatenate([own_g[0][first:last], own_g[1][first:last]], axis=0)
        key_grads.append(dot_nn(jnp.concatenate(key_ds[place], axis=1), stacked_q))
        value_grads.append(dot_nn(jnp.concatenate(value_ws[place], axis=1), stacked_g))
    return grad_query, key_grads, value_grads


def backward_kernel(
    leaves_ref,
    near_ref,
    far_ref,
    near_grads_ref,
    far_grads_ref,
    near_outs_ref,
    far_outs_ref,
    trunk_log_ref,
    family_log_ref,
    near_result_ref,
    far_result_ref,
    qkv_ref,
    grads_ref,
    outs_ref,
    result_ref,
    keys_t_ref,
    trunk_keys_ref,
    trunk_values_ref,
):
    for offset in range(4):
        rows = quarter_rows(leaves_ref, offset)
        at = offset % 2
        qkv_ref[:, rows, :] = (near_ref if offset < 2 else far_ref)[:, at]
        grads_ref[rows, :] = (near_grads_ref if offset < 2 else far_grads_ref)[at]
        outs_ref[rows, :] = (near_outs_ref if offset < 2 else far_outs_ref)[at]
    transpose_into(keys_t_ref, qkv_ref, 1)
    trunk_keys_ref[...] = jnp.zeros_like(trunk_keys_ref)
    trunk_values_ref[...] = jnp.zeros_like(trunk_values_ref)
    for block in range(TRUNK // QROWS):
        first = block * QROWS
        rows = pl.ds(first, QROWS)
        groups = trunk_groups(block)
        grad_query, key_grads, value_grads = backward_block(
            qkv_ref,
            keys_t_ref,
            scaled_queries(qkv_ref, [first], QROWS),
            grads_ref[rows, :],
            outs_ref[rows, :],
            trunk_log_ref[0, :, rows],
            groups,
        )
        result_ref[0, rows, :] = grad_query
        for (start, size, _, _, _), key_grad, value_grad in zip(groups, key_grads, value_grads):
            trunk_keys_ref[pl.ds(start, size), :] += key_grad
            trunk_values_ref[pl.ds(start, size), :] += value_grad

    def one_family(branch, carry):
        starts = family_rows(leaves_ref, branch)
        groups = family_groups(starts)
        grad_query, key_grads, value_grads = backward_block(
            qkv_ref,
            keys_t_ref,
            scaled_queries(qkv_ref, starts, SEG),
            jnp.concatenate([grads_ref[pl.ds(start, SEG), :] for start in starts], axis=0),
            jnp.concatenate([outs_ref[pl.ds(start, SEG), :] for start in starts], axis=0),
            family_log_ref[0, branch],
            groups,
        )
        trunk_keys_ref[...] += key_grads[0]
        trunk_values_ref[...] += value_grads[0]
        for place, start in enumerate(starts):
            rows = pl.ds(start, SEG)
            result_ref[0, rows, :] = grad_query[place * SEG : (place + 1) * SEG]
            result_ref[1, rows, :] = key_grads[1 + place].astype(BF16)
            result_ref[2, rows, :] = value_grads[1 + place].astype(BF16)
        return carry

    lax.fori_loop(0, BRANCHES, one_family, 0)
    result_ref[1, pl.ds(0, TRUNK), :] = trunk_keys_ref[...].astype(BF16)
    result_ref[2, pl.ds(0, TRUNK), :] = trunk_values_ref[...].astype(BF16)
    for offset in range(4):
        half_ref = near_result_ref if offset < 2 else far_result_ref
        half_ref[:, offset % 2] = result_ref[:, quarter_rows(leaves_ref, offset), :]


def attention_backward(leaves, near, far, near_grads, far_grads, near_outs, far_outs, logs):
    pairs = near.shape[3] // PAIR
    return pl.pallas_call(
        backward_kernel,
        grid_spec=pltpu.PrefetchScalarGridSpec(
            num_scalar_prefetch=1,
            grid=(pairs,),
            in_specs=[
                halves_spec(3),
                halves_spec(3),
                halves_spec(1),
                halves_spec(1),
                halves_spec(1),
                halves_spec(1),
                pl.BlockSpec((1, 2, TRUNK), lambda p, leaves: (p, 0, 0)),
                pl.BlockSpec((1, BRANCHES, 2, FAMILY), lambda p, leaves: (p, 0, 0, 0)),
            ],
            out_specs=[halves_spec(3), halves_spec(3)],
            scratch_shapes=[
                pltpu.VMEM((3, TREE_LEN, PAIR), BF16),
                pltpu.VMEM((TREE_LEN, PAIR), BF16),
                pltpu.VMEM((TREE_LEN, PAIR), BF16),
                pltpu.VMEM((3, TREE_LEN, PAIR), BF16),
                pltpu.VMEM((PAIR, TREE_LEN), BF16),
                pltpu.VMEM((TRUNK, PAIR), F32),
                pltpu.VMEM((TRUNK, PAIR), F32),
            ],
        ),
        out_shape=[jax.ShapeDtypeStruct(near.shape, BF16), jax.ShapeDtypeStruct(far.shape, BF16)],
        cost_estimate=attention_cost(5),
        name="tree_attention_back",
    )(leaves, near, far, near_grads, far_grads, near_outs, far_outs, *logs)


def leaf_order(parents_row):
    first_leaf = BRANCHES + 1
    leaf_parents = parents_row[first_leaf:]
    segments = first_leaf + jnp.arange(leaf_parents.shape[0], dtype=jnp.int32)
    same = leaf_parents[:, None] == leaf_parents[None, :]
    later = segments[None, :] < segments[:, None]
    place = 2 * (leaf_parents - 1) + jnp.sum(jnp.where(same & later, 1, 0), axis=1)
    slots = jnp.arange(2 * BRANCHES, dtype=jnp.int32)
    return jnp.sum(jnp.where(slots[:, None] == place[None, :], segments[None, :], 0), axis=1)


def gates(logits, experts, expert):
    lane = lax.broadcasted_iota(jnp.int32, logits.shape, 1)
    first, second = logits[:, experts : experts + 1], logits[:, experts + 1 : experts + 2]
    top = jnp.maximum(first, second)
    first, second = jnp.exp(first - top), jnp.exp(second - top)
    total = first + second
    first, second = first / total, second / total
    if expert is None:
        return lane, first, second, None, None
    routed = jnp.where(lane < experts, logits, NEGATIVE_FILL)
    raised = jnp.exp(routed - jnp.max(routed, axis=1, keepdims=True))
    probs = raised / jnp.sum(raised, axis=1, keepdims=True)
    gate = jnp.sum(jnp.where(lane == expert, probs, 0.0), axis=1, keepdims=True)
    return lane, first, second, probs, gate


def feed_kernel(
    experts,
    routed,
    expert_ref,
    own_ref,
    side_ref,
    own_grads_ref,
    side_grads_ref,
    head_ref,
    up_ref,
    down_ref,
    own_out_ref,
    side_out_ref,
    own_back_ref,
    side_back_ref,
    active_ref,
    pre_ref,
    grad_ref,
    head_grad_ref,
):
    step = pl.program_id(0)
    early = step < pl.num_programs(0) // 2
    rows = jnp.where(early, own_ref[...], side_ref[...])
    grads = jnp.where(early, own_grads_ref[...], side_grads_ref[...]).astype(F32)
    logits = dot_nn(rows, head_ref[...])
    expert = expert_ref[0] if routed else None
    lane, first, second, probs, gate = gates(logits, experts, expert)
    coef = second * gate if routed else first
    weighted = (coef * grads).astype(BF16)
    grad_ref[...] = weighted
    pre = dot_nn(rows, up_ref[...])
    grad_active = dot_nt(weighted, down_ref[...])
    cumulative = 0.5 + 0.5 * lax.erf(pre * 0.7071067811865476)
    slope = cumulative + pre * jnp.exp(-0.5 * pre * pre) * 0.3989422804014327
    active = (pre * cumulative).astype(BF16)
    active_ref[...] = active
    grad_pre = (grad_active * slope).astype(BF16)
    pre_ref[...] = grad_pre
    out = dot_nn(active, down_ref[...])
    out_rows = (coef * out).astype(BF16)
    inner = jnp.sum(grads * out, axis=1, keepdims=True)
    swing = first * second * inner
    if routed:
        swing = -gate * swing
    grad_logits = jnp.where(lane == experts, swing, jnp.where(lane == experts + 1, -swing, 0.0))
    if routed:
        picked = jnp.where(lane == expert, 1.0, 0.0) - gate
        grad_logits = grad_logits + jnp.where(
            lane < experts, probs * picked * (second * inner), 0.0
        )
    back = dot_nt(grad_pre, up_ref[...]) + dot_nt(grad_logits.astype(BF16), head_ref[...])
    back_rows = back.astype(BF16)

    @pl.when(early)
    def _():
        own_out_ref[...] = out_rows
        own_back_ref[...] = back_rows

    @pl.when(jnp.logical_not(early))
    def _():
        side_out_ref[...] = out_rows
        side_back_ref[...] = back_rows

    @pl.when(step == 0)
    def _():
        head_grad_ref[...] = jnp.zeros_like(head_grad_ref)

    head_grad_ref[...] += dot_nn(grad_logits.T.astype(BF16), rows)


def feed(own, side, own_grads, side_grads, head, up, down, experts, expert, size):
    count = own.shape[0]
    width, hidden = up.shape
    half = count // size
    lanes = head.shape[1]
    routed = expert is not None
    pick = jnp.reshape(expert, (1,)) if routed else jnp.zeros((1,), jnp.int32)
    early = pl.BlockSpec((size, width), lambda i, pick: (jnp.minimum(i, half - 1), 0))
    late = pl.BlockSpec((size, width), lambda i, pick: (jnp.maximum(i - half, 0), 0))

    def held(shape):
        return pl.BlockSpec(shape, lambda i, pick: (0, 0), pipeline_mode=pl.Buffered(1))

    wide = pl.BlockSpec((size, width), lambda i, pick: (i, 0))
    deep = pl.BlockSpec((size, hidden), lambda i, pick: (i, 0))
    quarter = jax.ShapeDtypeStruct((count, width), BF16)
    return pl.pallas_call(
        functools.partial(feed_kernel, experts, routed),
        grid_spec=pltpu.PrefetchScalarGridSpec(
            num_scalar_prefetch=1,
            grid=(2 * half,),
            in_specs=[
                early,
                late,
                early,
                late,
                held((width, lanes)),
                held((width, hidden)),
                held((hidden, width)),
            ],
            out_specs=[
                early,
                late,
                early,
                late,
                deep,
                deep,
                wide,
                pl.BlockSpec((lanes, width), lambda i, pick: (0, 0)),
            ],
        ),
        out_shape=[
            quarter,
            quarter,
            quarter,
            quarter,
            jax.ShapeDtypeStruct((2 * count, hidden), BF16),
            jax.ShapeDtypeStruct((2 * count, hidden), BF16),
            jax.ShapeDtypeStruct((2 * count, width), BF16),
            jax.ShapeDtypeStruct((lanes, width), F32),
        ],
        cost_estimate=pl.CostEstimate(
            flops=16 * count * width * hidden // COVER,
            transcendentals=4 * count * hidden // COVER,
            bytes_accessed=2 * (8 * count * width + 4 * count * hidden + 2 * width * hidden) // COVER,
        ),
        compiler_params=pltpu.CompilerParams(vmem_limit_bytes=60 * 1024 * 1024),
        name="feed_routed" if routed else "feed_dense",
    )(pick, own, side, own_grads, side_grads, head, up, down)


LANES = 128
DENSE_ROWS = 320
EXPERT_ROWS = 448


def norm_parts(values):
    row_mean = jnp.mean(values, axis=-1, keepdims=True)
    centred = values - row_mean
    row_var = jnp.mean(centred * centred, axis=-1, keepdims=True)
    inverse = lax.rsqrt(row_var + EPSILON)
    return (centred * inverse, inverse)


def norm_back(grad_normed, gain_vec, scaled, inverse):
    grad_scaled = grad_normed * gain_vec
    first_mean = jnp.mean(grad_scaled, axis=-1, keepdims=True)
    second = jnp.mean(grad_scaled * scaled, axis=-1, keepdims=True)
    return inverse * (grad_scaled - first_mean - scaled * second)


def after(value, *others):
    return lax.optimization_barrier((value, *others))[0]


def from_side(values):
    return lax.ppermute(values, "tensor", [(i, i ^ 1) for i in range(4)])


def from_far(values):
    return lax.ppermute(values, "tensor", [(i, i ^ 2) for i in range(4)])


def plus_side(own, side):
    return own.astype(F32) + from_side(side.astype(BF16)).astype(F32)


def sum_over(values, axis):
    count, step = lax.axis_size(axis), 1
    while step < count:
        pairs = [(i, i ^ step) for i in range(count)]
        values = values + lax.ppermute(values, axis, pairs)
        step *= 2
    return values


def exchange(blocks):
    return lax.all_to_all(blocks, "expert", split_axis=0, concat_axis=0, tiled=True)


def scatter_sum(strips):
    strips = with_layout_constraint(strips.astype(BF16), Layout(major_to_minor=(0, 1)))
    return lax.psum_scatter(strips, "expert", scatter_dimension=0, tiled=True).astype(F32)


def slots_of(expert_ids, experts, capacity):
    rows = expert_ids.shape[0]
    chosen = expert_ids[:, None] == jnp.arange(experts, dtype=jnp.int32)[None, :]
    at = jnp.arange(rows, dtype=jnp.int32)
    before = (at[None, :] < at[:, None]).astype(BF16)
    earlier = jnp.dot(before, chosen.astype(BF16), preferred_element_type=F32)
    slot = jnp.sum(jnp.where(chosen, earlier, 0.0), axis=1).astype(jnp.int32)
    place = expert_ids * capacity + slot
    places = jnp.arange(experts * capacity, dtype=jnp.int32)
    return (places[:, None] == place[None, :]).astype(BF16)


def per_device(
    tokens,
    cotangent,
    routes,
    parents,
    ln_attn,
    w_qkv,
    w_out,
    ln_mlp,
    w_up,
    w_down,
    w_router,
    w_mix,
    ex_up,
    ex_down,
):
    tok_dev, width = tokens.shape
    mine = lax.axis_index("tensor")
    experts = w_router.shape[1]
    capacity = max(2, tok_dev * 7 // (5 * experts))
    heads_width = w_qkv.shape[2]
    hidden = w_up.shape[1]
    leaves = jnp.concatenate([leaf_order(parents[0]), mine.astype(jnp.int32)[None]])

    scaled_one, inverse_one = norm_parts(tokens.astype(F32))
    normed_own = (scaled_one * ln_attn).astype(BF16)
    normed_far = from_far(normed_own)
    near_one = jnp.concatenate([normed_own, from_side(normed_own)], axis=0)

    quarter_ids = routes[:, 0].reshape(4, tok_dev)

    def slots_at(offset):
        ids = lax.dynamic_index_in_dim(quarter_ids, mine ^ offset, 0, keepdims=False)
        return slots_of(ids, experts, capacity)

    own_slots, far_slots = slots_at(0), slots_at(2)

    def dispatch(slots, rows):
        placed = jnp.dot(slots, rows, preferred_element_type=F32).astype(BF16)
        return exchange(placed.reshape(experts, capacity, width)).reshape(-1, width)

    own_grads = dispatch(own_slots, cotangent)
    cotangent_side = from_side(cotangent)

    def project(rows):
        qkv = jnp.einsum("td,sdc->stc", rows, w_qkv, preferred_element_type=F32)
        return qkv.astype(BF16).reshape(3, 2, tok_dev, heads_width)

    lanes = -(-(experts + 2) // LANES) * LANES
    head = jnp.concatenate(
        [w_router, w_mix, jnp.zeros((width, lanes - experts - 2), BF16)], axis=1
    )
    near_qkv = project(near_one)
    cotangent_far = from_far(after(cotangent, normed_far))
    normed_far, near_qkv, head = lax.optimization_barrier((normed_far, near_qkv, head))
    far_one = jnp.concatenate([normed_far, from_side(normed_far)], axis=0)
    far_qkv = project(far_one)
    near_out, far_out, *logs = attention_forward(leaves, near_qkv, far_qkv)
    far_out, own_grads, cotangent_far, cotangent_side = lax.optimization_barrier(
        (far_out, own_grads, cotangent_far, cotangent_side)
    )

    def branch_part(rows):
        return jnp.dot(rows, w_out, preferred_element_type=F32)

    far_sum = plus_side(branch_part(far_out[0]), branch_part(far_out[1])).astype(BF16)
    branch = plus_side(branch_part(near_out[0]), branch_part(near_out[1]))
    branch_far = from_far(far_sum)
    side_grads = from_side(own_grads)
    cotangent_corner = from_side(cotangent_far)
    branch_far, side_grads, cotangent_corner = lax.optimization_barrier(
        (branch_far, side_grads, cotangent_corner)
    )
    residual = tokens.astype(F32) + (branch + branch_far.astype(F32))

    scaled_two, inverse_two = norm_parts(residual)
    normed_two = (scaled_two * ln_mlp).astype(BF16)
    normed_two_far = from_far(normed_two)
    normed_two_side = from_side(normed_two)
    own_rows = dispatch(own_slots, normed_two)

    def dense(own, side, own_cotangent, side_cotangent):
        return feed(
            own, side, own_cotangent, side_cotangent, head, w_up, w_down, experts, None, DENSE_ROWS
        )

    def product(left, right):
        return jnp.einsum("gd,gf->df", left, right, preferred_element_type=F32)

    def weight_grads(near_left, far_left, near_right, far_right):
        return product(near_left, near_right) + product(far_left, far_right)

    near_dense = dense(normed_two, normed_two_side, cotangent, cotangent_side)
    near_two = jnp.concatenate([normed_two, normed_two_side], axis=0)
    grad_up = product(near_two, near_dense[5])
    grad_down = product(near_dense[6], near_dense[4])
    normed_two_far, grad_up, grad_down, own_rows = lax.optimization_barrier(
        (normed_two_far, grad_up, grad_down, own_rows)
    )
    far_rows = from_far(own_rows)
    far_grads = dispatch(far_slots, after(cotangent_far, own_rows))
    normed_two_corner = from_side(normed_two_far)
    far_dense = list(dense(normed_two_far, normed_two_corner, cotangent_far, cotangent_corner))
    far_rows, far_dense[6], far_dense[5] = lax.optimization_barrier(
        (far_rows, far_dense[6], far_dense[5])
    )
    far_two = jnp.concatenate([normed_two_far, normed_two_corner], axis=0)
    grad_up = grad_up + product(far_two, far_dense[5])
    grad_down = grad_down + product(far_dense[6], far_dense[4])
    dense_grads = jnp.concatenate([grad_up.astype(BF16), grad_down.astype(BF16)], axis=1)

    expert = lax.axis_index("expert").astype(jnp.int32)

    def routed(own, side, own_cotangent, side_cotangent):
        return feed(
            own,
            side,
            own_cotangent,
            side_cotangent,
            head,
            ex_up[0],
            ex_down[0],
            experts,
            expert,
            EXPERT_ROWS,
        )

    far_rows, dense_grads = lax.optimization_barrier((far_rows, dense_grads))
    dense_grads = scatter_sum(dense_grads)
    corner_rows = from_side(far_rows)
    side_rows = from_side(own_rows)

    def chip_sum(parts, place, *others):
        return plus_side(parts[place], after(parts[place + 1], *others))

    far_expert = routed(far_rows, corner_rows, far_grads, from_side(far_grads))
    dense_back_far = from_far(chip_sum(far_dense, 2).astype(BF16))
    dense_out_far = from_far(chip_sum(far_dense, 0).astype(BF16))
    dense_back, dense_out = chip_sum(near_dense, 2), chip_sum(near_dense, 0)
    far_back = chip_sum(far_expert, 2).astype(BF16)
    own_rows, far_back, dense_back_far, dense_out_far = lax.optimization_barrier(
        (own_rows, far_back, dense_back_far, dense_out_far)
    )
    near_expert = routed(own_rows, side_rows, own_grads, side_grads)
    dense_back = dense_back + dense_back_far.astype(F32)
    dense_out = dense_out + dense_out_far.astype(F32)

    def send_back(rows):
        rows = rows.astype(BF16).reshape(experts, capacity, width)
        return exchange(rows).reshape(-1, width)

    def picked(rows):
        return lax.dot_general(
            own_slots, rows, (((0,), (0,)), ((), ())), preferred_element_type=F32
        )

    expert_back = chip_sum(near_expert, 2) + from_far(far_back).astype(F32)
    grad_normed_two, dense_grads = lax.optimization_barrier(
        (dense_back + picked(send_back(expert_back)), dense_grads)
    )
    far_expert_out = chip_sum(far_expert, 0, near_expert[2]).astype(BF16)
    expert_out = chip_sum(near_expert, 0, expert_back) + from_far(far_expert_out).astype(F32)
    expert_out = send_back(after(expert_out, grad_normed_two))

    near_tokens = jnp.concatenate([own_rows, side_rows], axis=0)
    far_tokens = jnp.concatenate([far_rows, corner_rows], axis=0)
    grad_ex_up = weight_grads(near_tokens, far_tokens, near_expert[5], far_expert[5])[None]
    grad_ex_down = weight_grads(near_expert[4], far_expert[4], near_expert[6], far_expert[6])[None]

    gain_two = jnp.sum(grad_normed_two * scaled_two, axis=0)
    grad_residual = cotangent.astype(F32) + norm_back(
        grad_normed_two, ln_mlp, scaled_two, inverse_two
    )
    grad_branch = grad_residual.astype(BF16)
    grad_branch_far = from_far(grad_branch)
    near_branch = jnp.concatenate([grad_branch, from_side(grad_branch)], axis=0)
    far_branch = jnp.concatenate([grad_branch_far, from_side(grad_branch_far)], axis=0)
    head_grads = near_dense[7] + far_dense[7] + near_expert[7] + far_expert[7]
    small = jnp.concatenate([head_grads[: experts + 2], gain_two[None]], axis=0)
    small = sum_over(small, "tensor")

    def into_heads(rows):
        grads = jnp.einsum("gd,cd->gc", rows, w_out, preferred_element_type=F32)
        return grads.astype(BF16).reshape(2, tok_dev, heads_width)

    near_heads, far_heads = into_heads(near_branch), into_heads(far_branch)
    near_heads, grad_ex_up, grad_ex_down, small = lax.optimization_barrier(
        (near_heads, grad_ex_up, grad_ex_down, small)
    )
    near_result, far_result = attention_backward(
        leaves, near_qkv, far_qkv, near_heads, far_heads, near_out, far_out, logs
    )
    near_result, expert_out = lax.optimization_barrier((near_result, expert_out))

    def normed_part(grads):
        return jnp.einsum("sgc,sdc->gd", grads, w_qkv, preferred_element_type=F32)

    corner_part = normed_part(far_result[:, 1])
    far_result, corner_part = lax.optimization_barrier((far_result, corner_part))
    far_sum = plus_side(normed_part(far_result[:, 0]), corner_part).astype(BF16)
    near_result, far_result, near_branch, expert_out, far_sum = lax.optimization_barrier(
        (near_result, far_result, near_branch, expert_out, far_sum)
    )
    near_sum = plus_side(normed_part(near_result[:, 0]), normed_part(near_result[:, 1]))
    grad_normed_one = near_sum + from_far(far_sum).astype(F32)
    out = (residual + dense_out + picked(expert_out)).astype(BF16)

    near_result = near_result.reshape(3, 2 * tok_dev, heads_width)
    far_result = far_result.reshape(3, 2 * tok_dev, heads_width)
    grad_w_qkv = jnp.einsum(
        "gd,sgc->dsc", near_one, near_result, preferred_element_type=F32
    ) + jnp.einsum("gd,sgc->dsc", far_one, far_result, preferred_element_type=F32)
    flat = (2 * tok_dev, heads_width)
    grad_w_out = weight_grads(near_branch, far_branch, near_out.reshape(flat), far_out.reshape(flat))
    small_columns = -(-small.shape[0] // LANES) * LANES
    small_block = jnp.pad(small, ((0, small_columns - small.shape[0]), (0, 0))).T
    last_grads = scatter_sum(
        jnp.concatenate(
            [
                grad_w_qkv.reshape(width, 3 * heads_width).astype(BF16),
                grad_w_out.astype(BF16),
                small_block.astype(BF16),
            ],
            axis=1,
        )
    )
    scaled_far = normed_far.astype(F32) / ln_attn
    gain_one = jnp.sum(near_sum * scaled_one + far_sum.astype(F32) * scaled_far, axis=0, keepdims=True)
    grad_ln_attn = sum_over(sum_over(gain_one, "tensor"), "expert")[0]
    grad_tokens = grad_residual + norm_back(grad_normed_one, ln_attn, scaled_one, inverse_one)

    strip = last_grads.shape[0]
    after_qkv = 3 * heads_width
    after_out = after_qkv + heads_width
    return (
        out,
        grad_tokens,
        grad_ln_attn,
        last_grads[:, :after_qkv].reshape(strip, 3, heads_width).transpose(1, 0, 2),
        last_grads[:, after_qkv:after_out].T,
        last_grads[:, after_out + experts + 2],
        dense_grads[:, :hidden],
        dense_grads[:, hidden:].T,
        last_grads[:, after_out : after_out + experts],
        last_grads[:, after_out + experts : after_out + experts + 2],
        grad_ex_up,
        grad_ex_down,
    )


def solution(mesh):
    return jax.shard_map(
        per_device,
        mesh=mesh,
        in_specs=(
            P(("expert", "tensor"), None),
            P(("expert", "tensor"), None),
            P("expert", None),
            P("expert", None),
            P(),
            P(None, None, "tensor"),
            P("tensor", None),
            P(),
            P(None, "tensor"),
            P("tensor", None),
            P(),
            P(),
            P("expert", None, "tensor"),
            P("expert", "tensor", None),
        ),
        out_specs=(
            P(("expert", "tensor"), None),
            P(("expert", "tensor"), None),
            P(),
            P(None, "expert", "tensor"),
            P("tensor", "expert"),
            P("expert"),
            P("expert", "tensor"),
            P("tensor", "expert"),
            P("expert", None),
            P("expert", None),
            P("expert", None, "tensor"),
            P("expert", "tensor", None),
        ),
        check_vma=False,
    )
```

```python
import functools

import jax
import jax.numpy as jnp
from jax import lax
from jax.experimental import pallas as pl
from jax.experimental.layout import Layout, with_layout_constraint
from jax.experimental.pallas import tpu as pltpu
from jax.sharding import PartitionSpec as P

HEAD_DIM = 64
TRUNK = 1024
SEG = 128
SEGS = 13
TREE_LEN = 2560
BRANCHES = 4
FAMILY = 3 * SEG
QROWS = 256
COVER = 8
PAIR = 2 * HEAD_DIM
NEGATIVE_FILL = -1e30
F32 = jnp.float32
BF16 = jnp.bfloat16
EPSILON = 1e-05


def dot_nn(a, b):
    return lax.dot_general(a, b, (((1,), (0,)), ((), ())), preferred_element_type=F32)


def dot_nt(a, b):
    return lax.dot_general(a, b, (((1,), (1,)), ((), ())), preferred_element_type=F32)


def head_lanes(rows, head):
    lane = lax.broadcasted_iota(jnp.int32, rows.shape, 1)
    return jnp.where(lane // HEAD_DIM == head, rows, jnp.zeros_like(rows))


def causal(scores):
    key = lax.broadcasted_iota(jnp.int32, scores.shape, 0)
    query = lax.broadcasted_iota(jnp.int32, scores.shape, 1)
    return jnp.where(key <= query, scores, NEGATIVE_FILL)


def family_rows(leaves_ref, branch):
    def start(segment):
        return pl.multiple_of(TRUNK + (segment - 1) * SEG, SEG)

    return [start(branch + 1), start(leaves_ref[2 * branch]), start(leaves_ref[2 * branch + 1])]


def transpose_into(target_ref, source_ref, part):
    for first in range(0, TREE_LEN, 512):
        piece = source_ref[part, pl.ds(first, 512), :].astype(F32)
        target_ref[:, pl.ds(first, 512)] = piece.T.astype(BF16)


def widen(piece, first, width, fill):
    parts = []
    if first:
        parts.append(jnp.full((piece.shape[0], first), fill, piece.dtype))
    parts.append(piece)
    rest = width - first - piece.shape[1]
    if rest:
        parts.append(jnp.full((piece.shape[0], rest), fill, piece.dtype))
    return parts[0] if len(parts) == 1 else jnp.concatenate(parts, axis=1)


def trunk_groups(block):
    first = block * QROWS
    groups = [(0, first, 0, QROWS, None)] if first else []
    return groups + [(first, QROWS, 0, QROWS, "causal")]


def family_groups(starts):
    return [
        (0, TRUNK, 0, FAMILY, None),
        (starts[0], SEG, 0, FAMILY, "branch"),
        (starts[1], SEG, SEG, 2 * SEG, "causal"),
        (starts[2], SEG, 2 * SEG, FAMILY, "causal"),
    ]


def masked_scores(keys, queries, rule):
    scores = dot_nt(keys, queries)
    if rule == "causal":
        return causal(scores)
    if rule == "branch":
        return jnp.concatenate([causal(scores[:, :SEG]), scores[:, SEG:]], axis=1)
    return scores


def forward_block(qkv_ref, values_t_ref, queries, groups):
    width = queries.shape[0]
    outs, logs = [], []
    for head in range(2):
        own = head_lanes(queries, head)
        all_scores = [
            masked_scores(qkv_ref[1, pl.ds(start, size), :], own[first:last], rule)
            for start, size, first, last, rule in groups
        ]
        top = functools.reduce(
            jnp.maximum,
            [
                widen(jnp.max(s, axis=0, keepdims=True), first, width, NEGATIVE_FILL)
                for s, (_, _, first, last, _) in zip(all_scores, groups)
            ],
        )
        total, output = None, None
        for s, (start, size, first, last, _) in zip(all_scores, groups):
            weights = jnp.exp(s - top[:, first:last])
            part = widen(jnp.sum(weights, axis=0, keepdims=True), first, width, 0.0)
            values_t = values_t_ref[pl.ds(head * HEAD_DIM, HEAD_DIM), pl.ds(start, size)]
            mixed = widen(dot_nn(values_t, weights.astype(BF16)), first, width, 0.0)
            total = part if total is None else total + part
            output = mixed if output is None else output + mixed
        outs.append(output / total)
        logs.append(top + jnp.log(total))
    return jnp.concatenate(outs, axis=0).T.astype(BF16), jnp.concatenate(logs, axis=0)


def scaled_queries(qkv_ref, starts, size):
    rows = [qkv_ref[0, pl.ds(start, size), :] for start in starts]
    rows = rows[0] if len(rows) == 1 else jnp.concatenate(rows, axis=0)
    return rows * jnp.asarray(HEAD_DIM ** (-0.5), BF16)


def quarter_rows(leaves_ref, offset):
    quarter = TREE_LEN // 4
    return pl.ds(pl.multiple_of((leaves_ref[2 * BRANCHES] ^ offset) * quarter, quarter), quarter)


def forward_kernel(
    leaves_ref,
    near_ref,
    far_ref,
    near_out_ref,
    far_out_ref,
    trunk_log_ref,
    family_log_ref,
    qkv_ref,
    out_ref,
    values_t_ref,
):
    for offset in range(4):
        half_ref = near_ref if offset < 2 else far_ref
        qkv_ref[:, quarter_rows(leaves_ref, offset), :] = half_ref[:, offset % 2]
    transpose_into(values_t_ref, qkv_ref, 2)
    for block in range(TRUNK // QROWS):
        first = block * QROWS
        queries = scaled_queries(qkv_ref, [first], QROWS)
        out, logs = forward_block(qkv_ref, values_t_ref, queries, trunk_groups(block))
        out_ref[pl.ds(first, QROWS), :] = out
        trunk_log_ref[0, :, pl.ds(first, QROWS)] = logs

    def one_family(branch, carry):
        starts = family_rows(leaves_ref, branch)
        queries = scaled_queries(qkv_ref, starts, SEG)
        out, logs = forward_block(qkv_ref, values_t_ref, queries, family_groups(starts))
        for place, start in enumerate(starts):
            out_ref[pl.ds(start, SEG), :] = out[place * SEG : (place + 1) * SEG]
        family_log_ref[0, branch] = logs
        return carry

    lax.fori_loop(0, BRANCHES, one_family, 0)
    for offset in range(4):
        half_ref = near_out_ref if offset < 2 else far_out_ref
        half_ref[offset % 2] = out_ref[quarter_rows(leaves_ref, offset), :]


def halves_spec(parts):
    quarter = TREE_LEN // 4
    if parts == 1:
        return pl.BlockSpec((2, quarter, PAIR), lambda p, leaves: (0, 0, p))
    return pl.BlockSpec((parts, 2, quarter, PAIR), lambda p, leaves: (0, 0, 0, p))


def attention_cost(products, cover):
    visited = (TRUNK * (TRUNK + QROWS) // 2 + BRANCHES * FAMILY * (TRUNK + SEG)) // cover
    return pl.CostEstimate(
        flops=2 * products * 4 * visited * 2 * PAIR,
        transcendentals=4 * visited,
        bytes_accessed=8 * TREE_LEN * 4 * HEAD_DIM * 2 // cover,
    )


def attention_forward(leaves, near, far):
    width = near.shape[3]
    quarter = TREE_LEN // 4
    pairs = width // PAIR
    return pl.pallas_call(
        forward_kernel,
        grid_spec=pltpu.PrefetchScalarGridSpec(
            num_scalar_prefetch=1,
            grid=(pairs,),
            in_specs=[halves_spec(3), halves_spec(3)],
            out_specs=[
                halves_spec(1),
                halves_spec(1),
                pl.BlockSpec((1, 2, TRUNK), lambda p, leaves: (p, 0, 0)),
                pl.BlockSpec((1, BRANCHES, 2, FAMILY), lambda p, leaves: (p, 0, 0, 0)),
            ],
            scratch_shapes=[
                pltpu.VMEM((3, TREE_LEN, PAIR), BF16),
                pltpu.VMEM((TREE_LEN, PAIR), BF16),
                pltpu.VMEM((PAIR, TREE_LEN), BF16),
            ],
        ),
        out_shape=[
            jax.ShapeDtypeStruct((2, quarter, width), BF16),
            jax.ShapeDtypeStruct((2, quarter, width), BF16),
            jax.ShapeDtypeStruct((pairs, 2, TRUNK), F32),
            jax.ShapeDtypeStruct((pairs, BRANCHES, 2, FAMILY), F32),
        ],
        cost_estimate=attention_cost(2, COVER),
        name="tree_attention",
    )(leaves, near, far)


def backward_block(qkv_ref, keys_t_ref, queries, grads, outs, logs, groups):
    products = grads.astype(F32) * outs.astype(F32)
    products_t = products.T
    key_ds = [[] for _ in groups]
    value_ws = [[] for _ in groups]
    own_q, own_g, query_grads = [], [], []
    for head in range(2):
        own = head_lanes(queries, head)
        own_grads = head_lanes(grads, head)
        own_q.append(own)
        own_g.append(own_grads)
        inner = jnp.sum(
            products_t[head * HEAD_DIM : (head + 1) * HEAD_DIM], axis=0, keepdims=True
        )
        log = logs[head : head + 1]
        query_grad = None
        for place, (start, size, first, last, rule) in enumerate(groups):
            scores = masked_scores(qkv_ref[1, pl.ds(start, size), :], own[first:last], rule)
            weights = jnp.exp(scores - log[:, first:last])
            grad_weights = dot_nt(qkv_ref[2, pl.ds(start, size), :], own_grads[first:last])
            grad_scores = (weights * (grad_weights - inner[:, first:last])).astype(BF16)
            keys_t = keys_t_ref[pl.ds(head * HEAD_DIM, HEAD_DIM), pl.ds(start, size)]
            part = widen(dot_nn(keys_t, grad_scores), first, queries.shape[0], 0.0)
            query_grad = part if query_grad is None else query_grad + part
            key_ds[place].append(grad_scores)
            value_ws[place].append(weights.astype(BF16))
        query_grads.append(query_grad)
    grad_query = (jnp.concatenate(query_grads, axis=0) * HEAD_DIM ** (-0.5)).T.astype(BF16)
    key_grads, value_grads = [], []
    for place, (start, size, first, last, rule) in enumerate(groups):
        stacked_q = jnp.concatenate([own_q[0][first:last], own_q[1][first:last]], axis=0)
        stacked_g = jnp.concatenate([own_g[0][first:last], own_g[1][first:last]], axis=0)
        key_grads.append(dot_nn(jnp.concatenate(key_ds[place], axis=1), stacked_q))
        value_grads.append(dot_nn(jnp.concatenate(value_ws[place], axis=1), stacked_g))
    return grad_query, key_grads, value_grads


def backward_kernel(
    leaves_ref,
    near_ref,
    far_ref,
    near_grads_ref,
    far_grads_ref,
    near_outs_ref,
    far_outs_ref,
    trunk_log_ref,
    family_log_ref,
    near_result_ref,
    far_result_ref,
    qkv_ref,
    grads_ref,
    outs_ref,
    result_ref,
    keys_t_ref,
    trunk_keys_ref,
    trunk_values_ref,
):
    for offset in range(4):
        rows = quarter_rows(leaves_ref, offset)
        at = offset % 2
        qkv_ref[:, rows, :] = (near_ref if offset < 2 else far_ref)[:, at]
        grads_ref[rows, :] = (near_grads_ref if offset < 2 else far_grads_ref)[at]
        outs_ref[rows, :] = (near_outs_ref if offset < 2 else far_outs_ref)[at]
    transpose_into(keys_t_ref, qkv_ref, 1)
    trunk_keys_ref[...] = jnp.zeros_like(trunk_keys_ref)
    trunk_values_ref[...] = jnp.zeros_like(trunk_values_ref)
    for block in range(TRUNK // QROWS):
        first = block * QROWS
        rows = pl.ds(first, QROWS)
        groups = trunk_groups(block)
        grad_query, key_grads, value_grads = backward_block(
            qkv_ref,
            keys_t_ref,
            scaled_queries(qkv_ref, [first], QROWS),
            grads_ref[rows, :],
            outs_ref[rows, :],
            trunk_log_ref[0, :, rows],
            groups,
        )
        result_ref[0, rows, :] = grad_query
        for (start, size, _, _, _), key_grad, value_grad in zip(groups, key_grads, value_grads):
            trunk_keys_ref[pl.ds(start, size), :] += key_grad
            trunk_values_ref[pl.ds(start, size), :] += value_grad

    def one_family(branch, carry):
        starts = family_rows(leaves_ref, branch)
        groups = family_groups(starts)
        grad_query, key_grads, value_grads = backward_block(
            qkv_ref,
            keys_t_ref,
            scaled_queries(qkv_ref, starts, SEG),
            jnp.concatenate([grads_ref[pl.ds(start, SEG), :] for start in starts], axis=0),
            jnp.concatenate([outs_ref[pl.ds(start, SEG), :] for start in starts], axis=0),
            family_log_ref[0, branch],
            groups,
        )
        trunk_keys_ref[...] += key_grads[0]
        trunk_values_ref[...] += value_grads[0]
        for place, start in enumerate(starts):
            rows = pl.ds(start, SEG)
            result_ref[0, rows, :] = grad_query[place * SEG : (place + 1) * SEG]
            result_ref[1, rows, :] = key_grads[1 + place].astype(BF16)
            result_ref[2, rows, :] = value_grads[1 + place].astype(BF16)
        return carry

    lax.fori_loop(0, BRANCHES, one_family, 0)
    result_ref[1, pl.ds(0, TRUNK), :] = trunk_keys_ref[...].astype(BF16)
    result_ref[2, pl.ds(0, TRUNK), :] = trunk_values_ref[...].astype(BF16)
    for offset in range(4):
        half_ref = near_result_ref if offset < 2 else far_result_ref
        half_ref[:, offset % 2] = result_ref[:, quarter_rows(leaves_ref, offset), :]


def attention_backward(leaves, near, far, near_grads, far_grads, near_outs, far_outs, logs):
    pairs = near.shape[3] // PAIR
    return pl.pallas_call(
        backward_kernel,
        grid_spec=pltpu.PrefetchScalarGridSpec(
            num_scalar_prefetch=1,
            grid=(pairs,),
            in_specs=[
                halves_spec(3),
                halves_spec(3),
                halves_spec(1),
                halves_spec(1),
                halves_spec(1),
                halves_spec(1),
                pl.BlockSpec((1, 2, TRUNK), lambda p, leaves: (p, 0, 0)),
                pl.BlockSpec((1, BRANCHES, 2, FAMILY), lambda p, leaves: (p, 0, 0, 0)),
            ],
            out_specs=[halves_spec(3), halves_spec(3)],
            scratch_shapes=[
                pltpu.VMEM((3, TREE_LEN, PAIR), BF16),
                pltpu.VMEM((TREE_LEN, PAIR), BF16),
                pltpu.VMEM((TREE_LEN, PAIR), BF16),
                pltpu.VMEM((3, TREE_LEN, PAIR), BF16),
                pltpu.VMEM((PAIR, TREE_LEN), BF16),
                pltpu.VMEM((TRUNK, PAIR), F32),
                pltpu.VMEM((TRUNK, PAIR), F32),
            ],
        ),
        out_shape=[jax.ShapeDtypeStruct(near.shape, BF16), jax.ShapeDtypeStruct(far.shape, BF16)],
        cost_estimate=attention_cost(5, 1),
        name="tree_attention_back",
    )(leaves, near, far, near_grads, far_grads, near_outs, far_outs, *logs)


def leaf_order(parents_row):
    first_leaf = BRANCHES + 1
    leaf_parents = parents_row[first_leaf:]
    segments = first_leaf + jnp.arange(leaf_parents.shape[0], dtype=jnp.int32)
    same = leaf_parents[:, None] == leaf_parents[None, :]
    later = segments[None, :] < segments[:, None]
    place = 2 * (leaf_parents - 1) + jnp.sum(jnp.where(same & later, 1, 0), axis=1)
    slots = jnp.arange(2 * BRANCHES, dtype=jnp.int32)
    return jnp.sum(jnp.where(slots[:, None] == place[None, :], segments[None, :], 0), axis=1)


def gates(logits, experts, expert):
    lane = lax.broadcasted_iota(jnp.int32, logits.shape, 1)
    first, second = logits[:, experts : experts + 1], logits[:, experts + 1 : experts + 2]
    top = jnp.maximum(first, second)
    first, second = jnp.exp(first - top), jnp.exp(second - top)
    total = first + second
    first, second = first / total, second / total
    if expert is None:
        return lane, first, second, None, None
    routed = jnp.where(lane < experts, logits, NEGATIVE_FILL)
    raised = jnp.exp(routed - jnp.max(routed, axis=1, keepdims=True))
    probs = raised / jnp.sum(raised, axis=1, keepdims=True)
    gate = jnp.sum(jnp.where(lane == expert, probs, 0.0), axis=1, keepdims=True)
    return lane, first, second, probs, gate


def feed_kernel(
    experts,
    routed,
    expert_ref,
    own_ref,
    side_ref,
    own_grads_ref,
    side_grads_ref,
    head_ref,
    up_ref,
    down_ref,
    own_out_ref,
    side_out_ref,
    own_back_ref,
    side_back_ref,
    active_ref,
    pre_ref,
    grad_ref,
    head_grad_ref,
):
    step = pl.program_id(0)
    early = step < pl.num_programs(0) // 2
    rows = jnp.where(early, own_ref[...], side_ref[...])
    grads = jnp.where(early, own_grads_ref[...], side_grads_ref[...]).astype(F32)
    logits = dot_nn(rows, head_ref[...])
    expert = expert_ref[0] if routed else None
    lane, first, second, probs, gate = gates(logits, experts, expert)
    coef = second * gate if routed else first
    weighted = (coef * grads).astype(BF16)
    grad_ref[...] = weighted
    pre = dot_nn(rows, up_ref[...])
    grad_active = dot_nt(weighted, down_ref[...])
    cumulative = 0.5 + 0.5 * lax.erf(pre * 0.7071067811865476)
    slope = cumulative + pre * jnp.exp(-0.5 * pre * pre) * 0.3989422804014327
    active = (pre * cumulative).astype(BF16)
    active_ref[...] = active
    grad_pre = (grad_active * slope).astype(BF16)
    pre_ref[...] = grad_pre
    out = dot_nn(active, down_ref[...])
    out_rows = (coef * out).astype(BF16)
    inner = jnp.sum(grads * out, axis=1, keepdims=True)
    swing = first * second * inner
    if routed:
        swing = -gate * swing
    grad_logits = jnp.where(lane == experts, swing, jnp.where(lane == experts + 1, -swing, 0.0))
    if routed:
        picked = jnp.where(lane == expert, 1.0, 0.0) - gate
        grad_logits = grad_logits + jnp.where(
            lane < experts, probs * picked * (second * inner), 0.0
        )
    back = dot_nt(grad_pre, up_ref[...]) + dot_nt(grad_logits.astype(BF16), head_ref[...])
    back_rows = back.astype(BF16)

    @pl.when(early)
    def _():
        own_out_ref[...] = out_rows
        own_back_ref[...] = back_rows

    @pl.when(jnp.logical_not(early))
    def _():
        side_out_ref[...] = out_rows
        side_back_ref[...] = back_rows

    @pl.when(step == 0)
    def _():
        head_grad_ref[...] = jnp.zeros_like(head_grad_ref)

    head_grad_ref[...] += dot_nn(grad_logits.T.astype(BF16), rows)


def feed(own, side, own_grads, side_grads, head, up, down, experts, expert, size):
    count = own.shape[0]
    width, hidden = up.shape
    half = count // size
    lanes = head.shape[1]
    routed = expert is not None
    pick = jnp.reshape(expert, (1,)) if routed else jnp.zeros((1,), jnp.int32)
    early = pl.BlockSpec((size, width), lambda i, pick: (jnp.minimum(i, half - 1), 0))
    late = pl.BlockSpec((size, width), lambda i, pick: (jnp.maximum(i - half, 0), 0))

    def held(shape):
        return pl.BlockSpec(shape, lambda i, pick: (0, 0), pipeline_mode=pl.Buffered(1))

    wide = pl.BlockSpec((size, width), lambda i, pick: (i, 0))
    deep = pl.BlockSpec((size, hidden), lambda i, pick: (i, 0))
    quarter = jax.ShapeDtypeStruct((count, width), BF16)
    return pl.pallas_call(
        functools.partial(feed_kernel, experts, routed),
        grid_spec=pltpu.PrefetchScalarGridSpec(
            num_scalar_prefetch=1,
            grid=(2 * half,),
            in_specs=[
                early,
                late,
                early,
                late,
                held((width, lanes)),
                held((width, hidden)),
                held((hidden, width)),
            ],
            out_specs=[
                early,
                late,
                early,
                late,
                deep,
                deep,
                wide,
                pl.BlockSpec((lanes, width), lambda i, pick: (0, 0)),
            ],
        ),
        out_shape=[
            quarter,
            quarter,
            quarter,
            quarter,
            jax.ShapeDtypeStruct((2 * count, hidden), BF16),
            jax.ShapeDtypeStruct((2 * count, hidden), BF16),
            jax.ShapeDtypeStruct((2 * count, width), BF16),
            jax.ShapeDtypeStruct((lanes, width), F32),
        ],
        cost_estimate=pl.CostEstimate(
            flops=16 * count * width * hidden // COVER,
            transcendentals=4 * count * hidden // COVER,
            bytes_accessed=2 * (8 * count * width + 4 * count * hidden + 2 * width * hidden) // COVER,
        ),
        compiler_params=pltpu.CompilerParams(vmem_limit_bytes=60 * 1024 * 1024),
        name="feed_routed" if routed else "feed_dense",
    )(pick, own, side, own_grads, side_grads, head, up, down)


LANES = 128
DENSE_ROWS = 320
EXPERT_ROWS = 448


def norm_parts(values):
    row_mean = jnp.mean(values, axis=-1, keepdims=True)
    centred = values - row_mean
    row_var = jnp.mean(centred * centred, axis=-1, keepdims=True)
    inverse = lax.rsqrt(row_var + EPSILON)
    return (centred * inverse, inverse)


def norm_back(grad_normed, gain_vec, scaled, inverse):
    grad_scaled = grad_normed * gain_vec
    first_mean = jnp.mean(grad_scaled, axis=-1, keepdims=True)
    second = jnp.mean(grad_scaled * scaled, axis=-1, keepdims=True)
    return inverse * (grad_scaled - first_mean - scaled * second)


def after(value, *others):
    return lax.optimization_barrier((value, *others))[0]


def from_side(values):
    return lax.ppermute(values, "tensor", [(i, i ^ 1) for i in range(4)])


def from_far(values):
    return lax.ppermute(values, "tensor", [(i, i ^ 2) for i in range(4)])


def plus_side(own, side):
    return own.astype(F32) + from_side(side.astype(BF16)).astype(F32)


def sum_over(values, axis):
    count, step = lax.axis_size(axis), 1
    while step < count:
        pairs = [(i, i ^ step) for i in range(count)]
        values = values + lax.ppermute(values, axis, pairs)
        step *= 2
    return values


def exchange(blocks):
    return lax.all_to_all(blocks, "expert", split_axis=0, concat_axis=0, tiled=True)


def scatter_sum(strips):
    strips = with_layout_constraint(strips.astype(BF16), Layout(major_to_minor=(0, 1)))
    return lax.psum_scatter(strips, "expert", scatter_dimension=0, tiled=True).astype(F32)


def strips_sum(strips):
    count = lax.axis_size("expert")
    strips = strips.reshape(count, -1, strips.shape[1])
    return jnp.sum(exchange(strips).astype(F32), axis=0)


def slots_of(expert_ids, experts, capacity):
    rows = expert_ids.shape[0]
    chosen = expert_ids[:, None] == jnp.arange(experts, dtype=jnp.int32)[None, :]
    at = jnp.arange(rows, dtype=jnp.int32)
    before = (at[None, :] < at[:, None]).astype(BF16)
    earlier = jnp.dot(before, chosen.astype(BF16), preferred_element_type=F32)
    slot = jnp.sum(jnp.where(chosen, earlier, 0.0), axis=1).astype(jnp.int32)
    place = expert_ids * capacity + slot
    places = jnp.arange(experts * capacity, dtype=jnp.int32)
    return (places[:, None] == place[None, :]).astype(BF16)


def per_device(
    tokens,
    cotangent,
    routes,
    parents,
    ln_attn,
    w_qkv,
    w_out,
    ln_mlp,
    w_up,
    w_down,
    w_router,
    w_mix,
    ex_up,
    ex_down,
):
    tok_dev, width = tokens.shape
    mine = lax.axis_index("tensor")
    experts = w_router.shape[1]
    capacity = max(2, tok_dev * 7 // (5 * experts))
    heads_width = w_qkv.shape[2]
    hidden = w_up.shape[1]
    leaves = jnp.concatenate([leaf_order(parents[0]), mine.astype(jnp.int32)[None]])

    scaled_one, inverse_one = norm_parts(tokens.astype(F32))
    normed_own = (scaled_one * ln_attn).astype(BF16)
    normed_far = from_far(normed_own)
    near_one = jnp.concatenate([normed_own, from_side(normed_own)], axis=0)

    quarter_ids = routes[:, 0].reshape(4, tok_dev)

    def slots_at(offset):
        ids = lax.dynamic_index_in_dim(quarter_ids, mine ^ offset, 0, keepdims=False)
        return slots_of(ids, experts, capacity)

    own_slots, far_slots = slots_at(0), slots_at(2)

    def placed(slots, rows):
        return jnp.dot(slots, rows, preferred_element_type=F32).astype(BF16)

    def sent(rows):
        return exchange(rows.reshape(experts, capacity, width)).reshape(-1, width)

    own_grads = sent(placed(own_slots, cotangent))
    cotangent_side = from_side(cotangent)

    def project(rows):
        qkv = jnp.einsum("td,sdc->stc", rows, w_qkv, preferred_element_type=F32)
        return qkv.astype(BF16).reshape(3, 2, tok_dev, heads_width)

    lanes = -(-(experts + 2) // LANES) * LANES
    head = jnp.concatenate(
        [w_router, w_mix, jnp.zeros((width, lanes - experts - 2), BF16)], axis=1
    )
    near_qkv = project(near_one)
    cotangent_far = from_far(after(cotangent, normed_far))
    normed_far, near_qkv, head = lax.optimization_barrier((normed_far, near_qkv, head))
    far_one = jnp.concatenate([normed_far, from_side(normed_far)], axis=0)
    far_qkv = project(far_one)
    near_out, far_out, *logs = attention_forward(leaves, near_qkv, far_qkv)
    far_out, own_grads, cotangent_far, cotangent_side = lax.optimization_barrier(
        (far_out, own_grads, cotangent_far, cotangent_side)
    )

    def branch_part(rows):
        return jnp.dot(rows, w_out, preferred_element_type=F32)

    far_sum = plus_side(branch_part(far_out[0]), branch_part(far_out[1])).astype(BF16)
    branch = plus_side(branch_part(near_out[0]), branch_part(near_out[1]))
    branch_far = from_far(far_sum)
    side_grads = from_side(own_grads)
    cotangent_corner = from_side(cotangent_far)
    far_placed = placed(far_slots, cotangent_far)
    branch_far, side_grads, cotangent_corner, far_placed = lax.optimization_barrier(
        (branch_far, side_grads, cotangent_corner, far_placed)
    )
    residual = tokens.astype(F32) + (branch + branch_far.astype(F32))

    scaled_two, inverse_two = norm_parts(residual)
    normed_two = (scaled_two * ln_mlp).astype(BF16)
    normed_two_far = from_far(normed_two)
    normed_two_side = from_side(normed_two)
    own_rows = sent(placed(own_slots, normed_two))

    def dense(own, side, own_cotangent, side_cotangent):
        return feed(
            own, side, own_cotangent, side_cotangent, head, w_up, w_down, experts, None, DENSE_ROWS
        )

    def product(left, right):
        return jnp.einsum("gd,gf->df", left, right, preferred_element_type=F32)

    def weight_grads(near_left, far_left, near_right, far_right):
        return product(near_left, near_right) + product(far_left, far_right)

    near_dense = dense(normed_two, normed_two_side, cotangent, cotangent_side)
    near_two = jnp.concatenate([normed_two, normed_two_side], axis=0)
    grad_up = product(near_two, near_dense[5])
    grad_down = product(near_dense[6], near_dense[4])
    normed_two_far, grad_up, grad_down, own_rows = lax.optimization_barrier(
        (normed_two_far, grad_up, grad_down, own_rows)
    )
    far_rows = from_far(own_rows)
    far_grads = sent(after(far_placed, own_rows))
    normed_two_corner = from_side(normed_two_far)
    far_dense = list(dense(normed_two_far, normed_two_corner, cotangent_far, cotangent_corner))
    far_rows, far_dense[6], far_dense[5] = lax.optimization_barrier(
        (far_rows, far_dense[6], far_dense[5])
    )
    far_two = jnp.concatenate([normed_two_far, normed_two_corner], axis=0)
    grad_up = grad_up + product(far_two, far_dense[5])
    grad_down = grad_down + product(far_dense[6], far_dense[4])
    dense_grads = jnp.concatenate([grad_up.astype(BF16), grad_down.astype(BF16)], axis=1)

    expert = lax.axis_index("expert").astype(jnp.int32)

    def routed(own, side, own_cotangent, side_cotangent):
        return feed(
            own,
            side,
            own_cotangent,
            side_cotangent,
            head,
            ex_up[0],
            ex_down[0],
            experts,
            expert,
            EXPERT_ROWS,
        )

    def chip_sum(parts, place, *others):
        return plus_side(parts[place], after(parts[place + 1], *others))

    dense_back_far = chip_sum(far_dense, 2).astype(BF16)
    dense_out_far = chip_sum(far_dense, 0).astype(BF16)
    far_rows, dense_grads, dense_back_far, dense_out_far = lax.optimization_barrier(
        (far_rows, dense_grads, dense_back_far, dense_out_far)
    )
    dense_grads = scatter_sum(dense_grads)
    corner_rows = from_side(far_rows)
    side_rows = from_side(own_rows)
    far_expert = routed(far_rows, corner_rows, far_grads, from_side(far_grads))
    dense_back, dense_out = chip_sum(near_dense, 2), chip_sum(near_dense, 0)
    far_back = chip_sum(far_expert, 2).astype(BF16)
    own_rows, far_back = lax.optimization_barrier((own_rows, far_back))
    near_expert = routed(own_rows, side_rows, own_grads, side_grads)
    dense_back = dense_back + from_far(after(dense_back_far, near_expert[2])).astype(F32)

    def picked(rows):
        return lax.dot_general(
            own_slots, rows, (((0,), (0,)), ((), ())), preferred_element_type=F32
        )

    expert_back = chip_sum(near_expert, 2) + from_far(far_back).astype(F32)
    far_expert_out = chip_sum(far_expert, 0, far_back).astype(BF16)
    expert_back, far_expert_out = lax.optimization_barrier(
        (expert_back.astype(BF16), far_expert_out)
    )
    grad_normed_two, dense_grads = lax.optimization_barrier(
        (dense_back + picked(sent(expert_back)), dense_grads)
    )
    expert_out = chip_sum(near_expert, 0, expert_back) + from_far(far_expert_out).astype(F32)
    expert_out = sent(after(expert_out.astype(BF16), grad_normed_two))

    near_tokens = jnp.concatenate([own_rows, side_rows], axis=0)
    far_tokens = jnp.concatenate([far_rows, corner_rows], axis=0)
    grad_ex_up = weight_grads(near_tokens, far_tokens, near_expert[5], far_expert[5])[None]
    grad_ex_down = weight_grads(near_expert[4], far_expert[4], near_expert[6], far_expert[6])[None]

    gain_two = jnp.sum(grad_normed_two * scaled_two, axis=0)
    grad_residual = cotangent.astype(F32) + norm_back(
        grad_normed_two, ln_mlp, scaled_two, inverse_two
    )
    grad_branch = grad_residual.astype(BF16)
    grad_branch_far = from_far(grad_branch)
    grad_branch_far, grad_ex_up, grad_ex_down = lax.optimization_barrier(
        (grad_branch_far, grad_ex_up, grad_ex_down)
    )
    near_branch = jnp.concatenate([grad_branch, from_side(grad_branch)], axis=0)
    far_branch = jnp.concatenate([grad_branch_far, from_side(grad_branch_far)], axis=0)
    head_grads = near_dense[7] + far_dense[7] + near_expert[7] + far_expert[7]
    small = jnp.concatenate([head_grads[: experts + 2], gain_two[None]], axis=0)
    small = sum_over(small, "tensor")

    def into_heads(rows):
        grads = jnp.einsum("gd,cd->gc", rows, w_out, preferred_element_type=F32)
        return grads.astype(BF16).reshape(2, tok_dev, heads_width)

    near_heads, far_heads = into_heads(near_branch), into_heads(far_branch)
    flat = (2 * tok_dev, heads_width)
    small_columns = -(-small.shape[0] // LANES) * LANES
    small_block = jnp.pad(small, ((0, small_columns - small.shape[0]), (0, 0))).T
    grad_w_out = weight_grads(near_branch, far_branch, near_out.reshape(flat), far_out.reshape(flat))
    side_grads = jnp.concatenate([grad_w_out.astype(BF16), small_block.astype(BF16)], axis=1)
    dense_out_far = from_far(after(dense_out_far, grad_branch_far))
    near_heads, side_grads = lax.optimization_barrier((near_heads, side_grads))
    side_grads = scatter_sum(side_grads)
    near_result, far_result = attention_backward(
        leaves, near_qkv, far_qkv, near_heads, far_heads, near_out, far_out, logs
    )
    near_result, far_result, expert_out, dense_out_far = lax.optimization_barrier(
        (near_result, far_result, expert_out, dense_out_far)
    )

    def normed_part(grads):
        return jnp.einsum("sgc,sdc->gd", grads, w_qkv, preferred_element_type=F32)

    corner_part = normed_part(far_result[:, 1])
    from_corner = from_side(corner_part.astype(BF16)).astype(F32)
    far_result, side_grads = lax.optimization_barrier((far_result, corner_part, side_grads))[::2]
    far_sum = (normed_part(far_result[:, 0]) + from_corner).astype(BF16)
    near_result, far_result, expert_out, far_sum = lax.optimization_barrier(
        (near_result, far_result, expert_out, far_sum)
    )
    near_sum = plus_side(normed_part(near_result[:, 0]), normed_part(near_result[:, 1]))
    out = (residual + dense_out + dense_out_far.astype(F32) + picked(expert_out)).astype(BF16)

    near_result = near_result.reshape(3, 2 * tok_dev, heads_width)
    far_result = far_result.reshape(3, 2 * tok_dev, heads_width)
    grad_w_qkv = jnp.einsum(
        "gd,sgc->dsc", near_one, near_result, preferred_element_type=F32
    ) + jnp.einsum("gd,sgc->dsc", far_one, far_result, preferred_element_type=F32)
    qkv_grads = strips_sum(grad_w_qkv.reshape(width, 3 * heads_width).astype(BF16))
    scaled_far = normed_far.astype(F32) / ln_attn
    gain_one = jnp.sum(near_sum * scaled_one + far_sum.astype(F32) * scaled_far, axis=0, keepdims=True)
    gain_one = sum_over(sum_over(gain_one, "tensor"), "expert")
    far_sum, grad_ln_attn = lax.optimization_barrier((from_far(far_sum), gain_one[0]))
    grad_normed_one = near_sum + far_sum.astype(F32)
    grad_tokens = grad_residual + norm_back(grad_normed_one, ln_attn, scaled_one, inverse_one)

    strip = qkv_grads.shape[0]
    return (
        out,
        grad_tokens,
        grad_ln_attn,
        qkv_grads.reshape(strip, 3, heads_width).transpose(1, 0, 2),
        side_grads[:, :heads_width].T,
        side_grads[:, heads_width + experts + 2],
        dense_grads[:, :hidden],
        dense_grads[:, hidden:].T,
        side_grads[:, heads_width : heads_width + experts],
        side_grads[:, heads_width + experts : heads_width + experts + 2],
        grad_ex_up,
        grad_ex_down,
    )


def solution(mesh):
    return jax.shard_map(
        per_device,
        mesh=mesh,
        in_specs=(
            P(("expert", "tensor"), None),
            P(("expert", "tensor"), None),
            P("expert", None),
            P("expert", None),
            P(),
            P(None, None, "tensor"),
            P("tensor", None),
            P(),
            P(None, "tensor"),
            P("tensor", None),
            P(),
            P(),
            P("expert", None, "tensor"),
            P("expert", "tensor", None),
        ),
        out_specs=(
            P(("expert", "tensor"), None),
            P(("expert", "tensor"), None),
            P(),
            P(None, "expert", "tensor"),
            P("tensor", "expert"),
            P("expert"),
            P("expert", "tensor"),
            P("tensor", "expert"),
            P("expert", None),
            P("expert", None),
            P("expert", None, "tensor"),
            P("expert", "tensor", None),
        ),
        check_vma=False,
    )
```

```python
import functools

import jax
import jax.numpy as jnp
from jax import lax
from jax.experimental import pallas as pl
from jax.experimental.layout import Layout, with_layout_constraint
from jax.experimental.pallas import tpu as pltpu
from jax.sharding import PartitionSpec as P

HEAD_DIM = 64
TRUNK = 1024
SEG = 128
SEGS = 13
TREE_LEN = 2560
BRANCHES = 4
FAMILY = 3 * SEG
QROWS = 256
COVER = 8
PAIR = 2 * HEAD_DIM
NEGATIVE_FILL = -1e30
F32 = jnp.float32
BF16 = jnp.bfloat16
EPSILON = 1e-05


def dot_nn(a, b):
    return lax.dot_general(a, b, (((1,), (0,)), ((), ())), preferred_element_type=F32)


def dot_nt(a, b):
    return lax.dot_general(a, b, (((1,), (1,)), ((), ())), preferred_element_type=F32)


def head_lanes(rows, head):
    lane = lax.broadcasted_iota(jnp.int32, rows.shape, 1)
    return jnp.where(lane // HEAD_DIM == head, rows, jnp.zeros_like(rows))


def causal(scores):
    key = lax.broadcasted_iota(jnp.int32, scores.shape, 0)
    query = lax.broadcasted_iota(jnp.int32, scores.shape, 1)
    return jnp.where(key <= query, scores, NEGATIVE_FILL)


def family_rows(leaves_ref, branch):
    def start(segment):
        return pl.multiple_of(TRUNK + (segment - 1) * SEG, SEG)

    return [start(branch + 1), start(leaves_ref[2 * branch]), start(leaves_ref[2 * branch + 1])]


def transpose_into(target_ref, source_ref, part):
    for first in range(0, TREE_LEN, 512):
        piece = source_ref[part, pl.ds(first, 512), :].astype(F32)
        target_ref[:, pl.ds(first, 512)] = piece.T.astype(BF16)


def widen(piece, first, width, fill):
    parts = []
    if first:
        parts.append(jnp.full((piece.shape[0], first), fill, piece.dtype))
    parts.append(piece)
    rest = width - first - piece.shape[1]
    if rest:
        parts.append(jnp.full((piece.shape[0], rest), fill, piece.dtype))
    return parts[0] if len(parts) == 1 else jnp.concatenate(parts, axis=1)


def trunk_groups(block):
    first = block * QROWS
    groups = [(0, first, 0, QROWS, None)] if first else []
    return groups + [(first, QROWS, 0, QROWS, "causal")]


def family_groups(starts):
    return [
        (0, TRUNK, 0, FAMILY, None),
        (starts[0], SEG, 0, FAMILY, "branch"),
        (starts[1], SEG, SEG, 2 * SEG, "causal"),
        (starts[2], SEG, 2 * SEG, FAMILY, "causal"),
    ]


def masked_scores(keys, queries, rule):
    scores = dot_nt(keys, queries)
    if rule == "causal":
        return causal(scores)
    if rule == "branch":
        return jnp.concatenate([causal(scores[:, :SEG]), scores[:, SEG:]], axis=1)
    return scores


def forward_block(qkv_ref, values_t_ref, queries, groups):
    width = queries.shape[0]
    outs, logs = [], []
    for head in range(2):
        own = head_lanes(queries, head)
        all_scores = [
            masked_scores(qkv_ref[1, pl.ds(start, size), :], own[first:last], rule)
            for start, size, first, last, rule in groups
        ]
        top = functools.reduce(
            jnp.maximum,
            [
                widen(jnp.max(s, axis=0, keepdims=True), first, width, NEGATIVE_FILL)
                for s, (_, _, first, last, _) in zip(all_scores, groups)
            ],
        )
        total, output = None, None
        for s, (start, size, first, last, _) in zip(all_scores, groups):
            weights = jnp.exp(s - top[:, first:last])
            part = widen(jnp.sum(weights, axis=0, keepdims=True), first, width, 0.0)
            values_t = values_t_ref[pl.ds(head * HEAD_DIM, HEAD_DIM), pl.ds(start, size)]
            mixed = widen(dot_nn(values_t, weights.astype(BF16)), first, width, 0.0)
            total = part if total is None else total + part
            output = mixed if output is None else output + mixed
        outs.append(output / total)
        logs.append(top + jnp.log(total))
    return jnp.concatenate(outs, axis=0).T.astype(BF16), jnp.concatenate(logs, axis=0)


def scaled_queries(qkv_ref, starts, size):
    rows = [qkv_ref[0, pl.ds(start, size), :] for start in starts]
    rows = rows[0] if len(rows) == 1 else jnp.concatenate(rows, axis=0)
    return rows * jnp.asarray(HEAD_DIM ** (-0.5), BF16)


def quarter_rows(leaves_ref, offset):
    quarter = TREE_LEN // 4
    return pl.ds(pl.multiple_of((leaves_ref[2 * BRANCHES] ^ offset) * quarter, quarter), quarter)


def forward_kernel(
    leaves_ref,
    near_ref,
    far_ref,
    near_out_ref,
    far_out_ref,
    trunk_log_ref,
    family_log_ref,
    qkv_ref,
    out_ref,
    values_t_ref,
):
    for offset in range(4):
        half_ref = near_ref if offset < 2 else far_ref
        qkv_ref[:, quarter_rows(leaves_ref, offset), :] = half_ref[:, offset % 2]
    transpose_into(values_t_ref, qkv_ref, 2)
    for block in range(TRUNK // QROWS):
        first = block * QROWS
        queries = scaled_queries(qkv_ref, [first], QROWS)
        out, logs = forward_block(qkv_ref, values_t_ref, queries, trunk_groups(block))
        out_ref[pl.ds(first, QROWS), :] = out
        trunk_log_ref[0, :, pl.ds(first, QROWS)] = logs

    def one_family(branch, carry):
        starts = family_rows(leaves_ref, branch)
        queries = scaled_queries(qkv_ref, starts, SEG)
        out, logs = forward_block(qkv_ref, values_t_ref, queries, family_groups(starts))
        for place, start in enumerate(starts):
            out_ref[pl.ds(start, SEG), :] = out[place * SEG : (place + 1) * SEG]
        family_log_ref[0, branch] = logs
        return carry

    lax.fori_loop(0, BRANCHES, one_family, 0)
    for offset in range(4):
        half_ref = near_out_ref if offset < 2 else far_out_ref
        half_ref[offset % 2] = out_ref[quarter_rows(leaves_ref, offset), :]


def halves_spec(parts):
    quarter = TREE_LEN // 4
    if parts == 1:
        return pl.BlockSpec((2, quarter, PAIR), lambda p, leaves: (0, 0, p))
    return pl.BlockSpec((parts, 2, quarter, PAIR), lambda p, leaves: (0, 0, 0, p))


def attention_cost(products, cover):
    visited = (TRUNK * (TRUNK + QROWS) // 2 + BRANCHES * FAMILY * (TRUNK + SEG)) // cover
    return pl.CostEstimate(
        flops=2 * products * 4 * visited * 2 * PAIR,
        transcendentals=4 * visited,
        bytes_accessed=8 * TREE_LEN * 4 * HEAD_DIM * 2 // cover,
    )


def attention_forward(leaves, near, far):
    width = near.shape[3]
    quarter = TREE_LEN // 4
    pairs = width // PAIR
    return pl.pallas_call(
        forward_kernel,
        grid_spec=pltpu.PrefetchScalarGridSpec(
            num_scalar_prefetch=1,
            grid=(pairs,),
            in_specs=[halves_spec(3), halves_spec(3)],
            out_specs=[
                halves_spec(1),
                halves_spec(1),
                pl.BlockSpec((1, 2, TRUNK), lambda p, leaves: (p, 0, 0)),
                pl.BlockSpec((1, BRANCHES, 2, FAMILY), lambda p, leaves: (p, 0, 0, 0)),
            ],
            scratch_shapes=[
                pltpu.VMEM((3, TREE_LEN, PAIR), BF16),
                pltpu.VMEM((TREE_LEN, PAIR), BF16),
                pltpu.VMEM((PAIR, TREE_LEN), BF16),
            ],
        ),
        out_shape=[
            jax.ShapeDtypeStruct((2, quarter, width), BF16),
            jax.ShapeDtypeStruct((2, quarter, width), BF16),
            jax.ShapeDtypeStruct((pairs, 2, TRUNK), F32),
            jax.ShapeDtypeStruct((pairs, BRANCHES, 2, FAMILY), F32),
        ],
        cost_estimate=attention_cost(2, COVER),
        name="tree_attention",
    )(leaves, near, far)


def backward_block(qkv_ref, keys_t_ref, queries, grads, outs, logs, groups):
    products = grads.astype(F32) * outs.astype(F32)
    products_t = products.T
    key_ds = [[] for _ in groups]
    value_ws = [[] for _ in groups]
    own_q, own_g, query_grads = [], [], []
    for head in range(2):
        own = head_lanes(queries, head)
        own_grads = head_lanes(grads, head)
        own_q.append(own)
        own_g.append(own_grads)
        inner = jnp.sum(
            products_t[head * HEAD_DIM : (head + 1) * HEAD_DIM], axis=0, keepdims=True
        )
        log = logs[head : head + 1]
        query_grad = None
        for place, (start, size, first, last, rule) in enumerate(groups):
            scores = masked_scores(qkv_ref[1, pl.ds(start, size), :], own[first:last], rule)
            weights = jnp.exp(scores - log[:, first:last])
            grad_weights = dot_nt(qkv_ref[2, pl.ds(start, size), :], own_grads[first:last])
            grad_scores = (weights * (grad_weights - inner[:, first:last])).astype(BF16)
            keys_t = keys_t_ref[pl.ds(head * HEAD_DIM, HEAD_DIM), pl.ds(start, size)]
            part = widen(dot_nn(keys_t, grad_scores), first, queries.shape[0], 0.0)
            query_grad = part if query_grad is None else query_grad + part
            key_ds[place].append(grad_scores)
            value_ws[place].append(weights.astype(BF16))
        query_grads.append(query_grad)
    grad_query = (jnp.concatenate(query_grads, axis=0) * HEAD_DIM ** (-0.5)).T.astype(BF16)
    key_grads, value_grads = [], []
    for place, (start, size, first, last, rule) in enumerate(groups):
        stacked_q = jnp.concatenate([own_q[0][first:last], own_q[1][first:last]], axis=0)
        stacked_g = jnp.concatenate([own_g[0][first:last], own_g[1][first:last]], axis=0)
        key_grads.append(dot_nn(jnp.concatenate(key_ds[place], axis=1), stacked_q))
        value_grads.append(dot_nn(jnp.concatenate(value_ws[place], axis=1), stacked_g))
    return grad_query, key_grads, value_grads


def backward_kernel(
    leaves_ref,
    near_ref,
    far_ref,
    near_grads_ref,
    far_grads_ref,
    near_outs_ref,
    far_outs_ref,
    trunk_log_ref,
    family_log_ref,
    near_result_ref,
    far_result_ref,
    qkv_ref,
    grads_ref,
    outs_ref,
    result_ref,
    keys_t_ref,
    trunk_keys_ref,
    trunk_values_ref,
):
    for offset in range(4):
        rows = quarter_rows(leaves_ref, offset)
        at = offset % 2
        qkv_ref[:, rows, :] = (near_ref if offset < 2 else far_ref)[:, at]
        grads_ref[rows, :] = (near_grads_ref if offset < 2 else far_grads_ref)[at]
        outs_ref[rows, :] = (near_outs_ref if offset < 2 else far_outs_ref)[at]
    transpose_into(keys_t_ref, qkv_ref, 1)
    trunk_keys_ref[...] = jnp.zeros_like(trunk_keys_ref)
    trunk_values_ref[...] = jnp.zeros_like(trunk_values_ref)
    for block in range(TRUNK // QROWS):
        first = block * QROWS
        rows = pl.ds(first, QROWS)
        groups = trunk_groups(block)
        grad_query, key_grads, value_grads = backward_block(
            qkv_ref,
            keys_t_ref,
            scaled_queries(qkv_ref, [first], QROWS),
            grads_ref[rows, :],
            outs_ref[rows, :],
            trunk_log_ref[0, :, rows],
            groups,
        )
        result_ref[0, rows, :] = grad_query
        for (start, size, _, _, _), key_grad, value_grad in zip(groups, key_grads, value_grads):
            trunk_keys_ref[pl.ds(start, size), :] += key_grad
            trunk_values_ref[pl.ds(start, size), :] += value_grad

    def one_family(branch, carry):
        starts = family_rows(leaves_ref, branch)
        groups = family_groups(starts)
        grad_query, key_grads, value_grads = backward_block(
            qkv_ref,
            keys_t_ref,
            scaled_queries(qkv_ref, starts, SEG),
            jnp.concatenate([grads_ref[pl.ds(start, SEG), :] for start in starts], axis=0),
            jnp.concatenate([outs_ref[pl.ds(start, SEG), :] for start in starts], axis=0),
            family_log_ref[0, branch],
            groups,
        )
        trunk_keys_ref[...] += key_grads[0]
        trunk_values_ref[...] += value_grads[0]
        for place, start in enumerate(starts):
            rows = pl.ds(start, SEG)
            result_ref[0, rows, :] = grad_query[place * SEG : (place + 1) * SEG]
            result_ref[1, rows, :] = key_grads[1 + place].astype(BF16)
            result_ref[2, rows, :] = value_grads[1 + place].astype(BF16)
        return carry

    lax.fori_loop(0, BRANCHES, one_family, 0)
    result_ref[1, pl.ds(0, TRUNK), :] = trunk_keys_ref[...].astype(BF16)
    result_ref[2, pl.ds(0, TRUNK), :] = trunk_values_ref[...].astype(BF16)
    for offset in range(4):
        half_ref = near_result_ref if offset < 2 else far_result_ref
        half_ref[:, offset % 2] = result_ref[:, quarter_rows(leaves_ref, offset), :]


def attention_backward(leaves, near, far, near_grads, far_grads, near_outs, far_outs, logs):
    pairs = near.shape[3] // PAIR
    return pl.pallas_call(
        backward_kernel,
        grid_spec=pltpu.PrefetchScalarGridSpec(
            num_scalar_prefetch=1,
            grid=(pairs,),
            in_specs=[
                halves_spec(3),
                halves_spec(3),
                halves_spec(1),
                halves_spec(1),
                halves_spec(1),
                halves_spec(1),
                pl.BlockSpec((1, 2, TRUNK), lambda p, leaves: (p, 0, 0)),
                pl.BlockSpec((1, BRANCHES, 2, FAMILY), lambda p, leaves: (p, 0, 0, 0)),
            ],
            out_specs=[halves_spec(3), halves_spec(3)],
            scratch_shapes=[
                pltpu.VMEM((3, TREE_LEN, PAIR), BF16),
                pltpu.VMEM((TREE_LEN, PAIR), BF16),
                pltpu.VMEM((TREE_LEN, PAIR), BF16),
                pltpu.VMEM((3, TREE_LEN, PAIR), BF16),
                pltpu.VMEM((PAIR, TREE_LEN), BF16),
                pltpu.VMEM((TRUNK, PAIR), F32),
                pltpu.VMEM((TRUNK, PAIR), F32),
            ],
        ),
        out_shape=[jax.ShapeDtypeStruct(near.shape, BF16), jax.ShapeDtypeStruct(far.shape, BF16)],
        cost_estimate=attention_cost(5, 1),
        name="tree_attention_back",
    )(leaves, near, far, near_grads, far_grads, near_outs, far_outs, *logs)


def leaf_order(parents_row):
    first_leaf = BRANCHES + 1
    leaf_parents = parents_row[first_leaf:]
    segments = first_leaf + jnp.arange(leaf_parents.shape[0], dtype=jnp.int32)
    same = leaf_parents[:, None] == leaf_parents[None, :]
    later = segments[None, :] < segments[:, None]
    place = 2 * (leaf_parents - 1) + jnp.sum(jnp.where(same & later, 1, 0), axis=1)
    slots = jnp.arange(2 * BRANCHES, dtype=jnp.int32)
    return jnp.sum(jnp.where(slots[:, None] == place[None, :], segments[None, :], 0), axis=1)


def gates(logits, experts, expert):
    lane = lax.broadcasted_iota(jnp.int32, logits.shape, 1)
    first, second = logits[:, experts : experts + 1], logits[:, experts + 1 : experts + 2]
    top = jnp.maximum(first, second)
    first, second = jnp.exp(first - top), jnp.exp(second - top)
    total = first + second
    first, second = first / total, second / total
    if expert is None:
        return lane, first, second, None, None
    routed = jnp.where(lane < experts, logits, NEGATIVE_FILL)
    raised = jnp.exp(routed - jnp.max(routed, axis=1, keepdims=True))
    probs = raised / jnp.sum(raised, axis=1, keepdims=True)
    gate = jnp.sum(jnp.where(lane == expert, probs, 0.0), axis=1, keepdims=True)
    return lane, first, second, probs, gate


def feed_kernel(
    experts,
    routed,
    expert_ref,
    own_ref,
    side_ref,
    own_grads_ref,
    side_grads_ref,
    head_ref,
    up_ref,
    down_ref,
    own_out_ref,
    side_out_ref,
    own_back_ref,
    side_back_ref,
    active_ref,
    pre_ref,
    grad_ref,
    head_grad_ref,
):
    step = pl.program_id(0)
    early = step < pl.num_programs(0) // 2
    rows = jnp.where(early, own_ref[...], side_ref[...])
    grads = jnp.where(early, own_grads_ref[...], side_grads_ref[...]).astype(F32)
    logits = dot_nn(rows, head_ref[...])
    expert = expert_ref[0] if routed else None
    lane, first, second, probs, gate = gates(logits, experts, expert)
    coef = second * gate if routed else first
    weighted = (coef * grads).astype(BF16)
    grad_ref[...] = weighted
    pre = dot_nn(rows, up_ref[...])
    grad_active = dot_nt(weighted, down_ref[...])
    cumulative = 0.5 + 0.5 * lax.erf(pre * 0.7071067811865476)
    slope = cumulative + pre * jnp.exp(-0.5 * pre * pre) * 0.3989422804014327
    active = (pre * cumulative).astype(BF16)
    active_ref[...] = active
    grad_pre = (grad_active * slope).astype(BF16)
    pre_ref[...] = grad_pre
    out = dot_nn(active, down_ref[...])
    out_rows = (coef * out).astype(BF16)
    inner = jnp.sum(grads * out, axis=1, keepdims=True)
    swing = first * second * inner
    if routed:
        swing = -gate * swing
    grad_logits = jnp.where(lane == experts, swing, jnp.where(lane == experts + 1, -swing, 0.0))
    if routed:
        picked = jnp.where(lane == expert, 1.0, 0.0) - gate
        grad_logits = grad_logits + jnp.where(
            lane < experts, probs * picked * (second * inner), 0.0
        )
    back = dot_nt(grad_pre, up_ref[...]) + dot_nt(grad_logits.astype(BF16), head_ref[...])
    back_rows = back.astype(BF16)

    @pl.when(early)
    def _():
        own_out_ref[...] = out_rows
        own_back_ref[...] = back_rows

    @pl.when(jnp.logical_not(early))
    def _():
        side_out_ref[...] = out_rows
        side_back_ref[...] = back_rows

    @pl.when(step == 0)
    def _():
        head_grad_ref[...] = jnp.zeros_like(head_grad_ref)

    head_grad_ref[...] += dot_nn(grad_logits.T.astype(BF16), rows)


def feed(own, side, own_grads, side_grads, head, up, down, experts, expert, size):
    count = own.shape[0]
    width, hidden = up.shape
    half = count // size
    lanes = head.shape[1]
    routed = expert is not None
    pick = jnp.reshape(expert, (1,)) if routed else jnp.zeros((1,), jnp.int32)
    early = pl.BlockSpec((size, width), lambda i, pick: (jnp.minimum(i, half - 1), 0))
    late = pl.BlockSpec((size, width), lambda i, pick: (jnp.maximum(i - half, 0), 0))

    def held(shape):
        return pl.BlockSpec(shape, lambda i, pick: (0, 0), pipeline_mode=pl.Buffered(1))

    wide = pl.BlockSpec((size, width), lambda i, pick: (i, 0))
    deep = pl.BlockSpec((size, hidden), lambda i, pick: (i, 0))
    quarter = jax.ShapeDtypeStruct((count, width), BF16)
    return pl.pallas_call(
        functools.partial(feed_kernel, experts, routed),
        grid_spec=pltpu.PrefetchScalarGridSpec(
            num_scalar_prefetch=1,
            grid=(2 * half,),
            in_specs=[
                early,
                late,
                early,
                late,
                held((width, lanes)),
                held((width, hidden)),
                held((hidden, width)),
            ],
            out_specs=[
                early,
                late,
                early,
                late,
                deep,
                deep,
                wide,
                pl.BlockSpec((lanes, width), lambda i, pick: (0, 0)),
            ],
        ),
        out_shape=[
            quarter,
            quarter,
            quarter,
            quarter,
            jax.ShapeDtypeStruct((2 * count, hidden), BF16),
            jax.ShapeDtypeStruct((2 * count, hidden), BF16),
            jax.ShapeDtypeStruct((2 * count, width), BF16),
            jax.ShapeDtypeStruct((lanes, width), F32),
        ],
        cost_estimate=pl.CostEstimate(
            flops=16 * count * width * hidden // COVER,
            transcendentals=4 * count * hidden // COVER,
            bytes_accessed=2 * (8 * count * width + 4 * count * hidden + 2 * width * hidden) // COVER,
        ),
        compiler_params=pltpu.CompilerParams(vmem_limit_bytes=60 * 1024 * 1024),
        name="feed_routed" if routed else "feed_dense",
    )(pick, own, side, own_grads, side_grads, head, up, down)


LANES = 128
DENSE_ROWS = 320
EXPERT_ROWS = 448


def norm_parts(values):
    row_mean = jnp.mean(values, axis=-1, keepdims=True)
    centred = values - row_mean
    row_var = jnp.mean(centred * centred, axis=-1, keepdims=True)
    inverse = lax.rsqrt(row_var + EPSILON)
    return (centred * inverse, inverse)


def norm_back(grad_normed, gain_vec, scaled, inverse):
    grad_scaled = grad_normed * gain_vec
    first_mean = jnp.mean(grad_scaled, axis=-1, keepdims=True)
    second = jnp.mean(grad_scaled * scaled, axis=-1, keepdims=True)
    return inverse * (grad_scaled - first_mean - scaled * second)


def after(value, *others):
    return lax.optimization_barrier((value, *others))[0]


def from_side(values):
    return lax.ppermute(values, "tensor", [(i, i ^ 1) for i in range(4)])


def from_far(values):
    return lax.ppermute(values, "tensor", [(i, i ^ 2) for i in range(4)])


def plus_side(own, side):
    return own.astype(F32) + from_side(side.astype(BF16)).astype(F32)


def sum_over(values, axis):
    count, step = lax.axis_size(axis), 1
    while step < count:
        pairs = [(i, i ^ step) for i in range(count)]
        values = values + lax.ppermute(values, axis, pairs)
        step *= 2
    return values


def exchange(blocks):
    return lax.all_to_all(blocks, "expert", split_axis=0, concat_axis=0, tiled=True)


def scatter_sum(strips):
    strips = with_layout_constraint(strips.astype(BF16), Layout(major_to_minor=(0, 1)))
    return lax.psum_scatter(strips, "expert", scatter_dimension=0, tiled=True).astype(F32)


def strips_sent(grads):
    return exchange(grads.reshape(lax.axis_size("expert"), -1, grads.shape[1]))


def strips_total(strips):
    return jnp.sum(strips.astype(F32), axis=0)


def slots_of(expert_ids, experts, capacity):
    rows = expert_ids.shape[0]
    chosen = expert_ids[:, None] == jnp.arange(experts, dtype=jnp.int32)[None, :]
    at = jnp.arange(rows, dtype=jnp.int32)
    before = (at[None, :] < at[:, None]).astype(BF16)
    earlier = jnp.dot(before, chosen.astype(BF16), preferred_element_type=F32)
    slot = jnp.sum(jnp.where(chosen, earlier, 0.0), axis=1).astype(jnp.int32)
    place = expert_ids * capacity + slot
    places = jnp.arange(experts * capacity, dtype=jnp.int32)
    return (places[:, None] == place[None, :]).astype(BF16)


def per_device(
    tokens,
    cotangent,
    routes,
    parents,
    ln_attn,
    w_qkv,
    w_out,
    ln_mlp,
    w_up,
    w_down,
    w_router,
    w_mix,
    ex_up,
    ex_down,
):
    tok_dev, width = tokens.shape
    mine = lax.axis_index("tensor")
    experts = w_router.shape[1]
    capacity = max(2, tok_dev * 7 // (5 * experts))
    heads_width = w_qkv.shape[2]
    hidden = w_up.shape[1]
    leaves = jnp.concatenate([leaf_order(parents[0]), mine.astype(jnp.int32)[None]])

    scaled_one, inverse_one = norm_parts(tokens.astype(F32))
    normed_own = (scaled_one * ln_attn).astype(BF16)
    normed_far = from_far(normed_own)
    near_one = jnp.concatenate([normed_own, from_side(normed_own)], axis=0)

    quarter_ids = routes[:, 0].reshape(4, tok_dev)

    def slots_at(offset):
        ids = lax.dynamic_index_in_dim(quarter_ids, mine ^ offset, 0, keepdims=False)
        return slots_of(ids, experts, capacity)

    own_slots, far_slots = slots_at(0), slots_at(2)

    def placed(slots, rows):
        return jnp.dot(slots, rows, preferred_element_type=F32).astype(BF16)

    def sent(rows):
        return exchange(rows.reshape(experts, capacity, width)).reshape(-1, width)

    own_grads = sent(placed(own_slots, cotangent))
    cotangent_side = from_side(cotangent)

    def project(rows):
        qkv = jnp.einsum("td,sdc->stc", rows, w_qkv, preferred_element_type=F32)
        return qkv.astype(BF16).reshape(3, 2, tok_dev, heads_width)

    lanes = -(-(experts + 2) // LANES) * LANES
    head = jnp.concatenate(
        [w_router, w_mix, jnp.zeros((width, lanes - experts - 2), BF16)], axis=1
    )
    near_qkv = project(near_one)
    cotangent_far = from_far(after(cotangent, normed_far))
    normed_far, near_qkv, head = lax.optimization_barrier((normed_far, near_qkv, head))
    far_one = jnp.concatenate([normed_far, from_side(normed_far)], axis=0)
    far_qkv = project(far_one)
    near_out, far_out, *logs = attention_forward(leaves, near_qkv, far_qkv)
    far_out, own_grads, cotangent_far, cotangent_side = lax.optimization_barrier(
        (far_out, own_grads, cotangent_far, cotangent_side)
    )

    def branch_part(rows):
        return jnp.dot(rows, w_out, preferred_element_type=F32)

    far_sum = plus_side(branch_part(far_out[0]), branch_part(far_out[1])).astype(BF16)
    branch = plus_side(branch_part(near_out[0]), branch_part(near_out[1]))
    branch_far = from_far(far_sum)
    side_grads = from_side(own_grads)
    cotangent_corner = from_side(cotangent_far)
    far_placed = placed(far_slots, cotangent_far)
    branch_far, side_grads, cotangent_corner, far_placed = lax.optimization_barrier(
        (branch_far, side_grads, cotangent_corner, far_placed)
    )
    residual = tokens.astype(F32) + (branch + branch_far.astype(F32))

    scaled_two, inverse_two = norm_parts(residual)
    normed_two = (scaled_two * ln_mlp).astype(BF16)
    normed_two_far = from_far(normed_two)
    normed_two_side = from_side(normed_two)
    own_rows = sent(placed(own_slots, normed_two))

    def dense(own, side, own_cotangent, side_cotangent):
        return feed(
            own, side, own_cotangent, side_cotangent, head, w_up, w_down, experts, None, DENSE_ROWS
        )

    def product(left, right):
        return jnp.einsum("gd,gf->df", left, right, preferred_element_type=F32)

    def weight_grads(near_left, far_left, near_right, far_right):
        return product(near_left, near_right) + product(far_left, far_right)

    near_dense = dense(normed_two, normed_two_side, cotangent, cotangent_side)
    near_two = jnp.concatenate([normed_two, normed_two_side], axis=0)
    grad_up = product(near_two, near_dense[5])
    grad_down = product(near_dense[6], near_dense[4])
    normed_two_far, grad_up, grad_down, own_rows = lax.optimization_barrier(
        (normed_two_far, grad_up, grad_down, own_rows)
    )
    far_rows = from_far(own_rows)
    far_grads = sent(after(far_placed, own_rows))
    normed_two_corner = from_side(normed_two_far)
    far_dense = list(dense(normed_two_far, normed_two_corner, cotangent_far, cotangent_corner))

    expert = lax.axis_index("expert").astype(jnp.int32)

    def routed(own, side, own_cotangent, side_cotangent):
        return feed(
            own,
            side,
            own_cotangent,
            side_cotangent,
            head,
            ex_up[0],
            ex_down[0],
            experts,
            expert,
            EXPERT_ROWS,
        )

    def chip_sum(parts, place, *others):
        return plus_side(parts[place], after(parts[place + 1], *others))

    def chip_sum(parts, place, *others):
        return plus_side(parts[place], after(parts[place + 1], *others))

    dense_back_far = chip_sum(far_dense, 2).astype(BF16)
    far_rows, far_dense[6], far_dense[5] = lax.optimization_barrier(
        (far_rows, far_dense[6], far_dense[5])
    )
    far_two = jnp.concatenate([normed_two_far, normed_two_corner], axis=0)
    grad_up = (grad_up + product(far_two, far_dense[5])).astype(BF16)
    grad_down = (grad_down + product(far_dense[6], far_dense[4])).astype(BF16)
    dense_grads = jnp.concatenate([grad_up, grad_down], axis=1)
    far_rows, dense_back_far, dense_grads = lax.optimization_barrier(
        (far_rows, dense_back_far, dense_grads)
    )
    dense_grads = scatter_sum(dense_grads)
    dense_back_far = from_far(dense_back_far)
    corner_rows = from_side(far_rows)
    side_rows = from_side(own_rows)
    far_expert = routed(far_rows, corner_rows, far_grads, from_side(far_grads))
    *far_expert, dense_back_far = lax.optimization_barrier((*far_expert, dense_back_far))
    far_back = chip_sum(far_expert, 2).astype(BF16)
    own_rows, far_back = lax.optimization_barrier((own_rows, far_back))
    near_expert = routed(own_rows, side_rows, own_grads, side_grads)
    *near_expert, dense_grads = lax.optimization_barrier((*near_expert, dense_grads))

    def picked(rows):
        return lax.dot_general(
            own_slots, rows, (((0,), (0,)), ((), ())), preferred_element_type=F32
        )

    expert_back = (chip_sum(near_expert, 2) + from_far(far_back).astype(F32)).astype(BF16)
    far_expert_out = chip_sum(far_expert, 0, expert_back).astype(BF16)
    dense_out_far = chip_sum(far_dense, 0, expert_back).astype(BF16)
    dense_back = chip_sum(near_dense, 2, far_back) + dense_back_far.astype(F32)

    far_out_rows = from_far(far_expert_out)
    grad_normed_two, far_out_rows = lax.optimization_barrier(
        (dense_back + picked(sent(expert_back)), far_out_rows)
    )
    dense_out = chip_sum(near_dense, 0, expert_back)
    expert_out = chip_sum(near_expert, 0, expert_back) + far_out_rows.astype(F32)
    expert_out = sent(after(expert_out.astype(BF16), grad_normed_two))

    near_tokens = jnp.concatenate([own_rows, side_rows], axis=0)
    near_tokens, near_active, far_active, far_expert_out = lax.optimization_barrier(
        (near_tokens, near_expert[4], far_expert[4], far_expert_out)
    )
    far_tokens = jnp.concatenate([far_rows, corner_rows], axis=0)
    grad_ex_up = weight_grads(near_tokens, far_tokens, near_expert[5], far_expert[5])[None]
    grad_ex_down = weight_grads(near_active, far_active, near_expert[6], far_expert[6])[None]

    gain_two = jnp.sum(grad_normed_two * scaled_two, axis=0)
    grad_residual = cotangent.astype(F32) + norm_back(
        grad_normed_two, ln_mlp, scaled_two, inverse_two
    )
    grad_branch = grad_residual.astype(BF16)
    grad_branch_far = from_far(grad_branch)
    grad_branch_side = from_side(grad_branch)

    def into_heads(*rows):
        grads = [jnp.einsum("gd,cd->gc", part, w_out, preferred_element_type=F32) for part in rows]
        return jnp.stack(grads).astype(BF16)

    near_heads = into_heads(grad_branch, grad_branch_side)
    grad_branch_far, near_heads, grad_ex_up, grad_ex_down = lax.optimization_barrier(
        (grad_branch_far, near_heads, grad_ex_up, grad_ex_down)
    )
    grad_branch_corner = from_side(grad_branch_far)
    far_heads = into_heads(grad_branch_far, grad_branch_corner)
    head_grads = near_dense[7] + far_dense[7] + near_expert[7] + far_expert[7]
    small = jnp.concatenate([head_grads[: experts + 2], gain_two[None]], axis=0)
    small = sum_over(small, "tensor")
    small_columns = -(-small.shape[0] // LANES) * LANES
    small_block = jnp.pad(small, ((0, small_columns - small.shape[0]), (0, 0))).T
    dense_out_far = from_far(after(dense_out_far, grad_branch_far))
    near_result, far_result = attention_backward(
        leaves, near_qkv, far_qkv, near_heads, far_heads, near_out, far_out, logs
    )
    near_result, far_result, expert_out, dense_out_far = lax.optimization_barrier(
        (near_result, far_result, expert_out, dense_out_far)
    )

    def normed_part(grads):
        return jnp.einsum("sgc,sdc->gd", grads, w_qkv, preferred_element_type=F32)

    corner_part = normed_part(far_result[:, 1]).astype(BF16)
    from_corner = from_side(corner_part).astype(F32)

    flat = (2 * tok_dev, heads_width)
    near_branch = jnp.concatenate([grad_branch, grad_branch_side], axis=0)
    far_branch = jnp.concatenate([grad_branch_far, grad_branch_corner], axis=0)
    near_branch = after(near_branch, corner_part)
    grad_w_out = weight_grads(near_branch, far_branch, near_out.reshape(flat), far_out.reshape(flat))
    branch_grads = strips_total(strips_sent(
        jnp.concatenate([grad_w_out.astype(BF16), small_block.astype(BF16)], axis=1)
    ))
    far_sum = (normed_part(far_result[:, 0]) + from_corner).astype(BF16)
    near_result, far_result, expert_out, far_sum = lax.optimization_barrier(
        (near_result, far_result, expert_out, far_sum)
    )
    near_sum = plus_side(normed_part(near_result[:, 0]), normed_part(near_result[:, 1]))
    out = (residual + dense_out + dense_out_far.astype(F32) + picked(expert_out)).astype(BF16)

    near_result = near_result.reshape(3, *flat)
    far_result = far_result.reshape(3, *flat)
    qkv_grads = strips_total(strips_sent(
        jnp.concatenate(
            [
                weight_grads(near_one, far_one, near_result[part], far_result[part]).astype(BF16)
                for part in range(3)
            ],
            axis=1,
        )
    ))
    grad_normed_one = near_sum + from_far(far_sum).astype(F32)
    gain_one = jnp.sum(grad_normed_one * scaled_one, axis=0, keepdims=True)
    grad_ln_attn = sum_over(sum_over(gain_one, "tensor"), "expert")[0]
    grad_tokens = grad_residual + norm_back(grad_normed_one, ln_attn, scaled_one, inverse_one)

    strip = qkv_grads.shape[0]
    return (
        out,
        grad_tokens,
        grad_ln_attn,
        qkv_grads.reshape(strip, 3, heads_width).transpose(1, 0, 2),
        branch_grads[:, :heads_width].T,
        branch_grads[:, heads_width + experts + 2],
        dense_grads[:, :hidden],
        dense_grads[:, hidden:].T,
        branch_grads[:, heads_width : heads_width + experts],
        branch_grads[:, heads_width + experts : heads_width + experts + 2],
        grad_ex_up,
        grad_ex_down,
    )


def solution(mesh):
    return jax.shard_map(
        per_device,
        mesh=mesh,
        in_specs=(
            P(("expert", "tensor"), None),
            P(("expert", "tensor"), None),
            P("expert", None),
            P("expert", None),
            P(),
            P(None, None, "tensor"),
            P("tensor", None),
            P(),
            P(None, "tensor"),
            P("tensor", None),
            P(),
            P(),
            P("expert", None, "tensor"),
            P("expert", "tensor", None),
        ),
        out_specs=(
            P(("expert", "tensor"), None),
            P(("expert", "tensor"), None),
            P(),
            P(None, "expert", "tensor"),
            P("tensor", "expert"),
            P("expert"),
            P("expert", "tensor"),
            P("tensor", "expert"),
            P("expert", None),
            P("expert", None),
            P("expert", None, "tensor"),
            P("expert", "tensor", None),
        ),
        check_vma=False,
    )
```

```python
import functools

import jax
import jax.numpy as jnp
from jax import lax
from jax.experimental import pallas as pl
from jax.experimental.layout import Layout, with_layout_constraint
from jax.experimental.pallas import tpu as pltpu
from jax.sharding import PartitionSpec as P

HEAD_DIM = 64
TRUNK = 1024
SEG = 128
SEGS = 13
TREE_LEN = 2560
BRANCHES = 4
FAMILY = 3 * SEG
QROWS = 256
COVER = 8
PAIR = 2 * HEAD_DIM
NEGATIVE_FILL = -1e30
F32 = jnp.float32
BF16 = jnp.bfloat16
EPSILON = 1e-05


def dot_nn(a, b):
    return lax.dot_general(a, b, (((1,), (0,)), ((), ())), preferred_element_type=F32)


def dot_nt(a, b):
    return lax.dot_general(a, b, (((1,), (1,)), ((), ())), preferred_element_type=F32)


def head_lanes(rows, head):
    lane = lax.broadcasted_iota(jnp.int32, rows.shape, 1)
    return jnp.where(lane // HEAD_DIM == head, rows, jnp.zeros_like(rows))


def causal(scores):
    key = lax.broadcasted_iota(jnp.int32, scores.shape, 0)
    query = lax.broadcasted_iota(jnp.int32, scores.shape, 1)
    return jnp.where(key <= query, scores, NEGATIVE_FILL)


def family_rows(leaves_ref, branch):
    def start(segment):
        return pl.multiple_of(TRUNK + (segment - 1) * SEG, SEG)

    return [start(branch + 1), start(leaves_ref[2 * branch]), start(leaves_ref[2 * branch + 1])]


def transpose_into(target_ref, source_ref, part):
    for first in range(0, TREE_LEN, 512):
        piece = source_ref[part, pl.ds(first, 512), :].astype(F32)
        target_ref[:, pl.ds(first, 512)] = piece.T.astype(BF16)


def widen(piece, first, width, fill):
    parts = []
    if first:
        parts.append(jnp.full((piece.shape[0], first), fill, piece.dtype))
    parts.append(piece)
    rest = width - first - piece.shape[1]
    if rest:
        parts.append(jnp.full((piece.shape[0], rest), fill, piece.dtype))
    return parts[0] if len(parts) == 1 else jnp.concatenate(parts, axis=1)


def trunk_groups(block):
    first = block * QROWS
    groups = [(0, first, 0, QROWS, None)] if first else []
    return groups + [(first, QROWS, 0, QROWS, "causal")]


def family_groups(starts):
    return [
        (0, TRUNK, 0, FAMILY, None),
        (starts[0], SEG, 0, FAMILY, "branch"),
        (starts[1], SEG, SEG, 2 * SEG, "causal"),
        (starts[2], SEG, 2 * SEG, FAMILY, "causal"),
    ]


def masked_scores(keys, queries, rule):
    scores = dot_nt(keys, queries)
    if rule == "causal":
        return causal(scores)
    if rule == "branch":
        return jnp.concatenate([causal(scores[:, :SEG]), scores[:, SEG:]], axis=1)
    return scores


def forward_block(qkv_ref, values_t_ref, queries, groups):
    width = queries.shape[0]
    outs, logs = [], []
    for head in range(2):
        own = head_lanes(queries, head)
        all_scores = [
            masked_scores(qkv_ref[1, pl.ds(start, size), :], own[first:last], rule)
            for start, size, first, last, rule in groups
        ]
        top = functools.reduce(
            jnp.maximum,
            [
                widen(jnp.max(s, axis=0, keepdims=True), first, width, NEGATIVE_FILL)
                for s, (_, _, first, last, _) in zip(all_scores, groups)
            ],
        )
        total, output = None, None
        for s, (start, size, first, last, _) in zip(all_scores, groups):
            weights = jnp.exp(s - top[:, first:last])
            part = widen(jnp.sum(weights, axis=0, keepdims=True), first, width, 0.0)
            values_t = values_t_ref[pl.ds(head * HEAD_DIM, HEAD_DIM), pl.ds(start, size)]
            mixed = widen(dot_nn(values_t, weights.astype(BF16)), first, width, 0.0)
            total = part if total is None else total + part
            output = mixed if output is None else output + mixed
        outs.append(output / total)
        logs.append(top + jnp.log(total))
    return jnp.concatenate(outs, axis=0).T.astype(BF16), jnp.concatenate(logs, axis=0)


def scaled_queries(qkv_ref, starts, size):
    rows = [qkv_ref[0, pl.ds(start, size), :] for start in starts]
    rows = rows[0] if len(rows) == 1 else jnp.concatenate(rows, axis=0)
    return rows * jnp.asarray(HEAD_DIM ** (-0.5), BF16)


def quarter_rows(leaves_ref, offset):
    quarter = TREE_LEN // 4
    return pl.ds(pl.multiple_of((leaves_ref[2 * BRANCHES] ^ offset) * quarter, quarter), quarter)


def forward_kernel(
    leaves_ref,
    near_ref,
    far_ref,
    near_out_ref,
    far_out_ref,
    trunk_log_ref,
    family_log_ref,
    qkv_ref,
    out_ref,
    values_t_ref,
):
    for offset in range(4):
        half_ref = near_ref if offset < 2 else far_ref
        qkv_ref[:, quarter_rows(leaves_ref, offset), :] = half_ref[:, offset % 2]
    transpose_into(values_t_ref, qkv_ref, 2)
    for block in range(TRUNK // QROWS):
        first = block * QROWS
        queries = scaled_queries(qkv_ref, [first], QROWS)
        out, logs = forward_block(qkv_ref, values_t_ref, queries, trunk_groups(block))
        out_ref[pl.ds(first, QROWS), :] = out
        trunk_log_ref[0, :, pl.ds(first, QROWS)] = logs

    def one_family(branch, carry):
        starts = family_rows(leaves_ref, branch)
        queries = scaled_queries(qkv_ref, starts, SEG)
        out, logs = forward_block(qkv_ref, values_t_ref, queries, family_groups(starts))
        for place, start in enumerate(starts):
            out_ref[pl.ds(start, SEG), :] = out[place * SEG : (place + 1) * SEG]
        family_log_ref[0, branch] = logs
        return carry

    lax.fori_loop(0, BRANCHES, one_family, 0)
    for offset in range(4):
        half_ref = near_out_ref if offset < 2 else far_out_ref
        half_ref[offset % 2] = out_ref[quarter_rows(leaves_ref, offset), :]


def halves_spec(parts):
    quarter = TREE_LEN // 4
    if parts == 1:
        return pl.BlockSpec((2, quarter, PAIR), lambda p, leaves: (0, 0, p))
    return pl.BlockSpec((parts, 2, quarter, PAIR), lambda p, leaves: (0, 0, 0, p))


def attention_cost(products, cover):
    visited = (TRUNK * (TRUNK + QROWS) // 2 + BRANCHES * FAMILY * (TRUNK + SEG)) // cover
    return pl.CostEstimate(
        flops=2 * products * 4 * visited * 2 * PAIR,
        transcendentals=4 * visited,
        bytes_accessed=8 * TREE_LEN * 4 * HEAD_DIM * 2 // cover,
    )


def attention_forward(leaves, near, far):
    width = near.shape[3]
    quarter = TREE_LEN // 4
    pairs = width // PAIR
    return pl.pallas_call(
        forward_kernel,
        grid_spec=pltpu.PrefetchScalarGridSpec(
            num_scalar_prefetch=1,
            grid=(pairs,),
            in_specs=[halves_spec(3), halves_spec(3)],
            out_specs=[
                halves_spec(1),
                halves_spec(1),
                pl.BlockSpec((1, 2, TRUNK), lambda p, leaves: (p, 0, 0)),
                pl.BlockSpec((1, BRANCHES, 2, FAMILY), lambda p, leaves: (p, 0, 0, 0)),
            ],
            scratch_shapes=[
                pltpu.VMEM((3, TREE_LEN, PAIR), BF16),
                pltpu.VMEM((TREE_LEN, PAIR), BF16),
                pltpu.VMEM((PAIR, TREE_LEN), BF16),
            ],
        ),
        out_shape=[
            jax.ShapeDtypeStruct((2, quarter, width), BF16),
            jax.ShapeDtypeStruct((2, quarter, width), BF16),
            jax.ShapeDtypeStruct((pairs, 2, TRUNK), F32),
            jax.ShapeDtypeStruct((pairs, BRANCHES, 2, FAMILY), F32),
        ],
        cost_estimate=attention_cost(2, COVER),
        name="tree_attention",
    )(leaves, near, far)


def backward_block(qkv_ref, keys_t_ref, queries, grads, outs, logs, groups):
    products = grads.astype(F32) * outs.astype(F32)
    products_t = products.T
    key_ds = [[] for _ in groups]
    value_ws = [[] for _ in groups]
    own_q, own_g, query_grads = [], [], []
    for head in range(2):
        own = head_lanes(queries, head)
        own_grads = head_lanes(grads, head)
        own_q.append(own)
        own_g.append(own_grads)
        inner = jnp.sum(
            products_t[head * HEAD_DIM : (head + 1) * HEAD_DIM], axis=0, keepdims=True
        )
        log = logs[head : head + 1]
        query_grad = None
        for place, (start, size, first, last, rule) in enumerate(groups):
            scores = masked_scores(qkv_ref[1, pl.ds(start, size), :], own[first:last], rule)
            weights = jnp.exp(scores - log[:, first:last])
            grad_weights = dot_nt(qkv_ref[2, pl.ds(start, size), :], own_grads[first:last])
            grad_scores = (weights * (grad_weights - inner[:, first:last])).astype(BF16)
            keys_t = keys_t_ref[pl.ds(head * HEAD_DIM, HEAD_DIM), pl.ds(start, size)]
            part = widen(dot_nn(keys_t, grad_scores), first, queries.shape[0], 0.0)
            query_grad = part if query_grad is None else query_grad + part
            key_ds[place].append(grad_scores)
            value_ws[place].append(weights.astype(BF16))
        query_grads.append(query_grad)
    grad_query = (jnp.concatenate(query_grads, axis=0) * HEAD_DIM ** (-0.5)).T.astype(BF16)
    key_grads, value_grads = [], []
    for place, (start, size, first, last, rule) in enumerate(groups):
        stacked_q = jnp.concatenate([own_q[0][first:last], own_q[1][first:last]], axis=0)
        stacked_g = jnp.concatenate([own_g[0][first:last], own_g[1][first:last]], axis=0)
        key_grads.append(dot_nn(jnp.concatenate(key_ds[place], axis=1), stacked_q))
        value_grads.append(dot_nn(jnp.concatenate(value_ws[place], axis=1), stacked_g))
    return grad_query, key_grads, value_grads


def backward_kernel(
    leaves_ref,
    near_ref,
    far_ref,
    near_grads_ref,
    far_grads_ref,
    near_outs_ref,
    far_outs_ref,
    trunk_log_ref,
    family_log_ref,
    near_result_ref,
    far_result_ref,
    qkv_ref,
    grads_ref,
    outs_ref,
    result_ref,
    keys_t_ref,
    trunk_keys_ref,
    trunk_values_ref,
):
    for offset in range(4):
        rows = quarter_rows(leaves_ref, offset)
        at = offset % 2
        qkv_ref[:, rows, :] = (near_ref if offset < 2 else far_ref)[:, at]
        grads_ref[rows, :] = (near_grads_ref if offset < 2 else far_grads_ref)[at]
        outs_ref[rows, :] = (near_outs_ref if offset < 2 else far_outs_ref)[at]
    transpose_into(keys_t_ref, qkv_ref, 1)
    trunk_keys_ref[...] = jnp.zeros_like(trunk_keys_ref)
    trunk_values_ref[...] = jnp.zeros_like(trunk_values_ref)
    for block in range(TRUNK // QROWS):
        first = block * QROWS
        rows = pl.ds(first, QROWS)
        groups = trunk_groups(block)
        grad_query, key_grads, value_grads = backward_block(
            qkv_ref,
            keys_t_ref,
            scaled_queries(qkv_ref, [first], QROWS),
            grads_ref[rows, :],
            outs_ref[rows, :],
            trunk_log_ref[0, :, rows],
            groups,
        )
        result_ref[0, rows, :] = grad_query
        for (start, size, _, _, _), key_grad, value_grad in zip(groups, key_grads, value_grads):
            trunk_keys_ref[pl.ds(start, size), :] += key_grad
            trunk_values_ref[pl.ds(start, size), :] += value_grad

    def one_family(branch, carry):
        starts = family_rows(leaves_ref, branch)
        groups = family_groups(starts)
        grad_query, key_grads, value_grads = backward_block(
            qkv_ref,
            keys_t_ref,
            scaled_queries(qkv_ref, starts, SEG),
            jnp.concatenate([grads_ref[pl.ds(start, SEG), :] for start in starts], axis=0),
            jnp.concatenate([outs_ref[pl.ds(start, SEG), :] for start in starts], axis=0),
            family_log_ref[0, branch],
            groups,
        )
        trunk_keys_ref[...] += key_grads[0]
        trunk_values_ref[...] += value_grads[0]
        for place, start in enumerate(starts):
            rows = pl.ds(start, SEG)
            result_ref[0, rows, :] = grad_query[place * SEG : (place + 1) * SEG]
            result_ref[1, rows, :] = key_grads[1 + place].astype(BF16)
            result_ref[2, rows, :] = value_grads[1 + place].astype(BF16)
        return carry

    lax.fori_loop(0, BRANCHES, one_family, 0)
    result_ref[1, pl.ds(0, TRUNK), :] = trunk_keys_ref[...].astype(BF16)
    result_ref[2, pl.ds(0, TRUNK), :] = trunk_values_ref[...].astype(BF16)
    for offset in range(4):
        half_ref = near_result_ref if offset < 2 else far_result_ref
        half_ref[:, offset % 2] = result_ref[:, quarter_rows(leaves_ref, offset), :]


def attention_backward(leaves, near, far, near_grads, far_grads, near_outs, far_outs, logs):
    pairs = near.shape[3] // PAIR
    return pl.pallas_call(
        backward_kernel,
        grid_spec=pltpu.PrefetchScalarGridSpec(
            num_scalar_prefetch=1,
            grid=(pairs,),
            in_specs=[
                halves_spec(3),
                halves_spec(3),
                halves_spec(1),
                halves_spec(1),
                halves_spec(1),
                halves_spec(1),
                pl.BlockSpec((1, 2, TRUNK), lambda p, leaves: (p, 0, 0)),
                pl.BlockSpec((1, BRANCHES, 2, FAMILY), lambda p, leaves: (p, 0, 0, 0)),
            ],
            out_specs=[halves_spec(3), halves_spec(3)],
            scratch_shapes=[
                pltpu.VMEM((3, TREE_LEN, PAIR), BF16),
                pltpu.VMEM((TREE_LEN, PAIR), BF16),
                pltpu.VMEM((TREE_LEN, PAIR), BF16),
                pltpu.VMEM((3, TREE_LEN, PAIR), BF16),
                pltpu.VMEM((PAIR, TREE_LEN), BF16),
                pltpu.VMEM((TRUNK, PAIR), F32),
                pltpu.VMEM((TRUNK, PAIR), F32),
            ],
        ),
        out_shape=[jax.ShapeDtypeStruct(near.shape, BF16), jax.ShapeDtypeStruct(far.shape, BF16)],
        cost_estimate=attention_cost(5, 5),
        name="tree_attention_back",
    )(leaves, near, far, near_grads, far_grads, near_outs, far_outs, *logs)


def leaf_order(parents_row):
    first_leaf = BRANCHES + 1
    leaf_parents = parents_row[first_leaf:]
    segments = first_leaf + jnp.arange(leaf_parents.shape[0], dtype=jnp.int32)
    same = leaf_parents[:, None] == leaf_parents[None, :]
    later = segments[None, :] < segments[:, None]
    place = 2 * (leaf_parents - 1) + jnp.sum(jnp.where(same & later, 1, 0), axis=1)
    slots = jnp.arange(2 * BRANCHES, dtype=jnp.int32)
    return jnp.sum(jnp.where(slots[:, None] == place[None, :], segments[None, :], 0), axis=1)


def gates(logits, experts, expert):
    lane = lax.broadcasted_iota(jnp.int32, logits.shape, 1)
    first, second = logits[:, experts : experts + 1], logits[:, experts + 1 : experts + 2]
    top = jnp.maximum(first, second)
    first, second = jnp.exp(first - top), jnp.exp(second - top)
    total = first + second
    first, second = first / total, second / total
    if expert is None:
        return lane, first, second, None, None
    routed = jnp.where(lane < experts, logits, NEGATIVE_FILL)
    raised = jnp.exp(routed - jnp.max(routed, axis=1, keepdims=True))
    probs = raised / jnp.sum(raised, axis=1, keepdims=True)
    gate = jnp.sum(jnp.where(lane == expert, probs, 0.0), axis=1, keepdims=True)
    return lane, first, second, probs, gate


def both(own_ref, side_ref):
    return jnp.concatenate([own_ref[...], side_ref[...]], axis=0)


def split_store(own_ref, side_ref, rows):
    half = rows.shape[0] // 2
    own_ref[...] = rows[:half]
    side_ref[...] = rows[half:]


def feed_kernel(
    experts,
    routed,
    expert_ref,
    own_ref,
    side_ref,
    own_grads_ref,
    side_grads_ref,
    head_ref,
    up_ref,
    down_ref,
    own_out_ref,
    side_out_ref,
    own_back_ref,
    side_back_ref,
    active_ref,
    pre_ref,
    grad_ref,
    head_grad_ref,
):
    rows = both(own_ref, side_ref)
    grads = both(own_grads_ref, side_grads_ref).astype(F32)
    expert = expert_ref[0] if routed else None
    logits = dot_nn(rows, head_ref[...])
    lane, first, second, probs, gate = gates(logits, experts, expert)
    coef = second * gate if routed else first
    weighted = (coef * grads).astype(BF16)
    pre = dot_nn(rows, up_ref[...])
    grad_active = dot_nt(weighted, down_ref[...])
    cumulative = 0.5 + 0.5 * lax.erf(pre * 0.7071067811865476)
    slope = cumulative + pre * jnp.exp(-0.5 * pre * pre) * 0.3989422804014327
    active = (pre * cumulative).astype(BF16)
    grad_pre = (grad_active * slope).astype(BF16)
    half = rows.shape[0] // 2
    for ref, value in ((active_ref, active), (pre_ref, grad_pre), (grad_ref, weighted)):
        ref[0] = value[:half]
        ref[1] = value[half:]
    out = dot_nn(active, down_ref[...])
    split_store(own_out_ref, side_out_ref, (coef * out).astype(BF16))
    inner = jnp.sum(grads * out, axis=1, keepdims=True)
    swing = first * second * inner
    if routed:
        swing = -gate * swing
    grad_logits = jnp.where(lane == experts, swing, jnp.where(lane == experts + 1, -swing, 0.0))
    if routed:
        picked = jnp.where(lane == expert, 1.0, 0.0) - gate
        grad_logits = grad_logits + jnp.where(
            lane < experts, probs * picked * (second * inner), 0.0
        )
    back = dot_nt(grad_pre, up_ref[...]) + dot_nt(grad_logits.astype(BF16), head_ref[...])
    split_store(own_back_ref, side_back_ref, back.astype(BF16))
    head_grad = dot_nn(grad_logits.T.astype(BF16), rows)

    @pl.when(pl.program_id(0) == 0)
    def _():
        head_grad_ref[...] = jnp.zeros_like(head_grad_ref)

    head_grad_ref[...] += head_grad


def feed(own, side, own_grads, side_grads, head, up, down, experts, expert, size):
    count = own.shape[0]
    width, hidden = up.shape
    steps = count // size
    lanes = head.shape[1]
    routed = expert is not None
    pick = jnp.reshape(expert, (1,)) if routed else jnp.zeros((1,), jnp.int32)
    rows = pl.BlockSpec((size, width), lambda i, pick: (i, 0))

    def whole(shape):
        return pl.BlockSpec(shape, lambda i, pick: (0, 0), pipeline_mode=pl.Buffered(1))

    def pairs(columns):
        return pl.BlockSpec((2, size, columns), lambda i, pick: (0, i, 0))

    quarter = jax.ShapeDtypeStruct((count, width), BF16)
    *sums, active, pre, weighted, head_grad = pl.pallas_call(
        functools.partial(feed_kernel, experts, routed),
        grid_spec=pltpu.PrefetchScalarGridSpec(
            num_scalar_prefetch=1,
            grid=(steps,),
            in_specs=[
                rows,
                rows,
                rows,
                rows,
                whole((width, lanes)),
                whole((width, hidden)),
                whole((hidden, width)),
            ],
            out_specs=[
                rows,
                rows,
                rows,
                rows,
                pairs(hidden),
                pairs(hidden),
                pairs(width),
                pl.BlockSpec((lanes, width), lambda i, pick: (0, 0)),
            ],
        ),
        out_shape=[
            quarter,
            quarter,
            quarter,
            quarter,
            jax.ShapeDtypeStruct((2, count, hidden), BF16),
            jax.ShapeDtypeStruct((2, count, hidden), BF16),
            jax.ShapeDtypeStruct((2, count, width), BF16),
            jax.ShapeDtypeStruct((lanes, width), F32),
        ],
        cost_estimate=pl.CostEstimate(
            flops=16 * count * width * hidden // COVER,
            transcendentals=4 * count * hidden // COVER,
            bytes_accessed=2 * (8 * count * width + 4 * count * hidden + 2 * width * hidden) // COVER,
        ),
        compiler_params=pltpu.CompilerParams(vmem_limit_bytes=60 * 1024 * 1024),
        name="feed_routed" if routed else "feed_dense",
    )(pick, own, side, own_grads, side_grads, head, up, down)
    flat = [value.reshape(2 * count, value.shape[2]) for value in (active, pre, weighted)]
    return [*sums, *flat, head_grad]


LANES = 128
DIRECT = 8
EARLY = 4
QUARTER_ROWS = 128


def norm_parts(values):
    row_mean = jnp.mean(values, axis=-1, keepdims=True)
    centred = values - row_mean
    row_var = jnp.mean(centred * centred, axis=-1, keepdims=True)
    inverse = lax.rsqrt(row_var + EPSILON)
    return (centred * inverse, inverse)


def norm_back(grad_normed, gain_vec, scaled, inverse):
    grad_scaled = grad_normed * gain_vec
    first_mean = jnp.mean(grad_scaled, axis=-1, keepdims=True)
    second = jnp.mean(grad_scaled * scaled, axis=-1, keepdims=True)
    return inverse * (grad_scaled - first_mean - scaled * second)


def after(value, *others):
    return lax.optimization_barrier((value, *others))[0]


def from_side(values):
    return lax.ppermute(values, "tensor", [(i, i ^ 1) for i in range(4)])


def from_far(values):
    return lax.ppermute(values, "tensor", [(i, i ^ 2) for i in range(4)])


def plus_side(own, side):
    return own.astype(F32) + from_side(side.astype(BF16)).astype(F32)


def sum_over(values, axis):
    count, step = lax.axis_size(axis), 1
    while step < count:
        pairs = [(i, i ^ step) for i in range(count)]
        values = values + lax.ppermute(values, axis, pairs)
        step *= 2
    return values


def exchange(blocks):
    return lax.all_to_all(blocks, "expert", split_axis=0, concat_axis=0, tiled=True)


def scatter_sum(strips):
    strips = with_layout_constraint(strips.astype(BF16), Layout(major_to_minor=(0, 1)))
    return lax.psum_scatter(strips, "expert", scatter_dimension=0, tiled=True).astype(F32)


def strips_sent(grads):
    return exchange(grads.reshape(lax.axis_size("expert"), -1, grads.shape[1]))


def strips_sent_each(grads, before, since):
    count = lax.axis_size("expert")
    if count > DIRECT:
        return [] if before else [strips_total(strips_sent(grads))]
    here = lax.axis_index("expert")
    strips = grads.reshape(count, -1, grads.shape[1])
    parts = []
    for step in range(since, before or count):
        strip = lax.dynamic_index_in_dim(strips, (here + step) % count, 0, keepdims=False)
        pairs = [(i, (i + step) % count) for i in range(count)]
        parts.append(lax.ppermute(strip, "expert", pairs) if step else strip)
    return parts


def strips_total(strips):
    return jnp.sum(strips.astype(F32), axis=0)


def slots_of(expert_ids, experts, capacity):
    rows = expert_ids.shape[0]
    chosen = expert_ids[:, None] == jnp.arange(experts, dtype=jnp.int32)[None, :]
    at = jnp.arange(rows, dtype=jnp.int32)
    before = (at[None, :] < at[:, None]).astype(BF16)
    earlier = jnp.dot(before, chosen.astype(BF16), preferred_element_type=F32)
    slot = jnp.sum(jnp.where(chosen, earlier, 0.0), axis=1).astype(jnp.int32)
    place = expert_ids * capacity + slot
    places = jnp.arange(experts * capacity, dtype=jnp.int32)
    return (places[:, None] == place[None, :]).astype(BF16)


def per_device(
    tokens,
    cotangent,
    routes,
    parents,
    ln_attn,
    w_qkv,
    w_out,
    ln_mlp,
    w_up,
    w_down,
    w_router,
    w_mix,
    ex_up,
    ex_down,
):
    tok_dev, width = tokens.shape
    mine = lax.axis_index("tensor")
    experts = w_router.shape[1]
    capacity = max(2, tok_dev * 7 // (5 * experts))
    heads_width = w_qkv.shape[2]
    hidden = w_up.shape[1]
    leaves = jnp.concatenate([leaf_order(parents[0]), mine.astype(jnp.int32)[None]])

    scaled_one, inverse_one = norm_parts(tokens.astype(F32))
    normed_own = (scaled_one * ln_attn).astype(BF16)
    normed_far = from_far(normed_own)
    near_one = jnp.concatenate([normed_own, from_side(normed_own)], axis=0)

    quarter_ids = routes[:, 0].reshape(4, tok_dev)

    def slots_at(offset):
        ids = lax.dynamic_index_in_dim(quarter_ids, mine ^ offset, 0, keepdims=False)
        return slots_of(ids, experts, capacity)

    own_slots, far_slots = slots_at(0), slots_at(2)

    def placed(slots, rows):
        return jnp.dot(slots, rows, preferred_element_type=F32).astype(BF16)

    def sent(rows):
        return exchange(rows.reshape(experts, capacity, width)).reshape(-1, width)

    own_grads = sent(placed(own_slots, cotangent))
    cotangent_side = from_side(cotangent)

    def project(rows):
        qkv = jnp.einsum("td,sdc->stc", rows, w_qkv, preferred_element_type=F32)
        return qkv.astype(BF16).reshape(3, 2, tok_dev, heads_width)

    lanes = -(-(experts + 2) // LANES) * LANES
    head = jnp.concatenate(
        [w_router, w_mix, jnp.zeros((width, lanes - experts - 2), BF16)], axis=1
    )
    near_qkv = project(near_one)
    cotangent_far = from_far(after(cotangent, normed_far))
    normed_far, near_qkv, head = lax.optimization_barrier((normed_far, near_qkv, head))
    far_one = jnp.concatenate([normed_far, from_side(normed_far)], axis=0)
    far_qkv = project(far_one)
    near_out, far_out, *logs = attention_forward(leaves, near_qkv, far_qkv)
    far_out, own_grads, cotangent_far, cotangent_side = lax.optimization_barrier(
        (far_out, own_grads, cotangent_far, cotangent_side)
    )

    def branch_part(rows):
        return jnp.dot(rows, w_out, preferred_element_type=F32)

    far_sum = plus_side(branch_part(far_out[0]), branch_part(far_out[1])).astype(BF16)
    branch = plus_side(branch_part(near_out[0]), branch_part(near_out[1]))
    branch_far = from_far(far_sum)
    side_grads = from_side(own_grads)
    cotangent_corner = from_side(cotangent_far)
    far_placed = placed(far_slots, cotangent_far)
    branch_far, side_grads, cotangent_corner, far_placed = lax.optimization_barrier(
        (branch_far, side_grads, cotangent_corner, far_placed)
    )
    residual = tokens.astype(F32) + (branch + branch_far.astype(F32))

    scaled_two, inverse_two = norm_parts(residual)
    normed_two = (scaled_two * ln_mlp).astype(BF16)
    normed_two_far = from_far(normed_two)
    normed_two_side = from_side(normed_two)
    own_rows = sent(placed(own_slots, normed_two))

    def dense(own, side, own_cotangent, side_cotangent):
        return feed(
            own, side, own_cotangent, side_cotangent, head, w_up, w_down, experts, None, QUARTER_ROWS
        )

    def product(left, right):
        return jnp.einsum("gd,gf->df", left, right, preferred_element_type=F32)

    def weight_grads(near_left, far_left, near_right, far_right):
        return product(near_left, near_right) + product(far_left, far_right)

    near_dense = dense(normed_two, normed_two_side, cotangent, cotangent_side)
    near_two = jnp.concatenate([normed_two, normed_two_side], axis=0)
    grad_up = product(near_two, near_dense[5])
    grad_down = product(near_dense[6], near_dense[4])
    normed_two_far, grad_up, grad_down, own_rows = lax.optimization_barrier(
        (normed_two_far, grad_up, grad_down, own_rows)
    )
    far_rows = from_far(own_rows)
    far_grads = sent(after(far_placed, own_rows))
    normed_two_corner = from_side(normed_two_far)
    far_dense = list(dense(normed_two_far, normed_two_corner, cotangent_far, cotangent_corner))

    expert = lax.axis_index("expert").astype(jnp.int32)

    def routed(own, side, own_cotangent, side_cotangent):
        return feed(
            own,
            side,
            own_cotangent,
            side_cotangent,
            head,
            ex_up[0],
            ex_down[0],
            experts,
            expert,
            QUARTER_ROWS,
        )

    def chip_sum(parts, place, *others):
        return plus_side(parts[place], after(parts[place + 1], *others))

    def chip_sum(parts, place, *others):
        return plus_side(parts[place], after(parts[place + 1], *others))

    dense_back_far = chip_sum(far_dense, 2).astype(BF16)
    far_rows, far_dense[6], far_dense[5] = lax.optimization_barrier(
        (far_rows, far_dense[6], far_dense[5])
    )
    far_two = jnp.concatenate([normed_two_far, normed_two_corner], axis=0)
    grad_up = (grad_up + product(far_two, far_dense[5])).astype(BF16)
    grad_down = (grad_down + product(far_dense[6], far_dense[4])).astype(BF16)
    grad_up, grad_down, far_grads = lax.optimization_barrier((grad_up, grad_down, far_grads))
    dense_grads = jnp.concatenate([grad_up, grad_down], axis=1)
    far_rows, dense_back_far, dense_grads = lax.optimization_barrier(
        (far_rows, dense_back_far, dense_grads)
    )
    dense_grads = scatter_sum(dense_grads)
    dense_back_far = from_far(dense_back_far)
    corner_rows = from_side(far_rows)
    side_rows = from_side(own_rows)
    far_expert = routed(far_rows, corner_rows, far_grads, from_side(far_grads))
    *far_expert, dense_back_far = lax.optimization_barrier((*far_expert, dense_back_far))
    far_back = chip_sum(far_expert, 2).astype(BF16)
    own_rows, far_back = lax.optimization_barrier((own_rows, far_back))
    near_expert = routed(own_rows, side_rows, own_grads, side_grads)
    *near_expert, dense_grads = lax.optimization_barrier((*near_expert, dense_grads))

    def picked(rows):
        return lax.dot_general(
            own_slots, rows, (((0,), (0,)), ((), ())), preferred_element_type=F32
        )

    expert_back = (chip_sum(near_expert, 2) + from_far(far_back).astype(F32)).astype(BF16)
    far_expert_out = chip_sum(far_expert, 0, expert_back).astype(BF16)
    dense_out_far = chip_sum(far_dense, 0, expert_back).astype(BF16)
    dense_back = chip_sum(near_dense, 2, far_back) + dense_back_far.astype(F32)

    grad_normed_two = dense_back + picked(sent(expert_back))
    dense_out = chip_sum(near_dense, 0, expert_back)
    expert_out = chip_sum(near_expert, 0, expert_back) + from_far(far_expert_out).astype(F32)
    expert_out = after(expert_out.astype(BF16), grad_normed_two)

    near_active, far_active, near_pre, far_pre, far_expert_out = lax.optimization_barrier(
        (near_expert[4], far_expert[4], near_expert[5], far_expert[5], far_expert_out)
    )
    near_tokens = jnp.concatenate([own_rows, side_rows], axis=0)
    far_tokens = jnp.concatenate([far_rows, corner_rows], axis=0)
    grad_ex_up = weight_grads(near_tokens, far_tokens, near_pre, far_pre)[None]
    grad_ex_down = weight_grads(near_active, far_active, near_expert[6], far_expert[6])[None]

    gain_two = jnp.sum(grad_normed_two * scaled_two, axis=0)
    grad_residual = cotangent.astype(F32) + norm_back(
        grad_normed_two, ln_mlp, scaled_two, inverse_two
    )
    grad_branch = grad_residual.astype(BF16)
    grad_branch_far = from_far(grad_branch)
    grad_branch_side = from_side(grad_branch)

    def into_heads(*rows):
        grads = [jnp.einsum("gd,cd->gc", part, w_out, preferred_element_type=F32) for part in rows]
        return jnp.stack(grads).astype(BF16)

    near_heads = into_heads(grad_branch, grad_branch_side)
    head_grads = near_dense[7] + far_dense[7] + near_expert[7] + far_expert[7]
    small = jnp.concatenate([head_grads[: experts + 2], gain_two[None]], axis=0)
    small = sum_over(small, "tensor")
    out_rows = sent(expert_out)
    grad_branch_far, small, near_heads, grad_ex_up, grad_ex_down, _, dense_out_far, dense_out = (
        lax.optimization_barrier(
            (
                grad_branch_far,
                small,
                near_heads,
                grad_ex_up,
                grad_ex_down,
                expert_out,
                dense_out_far,
                dense_out,
            )
        )
    )
    grad_branch_corner = from_side(grad_branch_far)
    far_heads = into_heads(grad_branch_far, grad_branch_corner)
    small_columns = -(-small.shape[0] // LANES) * LANES
    small_block = jnp.pad(small, ((0, small_columns - small.shape[0]), (0, 0))).T
    dense_out_far = from_far(dense_out_far)

    flat = (2 * tok_dev, heads_width)
    near_branch = jnp.concatenate([grad_branch, grad_branch_side], axis=0)
    far_branch = jnp.concatenate([grad_branch_far, grad_branch_corner], axis=0)
    grad_w_out = weight_grads(near_branch, far_branch, near_out.reshape(flat), far_out.reshape(flat))
    branch_grads = jnp.concatenate([grad_w_out.astype(BF16), small_block.astype(BF16)], axis=1)
    branch_early = strips_sent_each(branch_grads, EARLY, 0)
    near_result, far_result = attention_backward(
        leaves, near_qkv, far_qkv, near_heads, far_heads, near_out, far_out, logs
    )
    near_result, far_result, out_rows, dense_out_far, *branch_early = lax.optimization_barrier(
        (near_result, far_result, out_rows, dense_out_far, *branch_early)
    )

    def normed_part(grads):
        return jnp.einsum("sgc,sdc->gd", grads, w_qkv, preferred_element_type=F32)

    corner_part = normed_part(far_result[:, 1]).astype(BF16)
    from_corner = from_side(corner_part).astype(F32)

    far_sum = (normed_part(far_result[:, 0]) + from_corner).astype(BF16)
    near_result, far_result, out_rows, far_sum, branch_grads = lax.optimization_barrier(
        (near_result, far_result, out_rows, far_sum, branch_grads)
    )
    branch_late = strips_sent_each(branch_grads, 0, EARLY)
    near_sum = plus_side(normed_part(near_result[:, 0]), normed_part(near_result[:, 1]))
    out = (residual + dense_out + dense_out_far.astype(F32) + picked(out_rows)).astype(BF16)

    near_result = near_result.reshape(3, *flat)
    far_result = far_result.reshape(3, *flat)
    branch_grads = functools.reduce(
        jnp.add, [part.astype(F32) for part in branch_early + branch_late]
    )
    qkv_grads = strips_total(strips_sent(
        jnp.concatenate(
            [
                weight_grads(near_one, far_one, near_result[part], far_result[part]).astype(BF16)
                for part in range(3)
            ],
            axis=1,
        )
    ))
    grad_normed_one = near_sum + from_far(far_sum).astype(F32)
    gain_one = jnp.sum(grad_normed_one * scaled_one, axis=0, keepdims=True)
    grad_ln_attn = sum_over(sum_over(gain_one, "tensor"), "expert")[0]
    grad_tokens = grad_residual + norm_back(grad_normed_one, ln_attn, scaled_one, inverse_one)

    strip = qkv_grads.shape[0]
    return (
        out,
        grad_tokens,
        grad_ln_attn,
        qkv_grads.reshape(strip, 3, heads_width).transpose(1, 0, 2),
        branch_grads[:, :heads_width].T,
        branch_grads[:, heads_width + experts + 2],
        dense_grads[:, :hidden],
        dense_grads[:, hidden:].T,
        branch_grads[:, heads_width : heads_width + experts],
        branch_grads[:, heads_width + experts : heads_width + experts + 2],
        grad_ex_up,
        grad_ex_down,
    )


def solution(mesh):
    return jax.shard_map(
        per_device,
        mesh=mesh,
        in_specs=(
            P(("expert", "tensor"), None),
            P(("expert", "tensor"), None),
            P("expert", None),
            P("expert", None),
            P(),
            P(None, None, "tensor"),
            P("tensor", None),
            P(),
            P(None, "tensor"),
            P("tensor", None),
            P(),
            P(),
            P("expert", None, "tensor"),
            P("expert", "tensor", None),
        ),
        out_specs=(
            P(("expert", "tensor"), None),
            P(("expert", "tensor"), None),
            P(),
            P(None, "expert", "tensor"),
            P("tensor", "expert"),
            P("expert"),
            P("expert", "tensor"),
            P("tensor", "expert"),
            P("expert", None),
            P("expert", None),
            P("expert", None, "tensor"),
            P("expert", "tensor", None),
        ),
        check_vma=False,
    )
```

```python
import functools

import jax
import jax.numpy as jnp
from jax import lax
from jax.experimental import pallas as pl
from jax.experimental.layout import Layout, with_layout_constraint
from jax.experimental.pallas import tpu as pltpu
from jax.sharding import PartitionSpec as P

HEAD_DIM = 64
TRUNK = 1024
SEG = 128
SEGS = 13
TREE_LEN = 2560
BRANCHES = 4
FAMILY = 3 * SEG
QROWS = 256
COVER = 8
PAIR = 2 * HEAD_DIM
NEGATIVE_FILL = -1e30
F32 = jnp.float32
BF16 = jnp.bfloat16
EPSILON = 1e-05


def dot_nn(a, b):
    return lax.dot_general(a, b, (((1,), (0,)), ((), ())), preferred_element_type=F32)


def dot_nt(a, b):
    return lax.dot_general(a, b, (((1,), (1,)), ((), ())), preferred_element_type=F32)


def head_lanes(rows, head):
    lane = lax.broadcasted_iota(jnp.int32, rows.shape, 1)
    return jnp.where(lane // HEAD_DIM == head, rows, jnp.zeros_like(rows))


def causal(scores):
    key = lax.broadcasted_iota(jnp.int32, scores.shape, 0)
    query = lax.broadcasted_iota(jnp.int32, scores.shape, 1)
    return jnp.where(key <= query, scores, NEGATIVE_FILL)


def family_rows(leaves_ref, branch):
    def start(segment):
        return pl.multiple_of(TRUNK + (segment - 1) * SEG, SEG)

    return [start(branch + 1), start(leaves_ref[2 * branch]), start(leaves_ref[2 * branch + 1])]


def transpose_into(target_ref, source_ref, part):
    for first in range(0, TREE_LEN, 512):
        piece = source_ref[part, pl.ds(first, 512), :].astype(F32)
        target_ref[:, pl.ds(first, 512)] = piece.T.astype(BF16)


def widen(piece, first, width, fill):
    parts = []
    if first:
        parts.append(jnp.full((piece.shape[0], first), fill, piece.dtype))
    parts.append(piece)
    rest = width - first - piece.shape[1]
    if rest:
        parts.append(jnp.full((piece.shape[0], rest), fill, piece.dtype))
    return parts[0] if len(parts) == 1 else jnp.concatenate(parts, axis=1)


def trunk_groups(block):
    first = block * QROWS
    groups = [(0, first, 0, QROWS, None)] if first else []
    return groups + [(first, QROWS, 0, QROWS, "causal")]


def family_groups(starts):
    return [
        (0, TRUNK, 0, FAMILY, None),
        (starts[0], SEG, 0, FAMILY, "branch"),
        (starts[1], SEG, SEG, 2 * SEG, "causal"),
        (starts[2], SEG, 2 * SEG, FAMILY, "causal"),
    ]


def masked_scores(keys, queries, rule):
    scores = dot_nt(keys, queries)
    if rule == "causal":
        return causal(scores)
    if rule == "branch":
        return jnp.concatenate([causal(scores[:, :SEG]), scores[:, SEG:]], axis=1)
    return scores


def forward_block(qkv_ref, values_t_ref, queries, groups):
    width = queries.shape[0]
    outs, logs = [], []
    for head in range(2):
        own = head_lanes(queries, head)
        all_scores = [
            masked_scores(qkv_ref[1, pl.ds(start, size), :], own[first:last], rule)
            for start, size, first, last, rule in groups
        ]
        top = functools.reduce(
            jnp.maximum,
            [
                widen(jnp.max(s, axis=0, keepdims=True), first, width, NEGATIVE_FILL)
                for s, (_, _, first, last, _) in zip(all_scores, groups)
            ],
        )
        total, output = None, None
        for s, (start, size, first, last, _) in zip(all_scores, groups):
            weights = jnp.exp(s - top[:, first:last])
            part = widen(jnp.sum(weights, axis=0, keepdims=True), first, width, 0.0)
            values_t = values_t_ref[pl.ds(head * HEAD_DIM, HEAD_DIM), pl.ds(start, size)]
            mixed = widen(dot_nn(values_t, weights.astype(BF16)), first, width, 0.0)
            total = part if total is None else total + part
            output = mixed if output is None else output + mixed
        outs.append(output / total)
        logs.append(top + jnp.log(total))
    return jnp.concatenate(outs, axis=0).T.astype(BF16), jnp.concatenate(logs, axis=0)


def scaled_queries(qkv_ref, starts, size):
    rows = [qkv_ref[0, pl.ds(start, size), :] for start in starts]
    rows = rows[0] if len(rows) == 1 else jnp.concatenate(rows, axis=0)
    return rows * jnp.asarray(HEAD_DIM ** (-0.5), BF16)


def quarter_rows(leaves_ref, offset):
    quarter = TREE_LEN // 4
    return pl.ds(pl.multiple_of((leaves_ref[2 * BRANCHES] ^ offset) * quarter, quarter), quarter)


def forward_kernel(
    leaves_ref,
    near_ref,
    far_ref,
    near_out_ref,
    far_out_ref,
    trunk_log_ref,
    family_log_ref,
    qkv_ref,
    out_ref,
    values_t_ref,
):
    for offset in range(4):
        half_ref = near_ref if offset < 2 else far_ref
        qkv_ref[:, quarter_rows(leaves_ref, offset), :] = half_ref[:, offset % 2]
    transpose_into(values_t_ref, qkv_ref, 2)
    for block in range(TRUNK // QROWS):
        first = block * QROWS
        queries = scaled_queries(qkv_ref, [first], QROWS)
        out, logs = forward_block(qkv_ref, values_t_ref, queries, trunk_groups(block))
        out_ref[pl.ds(first, QROWS), :] = out
        trunk_log_ref[0, :, pl.ds(first, QROWS)] = logs

    def one_family(branch, carry):
        starts = family_rows(leaves_ref, branch)
        queries = scaled_queries(qkv_ref, starts, SEG)
        out, logs = forward_block(qkv_ref, values_t_ref, queries, family_groups(starts))
        for place, start in enumerate(starts):
            out_ref[pl.ds(start, SEG), :] = out[place * SEG : (place + 1) * SEG]
        family_log_ref[0, branch] = logs
        return carry

    lax.fori_loop(0, BRANCHES, one_family, 0)
    for offset in range(4):
        half_ref = near_out_ref if offset < 2 else far_out_ref
        half_ref[offset % 2] = out_ref[quarter_rows(leaves_ref, offset), :]


def halves_spec(parts):
    quarter = TREE_LEN // 4
    if parts == 1:
        return pl.BlockSpec((2, quarter, PAIR), lambda p, leaves: (0, 0, p))
    return pl.BlockSpec((parts, 2, quarter, PAIR), lambda p, leaves: (0, 0, 0, p))


def attention_cost(products, cover):
    visited = (TRUNK * (TRUNK + QROWS) // 2 + BRANCHES * FAMILY * (TRUNK + SEG)) // cover
    return pl.CostEstimate(
        flops=2 * products * 4 * visited * 2 * PAIR,
        transcendentals=4 * visited,
        bytes_accessed=8 * TREE_LEN * 4 * HEAD_DIM * 2 // cover,
    )


def attention_forward(leaves, near, far):
    width = near.shape[3]
    quarter = TREE_LEN // 4
    pairs = width // PAIR
    return pl.pallas_call(
        forward_kernel,
        grid_spec=pltpu.PrefetchScalarGridSpec(
            num_scalar_prefetch=1,
            grid=(pairs,),
            in_specs=[halves_spec(3), halves_spec(3)],
            out_specs=[
                halves_spec(1),
                halves_spec(1),
                pl.BlockSpec((1, 2, TRUNK), lambda p, leaves: (p, 0, 0)),
                pl.BlockSpec((1, BRANCHES, 2, FAMILY), lambda p, leaves: (p, 0, 0, 0)),
            ],
            scratch_shapes=[
                pltpu.VMEM((3, TREE_LEN, PAIR), BF16),
                pltpu.VMEM((TREE_LEN, PAIR), BF16),
                pltpu.VMEM((PAIR, TREE_LEN), BF16),
            ],
        ),
        out_shape=[
            jax.ShapeDtypeStruct((2, quarter, width), BF16),
            jax.ShapeDtypeStruct((2, quarter, width), BF16),
            jax.ShapeDtypeStruct((pairs, 2, TRUNK), F32),
            jax.ShapeDtypeStruct((pairs, BRANCHES, 2, FAMILY), F32),
        ],
        cost_estimate=attention_cost(2, COVER),
        name="tree_attention",
    )(leaves, near, far)


def backward_block(qkv_ref, keys_t_ref, queries, grads, outs, logs, groups):
    products = grads.astype(F32) * outs.astype(F32)
    products_t = products.T
    key_ds = [[] for _ in groups]
    value_ws = [[] for _ in groups]
    own_q, own_g, query_grads = [], [], []
    for head in range(2):
        own = head_lanes(queries, head)
        own_grads = head_lanes(grads, head)
        own_q.append(own)
        own_g.append(own_grads)
        inner = jnp.sum(
            products_t[head * HEAD_DIM : (head + 1) * HEAD_DIM], axis=0, keepdims=True
        )
        log = logs[head : head + 1]
        query_grad = None
        for place, (start, size, first, last, rule) in enumerate(groups):
            scores = masked_scores(qkv_ref[1, pl.ds(start, size), :], own[first:last], rule)
            weights = jnp.exp(scores - log[:, first:last])
            grad_weights = dot_nt(qkv_ref[2, pl.ds(start, size), :], own_grads[first:last])
            grad_scores = (weights * (grad_weights - inner[:, first:last])).astype(BF16)
            keys_t = keys_t_ref[pl.ds(head * HEAD_DIM, HEAD_DIM), pl.ds(start, size)]
            part = widen(dot_nn(keys_t, grad_scores), first, queries.shape[0], 0.0)
            query_grad = part if query_grad is None else query_grad + part
            key_ds[place].append(grad_scores)
            value_ws[place].append(weights.astype(BF16))
        query_grads.append(query_grad)
    grad_query = (jnp.concatenate(query_grads, axis=0) * HEAD_DIM ** (-0.5)).T.astype(BF16)
    key_grads, value_grads = [], []
    for place, (start, size, first, last, rule) in enumerate(groups):
        stacked_q = jnp.concatenate([own_q[0][first:last], own_q[1][first:last]], axis=0)
        stacked_g = jnp.concatenate([own_g[0][first:last], own_g[1][first:last]], axis=0)
        key_grads.append(dot_nn(jnp.concatenate(key_ds[place], axis=1), stacked_q))
        value_grads.append(dot_nn(jnp.concatenate(value_ws[place], axis=1), stacked_g))
    return grad_query, key_grads, value_grads


def backward_kernel(
    leaves_ref,
    near_ref,
    far_ref,
    near_grads_ref,
    far_grads_ref,
    near_outs_ref,
    far_outs_ref,
    trunk_log_ref,
    family_log_ref,
    near_result_ref,
    far_result_ref,
    qkv_ref,
    grads_ref,
    outs_ref,
    result_ref,
    keys_t_ref,
    trunk_keys_ref,
    trunk_values_ref,
):
    for offset in range(4):
        rows = quarter_rows(leaves_ref, offset)
        at = offset % 2
        qkv_ref[:, rows, :] = (near_ref if offset < 2 else far_ref)[:, at]
        grads_ref[rows, :] = (near_grads_ref if offset < 2 else far_grads_ref)[at]
        outs_ref[rows, :] = (near_outs_ref if offset < 2 else far_outs_ref)[at]
    transpose_into(keys_t_ref, qkv_ref, 1)
    trunk_keys_ref[...] = jnp.zeros_like(trunk_keys_ref)
    trunk_values_ref[...] = jnp.zeros_like(trunk_values_ref)
    for block in range(TRUNK // QROWS):
        first = block * QROWS
        rows = pl.ds(first, QROWS)
        groups = trunk_groups(block)
        grad_query, key_grads, value_grads = backward_block(
            qkv_ref,
            keys_t_ref,
            scaled_queries(qkv_ref, [first], QROWS),
            grads_ref[rows, :],
            outs_ref[rows, :],
            trunk_log_ref[0, :, rows],
            groups,
        )
        result_ref[0, rows, :] = grad_query
        for (start, size, _, _, _), key_grad, value_grad in zip(groups, key_grads, value_grads):
            trunk_keys_ref[pl.ds(start, size), :] += key_grad
            trunk_values_ref[pl.ds(start, size), :] += value_grad

    def one_family(branch, carry):
        starts = family_rows(leaves_ref, branch)
        groups = family_groups(starts)
        grad_query, key_grads, value_grads = backward_block(
            qkv_ref,
            keys_t_ref,
            scaled_queries(qkv_ref, starts, SEG),
            jnp.concatenate([grads_ref[pl.ds(start, SEG), :] for start in starts], axis=0),
            jnp.concatenate([outs_ref[pl.ds(start, SEG), :] for start in starts], axis=0),
            family_log_ref[0, branch],
            groups,
        )
        trunk_keys_ref[...] += key_grads[0]
        trunk_values_ref[...] += value_grads[0]
        for place, start in enumerate(starts):
            rows = pl.ds(start, SEG)
            result_ref[0, rows, :] = grad_query[place * SEG : (place + 1) * SEG]
            result_ref[1, rows, :] = key_grads[1 + place].astype(BF16)
            result_ref[2, rows, :] = value_grads[1 + place].astype(BF16)
        return carry

    lax.fori_loop(0, BRANCHES, one_family, 0)
    result_ref[1, pl.ds(0, TRUNK), :] = trunk_keys_ref[...].astype(BF16)
    result_ref[2, pl.ds(0, TRUNK), :] = trunk_values_ref[...].astype(BF16)
    for offset in range(4):
        half_ref = near_result_ref if offset < 2 else far_result_ref
        half_ref[:, offset % 2] = result_ref[:, quarter_rows(leaves_ref, offset), :]


def attention_backward(leaves, near, far, near_grads, far_grads, near_outs, far_outs, logs):
    pairs = near.shape[3] // PAIR
    return pl.pallas_call(
        backward_kernel,
        grid_spec=pltpu.PrefetchScalarGridSpec(
            num_scalar_prefetch=1,
            grid=(pairs,),
            in_specs=[
                halves_spec(3),
                halves_spec(3),
                halves_spec(1),
                halves_spec(1),
                halves_spec(1),
                halves_spec(1),
                pl.BlockSpec((1, 2, TRUNK), lambda p, leaves: (p, 0, 0)),
                pl.BlockSpec((1, BRANCHES, 2, FAMILY), lambda p, leaves: (p, 0, 0, 0)),
            ],
            out_specs=[halves_spec(3), halves_spec(3)],
            scratch_shapes=[
                pltpu.VMEM((3, TREE_LEN, PAIR), BF16),
                pltpu.VMEM((TREE_LEN, PAIR), BF16),
                pltpu.VMEM((TREE_LEN, PAIR), BF16),
                pltpu.VMEM((3, TREE_LEN, PAIR), BF16),
                pltpu.VMEM((PAIR, TREE_LEN), BF16),
                pltpu.VMEM((TRUNK, PAIR), F32),
                pltpu.VMEM((TRUNK, PAIR), F32),
            ],
        ),
        out_shape=[jax.ShapeDtypeStruct(near.shape, BF16), jax.ShapeDtypeStruct(far.shape, BF16)],
        cost_estimate=attention_cost(5, 5),
        name="tree_attention_back",
    )(leaves, near, far, near_grads, far_grads, near_outs, far_outs, *logs)


def leaf_order(parents_row):
    first_leaf = BRANCHES + 1
    leaf_parents = parents_row[first_leaf:]
    segments = first_leaf + jnp.arange(leaf_parents.shape[0], dtype=jnp.int32)
    same = leaf_parents[:, None] == leaf_parents[None, :]
    later = segments[None, :] < segments[:, None]
    place = 2 * (leaf_parents - 1) + jnp.sum(jnp.where(same & later, 1, 0), axis=1)
    slots = jnp.arange(2 * BRANCHES, dtype=jnp.int32)
    return jnp.sum(jnp.where(slots[:, None] == place[None, :], segments[None, :], 0), axis=1)


def gates(logits, experts, expert):
    lane = lax.broadcasted_iota(jnp.int32, logits.shape, 1)
    first, second = logits[:, experts : experts + 1], logits[:, experts + 1 : experts + 2]
    top = jnp.maximum(first, second)
    first, second = jnp.exp(first - top), jnp.exp(second - top)
    total = first + second
    first, second = first / total, second / total
    if expert is None:
        return lane, first, second, None, None
    routed = jnp.where(lane < experts, logits, NEGATIVE_FILL)
    raised = jnp.exp(routed - jnp.max(routed, axis=1, keepdims=True))
    probs = raised / jnp.sum(raised, axis=1, keepdims=True)
    gate = jnp.sum(jnp.where(lane == expert, probs, 0.0), axis=1, keepdims=True)
    return lane, first, second, probs, gate


def both(own_ref, side_ref):
    return jnp.concatenate([own_ref[...], side_ref[...]], axis=0)


def split_store(own_ref, side_ref, rows):
    half = rows.shape[0] // 2
    own_ref[...] = rows[:half]
    side_ref[...] = rows[half:]


def feed_kernel(
    experts,
    routed,
    expert_ref,
    own_ref,
    side_ref,
    own_grads_ref,
    side_grads_ref,
    head_ref,
    up_ref,
    down_ref,
    own_out_ref,
    side_out_ref,
    own_back_ref,
    side_back_ref,
    active_ref,
    pre_ref,
    grad_ref,
    head_grad_ref,
):
    rows = both(own_ref, side_ref)
    grads = both(own_grads_ref, side_grads_ref).astype(F32)
    expert = expert_ref[0] if routed else None
    logits = dot_nn(rows, head_ref[...])
    lane, first, second, probs, gate = gates(logits, experts, expert)
    coef = second * gate if routed else first
    weighted = (coef * grads).astype(BF16)
    pre = dot_nn(rows, up_ref[...])
    grad_active = dot_nt(weighted, down_ref[...])
    cumulative = 0.5 + 0.5 * lax.erf(pre * 0.7071067811865476)
    slope = cumulative + pre * jnp.exp(-0.5 * pre * pre) * 0.3989422804014327
    active = (pre * cumulative).astype(BF16)
    grad_pre = (grad_active * slope).astype(BF16)
    half = rows.shape[0] // 2
    for ref, value in ((active_ref, active), (pre_ref, grad_pre), (grad_ref, weighted)):
        ref[0] = value[:half]
        ref[1] = value[half:]
    out = dot_nn(active, down_ref[...])
    split_store(own_out_ref, side_out_ref, (coef * out).astype(BF16))
    inner = jnp.sum(grads * out, axis=1, keepdims=True)
    swing = first * second * inner
    if routed:
        swing = -gate * swing
    grad_logits = jnp.where(lane == experts, swing, jnp.where(lane == experts + 1, -swing, 0.0))
    if routed:
        picked = jnp.where(lane == expert, 1.0, 0.0) - gate
        grad_logits = grad_logits + jnp.where(
            lane < experts, probs * picked * (second * inner), 0.0
        )
    back = dot_nt(grad_pre, up_ref[...]) + dot_nt(grad_logits.astype(BF16), head_ref[...])
    split_store(own_back_ref, side_back_ref, back.astype(BF16))
    head_grad = dot_nn(grad_logits.T.astype(BF16), rows)

    @pl.when(pl.program_id(0) == 0)
    def _():
        head_grad_ref[...] = jnp.zeros_like(head_grad_ref)

    head_grad_ref[...] += head_grad


def feed(own, side, own_grads, side_grads, head, up, down, experts, expert, size):
    count = own.shape[0]
    width, hidden = up.shape
    steps = count // size
    lanes = head.shape[1]
    routed = expert is not None
    pick = jnp.reshape(expert, (1,)) if routed else jnp.zeros((1,), jnp.int32)
    rows = pl.BlockSpec((size, width), lambda i, pick: (i, 0))

    def whole(shape):
        return pl.BlockSpec(shape, lambda i, pick: (0, 0), pipeline_mode=pl.Buffered(1))

    def pairs(columns):
        return pl.BlockSpec((2, size, columns), lambda i, pick: (0, i, 0))

    quarter = jax.ShapeDtypeStruct((count, width), BF16)
    *sums, active, pre, weighted, head_grad = pl.pallas_call(
        functools.partial(feed_kernel, experts, routed),
        grid_spec=pltpu.PrefetchScalarGridSpec(
            num_scalar_prefetch=1,
            grid=(steps,),
            in_specs=[
                rows,
                rows,
                rows,
                rows,
                whole((width, lanes)),
                whole((width, hidden)),
                whole((hidden, width)),
            ],
            out_specs=[
                rows,
                rows,
                rows,
                rows,
                pairs(hidden),
                pairs(hidden),
                pairs(width),
                pl.BlockSpec((lanes, width), lambda i, pick: (0, 0)),
            ],
        ),
        out_shape=[
            quarter,
            quarter,
            quarter,
            quarter,
            jax.ShapeDtypeStruct((2, count, hidden), BF16),
            jax.ShapeDtypeStruct((2, count, hidden), BF16),
            jax.ShapeDtypeStruct((2, count, width), BF16),
            jax.ShapeDtypeStruct((lanes, width), F32),
        ],
        cost_estimate=pl.CostEstimate(
            flops=16 * count * width * hidden // COVER,
            transcendentals=4 * count * hidden // COVER,
            bytes_accessed=2 * (8 * count * width + 4 * count * hidden + 2 * width * hidden) // COVER,
        ),
        compiler_params=pltpu.CompilerParams(vmem_limit_bytes=60 * 1024 * 1024),
        name="feed_routed" if routed else "feed_dense",
    )(pick, own, side, own_grads, side_grads, head, up, down)
    flat = [value.reshape(2 * count, value.shape[2]) for value in (active, pre, weighted)]
    return [*sums, *flat, head_grad]


LANES = 128
QUARTER_ROWS = 128


def norm_parts(values):
    row_mean = jnp.mean(values, axis=-1, keepdims=True)
    centred = values - row_mean
    row_var = jnp.mean(centred * centred, axis=-1, keepdims=True)
    inverse = lax.rsqrt(row_var + EPSILON)
    return (centred * inverse, inverse)


def norm_back(grad_normed, gain_vec, scaled, inverse):
    grad_scaled = grad_normed * gain_vec
    first_mean = jnp.mean(grad_scaled, axis=-1, keepdims=True)
    second = jnp.mean(grad_scaled * scaled, axis=-1, keepdims=True)
    return inverse * (grad_scaled - first_mean - scaled * second)


def after(value, *others):
    return lax.optimization_barrier((value, *others))[0]


def from_side(values):
    return lax.ppermute(values, "tensor", [(i, i ^ 1) for i in range(4)])


def from_far(values):
    return lax.ppermute(values, "tensor", [(i, i ^ 2) for i in range(4)])


def plus_side(own, side):
    return own.astype(F32) + from_side(side.astype(BF16)).astype(F32)


def sum_over(values, axis):
    count, step = lax.axis_size(axis), 1
    while step < count:
        pairs = [(i, i ^ step) for i in range(count)]
        values = values + lax.ppermute(values, axis, pairs)
        step *= 2
    return values


def exchange(blocks):
    return lax.all_to_all(blocks, "expert", split_axis=0, concat_axis=0, tiled=True)


def scatter_sum(strips):
    strips = with_layout_constraint(strips.astype(BF16), Layout(major_to_minor=(0, 1)))
    return lax.psum_scatter(strips, "expert", scatter_dimension=0, tiled=True)


def strips_sent(grads):
    return exchange(grads.reshape(lax.axis_size("expert"), -1, grads.shape[1]))


def strips_total(strips):
    return jnp.sum(strips.astype(F32), axis=0)


def slots_of(expert_ids, experts, capacity):
    rows = expert_ids.shape[0]
    chosen = expert_ids[:, None] == jnp.arange(experts, dtype=jnp.int32)[None, :]
    at = jnp.arange(rows, dtype=jnp.int32)
    before = (at[None, :] < at[:, None]).astype(BF16)
    earlier = jnp.dot(before, chosen.astype(BF16), preferred_element_type=F32)
    slot = jnp.sum(jnp.where(chosen, earlier, 0.0), axis=1).astype(jnp.int32)
    place = expert_ids * capacity + slot
    places = jnp.arange(experts * capacity, dtype=jnp.int32)
    return (places[:, None] == place[None, :]).astype(BF16)


def per_device(
    tokens,
    cotangent,
    routes,
    parents,
    ln_attn,
    w_qkv,
    w_out,
    ln_mlp,
    w_up,
    w_down,
    w_router,
    w_mix,
    ex_up,
    ex_down,
):
    tok_dev, width = tokens.shape
    mine = lax.axis_index("tensor")
    experts = w_router.shape[1]
    capacity = max(2, tok_dev * 7 // (5 * experts))
    heads_width = w_qkv.shape[2]
    hidden = w_up.shape[1]
    leaves = jnp.concatenate([leaf_order(parents[0]), mine.astype(jnp.int32)[None]])

    scaled_one, inverse_one = norm_parts(tokens.astype(F32))
    normed_own = (scaled_one * ln_attn).astype(BF16)
    normed_far = from_far(normed_own)
    near_one = jnp.concatenate([normed_own, from_side(normed_own)], axis=0)

    quarter_ids = routes[:, 0].reshape(4, tok_dev)

    def slots_at(offset):
        ids = lax.dynamic_index_in_dim(quarter_ids, mine ^ offset, 0, keepdims=False)
        return slots_of(ids, experts, capacity)

    own_slots, far_slots = slots_at(0), slots_at(2)

    def placed(slots, rows):
        return jnp.dot(slots, rows, preferred_element_type=F32).astype(BF16)

    def sent(rows):
        return exchange(rows.reshape(experts, capacity, width)).reshape(-1, width)

    own_grads = sent(placed(own_slots, cotangent))
    cotangent_side = from_side(cotangent)

    def project(rows):
        qkv = jnp.einsum("td,sdc->stc", rows, w_qkv, preferred_element_type=F32)
        return qkv.astype(BF16).reshape(3, 2, tok_dev, heads_width)

    lanes = -(-(experts + 2) // LANES) * LANES
    head = jnp.concatenate(
        [w_router, w_mix, jnp.zeros((width, lanes - experts - 2), BF16)], axis=1
    )
    near_qkv = project(near_one)
    cotangent_far = from_far(after(cotangent, normed_far))
    normed_far, near_qkv, head = lax.optimization_barrier((normed_far, near_qkv, head))
    far_one = jnp.concatenate([normed_far, from_side(normed_far)], axis=0)
    far_qkv = project(far_one)
    near_out, far_out, *logs = attention_forward(leaves, near_qkv, far_qkv)
    far_out, own_grads, cotangent_far, cotangent_side = lax.optimization_barrier(
        (far_out, own_grads, cotangent_far, cotangent_side)
    )

    def branch_part(rows):
        return jnp.dot(rows, w_out, preferred_element_type=F32)

    far_sum = plus_side(branch_part(far_out[0]), branch_part(far_out[1])).astype(BF16)
    branch = plus_side(branch_part(near_out[0]), branch_part(near_out[1]))
    branch_far = from_far(far_sum)
    side_grads = from_side(own_grads)
    cotangent_corner = from_side(cotangent_far)
    far_placed = placed(far_slots, cotangent_far)
    branch_far, side_grads, cotangent_corner, far_placed = lax.optimization_barrier(
        (branch_far, side_grads, cotangent_corner, far_placed)
    )
    residual = tokens.astype(F32) + (branch + branch_far.astype(F32))

    scaled_two, inverse_two = norm_parts(residual)
    normed_two = (scaled_two * ln_mlp).astype(BF16)
    normed_two_far = from_far(normed_two)
    normed_two_side = from_side(normed_two)
    own_rows = sent(placed(own_slots, normed_two))

    def dense(own, side, own_cotangent, side_cotangent):
        return feed(
            own, side, own_cotangent, side_cotangent, head, w_up, w_down, experts, None, QUARTER_ROWS
        )

    def product(left, right):
        return jnp.einsum("gd,gf->df", left, right, preferred_element_type=F32)

    def weight_grads(near_left, far_left, near_right, far_right):
        return product(near_left, near_right) + product(far_left, far_right)

    near_dense = dense(normed_two, normed_two_side, cotangent, cotangent_side)
    near_two = jnp.concatenate([normed_two, normed_two_side], axis=0)
    grad_up = product(near_two, near_dense[5])
    grad_down = product(near_dense[6], near_dense[4])
    normed_two_far, grad_up, grad_down, own_rows = lax.optimization_barrier(
        (normed_two_far, grad_up, grad_down, own_rows)
    )
    far_rows = from_far(own_rows)
    far_grads = sent(after(far_placed, own_rows))
    normed_two_corner = from_side(normed_two_far)
    far_dense = list(dense(normed_two_far, normed_two_corner, cotangent_far, cotangent_corner))

    expert = lax.axis_index("expert").astype(jnp.int32)

    def routed(own, side, own_cotangent, side_cotangent):
        return feed(
            own,
            side,
            own_cotangent,
            side_cotangent,
            head,
            ex_up[0],
            ex_down[0],
            experts,
            expert,
            QUARTER_ROWS,
        )

    def chip_sum(parts, place, *others):
        return plus_side(parts[place], after(parts[place + 1], *others))

    def chip_sum(parts, place, *others):
        return plus_side(parts[place], after(parts[place + 1], *others))

    dense_back_far = chip_sum(far_dense, 2).astype(BF16)
    far_two = jnp.concatenate([normed_two_far, normed_two_corner], axis=0)
    grad_down = (grad_down + product(far_dense[6], far_dense[4])).astype(BF16)
    far_two, far_rows, grad_down = lax.optimization_barrier((far_two, far_rows, grad_down))
    grad_up = (grad_up + product(far_two, far_dense[5])).astype(BF16)
    dense_grads = after(jnp.concatenate([grad_up, grad_down], axis=1), far_grads)
    far_rows, dense_back_far, dense_grads = lax.optimization_barrier(
        (far_rows, dense_back_far, dense_grads)
    )
    dense_grads = scatter_sum(dense_grads)
    dense_back_far = from_far(dense_back_far)
    corner_rows = from_side(far_rows)
    side_rows = from_side(own_rows)
    far_expert = routed(far_rows, corner_rows, far_grads, from_side(far_grads))
    *far_expert, dense_back_far = lax.optimization_barrier((*far_expert, dense_back_far))
    far_back = chip_sum(far_expert, 2).astype(BF16)
    own_rows, far_back = lax.optimization_barrier((own_rows, far_back))
    near_expert = routed(own_rows, side_rows, own_grads, side_grads)
    *near_expert, dense_grads = lax.optimization_barrier((*near_expert, dense_grads))

    def picked(rows):
        return lax.dot_general(
            own_slots, rows, (((0,), (0,)), ((), ())), preferred_element_type=F32
        )

    expert_back = (chip_sum(near_expert, 2) + from_far(far_back).astype(F32)).astype(BF16)
    far_expert_out = chip_sum(far_expert, 0, expert_back).astype(BF16)
    dense_out_far = chip_sum(far_dense, 0, expert_back).astype(BF16)
    dense_back = chip_sum(near_dense, 2, far_back) + dense_back_far.astype(F32)

    grad_normed_two = dense_back + picked(sent(expert_back))
    dense_out = chip_sum(near_dense, 0, expert_back)
    expert_out = chip_sum(near_expert, 0, expert_back) + from_far(far_expert_out).astype(F32)
    expert_out = after(expert_out.astype(BF16), grad_normed_two)

    near_active, far_active, near_pre, far_pre, far_expert_out = lax.optimization_barrier(
        (near_expert[4], far_expert[4], near_expert[5], far_expert[5], far_expert_out)
    )
    near_tokens = jnp.concatenate([own_rows, side_rows], axis=0)
    far_tokens = jnp.concatenate([far_rows, corner_rows], axis=0)
    grad_ex_up = weight_grads(near_tokens, far_tokens, near_pre, far_pre)[None]
    grad_ex_down = weight_grads(near_active, far_active, near_expert[6], far_expert[6])[None]

    gain_two = jnp.sum(grad_normed_two * scaled_two, axis=0)
    grad_residual = cotangent.astype(F32) + norm_back(
        grad_normed_two, ln_mlp, scaled_two, inverse_two
    )
    grad_branch = grad_residual.astype(BF16)
    grad_branch_far = from_far(grad_branch)
    grad_branch_side = from_side(grad_branch)

    def into_heads(*rows):
        grads = [jnp.einsum("gd,cd->gc", part, w_out, preferred_element_type=F32) for part in rows]
        return jnp.stack(grads).astype(BF16)

    near_heads = into_heads(grad_branch, grad_branch_side)
    out_rows = sent(expert_out)
    flat = (2 * tok_dev, heads_width)
    near_branch = jnp.concatenate([grad_branch, grad_branch_side], axis=0)
    grad_w_out = product(near_branch, near_out.reshape(flat))
    grad_branch_far, near_heads, grad_w_out, grad_ex_up, grad_ex_down, _, dense_out_far, dense_out = (
        lax.optimization_barrier(
            (
                grad_branch_far,
                near_heads,
                grad_w_out,
                grad_ex_up,
                grad_ex_down,
                expert_out,
                dense_out_far,
                dense_out,
            )
        )
    )
    grad_branch_corner = from_side(grad_branch_far)
    far_heads = into_heads(grad_branch_far, grad_branch_corner)
    dense_out_far = from_far(dense_out_far)
    head_grads = near_dense[7] + far_dense[7] + near_expert[7] + far_expert[7]
    small = jnp.concatenate([head_grads[: experts + 2], gain_two[None]], axis=0)
    near_result, far_result = attention_backward(
        leaves, near_qkv, far_qkv, near_heads, far_heads, near_out, far_out, logs
    )
    near_result, far_result, out_rows, dense_out_far, small = lax.optimization_barrier(
        (near_result, far_result, out_rows, dense_out_far, small)
    )
    small = sum_over(small, "tensor")

    def normed_part(grads):
        return jnp.einsum("sgc,sdc->gd", grads, w_qkv, preferred_element_type=F32)

    corner_part = normed_part(far_result[:, 1]).astype(BF16)
    from_corner = from_side(corner_part).astype(F32)

    far_branch = jnp.concatenate([grad_branch_far, grad_branch_corner], axis=0)
    grad_w_out = grad_w_out + product(after(far_branch, corner_part), far_out.reshape(flat))
    small_columns = -(-small.shape[0] // LANES) * LANES
    small_block = jnp.pad(small, ((0, small_columns - small.shape[0]), (0, 0))).T
    branch_grads = jnp.concatenate([grad_w_out.astype(BF16), small_block.astype(BF16)], axis=1)
    far_result, branch_grads = lax.optimization_barrier((far_result, branch_grads))
    branch_grads = strips_total(strips_sent(branch_grads))
    far_sum = (normed_part(far_result[:, 0]) + from_corner).astype(BF16)
    near_result, far_result, out_rows, far_sum = lax.optimization_barrier(
        (near_result, far_result, out_rows, far_sum)
    )
    near_sum = plus_side(normed_part(near_result[:, 0]), normed_part(near_result[:, 1]))
    out = (residual + dense_out + dense_out_far.astype(F32) + picked(out_rows)).astype(BF16)

    near_result = near_result.reshape(3, *flat)
    far_result = far_result.reshape(3, *flat)
    scaled_far = normed_far.astype(F32) / ln_attn
    gain_one = jnp.sum(
        near_sum * scaled_one + far_sum.astype(F32) * scaled_far, axis=0, keepdims=True
    )
    gain_one = sum_over(gain_one, "expert")
    near_result = after(near_result, gain_one)
    qkv_grads = strips_total(strips_sent(
        jnp.concatenate(
            [
                weight_grads(near_one, far_one, near_result[part], far_result[part]).astype(BF16)
                for part in range(3)
            ],
            axis=1,
        )
    ))
    grad_normed_one = near_sum + after(from_far(far_sum), gain_one).astype(F32)
    grad_ln_attn = sum_over(gain_one, "tensor")[0]
    grad_tokens = grad_residual + norm_back(grad_normed_one, ln_attn, scaled_one, inverse_one)

    strip = qkv_grads.shape[0]
    return (
        out,
        grad_tokens,
        grad_ln_attn,
        qkv_grads.reshape(strip, 3, heads_width).transpose(1, 0, 2),
        branch_grads[:, :heads_width].T,
        branch_grads[:, heads_width + experts + 2],
        dense_grads[:, :hidden].astype(F32),
        dense_grads[:, hidden:].T.astype(F32),
        branch_grads[:, heads_width : heads_width + experts],
        branch_grads[:, heads_width + experts : heads_width + experts + 2],
        grad_ex_up,
        grad_ex_down,
    )


def solution(mesh):
    return jax.shard_map(
        per_device,
        mesh=mesh,
        in_specs=(
            P(("expert", "tensor"), None),
            P(("expert", "tensor"), None),
            P("expert", None),
            P("expert", None),
            P(),
            P(None, None, "tensor"),
            P("tensor", None),
            P(),
            P(None, "tensor"),
            P("tensor", None),
            P(),
            P(),
            P("expert", None, "tensor"),
            P("expert", "tensor", None),
        ),
        out_specs=(
            P(("expert", "tensor"), None),
            P(("expert", "tensor"), None),
            P(),
            P(None, "expert", "tensor"),
            P("tensor", "expert"),
            P("expert"),
            P("expert", "tensor"),
            P("tensor", "expert"),
            P("expert", None),
            P("expert", None),
            P("expert", None, "tensor"),
            P("expert", "tensor", None),
        ),
        check_vma=False,
    )
```

```python
import functools

import jax
import jax.numpy as jnp
from jax import lax
from jax.experimental import pallas as pl
from jax.experimental.layout import Layout, with_layout_constraint
from jax.experimental.pallas import tpu as pltpu
from jax.sharding import PartitionSpec as P

HEAD_DIM = 64
TRUNK = 1024
SEG = 128
SEGS = 13
TREE_LEN = 2560
BRANCHES = 4
FAMILY = 3 * SEG
TEAM = 2 * FAMILY
TEAMS = BRANCHES // 2
QROWS = 256
COVER = 8
PAIR = 2 * HEAD_DIM
NEGATIVE_FILL = -1e30
F32 = jnp.float32
BF16 = jnp.bfloat16
EPSILON = 1e-05


def dot_nn(a, b):
    return lax.dot_general(a, b, (((1,), (0,)), ((), ())), preferred_element_type=F32)


def dot_nt(a, b):
    return lax.dot_general(a, b, (((1,), (1,)), ((), ())), preferred_element_type=F32)


def head_lanes(rows, head):
    lane = lax.broadcasted_iota(jnp.int32, rows.shape, 1)
    return jnp.where(lane // HEAD_DIM == head, rows, jnp.zeros_like(rows))


def causal(scores):
    key = lax.broadcasted_iota(jnp.int32, scores.shape, 0)
    query = lax.broadcasted_iota(jnp.int32, scores.shape, 1)
    return jnp.where(key <= query, scores, NEGATIVE_FILL)


def family_rows(leaves_ref, branch):
    def start(segment):
        return pl.multiple_of(TRUNK + (segment - 1) * SEG, SEG)

    return [start(branch + 1), start(leaves_ref[2 * branch]), start(leaves_ref[2 * branch + 1])]


def transpose_into(target_ref, source_ref, part):
    for first in range(0, TREE_LEN, 512):
        piece = source_ref[part, pl.ds(first, 512), :].astype(F32)
        target_ref[:, pl.ds(first, 512)] = piece.T.astype(BF16)


def widen(piece, first, width, fill):
    parts = []
    if first:
        parts.append(jnp.full((piece.shape[0], first), fill, piece.dtype))
    parts.append(piece)
    rest = width - first - piece.shape[1]
    if rest:
        parts.append(jnp.full((piece.shape[0], rest), fill, piece.dtype))
    return parts[0] if len(parts) == 1 else jnp.concatenate(parts, axis=1)


def trunk_groups(block):
    first = block * QROWS
    groups = [(0, first, 0, QROWS, None)] if first else []
    return groups + [(first, QROWS, 0, QROWS, "causal")]


def team_rows(leaves_ref, team):
    return family_rows(leaves_ref, 2 * team) + family_rows(leaves_ref, 2 * team + 1)


def team_groups(starts):
    groups = [(0, TRUNK, 0, TEAM, None)]
    for first in range(0, TEAM, FAMILY):
        at = first // SEG
        groups.append((starts[at], SEG, first, first + FAMILY, "branch"))
        for leaf in (1, 2):
            begin = first + leaf * SEG
            groups.append((starts[at + leaf], SEG, begin, begin + SEG, "causal"))
    return groups


def masked_scores(keys, queries, rule):
    scores = dot_nt(keys, queries)
    if rule == "causal":
        return causal(scores)
    if rule == "branch":
        return jnp.concatenate([causal(scores[:, :SEG]), scores[:, SEG:]], axis=1)
    return scores


def forward_block(qkv_ref, values_t_ref, queries, groups):
    width = queries.shape[0]
    outs, logs = [], []
    for head in range(2):
        own = head_lanes(queries, head)
        all_scores = [
            masked_scores(qkv_ref[1, pl.ds(start, size), :], own[first:last], rule)
            for start, size, first, last, rule in groups
        ]
        top = functools.reduce(
            jnp.maximum,
            [
                widen(jnp.max(s, axis=0, keepdims=True), first, width, NEGATIVE_FILL)
                for s, (_, _, first, last, _) in zip(all_scores, groups)
            ],
        )
        total, output = None, None
        for s, (start, size, first, last, _) in zip(all_scores, groups):
            weights = jnp.exp(s - top[:, first:last])
            part = widen(jnp.sum(weights, axis=0, keepdims=True), first, width, 0.0)
            values_t = values_t_ref[pl.ds(head * HEAD_DIM, HEAD_DIM), pl.ds(start, size)]
            mixed = widen(dot_nn(values_t, weights.astype(BF16)), first, width, 0.0)
            total = part if total is None else total + part
            output = mixed if output is None else output + mixed
        outs.append(output / total)
        logs.append(top + jnp.log(total))
    return jnp.concatenate(outs, axis=0).T.astype(BF16), jnp.concatenate(logs, axis=0)


def scaled_queries(qkv_ref, starts, size):
    rows = [qkv_ref[0, pl.ds(start, size), :] for start in starts]
    rows = rows[0] if len(rows) == 1 else jnp.concatenate(rows, axis=0)
    return rows * jnp.asarray(HEAD_DIM ** (-0.5), BF16)


def quarter_rows(leaves_ref, offset):
    quarter = TREE_LEN // 4
    return pl.ds(pl.multiple_of((leaves_ref[2 * BRANCHES] ^ offset) * quarter, quarter), quarter)


def forward_kernel(
    leaves_ref,
    near_ref,
    far_ref,
    near_out_ref,
    far_out_ref,
    trunk_log_ref,
    family_log_ref,
    qkv_ref,
    out_ref,
    values_t_ref,
):
    for offset in range(4):
        half_ref = near_ref if offset < 2 else far_ref
        qkv_ref[:, quarter_rows(leaves_ref, offset), :] = half_ref[:, offset % 2]
    transpose_into(values_t_ref, qkv_ref, 2)
    for block in range(TRUNK // QROWS):
        first = block * QROWS
        queries = scaled_queries(qkv_ref, [first], QROWS)
        out, logs = forward_block(qkv_ref, values_t_ref, queries, trunk_groups(block))
        out_ref[pl.ds(first, QROWS), :] = out
        trunk_log_ref[0, :, pl.ds(first, QROWS)] = logs

    def one_team(team, carry):
        starts = team_rows(leaves_ref, team)
        queries = scaled_queries(qkv_ref, starts, SEG)
        out, logs = forward_block(qkv_ref, values_t_ref, queries, team_groups(starts))
        for place, start in enumerate(starts):
            out_ref[pl.ds(start, SEG), :] = out[place * SEG : (place + 1) * SEG]
        family_log_ref[0, team] = logs
        return carry

    lax.fori_loop(0, TEAMS, one_team, 0)
    for offset in range(4):
        half_ref = near_out_ref if offset < 2 else far_out_ref
        half_ref[offset % 2] = out_ref[quarter_rows(leaves_ref, offset), :]


def halves_spec(parts):
    quarter = TREE_LEN // 4
    if parts == 1:
        return pl.BlockSpec((2, quarter, PAIR), lambda p, leaves: (0, 0, p))
    return pl.BlockSpec((parts, 2, quarter, PAIR), lambda p, leaves: (0, 0, 0, p))


def attention_cost(products, cover):
    visited = (TRUNK * (TRUNK + QROWS) // 2 + BRANCHES * FAMILY * (TRUNK + SEG)) // cover
    return pl.CostEstimate(
        flops=2 * products * 4 * visited * 2 * PAIR,
        transcendentals=4 * visited,
        bytes_accessed=8 * TREE_LEN * 4 * HEAD_DIM * 2 // cover,
    )


def attention_forward(leaves, near, far):
    width = near.shape[3]
    quarter = TREE_LEN // 4
    pairs = width // PAIR
    return pl.pallas_call(
        forward_kernel,
        grid_spec=pltpu.PrefetchScalarGridSpec(
            num_scalar_prefetch=1,
            grid=(pairs,),
            in_specs=[halves_spec(3), halves_spec(3)],
            out_specs=[
                halves_spec(1),
                halves_spec(1),
                pl.BlockSpec((1, 2, TRUNK), lambda p, leaves: (p, 0, 0)),
                pl.BlockSpec((1, TEAMS, 2, TEAM), lambda p, leaves: (p, 0, 0, 0)),
            ],
            scratch_shapes=[
                pltpu.VMEM((3, TREE_LEN, PAIR), BF16),
                pltpu.VMEM((TREE_LEN, PAIR), BF16),
                pltpu.VMEM((PAIR, TREE_LEN), BF16),
            ],
        ),
        out_shape=[
            jax.ShapeDtypeStruct((2, quarter, width), BF16),
            jax.ShapeDtypeStruct((2, quarter, width), BF16),
            jax.ShapeDtypeStruct((pairs, 2, TRUNK), F32),
            jax.ShapeDtypeStruct((pairs, TEAMS, 2, TEAM), F32),
        ],
        cost_estimate=attention_cost(2, COVER),
        name="tree_attention",
    )(leaves, near, far)


def backward_block(qkv_ref, keys_t_ref, queries, grads, outs, logs, groups):
    products = grads.astype(F32) * outs.astype(F32)
    products_t = products.T
    key_ds = [[] for _ in groups]
    value_ws = [[] for _ in groups]
    own_q, own_g, query_grads = [], [], []
    for head in range(2):
        own = head_lanes(queries, head)
        own_grads = head_lanes(grads, head)
        own_q.append(own)
        own_g.append(own_grads)
        inner = jnp.sum(
            products_t[head * HEAD_DIM : (head + 1) * HEAD_DIM], axis=0, keepdims=True
        )
        log = logs[head : head + 1]
        query_grad = None
        for place, (start, size, first, last, rule) in enumerate(groups):
            scores = masked_scores(qkv_ref[1, pl.ds(start, size), :], own[first:last], rule)
            weights = jnp.exp(scores - log[:, first:last])
            grad_weights = dot_nt(qkv_ref[2, pl.ds(start, size), :], own_grads[first:last])
            grad_scores = (weights * (grad_weights - inner[:, first:last])).astype(BF16)
            keys_t = keys_t_ref[pl.ds(head * HEAD_DIM, HEAD_DIM), pl.ds(start, size)]
            part = widen(dot_nn(keys_t, grad_scores), first, queries.shape[0], 0.0)
            query_grad = part if query_grad is None else query_grad + part
            key_ds[place].append(grad_scores)
            value_ws[place].append(weights.astype(BF16))
        query_grads.append(query_grad)
    grad_query = (jnp.concatenate(query_grads, axis=0) * HEAD_DIM ** (-0.5)).T.astype(BF16)
    key_grads, value_grads = [], []
    for place, (start, size, first, last, rule) in enumerate(groups):
        stacked_q = jnp.concatenate([own_q[0][first:last], own_q[1][first:last]], axis=0)
        stacked_g = jnp.concatenate([own_g[0][first:last], own_g[1][first:last]], axis=0)
        key_grads.append(dot_nn(jnp.concatenate(key_ds[place], axis=1), stacked_q))
        value_grads.append(dot_nn(jnp.concatenate(value_ws[place], axis=1), stacked_g))
    return grad_query, key_grads, value_grads


def backward_kernel(
    leaves_ref,
    near_ref,
    far_ref,
    near_grads_ref,
    far_grads_ref,
    near_outs_ref,
    far_outs_ref,
    trunk_log_ref,
    family_log_ref,
    near_result_ref,
    far_result_ref,
    qkv_ref,
    grads_ref,
    outs_ref,
    result_ref,
    keys_t_ref,
    trunk_keys_ref,
    trunk_values_ref,
):
    for offset in range(4):
        rows = quarter_rows(leaves_ref, offset)
        at = offset % 2
        qkv_ref[:, rows, :] = (near_ref if offset < 2 else far_ref)[:, at]
        grads_ref[rows, :] = (near_grads_ref if offset < 2 else far_grads_ref)[at]
        outs_ref[rows, :] = (near_outs_ref if offset < 2 else far_outs_ref)[at]
    transpose_into(keys_t_ref, qkv_ref, 1)
    trunk_keys_ref[...] = jnp.zeros_like(trunk_keys_ref)
    trunk_values_ref[...] = jnp.zeros_like(trunk_values_ref)
    for block in range(TRUNK // QROWS):
        first = block * QROWS
        rows = pl.ds(first, QROWS)
        groups = trunk_groups(block)
        grad_query, key_grads, value_grads = backward_block(
            qkv_ref,
            keys_t_ref,
            scaled_queries(qkv_ref, [first], QROWS),
            grads_ref[rows, :],
            outs_ref[rows, :],
            trunk_log_ref[0, :, rows],
            groups,
        )
        result_ref[0, rows, :] = grad_query
        for (start, size, _, _, _), key_grad, value_grad in zip(groups, key_grads, value_grads):
            trunk_keys_ref[pl.ds(start, size), :] += key_grad
            trunk_values_ref[pl.ds(start, size), :] += value_grad

    def one_team(team, carry):
        starts = team_rows(leaves_ref, team)
        groups = team_groups(starts)
        grad_query, key_grads, value_grads = backward_block(
            qkv_ref,
            keys_t_ref,
            scaled_queries(qkv_ref, starts, SEG),
            jnp.concatenate([grads_ref[pl.ds(start, SEG), :] for start in starts], axis=0),
            jnp.concatenate([outs_ref[pl.ds(start, SEG), :] for start in starts], axis=0),
            family_log_ref[0, team],
            groups,
        )
        trunk_keys_ref[...] += key_grads[0]
        trunk_values_ref[...] += value_grads[0]
        for place, start in enumerate(starts):
            rows = pl.ds(start, SEG)
            result_ref[0, rows, :] = grad_query[place * SEG : (place + 1) * SEG]
            result_ref[1, rows, :] = key_grads[1 + place].astype(BF16)
            result_ref[2, rows, :] = value_grads[1 + place].astype(BF16)
        return carry

    lax.fori_loop(0, TEAMS, one_team, 0)
    result_ref[1, pl.ds(0, TRUNK), :] = trunk_keys_ref[...].astype(BF16)
    result_ref[2, pl.ds(0, TRUNK), :] = trunk_values_ref[...].astype(BF16)
    for offset in range(4):
        half_ref = near_result_ref if offset < 2 else far_result_ref
        rows = quarter_rows(leaves_ref, offset)
        for part in range(3):
            half_ref[offset % 2, :, part * PAIR : (part + 1) * PAIR] = result_ref[part, rows, :]


def attention_backward(leaves, pair, near, far, near_grads, far_grads, near_outs, far_outs, logs):
    quarter = TREE_LEN // 4
    rows = pl.BlockSpec((2, quarter, PAIR), lambda i, leaves: (0, 0, pair))
    parts = pl.BlockSpec((3, 2, quarter, PAIR), lambda i, leaves: (0, 0, 0, pair))
    result = pl.BlockSpec((2, quarter, 3 * PAIR), lambda i, leaves: (0, 0, 0))
    shape = jax.ShapeDtypeStruct((2, quarter, 3 * PAIR), BF16)
    return pl.pallas_call(
        backward_kernel,
        grid_spec=pltpu.PrefetchScalarGridSpec(
            num_scalar_prefetch=1,
            grid=(1,),
            in_specs=[
                parts,
                parts,
                rows,
                rows,
                rows,
                rows,
                pl.BlockSpec((1, 2, TRUNK), lambda i, leaves: (pair, 0, 0)),
                pl.BlockSpec((1, TEAMS, 2, TEAM), lambda i, leaves: (pair, 0, 0, 0)),
            ],
            out_specs=[result, result],
            scratch_shapes=[
                pltpu.VMEM((3, TREE_LEN, PAIR), BF16),
                pltpu.VMEM((TREE_LEN, PAIR), BF16),
                pltpu.VMEM((TREE_LEN, PAIR), BF16),
                pltpu.VMEM((3, TREE_LEN, PAIR), BF16),
                pltpu.VMEM((PAIR, TREE_LEN), BF16),
                pltpu.VMEM((TRUNK, PAIR), F32),
                pltpu.VMEM((TRUNK, PAIR), F32),
            ],
        ),
        out_shape=[shape, shape],
        cost_estimate=attention_cost(5, 10),
        name="tree_attention_back",
    )(leaves, near, far, near_grads, far_grads, near_outs, far_outs, *logs)


def leaf_order(parents_row):
    first_leaf = BRANCHES + 1
    leaf_parents = parents_row[first_leaf:]
    segments = first_leaf + jnp.arange(leaf_parents.shape[0], dtype=jnp.int32)
    same = leaf_parents[:, None] == leaf_parents[None, :]
    later = segments[None, :] < segments[:, None]
    place = 2 * (leaf_parents - 1) + jnp.sum(jnp.where(same & later, 1, 0), axis=1)
    slots = jnp.arange(2 * BRANCHES, dtype=jnp.int32)
    return jnp.sum(jnp.where(slots[:, None] == place[None, :], segments[None, :], 0), axis=1)


def gates(logits, experts, expert):
    lane = lax.broadcasted_iota(jnp.int32, logits.shape, 1)
    first, second = logits[:, experts : experts + 1], logits[:, experts + 1 : experts + 2]
    top = jnp.maximum(first, second)
    first, second = jnp.exp(first - top), jnp.exp(second - top)
    total = first + second
    first, second = first / total, second / total
    if expert is None:
        return lane, first, second, None, None
    routed = jnp.where(lane < experts, logits, NEGATIVE_FILL)
    raised = jnp.exp(routed - jnp.max(routed, axis=1, keepdims=True))
    probs = raised / jnp.sum(raised, axis=1, keepdims=True)
    gate = jnp.sum(jnp.where(lane == expert, probs, 0.0), axis=1, keepdims=True)
    return lane, first, second, probs, gate


def both(own_ref, side_ref):
    return jnp.concatenate([own_ref[...], side_ref[...]], axis=0)


def split_store(own_ref, side_ref, rows):
    half = rows.shape[0] // 2
    own_ref[...] = rows[:half]
    side_ref[...] = rows[half:]


def feed_kernel(
    experts,
    routed,
    expert_ref,
    own_ref,
    side_ref,
    own_grads_ref,
    side_grads_ref,
    head_ref,
    up_ref,
    down_ref,
    own_out_ref,
    side_out_ref,
    own_back_ref,
    side_back_ref,
    active_ref,
    pre_ref,
    grad_ref,
    head_grad_ref,
):
    rows = both(own_ref, side_ref)
    grads = both(own_grads_ref, side_grads_ref).astype(F32)
    expert = expert_ref[0] if routed else None
    logits = dot_nn(rows, head_ref[...])
    lane, first, second, probs, gate = gates(logits, experts, expert)
    coef = second * gate if routed else first
    weighted = (coef * grads).astype(BF16)
    pre = dot_nn(rows, up_ref[...])
    grad_active = dot_nt(weighted, down_ref[...])
    cumulative = 0.5 + 0.5 * lax.erf(pre * 0.7071067811865476)
    slope = cumulative + pre * jnp.exp(-0.5 * pre * pre) * 0.3989422804014327
    active = (pre * cumulative).astype(BF16)
    grad_pre = (grad_active * slope).astype(BF16)
    half = rows.shape[0] // 2
    for ref, value in ((active_ref, active), (pre_ref, grad_pre), (grad_ref, weighted)):
        ref[0] = value[:half]
        ref[1] = value[half:]
    out = dot_nn(active, down_ref[...])
    split_store(own_out_ref, side_out_ref, (coef * out).astype(BF16))
    inner = jnp.sum(grads * out, axis=1, keepdims=True)
    swing = first * second * inner
    if routed:
        swing = -gate * swing
    grad_logits = jnp.where(lane == experts, swing, jnp.where(lane == experts + 1, -swing, 0.0))
    if routed:
        picked = jnp.where(lane == expert, 1.0, 0.0) - gate
        grad_logits = grad_logits + jnp.where(
            lane < experts, probs * picked * (second * inner), 0.0
        )
    back = dot_nt(grad_pre, up_ref[...]) + dot_nt(grad_logits.astype(BF16), head_ref[...])
    split_store(own_back_ref, side_back_ref, back.astype(BF16))
    head_grad = dot_nn(grad_logits.T.astype(BF16), rows)

    @pl.when(pl.program_id(0) == 0)
    def _():
        head_grad_ref[...] = jnp.zeros_like(head_grad_ref)

    head_grad_ref[...] += head_grad


def feed(own, side, own_grads, side_grads, head, up, down, experts, expert, size):
    count = own.shape[0]
    width, hidden = up.shape
    steps = count // size
    lanes = head.shape[1]
    routed = expert is not None
    pick = jnp.reshape(expert, (1,)) if routed else jnp.zeros((1,), jnp.int32)
    rows = pl.BlockSpec((size, width), lambda i, pick: (i, 0))

    def whole(shape):
        return pl.BlockSpec(shape, lambda i, pick: (0, 0), pipeline_mode=pl.Buffered(1))

    def pairs(columns):
        return pl.BlockSpec((2, size, columns), lambda i, pick: (0, i, 0))

    quarter = jax.ShapeDtypeStruct((count, width), BF16)
    *sums, active, pre, weighted, head_grad = pl.pallas_call(
        functools.partial(feed_kernel, experts, routed),
        grid_spec=pltpu.PrefetchScalarGridSpec(
            num_scalar_prefetch=1,
            grid=(steps,),
            in_specs=[
                rows,
                rows,
                rows,
                rows,
                whole((width, lanes)),
                whole((width, hidden)),
                whole((hidden, width)),
            ],
            out_specs=[
                rows,
                rows,
                rows,
                rows,
                pairs(hidden),
                pairs(hidden),
                pairs(width),
                pl.BlockSpec((lanes, width), lambda i, pick: (0, 0)),
            ],
        ),
        out_shape=[
            quarter,
            quarter,
            quarter,
            quarter,
            jax.ShapeDtypeStruct((2, count, hidden), BF16),
            jax.ShapeDtypeStruct((2, count, hidden), BF16),
            jax.ShapeDtypeStruct((2, count, width), BF16),
            jax.ShapeDtypeStruct((lanes, width), F32),
        ],
        cost_estimate=pl.CostEstimate(
            flops=16 * count * width * hidden // COVER,
            transcendentals=4 * count * hidden // COVER,
            bytes_accessed=2 * (8 * count * width + 4 * count * hidden + 2 * width * hidden) // COVER,
        ),
        compiler_params=pltpu.CompilerParams(vmem_limit_bytes=60 * 1024 * 1024),
        name="feed_routed" if routed else "feed_dense",
    )(pick, own, side, own_grads, side_grads, head, up, down)
    flat = [value.reshape(2 * count, value.shape[2]) for value in (active, pre, weighted)]
    return [*sums, *flat, head_grad]


LANES = 128
QUARTER_ROWS = 128


def norm_parts(values):
    row_mean = jnp.mean(values, axis=-1, keepdims=True)
    centred = values - row_mean
    row_var = jnp.mean(centred * centred, axis=-1, keepdims=True)
    inverse = lax.rsqrt(row_var + EPSILON)
    return (centred * inverse, inverse)


def norm_back(grad_normed, gain_vec, scaled, inverse):
    grad_scaled = grad_normed * gain_vec
    first_mean = jnp.mean(grad_scaled, axis=-1, keepdims=True)
    second = jnp.mean(grad_scaled * scaled, axis=-1, keepdims=True)
    return inverse * (grad_scaled - first_mean - scaled * second)


def after(value, *others):
    return lax.optimization_barrier((value, *others))[0]


def from_side(values):
    return lax.ppermute(values, "tensor", [(i, i ^ 1) for i in range(4)])


def from_far(values):
    return lax.ppermute(values, "tensor", [(i, i ^ 2) for i in range(4)])


def plus_side(own, side):
    return own.astype(F32) + from_side(side.astype(BF16)).astype(F32)


def sum_over(values, axis):
    count, step = lax.axis_size(axis), 1
    while step < count:
        pairs = [(i, i ^ step) for i in range(count)]
        values = values + lax.ppermute(values, axis, pairs)
        step *= 2
    return values


def exchange(blocks):
    return lax.all_to_all(blocks, "expert", split_axis=0, concat_axis=0, tiled=True)


def scatter_sum(strips):
    strips = with_layout_constraint(strips.astype(BF16), Layout(major_to_minor=(0, 1)))
    return lax.psum_scatter(strips, "expert", scatter_dimension=0, tiled=True)


def strips_sent(grads):
    return exchange(grads.reshape(lax.axis_size("expert"), -1, grads.shape[1]))


def strips_total(strips):
    return jnp.sum(strips.astype(F32), axis=0)


def slots_of(expert_ids, experts, capacity):
    rows = expert_ids.shape[0]
    chosen = expert_ids[:, None] == jnp.arange(experts, dtype=jnp.int32)[None, :]
    at = jnp.arange(rows, dtype=jnp.int32)
    before = (at[None, :] < at[:, None]).astype(BF16)
    earlier = jnp.dot(before, chosen.astype(BF16), preferred_element_type=F32)
    slot = jnp.sum(jnp.where(chosen, earlier, 0.0), axis=1).astype(jnp.int32)
    place = expert_ids * capacity + slot
    places = jnp.arange(experts * capacity, dtype=jnp.int32)
    return (places[:, None] == place[None, :]).astype(BF16)


def per_device(
    tokens,
    cotangent,
    routes,
    parents,
    ln_attn,
    w_qkv,
    w_out,
    ln_mlp,
    w_up,
    w_down,
    w_router,
    w_mix,
    ex_up,
    ex_down,
):
    tok_dev, width = tokens.shape
    mine = lax.axis_index("tensor")
    experts = w_router.shape[1]
    capacity = max(2, tok_dev * 7 // (5 * experts))
    heads_width = w_qkv.shape[2]
    hidden = w_up.shape[1]
    leaves = jnp.concatenate([leaf_order(parents[0]), mine.astype(jnp.int32)[None]])

    scaled_one, inverse_one = norm_parts(tokens.astype(F32))
    normed_own = (scaled_one * ln_attn).astype(BF16)
    normed_far = from_far(normed_own)
    near_one = jnp.concatenate([normed_own, from_side(normed_own)], axis=0)

    quarter_ids = routes[:, 0].reshape(4, tok_dev)

    def slots_at(offset):
        ids = lax.dynamic_index_in_dim(quarter_ids, mine ^ offset, 0, keepdims=False)
        return slots_of(ids, experts, capacity)

    own_slots, far_slots = slots_at(0), slots_at(2)

    def placed(slots, rows):
        return jnp.dot(slots, rows, preferred_element_type=F32).astype(BF16)

    def sent(rows):
        return exchange(rows.reshape(experts, capacity, width)).reshape(-1, width)

    own_grads = sent(placed(own_slots, cotangent))
    cotangent_side = from_side(cotangent)

    def project(rows):
        qkv = jnp.einsum("td,sdc->stc", rows, w_qkv, preferred_element_type=F32)
        return qkv.astype(BF16).reshape(3, 2, tok_dev, heads_width)

    lanes = -(-(experts + 2) // LANES) * LANES
    head = jnp.concatenate(
        [w_router, w_mix, jnp.zeros((width, lanes - experts - 2), BF16)], axis=1
    )
    near_qkv = project(near_one)
    cotangent_far = from_far(after(cotangent, normed_far))
    normed_far, near_qkv, head = lax.optimization_barrier((normed_far, near_qkv, head))
    far_one = jnp.concatenate([normed_far, from_side(normed_far)], axis=0)
    far_qkv = project(far_one)
    near_out, far_out, *logs = attention_forward(leaves, near_qkv, far_qkv)
    far_out, own_grads, cotangent_far, cotangent_side = lax.optimization_barrier(
        (far_out, own_grads, cotangent_far, cotangent_side)
    )

    def branch_part(rows):
        return jnp.dot(rows, w_out, preferred_element_type=F32)

    far_sum = plus_side(branch_part(far_out[0]), branch_part(far_out[1])).astype(BF16)
    branch = plus_side(branch_part(near_out[0]), branch_part(near_out[1]))
    branch_far = from_far(far_sum)
    side_grads = from_side(own_grads)
    cotangent_corner = from_side(cotangent_far)
    far_placed = placed(far_slots, cotangent_far)
    branch_far, side_grads, cotangent_corner, far_placed = lax.optimization_barrier(
        (branch_far, side_grads, cotangent_corner, far_placed)
    )
    residual = tokens.astype(F32) + (branch + branch_far.astype(F32))

    scaled_two, inverse_two = norm_parts(residual)
    normed_two = (scaled_two * ln_mlp).astype(BF16)
    normed_two_far = from_far(normed_two)
    normed_two_side = from_side(normed_two)
    own_rows = sent(placed(own_slots, normed_two))

    def dense(own, side, own_cotangent, side_cotangent):
        return feed(
            own, side, own_cotangent, side_cotangent, head, w_up, w_down, experts, None, QUARTER_ROWS
        )

    def product(left, right):
        return jnp.einsum("gd,gf->df", left, right, preferred_element_type=F32)

    def weight_grads(near_left, far_left, near_right, far_right):
        return product(near_left, near_right) + product(far_left, far_right)

    near_dense = dense(normed_two, normed_two_side, cotangent, cotangent_side)
    near_two = jnp.concatenate([normed_two, normed_two_side], axis=0)
    grad_up = product(near_two, near_dense[5])
    grad_down = product(near_dense[6], near_dense[4])
    normed_two_far, grad_up, grad_down, own_rows = lax.optimization_barrier(
        (normed_two_far, grad_up, grad_down, own_rows)
    )
    far_rows = from_far(own_rows)
    far_grads = sent(after(far_placed, own_rows))
    normed_two_corner = from_side(normed_two_far)
    far_dense = list(dense(normed_two_far, normed_two_corner, cotangent_far, cotangent_corner))

    expert = lax.axis_index("expert").astype(jnp.int32)

    def routed(own, side, own_cotangent, side_cotangent):
        return feed(
            own,
            side,
            own_cotangent,
            side_cotangent,
            head,
            ex_up[0],
            ex_down[0],
            experts,
            expert,
            QUARTER_ROWS,
        )

    def chip_sum(parts, place, *others):
        return plus_side(parts[place], after(parts[place + 1], *others))

    def chip_sum(parts, place, *others):
        return plus_side(parts[place], after(parts[place + 1], *others))

    dense_back_far = chip_sum(far_dense, 2).astype(BF16)
    far_two = jnp.concatenate([normed_two_far, normed_two_corner], axis=0)
    grad_down = (grad_down + product(far_dense[6], far_dense[4])).astype(BF16)
    far_two, far_rows, grad_down = lax.optimization_barrier((far_two, far_rows, grad_down))
    grad_up = (grad_up + product(far_two, far_dense[5])).astype(BF16)
    dense_grads = after(jnp.concatenate([grad_up, grad_down], axis=1), far_grads)
    far_rows, dense_back_far, dense_grads = lax.optimization_barrier(
        (far_rows, dense_back_far, dense_grads)
    )
    dense_grads = scatter_sum(dense_grads)
    dense_back_far = from_far(dense_back_far)
    corner_rows = from_side(far_rows)
    side_rows = from_side(own_rows)
    far_expert = routed(far_rows, corner_rows, far_grads, from_side(far_grads))
    *far_expert, dense_back_far = lax.optimization_barrier((*far_expert, dense_back_far))
    far_back = chip_sum(far_expert, 2).astype(BF16)
    own_rows, far_back = lax.optimization_barrier((own_rows, far_back))
    near_expert = routed(own_rows, side_rows, own_grads, side_grads)
    *near_expert, dense_grads = lax.optimization_barrier((*near_expert, dense_grads))

    def picked(rows):
        return lax.dot_general(
            own_slots, rows, (((0,), (0,)), ((), ())), preferred_element_type=F32
        )

    expert_back = (chip_sum(near_expert, 2) + from_far(far_back).astype(F32)).astype(BF16)
    far_expert_out = chip_sum(far_expert, 0, expert_back).astype(BF16)
    dense_out_far = chip_sum(far_dense, 0, expert_back).astype(BF16)
    dense_back = chip_sum(near_dense, 2, far_back) + dense_back_far.astype(F32)

    grad_normed_two = dense_back + picked(sent(expert_back))
    dense_out = chip_sum(near_dense, 0, expert_back)
    expert_out = chip_sum(near_expert, 0, expert_back) + from_far(far_expert_out).astype(F32)
    expert_out = after(expert_out.astype(BF16), grad_normed_two)

    near_active, far_active, near_pre, far_pre, far_expert_out = lax.optimization_barrier(
        (near_expert[4], far_expert[4], near_expert[5], far_expert[5], far_expert_out)
    )
    near_tokens = jnp.concatenate([own_rows, side_rows], axis=0)
    far_tokens = jnp.concatenate([far_rows, corner_rows], axis=0)
    grad_ex_up = weight_grads(near_tokens, far_tokens, near_pre, far_pre)[None]
    grad_ex_down = weight_grads(near_active, far_active, near_expert[6], far_expert[6])[None]

    gain_two = jnp.sum(grad_normed_two * scaled_two, axis=0)
    grad_residual = cotangent.astype(F32) + norm_back(
        grad_normed_two, ln_mlp, scaled_two, inverse_two
    )
    grad_branch = grad_residual.astype(BF16)
    grad_branch_far = from_far(grad_branch)
    grad_branch_side = from_side(grad_branch)

    def into_heads(*rows):
        grads = [jnp.einsum("gd,cd->gc", part, w_out, preferred_element_type=F32) for part in rows]
        return jnp.stack(grads).astype(BF16)

    near_heads = into_heads(grad_branch, grad_branch_side)
    out_rows = sent(expert_out)
    flat = (2 * tok_dev, heads_width)
    near_branch = jnp.concatenate([grad_branch, grad_branch_side], axis=0)
    grad_w_out = product(near_branch, near_out.reshape(flat))
    grad_branch_far, near_heads, grad_w_out, grad_ex_up, grad_ex_down, _, dense_out_far, dense_out = (
        lax.optimization_barrier(
            (
                grad_branch_far,
                near_heads,
                grad_w_out,
                grad_ex_up,
                grad_ex_down,
                expert_out,
                dense_out_far,
                dense_out,
            )
        )
    )
    grad_branch_corner = from_side(grad_branch_far)
    far_heads = into_heads(grad_branch_far, grad_branch_corner)
    dense_out_far = from_far(dense_out_far)
    head_grads = near_dense[7] + far_dense[7] + near_expert[7] + far_expert[7]
    small = jnp.concatenate([head_grads[: experts + 2], gain_two[None]], axis=0)

    def pair_back(pair, near_grads, far_grads):
        return attention_backward(
            leaves, pair, near_qkv, far_qkv, near_grads, far_grads, near_out, far_out, logs
        )

    def pair_weights(pair):
        lanes = slice(pair * PAIR, (pair + 1) * PAIR)
        return jnp.concatenate([w_qkv[part, :, lanes] for part in range(3)], axis=1)

    def total(values):
        return functools.reduce(jnp.add, values)

    pairs = heads_width // PAIR
    near_results, far_results = [None] * pairs, [None] * pairs
    near_results[0], far_results[0] = pair_back(0, near_heads, far_heads)
    far_branch = jnp.concatenate([grad_branch_far, grad_branch_corner], axis=0)
    grad_w_out = grad_w_out + product(far_branch, far_out.reshape(flat))
    small = sum_over(small, "tensor")
    small_columns = -(-small.shape[0] // LANES) * LANES
    small_block = jnp.pad(small, ((0, small_columns - small.shape[0]), (0, 0))).T
    branch_grads = jnp.concatenate([grad_w_out.astype(BF16), small_block.astype(BF16)], axis=1)
    near_results[0], far_results[0], out_rows, dense_out_far, branch_grads, near_heads = (
        lax.optimization_barrier(
            (near_results[0], far_results[0], out_rows, dense_out_far, branch_grads, near_heads)
        )
    )
    branch_grads = strips_sent(branch_grads)
    for pair in range(1, pairs):
        near_results[pair], far_results[pair] = pair_back(pair, near_heads, far_heads)
    near_results, far_results, branch_grads = lax.optimization_barrier(
        (near_results, far_results, branch_grads)
    )

    def normed_part(results, quarter):
        return total([dot_nt(results[pair][quarter], pair_weights(pair)) for pair in range(pairs)])

    def qkv_strips(pair, *others):
        near_rows = near_results[pair].reshape(2 * tok_dev, 3 * PAIR)
        far_rows = far_results[pair].reshape(2 * tok_dev, 3 * PAIR)
        near_rows = after(near_rows, *others)
        return strips_sent(weight_grads(near_one, far_one, near_rows, far_rows).astype(BF16))

    corner_part = normed_part(far_results, 1).astype(BF16)
    from_corner = from_side(corner_part).astype(F32)
    qkv_grads = [qkv_strips(0, corner_part)]
    far_sum = (normed_part(far_results, 0) + from_corner).astype(BF16)
    near_results, far_results, out_rows, far_sum = lax.optimization_barrier(
        (near_results, far_results, out_rows, far_sum)
    )
    near_sum = plus_side(normed_part(near_results, 0), normed_part(near_results, 1))
    out = (residual + dense_out + dense_out_far.astype(F32) + picked(out_rows)).astype(BF16)

    scaled_far = normed_far.astype(F32) / ln_attn
    gain_one = jnp.sum(
        near_sum * scaled_one + far_sum.astype(F32) * scaled_far, axis=0, keepdims=True
    )
    gain_one = sum_over(gain_one, "expert")
    qkv_grads += [qkv_strips(pair, gain_one) for pair in range(1, pairs)]
    grad_normed_one = near_sum + after(from_far(far_sum), gain_one).astype(F32)
    grad_ln_attn = sum_over(gain_one, "tensor")[0]
    branch_grads = strips_total(branch_grads)
    qkv_grads = jnp.stack(
        [strips_total(grads).reshape(-1, 3, PAIR) for grads in qkv_grads], axis=2
    )
    grad_tokens = grad_residual + norm_back(grad_normed_one, ln_attn, scaled_one, inverse_one)

    strip = qkv_grads.shape[0]
    return (
        out,
        grad_tokens,
        grad_ln_attn,
        qkv_grads.reshape(strip, 3, heads_width).transpose(1, 0, 2),
        branch_grads[:, :heads_width].T,
        branch_grads[:, heads_width + experts + 2],
        dense_grads[:, :hidden].astype(F32),
        dense_grads[:, hidden:].T.astype(F32),
        branch_grads[:, heads_width : heads_width + experts],
        branch_grads[:, heads_width + experts : heads_width + experts + 2],
        grad_ex_up,
        grad_ex_down,
    )


def solution(mesh):
    return jax.shard_map(
        per_device,
        mesh=mesh,
        in_specs=(
            P(("expert", "tensor"), None),
            P(("expert", "tensor"), None),
            P("expert", None),
            P("expert", None),
            P(),
            P(None, None, "tensor"),
            P("tensor", None),
            P(),
            P(None, "tensor"),
            P("tensor", None),
            P(),
            P(),
            P("expert", None, "tensor"),
            P("expert", "tensor", None),
        ),
        out_specs=(
            P(("expert", "tensor"), None),
            P(("expert", "tensor"), None),
            P(),
            P(None, "expert", "tensor"),
            P("tensor", "expert"),
            P("expert"),
            P("expert", "tensor"),
            P("tensor", "expert"),
            P("expert", None),
            P("expert", None),
            P("expert", None, "tensor"),
            P("expert", "tensor", None),
        ),
        check_vma=False,
    )
```

```python
import functools

import jax
import jax.numpy as jnp
from jax import lax
from jax.experimental import pallas as pl
from jax.experimental.layout import Layout, with_layout_constraint
from jax.experimental.pallas import tpu as pltpu
from jax.sharding import PartitionSpec as P

HEAD_DIM = 64
TRUNK = 1024
SEG = 128
SEGS = 13
TREE_LEN = 2560
BRANCHES = 4
FAMILY = 3 * SEG
TEAM = 2 * FAMILY
TEAMS = BRANCHES // 2
QROWS = 256
COVER = 8
PAIR = 2 * HEAD_DIM
NEGATIVE_FILL = -1e30
F32 = jnp.float32
BF16 = jnp.bfloat16
EPSILON = 1e-05


def dot_nn(a, b):
    return lax.dot_general(a, b, (((1,), (0,)), ((), ())), preferred_element_type=F32)


def dot_nt(a, b):
    return lax.dot_general(a, b, (((1,), (1,)), ((), ())), preferred_element_type=F32)


def head_lanes(rows, head):
    lane = lax.broadcasted_iota(jnp.int32, rows.shape, 1)
    return jnp.where(lane // HEAD_DIM == head, rows, jnp.zeros_like(rows))


def causal(scores):
    key = lax.broadcasted_iota(jnp.int32, scores.shape, 0)
    query = lax.broadcasted_iota(jnp.int32, scores.shape, 1)
    return jnp.where(key <= query, scores, NEGATIVE_FILL)


def family_rows(leaves_ref, branch):
    def start(segment):
        return pl.multiple_of(TRUNK + (segment - 1) * SEG, SEG)

    return [start(branch + 1), start(leaves_ref[2 * branch]), start(leaves_ref[2 * branch + 1])]


def transpose_into(target_ref, source_ref, part):
    for first in range(0, TREE_LEN, 512):
        piece = source_ref[part, pl.ds(first, 512), :].astype(F32)
        target_ref[:, pl.ds(first, 512)] = piece.T.astype(BF16)


def widen(piece, first, width, fill):
    parts = []
    if first:
        parts.append(jnp.full((piece.shape[0], first), fill, piece.dtype))
    parts.append(piece)
    rest = width - first - piece.shape[1]
    if rest:
        parts.append(jnp.full((piece.shape[0], rest), fill, piece.dtype))
    return parts[0] if len(parts) == 1 else jnp.concatenate(parts, axis=1)


def trunk_groups(block):
    first = block * QROWS
    groups = [(0, first, 0, QROWS, None)] if first else []
    return groups + [(first, QROWS, 0, QROWS, "causal")]


def team_rows(leaves_ref, team):
    return family_rows(leaves_ref, 2 * team) + family_rows(leaves_ref, 2 * team + 1)


def team_groups(starts):
    groups = [(0, TRUNK, 0, TEAM, None)]
    for first in range(0, TEAM, FAMILY):
        at = first // SEG
        groups.append((starts[at], SEG, first, first + FAMILY, "branch"))
        for leaf in (1, 2):
            begin = first + leaf * SEG
            groups.append((starts[at + leaf], SEG, begin, begin + SEG, "causal"))
    return groups


def masked_scores(keys, queries, rule):
    scores = dot_nt(keys, queries)
    if rule == "causal":
        return causal(scores)
    if rule == "branch":
        return jnp.concatenate([causal(scores[:, :SEG]), scores[:, SEG:]], axis=1)
    return scores


def forward_block(qkv_ref, values_t_ref, queries, groups):
    width = queries.shape[0]
    outs, logs = [], []
    for head in range(2):
        own = head_lanes(queries, head)
        all_scores = [
            masked_scores(qkv_ref[1, pl.ds(start, size), :], own[first:last], rule)
            for start, size, first, last, rule in groups
        ]
        top = functools.reduce(
            jnp.maximum,
            [
                widen(jnp.max(s, axis=0, keepdims=True), first, width, NEGATIVE_FILL)
                for s, (_, _, first, last, _) in zip(all_scores, groups)
            ],
        )
        total, output = None, None
        for s, (start, size, first, last, _) in zip(all_scores, groups):
            weights = jnp.exp(s - top[:, first:last])
            part = widen(jnp.sum(weights, axis=0, keepdims=True), first, width, 0.0)
            values_t = values_t_ref[pl.ds(head * HEAD_DIM, HEAD_DIM), pl.ds(start, size)]
            mixed = widen(dot_nn(values_t, weights.astype(BF16)), first, width, 0.0)
            total = part if total is None else total + part
            output = mixed if output is None else output + mixed
        outs.append(output / total)
        logs.append(top + jnp.log(total))
    return jnp.concatenate(outs, axis=0).T.astype(BF16), jnp.concatenate(logs, axis=0)


def scaled_queries(qkv_ref, starts, size):
    rows = [qkv_ref[0, pl.ds(start, size), :] for start in starts]
    rows = rows[0] if len(rows) == 1 else jnp.concatenate(rows, axis=0)
    return rows * jnp.asarray(HEAD_DIM ** (-0.5), BF16)


def quarter_rows(leaves_ref, offset):
    quarter = TREE_LEN // 4
    return pl.ds(pl.multiple_of((leaves_ref[2 * BRANCHES] ^ offset) * quarter, quarter), quarter)


def forward_kernel(
    leaves_ref,
    near_ref,
    far_ref,
    near_out_ref,
    far_out_ref,
    trunk_log_ref,
    family_log_ref,
    qkv_ref,
    out_ref,
    values_t_ref,
):
    for offset in range(4):
        half_ref = near_ref if offset < 2 else far_ref
        qkv_ref[:, quarter_rows(leaves_ref, offset), :] = half_ref[:, offset % 2]
    transpose_into(values_t_ref, qkv_ref, 2)
    for block in range(TRUNK // QROWS):
        first = block * QROWS
        queries = scaled_queries(qkv_ref, [first], QROWS)
        out, logs = forward_block(qkv_ref, values_t_ref, queries, trunk_groups(block))
        out_ref[pl.ds(first, QROWS), :] = out
        trunk_log_ref[0, :, pl.ds(first, QROWS)] = logs

    def one_team(team, carry):
        starts = team_rows(leaves_ref, team)
        queries = scaled_queries(qkv_ref, starts, SEG)
        out, logs = forward_block(qkv_ref, values_t_ref, queries, team_groups(starts))
        for place, start in enumerate(starts):
            out_ref[pl.ds(start, SEG), :] = out[place * SEG : (place + 1) * SEG]
        family_log_ref[0, team] = logs
        return carry

    lax.fori_loop(0, TEAMS, one_team, 0)
    for offset in range(4):
        half_ref = near_out_ref if offset < 2 else far_out_ref
        half_ref[offset % 2] = out_ref[quarter_rows(leaves_ref, offset), :]


def halves_spec(parts):
    quarter = TREE_LEN // 4
    if parts == 1:
        return pl.BlockSpec((2, quarter, PAIR), lambda p, leaves: (0, 0, p))
    return pl.BlockSpec((parts, 2, quarter, PAIR), lambda p, leaves: (0, 0, 0, p))


def attention_cost(products, cover):
    visited = (TRUNK * (TRUNK + QROWS) // 2 + BRANCHES * FAMILY * (TRUNK + SEG)) // cover
    return pl.CostEstimate(
        flops=2 * products * 4 * visited * 2 * PAIR,
        transcendentals=4 * visited,
        bytes_accessed=8 * TREE_LEN * 4 * HEAD_DIM * 2 // cover,
    )


def attention_forward(leaves, near, far):
    width = near.shape[3]
    quarter = TREE_LEN // 4
    pairs = width // PAIR
    return pl.pallas_call(
        forward_kernel,
        grid_spec=pltpu.PrefetchScalarGridSpec(
            num_scalar_prefetch=1,
            grid=(pairs,),
            in_specs=[halves_spec(3), halves_spec(3)],
            out_specs=[
                halves_spec(1),
                halves_spec(1),
                pl.BlockSpec((1, 2, TRUNK), lambda p, leaves: (p, 0, 0)),
                pl.BlockSpec((1, TEAMS, 2, TEAM), lambda p, leaves: (p, 0, 0, 0)),
            ],
            scratch_shapes=[
                pltpu.VMEM((3, TREE_LEN, PAIR), BF16),
                pltpu.VMEM((TREE_LEN, PAIR), BF16),
                pltpu.VMEM((PAIR, TREE_LEN), BF16),
            ],
        ),
        out_shape=[
            jax.ShapeDtypeStruct((2, quarter, width), BF16),
            jax.ShapeDtypeStruct((2, quarter, width), BF16),
            jax.ShapeDtypeStruct((pairs, 2, TRUNK), F32),
            jax.ShapeDtypeStruct((pairs, TEAMS, 2, TEAM), F32),
        ],
        cost_estimate=attention_cost(2, COVER),
        name="tree_attention",
    )(leaves, near, far)


def backward_block(qkv_ref, keys_t_ref, queries, grads, outs, logs, groups):
    products = grads.astype(F32) * outs.astype(F32)
    products_t = products.T
    key_ds = [[] for _ in groups]
    value_ws = [[] for _ in groups]
    own_q, own_g, query_grads = [], [], []
    for head in range(2):
        own = head_lanes(queries, head)
        own_grads = head_lanes(grads, head)
        own_q.append(own)
        own_g.append(own_grads)
        inner = jnp.sum(
            products_t[head * HEAD_DIM : (head + 1) * HEAD_DIM], axis=0, keepdims=True
        )
        log = logs[head : head + 1]
        query_grad = None
        for place, (start, size, first, last, rule) in enumerate(groups):
            scores = masked_scores(qkv_ref[1, pl.ds(start, size), :], own[first:last], rule)
            weights = jnp.exp(scores - log[:, first:last])
            grad_weights = dot_nt(qkv_ref[2, pl.ds(start, size), :], own_grads[first:last])
            grad_scores = (weights * (grad_weights - inner[:, first:last])).astype(BF16)
            keys_t = keys_t_ref[pl.ds(head * HEAD_DIM, HEAD_DIM), pl.ds(start, size)]
            part = widen(dot_nn(keys_t, grad_scores), first, queries.shape[0], 0.0)
            query_grad = part if query_grad is None else query_grad + part
            key_ds[place].append(grad_scores)
            value_ws[place].append(weights.astype(BF16))
        query_grads.append(query_grad)
    grad_query = (jnp.concatenate(query_grads, axis=0) * HEAD_DIM ** (-0.5)).T.astype(BF16)
    key_grads, value_grads = [], []
    for place, (start, size, first, last, rule) in enumerate(groups):
        stacked_q = jnp.concatenate([own_q[0][first:last], own_q[1][first:last]], axis=0)
        stacked_g = jnp.concatenate([own_g[0][first:last], own_g[1][first:last]], axis=0)
        key_grads.append(dot_nn(jnp.concatenate(key_ds[place], axis=1), stacked_q))
        value_grads.append(dot_nn(jnp.concatenate(value_ws[place], axis=1), stacked_g))
    return grad_query, key_grads, value_grads


def backward_kernel(
    leaves_ref,
    near_ref,
    far_ref,
    near_grads_ref,
    far_grads_ref,
    near_outs_ref,
    far_outs_ref,
    trunk_log_ref,
    family_log_ref,
    near_result_ref,
    far_result_ref,
    qkv_ref,
    grads_ref,
    outs_ref,
    result_ref,
    keys_t_ref,
    trunk_keys_ref,
    trunk_values_ref,
):
    for offset in range(4):
        rows = quarter_rows(leaves_ref, offset)
        at = offset % 2
        qkv_ref[:, rows, :] = (near_ref if offset < 2 else far_ref)[:, at]
        grads_ref[rows, :] = (near_grads_ref if offset < 2 else far_grads_ref)[at]
        outs_ref[rows, :] = (near_outs_ref if offset < 2 else far_outs_ref)[at]
    transpose_into(keys_t_ref, qkv_ref, 1)
    trunk_keys_ref[...] = jnp.zeros_like(trunk_keys_ref)
    trunk_values_ref[...] = jnp.zeros_like(trunk_values_ref)
    for block in range(TRUNK // QROWS):
        first = block * QROWS
        rows = pl.ds(first, QROWS)
        groups = trunk_groups(block)
        grad_query, key_grads, value_grads = backward_block(
            qkv_ref,
            keys_t_ref,
            scaled_queries(qkv_ref, [first], QROWS),
            grads_ref[rows, :],
            outs_ref[rows, :],
            trunk_log_ref[0, :, rows],
            groups,
        )
        result_ref[0, rows, :] = grad_query
        for (start, size, _, _, _), key_grad, value_grad in zip(groups, key_grads, value_grads):
            trunk_keys_ref[pl.ds(start, size), :] += key_grad
            trunk_values_ref[pl.ds(start, size), :] += value_grad

    def one_team(team, carry):
        starts = team_rows(leaves_ref, team)
        groups = team_groups(starts)
        grad_query, key_grads, value_grads = backward_block(
            qkv_ref,
            keys_t_ref,
            scaled_queries(qkv_ref, starts, SEG),
            jnp.concatenate([grads_ref[pl.ds(start, SEG), :] for start in starts], axis=0),
            jnp.concatenate([outs_ref[pl.ds(start, SEG), :] for start in starts], axis=0),
            family_log_ref[0, team],
            groups,
        )
        trunk_keys_ref[...] += key_grads[0]
        trunk_values_ref[...] += value_grads[0]
        for place, start in enumerate(starts):
            rows = pl.ds(start, SEG)
            result_ref[0, rows, :] = grad_query[place * SEG : (place + 1) * SEG]
            result_ref[1, rows, :] = key_grads[1 + place].astype(BF16)
            result_ref[2, rows, :] = value_grads[1 + place].astype(BF16)
        return carry

    lax.fori_loop(0, TEAMS, one_team, 0)
    result_ref[1, pl.ds(0, TRUNK), :] = trunk_keys_ref[...].astype(BF16)
    result_ref[2, pl.ds(0, TRUNK), :] = trunk_values_ref[...].astype(BF16)
    for offset in range(4):
        half_ref = near_result_ref if offset < 2 else far_result_ref
        rows = quarter_rows(leaves_ref, offset)
        for part in range(3):
            half_ref[offset % 2, :, part * PAIR : (part + 1) * PAIR] = result_ref[part, rows, :]


def attention_backward(leaves, pair, near, far, near_grads, far_grads, near_outs, far_outs, logs):
    quarter = TREE_LEN // 4
    rows = pl.BlockSpec((2, quarter, PAIR), lambda i, leaves: (0, 0, pair))
    parts = pl.BlockSpec((3, 2, quarter, PAIR), lambda i, leaves: (0, 0, 0, pair))
    result = pl.BlockSpec((2, quarter, 3 * PAIR), lambda i, leaves: (0, 0, 0))
    shape = jax.ShapeDtypeStruct((2, quarter, 3 * PAIR), BF16)
    return pl.pallas_call(
        backward_kernel,
        grid_spec=pltpu.PrefetchScalarGridSpec(
            num_scalar_prefetch=1,
            grid=(1,),
            in_specs=[
                parts,
                parts,
                rows,
                rows,
                rows,
                rows,
                pl.BlockSpec((1, 2, TRUNK), lambda i, leaves: (pair, 0, 0)),
                pl.BlockSpec((1, TEAMS, 2, TEAM), lambda i, leaves: (pair, 0, 0, 0)),
            ],
            out_specs=[result, result],
            scratch_shapes=[
                pltpu.VMEM((3, TREE_LEN, PAIR), BF16),
                pltpu.VMEM((TREE_LEN, PAIR), BF16),
                pltpu.VMEM((TREE_LEN, PAIR), BF16),
                pltpu.VMEM((3, TREE_LEN, PAIR), BF16),
                pltpu.VMEM((PAIR, TREE_LEN), BF16),
                pltpu.VMEM((TRUNK, PAIR), F32),
                pltpu.VMEM((TRUNK, PAIR), F32),
            ],
        ),
        out_shape=[shape, shape],
        cost_estimate=attention_cost(5, 10),
        name="tree_attention_back",
    )(leaves, near, far, near_grads, far_grads, near_outs, far_outs, *logs)


def leaf_order(parents_row):
    first_leaf = BRANCHES + 1
    leaf_parents = parents_row[first_leaf:]
    segments = first_leaf + jnp.arange(leaf_parents.shape[0], dtype=jnp.int32)
    same = leaf_parents[:, None] == leaf_parents[None, :]
    later = segments[None, :] < segments[:, None]
    place = 2 * (leaf_parents - 1) + jnp.sum(jnp.where(same & later, 1, 0), axis=1)
    slots = jnp.arange(2 * BRANCHES, dtype=jnp.int32)
    return jnp.sum(jnp.where(slots[:, None] == place[None, :], segments[None, :], 0), axis=1)


def gates(logits, experts, expert):
    lane = lax.broadcasted_iota(jnp.int32, logits.shape, 1)
    first, second = logits[:, experts : experts + 1], logits[:, experts + 1 : experts + 2]
    top = jnp.maximum(first, second)
    first, second = jnp.exp(first - top), jnp.exp(second - top)
    total = first + second
    first, second = first / total, second / total
    if expert is None:
        return lane, first, second, None, None
    routed = jnp.where(lane < experts, logits, NEGATIVE_FILL)
    raised = jnp.exp(routed - jnp.max(routed, axis=1, keepdims=True))
    probs = raised / jnp.sum(raised, axis=1, keepdims=True)
    gate = jnp.sum(jnp.where(lane == expert, probs, 0.0), axis=1, keepdims=True)
    return lane, first, second, probs, gate


def both(own_ref, side_ref):
    return jnp.concatenate([own_ref[...], side_ref[...]], axis=0)


def split_store(own_ref, side_ref, rows):
    half = rows.shape[0] // 2
    own_ref[...] = rows[:half]
    side_ref[...] = rows[half:]


def feed_kernel(
    experts,
    routed,
    expert_ref,
    own_ref,
    side_ref,
    own_grads_ref,
    side_grads_ref,
    head_ref,
    up_ref,
    down_ref,
    own_out_ref,
    side_out_ref,
    own_back_ref,
    side_back_ref,
    active_ref,
    pre_ref,
    grad_ref,
    head_grad_ref,
):
    rows = both(own_ref, side_ref)
    grads = both(own_grads_ref, side_grads_ref).astype(F32)
    expert = expert_ref[0] if routed else None
    logits = dot_nn(rows, head_ref[...])
    lane, first, second, probs, gate = gates(logits, experts, expert)
    coef = second * gate if routed else first
    weighted = (coef * grads).astype(BF16)
    pre = dot_nn(rows, up_ref[...])
    grad_active = dot_nt(weighted, down_ref[...])
    cumulative = 0.5 + 0.5 * lax.erf(pre * 0.7071067811865476)
    slope = cumulative + pre * jnp.exp(-0.5 * pre * pre) * 0.3989422804014327
    active = (pre * cumulative).astype(BF16)
    grad_pre = (grad_active * slope).astype(BF16)
    half = rows.shape[0] // 2
    for ref, value in ((active_ref, active), (pre_ref, grad_pre), (grad_ref, weighted)):
        ref[0] = value[:half]
        ref[1] = value[half:]
    out = dot_nn(active, down_ref[...])
    split_store(own_out_ref, side_out_ref, (coef * out).astype(BF16))
    inner = jnp.sum(grads * out, axis=1, keepdims=True)
    swing = first * second * inner
    if routed:
        swing = -gate * swing
    grad_logits = jnp.where(lane == experts, swing, jnp.where(lane == experts + 1, -swing, 0.0))
    if routed:
        picked = jnp.where(lane == expert, 1.0, 0.0) - gate
        grad_logits = grad_logits + jnp.where(
            lane < experts, probs * picked * (second * inner), 0.0
        )
    back = dot_nt(grad_pre, up_ref[...]) + dot_nt(grad_logits.astype(BF16), head_ref[...])
    split_store(own_back_ref, side_back_ref, back.astype(BF16))
    head_grad = dot_nn(grad_logits.T.astype(BF16), rows)

    @pl.when(pl.program_id(0) == 0)
    def _():
        head_grad_ref[...] = jnp.zeros_like(head_grad_ref)

    head_grad_ref[...] += head_grad


def feed(own, side, own_grads, side_grads, head, up, down, experts, expert, size):
    count = own.shape[0]
    width, hidden = up.shape
    steps = count // size
    lanes = head.shape[1]
    routed = expert is not None
    pick = jnp.reshape(expert, (1,)) if routed else jnp.zeros((1,), jnp.int32)
    rows = pl.BlockSpec((size, width), lambda i, pick: (i, 0))

    def whole(shape):
        return pl.BlockSpec(shape, lambda i, pick: (0, 0), pipeline_mode=pl.Buffered(1))

    def pairs(columns):
        return pl.BlockSpec((2, size, columns), lambda i, pick: (0, i, 0))

    quarter = jax.ShapeDtypeStruct((count, width), BF16)
    *sums, active, pre, weighted, head_grad = pl.pallas_call(
        functools.partial(feed_kernel, experts, routed),
        grid_spec=pltpu.PrefetchScalarGridSpec(
            num_scalar_prefetch=1,
            grid=(steps,),
            in_specs=[
                rows,
                rows,
                rows,
                rows,
                whole((width, lanes)),
                whole((width, hidden)),
                whole((hidden, width)),
            ],
            out_specs=[
                rows,
                rows,
                rows,
                rows,
                pairs(hidden),
                pairs(hidden),
                pairs(width),
                pl.BlockSpec((lanes, width), lambda i, pick: (0, 0)),
            ],
        ),
        out_shape=[
            quarter,
            quarter,
            quarter,
            quarter,
            jax.ShapeDtypeStruct((2, count, hidden), BF16),
            jax.ShapeDtypeStruct((2, count, hidden), BF16),
            jax.ShapeDtypeStruct((2, count, width), BF16),
            jax.ShapeDtypeStruct((lanes, width), F32),
        ],
        cost_estimate=pl.CostEstimate(
            flops=16 * count * width * hidden // COVER,
            transcendentals=4 * count * hidden // COVER,
            bytes_accessed=2 * (8 * count * width + 4 * count * hidden + 2 * width * hidden) // COVER,
        ),
        compiler_params=pltpu.CompilerParams(vmem_limit_bytes=60 * 1024 * 1024),
        name="feed_routed" if routed else "feed_dense",
    )(pick, own, side, own_grads, side_grads, head, up, down)
    flat = [value.reshape(2 * count, value.shape[2]) for value in (active, pre, weighted)]
    return [*sums, *flat, head_grad]


LANES = 128
DIRECT = 8
EARLY = 5
QUARTER_ROWS = 128


def norm_parts(values):
    row_mean = jnp.mean(values, axis=-1, keepdims=True)
    centred = values - row_mean
    row_var = jnp.mean(centred * centred, axis=-1, keepdims=True)
    inverse = lax.rsqrt(row_var + EPSILON)
    return (centred * inverse, inverse)


def norm_back(grad_normed, gain_vec, scaled, inverse):
    grad_scaled = grad_normed * gain_vec
    first_mean = jnp.mean(grad_scaled, axis=-1, keepdims=True)
    second = jnp.mean(grad_scaled * scaled, axis=-1, keepdims=True)
    return inverse * (grad_scaled - first_mean - scaled * second)


def after(value, *others):
    return lax.optimization_barrier((value, *others))[0]


def from_side(values):
    return lax.ppermute(values, "tensor", [(i, i ^ 1) for i in range(4)])


def from_far(values):
    return lax.ppermute(values, "tensor", [(i, i ^ 2) for i in range(4)])


def plus_side(own, side):
    return own.astype(F32) + from_side(side.astype(BF16)).astype(F32)


def sum_over(values, axis):
    count, step = lax.axis_size(axis), 1
    while step < count:
        pairs = [(i, i ^ step) for i in range(count)]
        values = values + lax.ppermute(values, axis, pairs)
        step *= 2
    return values


def exchange(blocks):
    return lax.all_to_all(blocks, "expert", split_axis=0, concat_axis=0, tiled=True)


def steps_sent(blocks):
    count = lax.axis_size("expert")
    parts = [blocks[0]]
    for step in range(1, count):
        pairs = [(i, (i + step) % count) for i in range(count)]
        parts.append(lax.ppermute(blocks[step], "expert", pairs))
    return parts


def in_order(parts):
    count = len(parts)
    onward = jnp.stack([parts[-step % count] for step in range(count)] * 2)
    start = count - lax.axis_index("expert")
    return lax.dynamic_slice_in_dim(onward, start, count, 0)


def scatter_sum(strips):
    strips = with_layout_constraint(strips.astype(BF16), Layout(major_to_minor=(0, 1)))
    return lax.psum_scatter(strips, "expert", scatter_dimension=0, tiled=True)


def strips_sent(grads):
    return exchange(grads.reshape(lax.axis_size("expert"), -1, grads.shape[1]))


def strips_total(strips):
    return jnp.sum(strips.astype(F32), axis=0)


def slots_of(expert_ids, experts, capacity, relative):
    rows = expert_ids.shape[0]
    chosen = expert_ids[:, None] == jnp.arange(experts, dtype=jnp.int32)[None, :]
    at = jnp.arange(rows, dtype=jnp.int32)
    before = (at[None, :] < at[:, None]).astype(BF16)
    earlier = jnp.dot(before, chosen.astype(BF16), preferred_element_type=F32)
    slot = jnp.sum(jnp.where(chosen, earlier, 0.0), axis=1).astype(jnp.int32)
    block = (expert_ids - lax.axis_index("expert")) % experts if relative else expert_ids
    place = block * capacity + slot
    places = jnp.arange(experts * capacity, dtype=jnp.int32)
    return (places[:, None] == place[None, :]).astype(BF16)


def per_device(
    tokens,
    cotangent,
    routes,
    parents,
    ln_attn,
    w_qkv,
    w_out,
    ln_mlp,
    w_up,
    w_down,
    w_router,
    w_mix,
    ex_up,
    ex_down,
):
    tok_dev, width = tokens.shape
    mine = lax.axis_index("tensor")
    experts = w_router.shape[1]
    capacity = max(2, tok_dev * 7 // (5 * experts))
    heads_width = w_qkv.shape[2]
    hidden = w_up.shape[1]
    leaves = jnp.concatenate([leaf_order(parents[0]), mine.astype(jnp.int32)[None]])

    scaled_one, inverse_one = norm_parts(tokens.astype(F32))
    normed_own = (scaled_one * ln_attn).astype(BF16)
    normed_far = from_far(normed_own)
    near_one = jnp.concatenate([normed_own, from_side(normed_own)], axis=0)

    quarter_ids = routes[:, 0].reshape(4, tok_dev)

    def slots_at(offset, relative):
        ids = lax.dynamic_index_in_dim(quarter_ids, mine ^ offset, 0, keepdims=False)
        return slots_of(ids, experts, capacity, relative)

    direct = experts <= DIRECT
    own_slots, far_slots = slots_at(0, False), slots_at(2, direct)

    def placed(slots, rows):
        return jnp.dot(slots, rows, preferred_element_type=F32).astype(BF16)

    def sent(rows):
        return exchange(rows.reshape(experts, capacity, width)).reshape(-1, width)

    own_grads = sent(placed(own_slots, cotangent))
    cotangent_side = from_side(cotangent)

    def project(rows):
        qkv = jnp.einsum("td,sdc->stc", rows, w_qkv, preferred_element_type=F32)
        return qkv.astype(BF16).reshape(3, 2, tok_dev, heads_width)

    lanes = -(-(experts + 2) // LANES) * LANES
    head = jnp.concatenate(
        [w_router, w_mix, jnp.zeros((width, lanes - experts - 2), BF16)], axis=1
    )
    near_qkv = project(near_one)
    cotangent_far = from_far(after(cotangent, normed_far))
    normed_far, near_qkv, head = lax.optimization_barrier((normed_far, near_qkv, head))
    far_one = jnp.concatenate([normed_far, from_side(normed_far)], axis=0)
    far_qkv = project(far_one)
    near_out, far_out, *logs = attention_forward(leaves, near_qkv, far_qkv)
    far_out, own_grads, cotangent_far, cotangent_side = lax.optimization_barrier(
        (far_out, own_grads, cotangent_far, cotangent_side)
    )

    def branch_part(rows):
        return jnp.dot(rows, w_out, preferred_element_type=F32)

    far_sum = plus_side(branch_part(far_out[0]), branch_part(far_out[1])).astype(BF16)
    branch = plus_side(branch_part(near_out[0]), branch_part(near_out[1]))
    branch_far = from_far(far_sum)
    side_grads = from_side(own_grads)
    cotangent_corner = from_side(cotangent_far)
    far_placed = placed(far_slots, cotangent_far)
    far_parts = steps_sent(far_placed.reshape(experts, capacity, width)) if direct else []
    branch_far, side_grads, cotangent_corner, far_placed, *far_parts[:EARLY] = (
        lax.optimization_barrier(
            (branch_far, side_grads, cotangent_corner, far_placed, *far_parts[:EARLY])
        )
    )
    residual = tokens.astype(F32) + (branch + branch_far.astype(F32))

    scaled_two, inverse_two = norm_parts(residual)
    normed_two = (scaled_two * ln_mlp).astype(BF16)
    normed_two_far = from_far(normed_two)
    normed_two_side = from_side(normed_two)
    own_rows = sent(placed(own_slots, normed_two))

    def dense(own, side, own_cotangent, side_cotangent):
        return feed(
            own, side, own_cotangent, side_cotangent, head, w_up, w_down, experts, None, QUARTER_ROWS
        )

    def product(left, right):
        return jnp.einsum("gd,gf->df", left, right, preferred_element_type=F32)

    def weight_grads(near_left, far_left, near_right, far_right):
        return product(near_left, near_right) + product(far_left, far_right)

    near_dense = dense(normed_two, normed_two_side, cotangent, cotangent_side)
    near_two = jnp.concatenate([normed_two, normed_two_side], axis=0)
    grad_up = product(near_two, near_dense[5])
    grad_down = product(near_dense[6], near_dense[4])
    normed_two_far, grad_up, grad_down, own_rows = lax.optimization_barrier(
        (normed_two_far, grad_up, grad_down, own_rows)
    )
    far_rows = from_far(own_rows)
    if direct:
        normed_two_far, *far_parts = lax.optimization_barrier((normed_two_far, *far_parts))
        far_grads = in_order(far_parts).reshape(-1, width)
    else:
        far_grads = sent(after(far_placed, own_rows))
    normed_two_corner = from_side(normed_two_far)
    far_dense = list(dense(normed_two_far, normed_two_corner, cotangent_far, cotangent_corner))

    expert = lax.axis_index("expert").astype(jnp.int32)

    def routed(own, side, own_cotangent, side_cotangent):
        return feed(
            own,
            side,
            own_cotangent,
            side_cotangent,
            head,
            ex_up[0],
            ex_down[0],
            experts,
            expert,
            QUARTER_ROWS,
        )

    def chip_sum(parts, place, *others):
        return plus_side(parts[place], after(parts[place + 1], *others))

    def chip_sum(parts, place, *others):
        return plus_side(parts[place], after(parts[place + 1], *others))

    dense_back_far = chip_sum(far_dense, 2).astype(BF16)
    far_two = jnp.concatenate([normed_two_far, normed_two_corner], axis=0)
    grad_down = (grad_down + product(far_dense[6], far_dense[4])).astype(BF16)
    far_two, grad_down = lax.optimization_barrier((far_two, grad_down))
    grad_up = (grad_up + product(far_two, far_dense[5])).astype(BF16)
    dense_grads = jnp.concatenate([grad_up, grad_down], axis=1)
    far_rows, dense_back_far, dense_grads = lax.optimization_barrier(
        (far_rows, dense_back_far, dense_grads)
    )
    dense_grads = scatter_sum(dense_grads)
    dense_back_far = from_far(dense_back_far)
    corner_rows = from_side(far_rows)
    side_rows = from_side(own_rows)
    far_expert = routed(far_rows, corner_rows, far_grads, from_side(far_grads))
    *far_expert, dense_back_far = lax.optimization_barrier((*far_expert, dense_back_far))
    far_back = chip_sum(far_expert, 2).astype(BF16)
    own_rows, far_back = lax.optimization_barrier((own_rows, far_back))
    near_expert = routed(own_rows, side_rows, own_grads, side_grads)
    *near_expert, dense_grads = lax.optimization_barrier((*near_expert, dense_grads))

    def picked(rows):
        return lax.dot_general(
            own_slots, rows, (((0,), (0,)), ((), ())), preferred_element_type=F32
        )

    expert_back = (chip_sum(near_expert, 2) + from_far(far_back).astype(F32)).astype(BF16)
    far_expert_out = chip_sum(far_expert, 0, expert_back).astype(BF16)
    dense_out_far = chip_sum(far_dense, 0, expert_back).astype(BF16)
    dense_back = chip_sum(near_dense, 2, far_back) + dense_back_far.astype(F32)

    grad_normed_two = dense_back + picked(sent(expert_back))
    dense_out = chip_sum(near_dense, 0, expert_back)
    expert_out = chip_sum(near_expert, 0, expert_back) + from_far(far_expert_out).astype(F32)
    expert_out = after(expert_out.astype(BF16), grad_normed_two)

    near_active, far_active, near_pre, far_pre, far_expert_out = lax.optimization_barrier(
        (near_expert[4], far_expert[4], near_expert[5], far_expert[5], far_expert_out)
    )
    near_tokens = jnp.concatenate([own_rows, side_rows], axis=0)
    far_tokens = jnp.concatenate([far_rows, corner_rows], axis=0)
    grad_ex_up = weight_grads(near_tokens, far_tokens, near_pre, far_pre)[None]
    grad_ex_down = weight_grads(near_active, far_active, near_expert[6], far_expert[6])[None]

    gain_two = jnp.sum(grad_normed_two * scaled_two, axis=0)
    grad_residual = cotangent.astype(F32) + norm_back(
        grad_normed_two, ln_mlp, scaled_two, inverse_two
    )
    grad_branch = grad_residual.astype(BF16)
    grad_branch_far = from_far(grad_branch)
    grad_branch_side = from_side(grad_branch)

    def into_heads(*rows):
        grads = [jnp.einsum("gd,cd->gc", part, w_out, preferred_element_type=F32) for part in rows]
        return jnp.stack(grads).astype(BF16)

    near_heads = into_heads(grad_branch, grad_branch_side)
    out_rows = sent(expert_out)
    flat = (2 * tok_dev, heads_width)
    near_branch = jnp.concatenate([grad_branch, grad_branch_side], axis=0)
    grad_w_out = product(near_branch, near_out.reshape(flat))
    grad_branch_far, near_heads, grad_w_out, grad_ex_up, grad_ex_down, _, dense_out_far, dense_out = (
        lax.optimization_barrier(
            (
                grad_branch_far,
                near_heads,
                grad_w_out,
                grad_ex_up,
                grad_ex_down,
                expert_out,
                dense_out_far,
                dense_out,
            )
        )
    )
    grad_branch_corner = from_side(grad_branch_far)
    far_heads = into_heads(grad_branch_far, grad_branch_corner)
    dense_out_far = from_far(dense_out_far)
    head_grads = near_dense[7] + far_dense[7] + near_expert[7] + far_expert[7]
    small = jnp.concatenate([head_grads[: experts + 2], gain_two[None]], axis=0)

    def pair_back(pair, near_grads, far_grads):
        return attention_backward(
            leaves, pair, near_qkv, far_qkv, near_grads, far_grads, near_out, far_out, logs
        )

    def pair_weights(pair):
        lanes = slice(pair * PAIR, (pair + 1) * PAIR)
        return jnp.concatenate([w_qkv[part, :, lanes] for part in range(3)], axis=1)

    def total(values):
        return functools.reduce(jnp.add, values)

    pairs = heads_width // PAIR
    near_results, far_results = [None] * pairs, [None] * pairs
    near_results[0], far_results[0] = pair_back(0, near_heads, far_heads)
    far_branch = jnp.concatenate([grad_branch_far, grad_branch_corner], axis=0)
    grad_w_out = grad_w_out + product(far_branch, far_out.reshape(flat))
    small_columns = -(-small.shape[0] // LANES) * LANES
    small_block = jnp.pad(small, ((0, small_columns - small.shape[0]), (0, 0))).T
    branch_grads = jnp.concatenate([grad_w_out.astype(BF16), small_block.astype(BF16)], axis=1)
    near_results[0], far_results[0], out_rows, dense_out_far, branch_grads, near_heads = (
        lax.optimization_barrier(
            (near_results[0], far_results[0], out_rows, dense_out_far, branch_grads, near_heads)
        )
    )
    branch_grads = strips_sent(branch_grads)
    for pair in range(1, pairs):
        near_results[pair], far_results[pair] = pair_back(pair, near_heads, far_heads)
    near_results, far_results, branch_grads = lax.optimization_barrier(
        (near_results, far_results, branch_grads)
    )

    def normed_part(results, quarter):
        return total([dot_nt(results[pair][quarter], pair_weights(pair)) for pair in range(pairs)])

    def qkv_weights(pair, *others):
        near_rows = near_results[pair].reshape(2 * tok_dev, 3 * PAIR)
        far_rows = far_results[pair].reshape(2 * tok_dev, 3 * PAIR)
        near_rows = after(near_rows, *others)
        return weight_grads(near_one, far_one, near_rows, far_rows).astype(BF16)

    corner_part = normed_part(far_results, 1).astype(BF16)
    from_corner = from_side(corner_part).astype(F32)
    first_grads = qkv_weights(0, corner_part)
    far_results, first_grads = lax.optimization_barrier((far_results, first_grads))
    qkv_grads = [strips_sent(first_grads)]
    far_sum = (normed_part(far_results, 0) + from_corner).astype(BF16)
    near_results, far_results, out_rows, far_sum = lax.optimization_barrier(
        (near_results, far_results, out_rows, far_sum)
    )
    near_sum = plus_side(normed_part(near_results, 0), normed_part(near_results, 1))
    out = (residual + dense_out + dense_out_far.astype(F32) + picked(out_rows)).astype(BF16)

    scaled_far = normed_far.astype(F32) / ln_attn
    gain_one = jnp.sum(
        near_sum * scaled_one + far_sum.astype(F32) * scaled_far, axis=0, keepdims=True
    )
    gain_one = sum_over(gain_one, "expert")
    qkv_grads += [strips_sent(qkv_weights(pair, gain_one)) for pair in range(1, pairs)]
    grad_normed_one = near_sum + after(from_far(far_sum), gain_one).astype(F32)
    grad_ln_attn = sum_over(gain_one, "tensor")[0]
    branch_grads = strips_total(after(branch_grads, gain_one))
    small = sum_over(branch_grads[:, heads_width:], "tensor")
    qkv_grads = jnp.stack(
        [strips_total(grads).reshape(-1, 3, PAIR) for grads in qkv_grads], axis=2
    )
    grad_tokens = grad_residual + norm_back(grad_normed_one, ln_attn, scaled_one, inverse_one)

    strip = qkv_grads.shape[0]
    return (
        out,
        grad_tokens,
        grad_ln_attn,
        qkv_grads.reshape(strip, 3, heads_width).transpose(1, 0, 2),
        branch_grads[:, :heads_width].T,
        small[:, experts + 2],
        dense_grads[:, :hidden].astype(F32),
        dense_grads[:, hidden:].T.astype(F32),
        small[:, :experts],
        small[:, experts : experts + 2],
        grad_ex_up,
        grad_ex_down,
    )


def solution(mesh):
    return jax.shard_map(
        per_device,
        mesh=mesh,
        in_specs=(
            P(("expert", "tensor"), None),
            P(("expert", "tensor"), None),
            P("expert", None),
            P("expert", None),
            P(),
            P(None, None, "tensor"),
            P("tensor", None),
            P(),
            P(None, "tensor"),
            P("tensor", None),
            P(),
            P(),
            P("expert", None, "tensor"),
            P("expert", "tensor", None),
        ),
        out_specs=(
            P(("expert", "tensor"), None),
            P(("expert", "tensor"), None),
            P(),
            P(None, "expert", "tensor"),
            P("tensor", "expert"),
            P("expert"),
            P("expert", "tensor"),
            P("tensor", "expert"),
            P("expert", None),
            P("expert", None),
            P("expert", None, "tensor"),
            P("expert", "tensor", None),
        ),
        check_vma=False,
    )
```

```python
import functools

import jax
import jax.numpy as jnp
from jax import lax
from jax.experimental import pallas as pl
from jax.experimental.layout import Layout, with_layout_constraint
from jax.experimental.pallas import tpu as pltpu
from jax.sharding import PartitionSpec as P

HEAD_DIM = 64
TRUNK = 1024
SEG = 128
SEGS = 13
TREE_LEN = 2560
BRANCHES = 4
FAMILY = 3 * SEG
TEAM = 2 * FAMILY
TEAMS = BRANCHES // 2
QROWS = 256
COVER = 8
PAIR = 2 * HEAD_DIM
NEGATIVE_FILL = -1e30
F32 = jnp.float32
BF16 = jnp.bfloat16
EPSILON = 1e-05


def dot_nn(a, b):
    return lax.dot_general(a, b, (((1,), (0,)), ((), ())), preferred_element_type=F32)


def dot_nt(a, b):
    return lax.dot_general(a, b, (((1,), (1,)), ((), ())), preferred_element_type=F32)


def head_lanes(rows, head):
    lane = lax.broadcasted_iota(jnp.int32, rows.shape, 1)
    return jnp.where(lane // HEAD_DIM == head, rows, jnp.zeros_like(rows))


def causal(scores):
    key = lax.broadcasted_iota(jnp.int32, scores.shape, 0)
    query = lax.broadcasted_iota(jnp.int32, scores.shape, 1)
    return jnp.where(key <= query, scores, NEGATIVE_FILL)


def family_rows(leaves_ref, branch):
    def start(segment):
        return pl.multiple_of(TRUNK + (segment - 1) * SEG, SEG)

    return [start(branch + 1), start(leaves_ref[2 * branch]), start(leaves_ref[2 * branch + 1])]


def transpose_into(target_ref, source_ref, part):
    for first in range(0, TREE_LEN, 512):
        piece = source_ref[part, pl.ds(first, 512), :].astype(F32)
        target_ref[:, pl.ds(first, 512)] = piece.T.astype(BF16)


def widen(piece, first, width, fill):
    parts = []
    if first:
        parts.append(jnp.full((piece.shape[0], first), fill, piece.dtype))
    parts.append(piece)
    rest = width - first - piece.shape[1]
    if rest:
        parts.append(jnp.full((piece.shape[0], rest), fill, piece.dtype))
    return parts[0] if len(parts) == 1 else jnp.concatenate(parts, axis=1)


def trunk_groups(block):
    first = block * QROWS
    groups = [(0, first, 0, QROWS, None)] if first else []
    return groups + [(first, QROWS, 0, QROWS, "causal")]


def team_rows(leaves_ref, team):
    return family_rows(leaves_ref, 2 * team) + family_rows(leaves_ref, 2 * team + 1)


def team_groups(starts):
    groups = [(0, TRUNK, 0, TEAM, None)]
    for first in range(0, TEAM, FAMILY):
        at = first // SEG
        groups.append((starts[at], SEG, first, first + FAMILY, "branch"))
        for leaf in (1, 2):
            begin = first + leaf * SEG
            groups.append((starts[at + leaf], SEG, begin, begin + SEG, "causal"))
    return groups


def masked_scores(keys, queries, rule):
    scores = dot_nt(keys, queries)
    if rule == "causal":
        return causal(scores)
    if rule == "branch":
        return jnp.concatenate([causal(scores[:, :SEG]), scores[:, SEG:]], axis=1)
    return scores


def forward_block(qkv_ref, values_t_ref, queries, groups):
    width = queries.shape[0]
    outs, logs = [], []
    for head in range(2):
        own = head_lanes(queries, head)
        all_scores = [
            masked_scores(qkv_ref[1, pl.ds(start, size), :], own[first:last], rule)
            for start, size, first, last, rule in groups
        ]
        top = functools.reduce(
            jnp.maximum,
            [
                widen(jnp.max(s, axis=0, keepdims=True), first, width, NEGATIVE_FILL)
                for s, (_, _, first, last, _) in zip(all_scores, groups)
            ],
        )
        total, output = None, None
        for s, (start, size, first, last, _) in zip(all_scores, groups):
            weights = jnp.exp(s - top[:, first:last])
            part = widen(jnp.sum(weights, axis=0, keepdims=True), first, width, 0.0)
            values_t = values_t_ref[pl.ds(head * HEAD_DIM, HEAD_DIM), pl.ds(start, size)]
            mixed = widen(dot_nn(values_t, weights.astype(BF16)), first, width, 0.0)
            total = part if total is None else total + part
            output = mixed if output is None else output + mixed
        outs.append(output / total)
        logs.append(top + jnp.log(total))
    return jnp.concatenate(outs, axis=0).T.astype(BF16), jnp.concatenate(logs, axis=0)


def scaled_queries(qkv_ref, starts, size):
    rows = [qkv_ref[0, pl.ds(start, size), :] for start in starts]
    rows = rows[0] if len(rows) == 1 else jnp.concatenate(rows, axis=0)
    return rows * jnp.asarray(HEAD_DIM ** (-0.5), BF16)


def quarter_rows(leaves_ref, offset):
    quarter = TREE_LEN // 4
    return pl.ds(pl.multiple_of((leaves_ref[2 * BRANCHES] ^ offset) * quarter, quarter), quarter)


def forward_kernel(
    leaves_ref,
    near_ref,
    far_ref,
    near_out_ref,
    far_out_ref,
    trunk_log_ref,
    family_log_ref,
    qkv_ref,
    out_ref,
    values_t_ref,
):
    for offset in range(4):
        half_ref = near_ref if offset < 2 else far_ref
        qkv_ref[:, quarter_rows(leaves_ref, offset), :] = half_ref[:, offset % 2]
    transpose_into(values_t_ref, qkv_ref, 2)
    for block in range(TRUNK // QROWS):
        first = block * QROWS
        queries = scaled_queries(qkv_ref, [first], QROWS)
        out, logs = forward_block(qkv_ref, values_t_ref, queries, trunk_groups(block))
        out_ref[pl.ds(first, QROWS), :] = out
        trunk_log_ref[0, :, pl.ds(first, QROWS)] = logs

    def one_team(team, carry):
        starts = team_rows(leaves_ref, team)
        queries = scaled_queries(qkv_ref, starts, SEG)
        out, logs = forward_block(qkv_ref, values_t_ref, queries, team_groups(starts))
        for place, start in enumerate(starts):
            out_ref[pl.ds(start, SEG), :] = out[place * SEG : (place + 1) * SEG]
        family_log_ref[0, team] = logs
        return carry

    lax.fori_loop(0, TEAMS, one_team, 0)
    for offset in range(4):
        half_ref = near_out_ref if offset < 2 else far_out_ref
        half_ref[offset % 2] = out_ref[quarter_rows(leaves_ref, offset), :]


def halves_spec(parts):
    quarter = TREE_LEN // 4
    if parts == 1:
        return pl.BlockSpec((2, quarter, PAIR), lambda p, leaves: (0, 0, p))
    return pl.BlockSpec((parts, 2, quarter, PAIR), lambda p, leaves: (0, 0, 0, p))


def attention_cost(products, cover):
    visited = (TRUNK * (TRUNK + QROWS) // 2 + BRANCHES * FAMILY * (TRUNK + SEG)) // cover
    return pl.CostEstimate(
        flops=2 * products * 4 * visited * 2 * PAIR,
        transcendentals=4 * visited,
        bytes_accessed=8 * TREE_LEN * 4 * HEAD_DIM * 2 // cover,
    )


def attention_forward(leaves, near, far):
    width = near.shape[3]
    quarter = TREE_LEN // 4
    pairs = width // PAIR
    return pl.pallas_call(
        forward_kernel,
        grid_spec=pltpu.PrefetchScalarGridSpec(
            num_scalar_prefetch=1,
            grid=(pairs,),
            in_specs=[halves_spec(3), halves_spec(3)],
            out_specs=[
                halves_spec(1),
                halves_spec(1),
                pl.BlockSpec((1, 2, TRUNK), lambda p, leaves: (p, 0, 0)),
                pl.BlockSpec((1, TEAMS, 2, TEAM), lambda p, leaves: (p, 0, 0, 0)),
            ],
            scratch_shapes=[
                pltpu.VMEM((3, TREE_LEN, PAIR), BF16),
                pltpu.VMEM((TREE_LEN, PAIR), BF16),
                pltpu.VMEM((PAIR, TREE_LEN), BF16),
            ],
        ),
        out_shape=[
            jax.ShapeDtypeStruct((2, quarter, width), BF16),
            jax.ShapeDtypeStruct((2, quarter, width), BF16),
            jax.ShapeDtypeStruct((pairs, 2, TRUNK), F32),
            jax.ShapeDtypeStruct((pairs, TEAMS, 2, TEAM), F32),
        ],
        cost_estimate=attention_cost(2, COVER),
        name="tree_attention",
    )(leaves, near, far)


def backward_block(qkv_ref, keys_t_ref, queries, grads, outs, logs, groups):
    products = grads.astype(F32) * outs.astype(F32)
    products_t = products.T
    key_ds = [[] for _ in groups]
    value_ws = [[] for _ in groups]
    own_q, own_g, query_grads = [], [], []
    for head in range(2):
        own = head_lanes(queries, head)
        own_grads = head_lanes(grads, head)
        own_q.append(own)
        own_g.append(own_grads)
        inner = jnp.sum(
            products_t[head * HEAD_DIM : (head + 1) * HEAD_DIM], axis=0, keepdims=True
        )
        log = logs[head : head + 1]
        query_grad = None
        for place, (start, size, first, last, rule) in enumerate(groups):
            scores = masked_scores(qkv_ref[1, pl.ds(start, size), :], own[first:last], rule)
            weights = jnp.exp(scores - log[:, first:last])
            grad_weights = dot_nt(qkv_ref[2, pl.ds(start, size), :], own_grads[first:last])
            grad_scores = (weights * (grad_weights - inner[:, first:last])).astype(BF16)
            keys_t = keys_t_ref[pl.ds(head * HEAD_DIM, HEAD_DIM), pl.ds(start, size)]
            part = widen(dot_nn(keys_t, grad_scores), first, queries.shape[0], 0.0)
            query_grad = part if query_grad is None else query_grad + part
            key_ds[place].append(grad_scores)
            value_ws[place].append(weights.astype(BF16))
        query_grads.append(query_grad)
    grad_query = (jnp.concatenate(query_grads, axis=0) * HEAD_DIM ** (-0.5)).T.astype(BF16)
    key_grads, value_grads = [], []
    for place, (start, size, first, last, rule) in enumerate(groups):
        stacked_q = jnp.concatenate([own_q[0][first:last], own_q[1][first:last]], axis=0)
        stacked_g = jnp.concatenate([own_g[0][first:last], own_g[1][first:last]], axis=0)
        key_grads.append(dot_nn(jnp.concatenate(key_ds[place], axis=1), stacked_q))
        value_grads.append(dot_nn(jnp.concatenate(value_ws[place], axis=1), stacked_g))
    return grad_query, key_grads, value_grads


def backward_kernel(
    leaves_ref,
    near_ref,
    far_ref,
    near_grads_ref,
    far_grads_ref,
    near_outs_ref,
    far_outs_ref,
    trunk_log_ref,
    family_log_ref,
    near_result_ref,
    far_result_ref,
    qkv_ref,
    grads_ref,
    outs_ref,
    result_ref,
    keys_t_ref,
    trunk_keys_ref,
    trunk_values_ref,
):
    for offset in range(4):
        rows = quarter_rows(leaves_ref, offset)
        at = offset % 2
        qkv_ref[:, rows, :] = (near_ref if offset < 2 else far_ref)[:, at]
        grads_ref[rows, :] = (near_grads_ref if offset < 2 else far_grads_ref)[at]
        outs_ref[rows, :] = (near_outs_ref if offset < 2 else far_outs_ref)[at]
    transpose_into(keys_t_ref, qkv_ref, 1)
    trunk_keys_ref[...] = jnp.zeros_like(trunk_keys_ref)
    trunk_values_ref[...] = jnp.zeros_like(trunk_values_ref)
    for block in range(TRUNK // QROWS):
        first = block * QROWS
        rows = pl.ds(first, QROWS)
        groups = trunk_groups(block)
        grad_query, key_grads, value_grads = backward_block(
            qkv_ref,
            keys_t_ref,
            scaled_queries(qkv_ref, [first], QROWS),
            grads_ref[rows, :],
            outs_ref[rows, :],
            trunk_log_ref[0, :, rows],
            groups,
        )
        result_ref[0, rows, :] = grad_query
        for (start, size, _, _, _), key_grad, value_grad in zip(groups, key_grads, value_grads):
            trunk_keys_ref[pl.ds(start, size), :] += key_grad
            trunk_values_ref[pl.ds(start, size), :] += value_grad

    def one_team(team, carry):
        starts = team_rows(leaves_ref, team)
        groups = team_groups(starts)
        grad_query, key_grads, value_grads = backward_block(
            qkv_ref,
            keys_t_ref,
            scaled_queries(qkv_ref, starts, SEG),
            jnp.concatenate([grads_ref[pl.ds(start, SEG), :] for start in starts], axis=0),
            jnp.concatenate([outs_ref[pl.ds(start, SEG), :] for start in starts], axis=0),
            family_log_ref[0, team],
            groups,
        )
        trunk_keys_ref[...] += key_grads[0]
        trunk_values_ref[...] += value_grads[0]
        for place, start in enumerate(starts):
            rows = pl.ds(start, SEG)
            result_ref[0, rows, :] = grad_query[place * SEG : (place + 1) * SEG]
            result_ref[1, rows, :] = key_grads[1 + place].astype(BF16)
            result_ref[2, rows, :] = value_grads[1 + place].astype(BF16)
        return carry

    lax.fori_loop(0, TEAMS, one_team, 0)
    result_ref[1, pl.ds(0, TRUNK), :] = trunk_keys_ref[...].astype(BF16)
    result_ref[2, pl.ds(0, TRUNK), :] = trunk_values_ref[...].astype(BF16)
    for offset in range(4):
        half_ref = near_result_ref if offset < 2 else far_result_ref
        rows = quarter_rows(leaves_ref, offset)
        for part in range(3):
            half_ref[offset % 2, :, part * PAIR : (part + 1) * PAIR] = result_ref[part, rows, :]


def attention_backward(leaves, pair, near, far, near_grads, far_grads, near_outs, far_outs, logs):
    quarter = TREE_LEN // 4
    rows = pl.BlockSpec((2, quarter, PAIR), lambda i, leaves: (0, 0, pair))
    parts = pl.BlockSpec((3, 2, quarter, PAIR), lambda i, leaves: (0, 0, 0, pair))
    result = pl.BlockSpec((2, quarter, 3 * PAIR), lambda i, leaves: (0, 0, 0))
    shape = jax.ShapeDtypeStruct((2, quarter, 3 * PAIR), BF16)
    return pl.pallas_call(
        backward_kernel,
        grid_spec=pltpu.PrefetchScalarGridSpec(
            num_scalar_prefetch=1,
            grid=(1,),
            in_specs=[
                parts,
                parts,
                rows,
                rows,
                rows,
                rows,
                pl.BlockSpec((1, 2, TRUNK), lambda i, leaves: (pair, 0, 0)),
                pl.BlockSpec((1, TEAMS, 2, TEAM), lambda i, leaves: (pair, 0, 0, 0)),
            ],
            out_specs=[result, result],
            scratch_shapes=[
                pltpu.VMEM((3, TREE_LEN, PAIR), BF16),
                pltpu.VMEM((TREE_LEN, PAIR), BF16),
                pltpu.VMEM((TREE_LEN, PAIR), BF16),
                pltpu.VMEM((3, TREE_LEN, PAIR), BF16),
                pltpu.VMEM((PAIR, TREE_LEN), BF16),
                pltpu.VMEM((TRUNK, PAIR), F32),
                pltpu.VMEM((TRUNK, PAIR), F32),
            ],
        ),
        out_shape=[shape, shape],
        cost_estimate=attention_cost(5, 10),
        name="tree_attention_back",
    )(leaves, near, far, near_grads, far_grads, near_outs, far_outs, *logs)


def leaf_order(parents_row):
    first_leaf = BRANCHES + 1
    leaf_parents = parents_row[first_leaf:]
    segments = first_leaf + jnp.arange(leaf_parents.shape[0], dtype=jnp.int32)
    same = leaf_parents[:, None] == leaf_parents[None, :]
    later = segments[None, :] < segments[:, None]
    place = 2 * (leaf_parents - 1) + jnp.sum(jnp.where(same & later, 1, 0), axis=1)
    slots = jnp.arange(2 * BRANCHES, dtype=jnp.int32)
    return jnp.sum(jnp.where(slots[:, None] == place[None, :], segments[None, :], 0), axis=1)


def gates(logits, experts, expert):
    lane = lax.broadcasted_iota(jnp.int32, logits.shape, 1)
    first, second = logits[:, experts : experts + 1], logits[:, experts + 1 : experts + 2]
    top = jnp.maximum(first, second)
    first, second = jnp.exp(first - top), jnp.exp(second - top)
    total = first + second
    first, second = first / total, second / total
    if expert is None:
        return lane, first, second, None, None
    routed = jnp.where(lane < experts, logits, NEGATIVE_FILL)
    raised = jnp.exp(routed - jnp.max(routed, axis=1, keepdims=True))
    probs = raised / jnp.sum(raised, axis=1, keepdims=True)
    gate = jnp.sum(jnp.where(lane == expert, probs, 0.0), axis=1, keepdims=True)
    return lane, first, second, probs, gate


def both(own_ref, side_ref):
    return jnp.concatenate([own_ref[...], side_ref[...]], axis=0)


def split_store(own_ref, side_ref, rows):
    half = rows.shape[0] // 2
    own_ref[...] = rows[:half]
    side_ref[...] = rows[half:]


def feed_kernel(
    experts,
    routed,
    expert_ref,
    own_ref,
    side_ref,
    own_grads_ref,
    side_grads_ref,
    head_ref,
    up_ref,
    down_ref,
    own_out_ref,
    side_out_ref,
    own_back_ref,
    side_back_ref,
    active_ref,
    pre_ref,
    grad_ref,
    head_grad_ref,
):
    rows = both(own_ref, side_ref)
    grads = both(own_grads_ref, side_grads_ref).astype(F32)
    expert = expert_ref[0] if routed else None
    logits = dot_nn(rows, head_ref[...])
    lane, first, second, probs, gate = gates(logits, experts, expert)
    coef = second * gate if routed else first
    weighted = (coef * grads).astype(BF16)
    pre = dot_nn(rows, up_ref[...])
    grad_active = dot_nt(weighted, down_ref[...])
    cumulative = 0.5 + 0.5 * lax.erf(pre * 0.7071067811865476)
    slope = cumulative + pre * jnp.exp(-0.5 * pre * pre) * 0.3989422804014327
    active = (pre * cumulative).astype(BF16)
    grad_pre = (grad_active * slope).astype(BF16)
    half = rows.shape[0] // 2
    for ref, value in ((active_ref, active), (pre_ref, grad_pre), (grad_ref, weighted)):
        ref[0] = value[:half]
        ref[1] = value[half:]
    out = dot_nn(active, down_ref[...])
    split_store(own_out_ref, side_out_ref, (coef * out).astype(BF16))
    inner = jnp.sum(grads * out, axis=1, keepdims=True)
    swing = first * second * inner
    if routed:
        swing = -gate * swing
    grad_logits = jnp.where(lane == experts, swing, jnp.where(lane == experts + 1, -swing, 0.0))
    if routed:
        picked = jnp.where(lane == expert, 1.0, 0.0) - gate
        grad_logits = grad_logits + jnp.where(
            lane < experts, probs * picked * (second * inner), 0.0
        )
    back = dot_nt(grad_pre, up_ref[...]) + dot_nt(grad_logits.astype(BF16), head_ref[...])
    split_store(own_back_ref, side_back_ref, back.astype(BF16))
    head_grad = dot_nn(grad_logits.T.astype(BF16), rows)

    @pl.when(pl.program_id(0) == 0)
    def _():
        head_grad_ref[...] = jnp.zeros_like(head_grad_ref)

    head_grad_ref[...] += head_grad


def feed(own, side, own_grads, side_grads, head, up, down, experts, expert, size):
    count = own.shape[0]
    width, hidden = up.shape
    steps = count // size
    lanes = head.shape[1]
    routed = expert is not None
    pick = jnp.reshape(expert, (1,)) if routed else jnp.zeros((1,), jnp.int32)
    rows = pl.BlockSpec((size, width), lambda i, pick: (i, 0))

    def whole(shape):
        return pl.BlockSpec(shape, lambda i, pick: (0, 0), pipeline_mode=pl.Buffered(1))

    def pairs(columns):
        return pl.BlockSpec((2, size, columns), lambda i, pick: (0, i, 0))

    quarter = jax.ShapeDtypeStruct((count, width), BF16)
    *sums, active, pre, weighted, head_grad = pl.pallas_call(
        functools.partial(feed_kernel, experts, routed),
        grid_spec=pltpu.PrefetchScalarGridSpec(
            num_scalar_prefetch=1,
            grid=(steps,),
            in_specs=[
                rows,
                rows,
                rows,
                rows,
                whole((width, lanes)),
                whole((width, hidden)),
                whole((hidden, width)),
            ],
            out_specs=[
                rows,
                rows,
                rows,
                rows,
                pairs(hidden),
                pairs(hidden),
                pairs(width),
                pl.BlockSpec((lanes, width), lambda i, pick: (0, 0)),
            ],
        ),
        out_shape=[
            quarter,
            quarter,
            quarter,
            quarter,
            jax.ShapeDtypeStruct((2, count, hidden), BF16),
            jax.ShapeDtypeStruct((2, count, hidden), BF16),
            jax.ShapeDtypeStruct((2, count, width), BF16),
            jax.ShapeDtypeStruct((lanes, width), F32),
        ],
        cost_estimate=pl.CostEstimate(
            flops=16 * count * width * hidden // COVER,
            transcendentals=4 * count * hidden // COVER,
            bytes_accessed=2 * (8 * count * width + 4 * count * hidden + 2 * width * hidden) // COVER,
        ),
        compiler_params=pltpu.CompilerParams(vmem_limit_bytes=60 * 1024 * 1024),
        name="feed_routed" if routed else "feed_dense",
    )(pick, own, side, own_grads, side_grads, head, up, down)
    flat = [value.reshape(2 * count, value.shape[2]) for value in (active, pre, weighted)]
    return [*sums, *flat, head_grad]


LANES = 128
QUARTER_ROWS = 128


def norm_parts(values):
    row_mean = jnp.mean(values, axis=-1, keepdims=True)
    centred = values - row_mean
    row_var = jnp.mean(centred * centred, axis=-1, keepdims=True)
    inverse = lax.rsqrt(row_var + EPSILON)
    return (centred * inverse, inverse)


def norm_back(grad_normed, gain_vec, scaled, inverse):
    grad_scaled = grad_normed * gain_vec
    first_mean = jnp.mean(grad_scaled, axis=-1, keepdims=True)
    second = jnp.mean(grad_scaled * scaled, axis=-1, keepdims=True)
    return inverse * (grad_scaled - first_mean - scaled * second)


def after(value, *others):
    return lax.optimization_barrier((value, *others))[0]


def from_side(values):
    return lax.ppermute(values, "tensor", [(i, i ^ 1) for i in range(4)])


def from_far(values):
    return lax.ppermute(values, "tensor", [(i, i ^ 2) for i in range(4)])


def plus_side(own, side):
    return own.astype(F32) + from_side(side.astype(BF16)).astype(F32)


def sum_over(values, axis):
    count, step = lax.axis_size(axis), 1
    while step < count:
        pairs = [(i, i ^ step) for i in range(count)]
        values = values + lax.ppermute(values, axis, pairs)
        step *= 2
    return values


def exchange(blocks):
    return lax.all_to_all(blocks, "expert", split_axis=0, concat_axis=0, tiled=True)


def scatter_sum(strips):
    strips = with_layout_constraint(strips.astype(BF16), Layout(major_to_minor=(0, 1)))
    return lax.psum_scatter(strips, "expert", scatter_dimension=0, tiled=True)


def strips_sent(grads):
    return exchange(grads.reshape(lax.axis_size("expert"), -1, grads.shape[1]))


def strips_total(strips):
    return jnp.sum(strips.astype(F32), axis=0)


def slots_of(expert_ids, experts, capacity):
    rows = expert_ids.shape[0]
    chosen = expert_ids[:, None] == jnp.arange(experts, dtype=jnp.int32)[None, :]
    at = jnp.arange(rows, dtype=jnp.int32)
    before = (at[None, :] < at[:, None]).astype(BF16)
    earlier = jnp.dot(before, chosen.astype(BF16), preferred_element_type=F32)
    slot = jnp.sum(jnp.where(chosen, earlier, 0.0), axis=1).astype(jnp.int32)
    place = expert_ids * capacity + slot
    places = jnp.arange(experts * capacity, dtype=jnp.int32)
    return (places[:, None] == place[None, :]).astype(BF16)


def per_device(
    tokens,
    cotangent,
    routes,
    parents,
    ln_attn,
    w_qkv,
    w_out,
    ln_mlp,
    w_up,
    w_down,
    w_router,
    w_mix,
    ex_up,
    ex_down,
):
    tok_dev, width = tokens.shape
    mine = lax.axis_index("tensor")
    experts = w_router.shape[1]
    capacity = max(2, tok_dev * 7 // (5 * experts))
    heads_width = w_qkv.shape[2]
    hidden = w_up.shape[1]
    leaves = jnp.concatenate([leaf_order(parents[0]), mine.astype(jnp.int32)[None]])

    scaled_one, inverse_one = norm_parts(tokens.astype(F32))
    normed_own = (scaled_one * ln_attn).astype(BF16)
    normed_far = from_far(normed_own)
    near_one = jnp.concatenate([normed_own, from_side(normed_own)], axis=0)

    quarter_ids = routes[:, 0].reshape(4, tok_dev)

    def slots_at(offset):
        ids = lax.dynamic_index_in_dim(quarter_ids, mine ^ offset, 0, keepdims=False)
        return slots_of(ids, experts, capacity)

    own_slots, far_slots = slots_at(0), slots_at(2)

    def placed(slots, rows):
        return jnp.dot(slots, rows, preferred_element_type=F32).astype(BF16)

    def sent(rows):
        return exchange(rows.reshape(experts, capacity, width)).reshape(-1, width)

    own_grads = sent(placed(own_slots, cotangent))
    cotangent_side = from_side(cotangent)

    def project(rows):
        qkv = jnp.einsum("td,sdc->stc", rows, w_qkv, preferred_element_type=F32)
        return qkv.astype(BF16).reshape(3, 2, tok_dev, heads_width)

    lanes = -(-(experts + 2) // LANES) * LANES
    head = jnp.concatenate(
        [w_router, w_mix, jnp.zeros((width, lanes - experts - 2), BF16)], axis=1
    )
    near_qkv = project(near_one)
    cotangent_far = from_far(after(cotangent, normed_far))
    normed_far, near_qkv, head = lax.optimization_barrier((normed_far, near_qkv, head))
    far_one = jnp.concatenate([normed_far, from_side(normed_far)], axis=0)
    far_qkv = project(far_one)
    near_out, far_out, *logs = attention_forward(leaves, near_qkv, far_qkv)
    far_out, own_grads, cotangent_far, cotangent_side = lax.optimization_barrier(
        (far_out, own_grads, cotangent_far, cotangent_side)
    )

    def branch_part(rows):
        return jnp.dot(rows, w_out, preferred_element_type=F32)

    far_sum = plus_side(branch_part(far_out[0]), branch_part(far_out[1])).astype(BF16)
    branch = plus_side(branch_part(near_out[0]), branch_part(near_out[1]))
    branch_far = from_far(far_sum)
    side_grads = from_side(own_grads)
    cotangent_corner = from_side(cotangent_far)
    far_placed = placed(far_slots, cotangent_far)
    branch_far, side_grads, cotangent_corner, far_placed = lax.optimization_barrier(
        (branch_far, side_grads, cotangent_corner, far_placed)
    )
    residual = tokens.astype(F32) + (branch + branch_far.astype(F32))

    scaled_two, inverse_two = norm_parts(residual)
    normed_two = (scaled_two * ln_mlp).astype(BF16)
    normed_two_far = from_far(normed_two)
    normed_two_side = from_side(normed_two)
    own_rows = sent(placed(own_slots, normed_two))

    def dense(own, side, own_cotangent, side_cotangent):
        return feed(
            own, side, own_cotangent, side_cotangent, head, w_up, w_down, experts, None, QUARTER_ROWS
        )

    def product(left, right):
        return jnp.einsum("gd,gf->df", left, right, preferred_element_type=F32)

    def weight_grads(near_left, far_left, near_right, far_right):
        return product(near_left, near_right) + product(far_left, far_right)

    near_dense = dense(normed_two, normed_two_side, cotangent, cotangent_side)
    near_two = jnp.concatenate([normed_two, normed_two_side], axis=0)
    grad_up = product(near_two, near_dense[5])
    grad_down = product(near_dense[6], near_dense[4])
    normed_two_far, grad_up, grad_down, own_rows = lax.optimization_barrier(
        (normed_two_far, grad_up, grad_down, own_rows)
    )
    far_rows = from_far(own_rows)
    far_grads = sent(after(far_placed, own_rows))
    normed_two_corner = from_side(normed_two_far)
    far_dense = list(dense(normed_two_far, normed_two_corner, cotangent_far, cotangent_corner))

    expert = lax.axis_index("expert").astype(jnp.int32)

    def routed(own, side, own_cotangent, side_cotangent):
        return feed(
            own,
            side,
            own_cotangent,
            side_cotangent,
            head,
            ex_up[0],
            ex_down[0],
            experts,
            expert,
            QUARTER_ROWS,
        )

    def chip_sum(parts, place, *others):
        return plus_side(parts[place], after(parts[place + 1], *others))

    def chip_sum(parts, place, *others):
        return plus_side(parts[place], after(parts[place + 1], *others))

    dense_back_far = chip_sum(far_dense, 2).astype(BF16)
    far_two = jnp.concatenate([normed_two_far, normed_two_corner], axis=0)
    grad_down = (grad_down + product(far_dense[6], far_dense[4])).astype(BF16)
    far_two, far_rows, grad_down = lax.optimization_barrier((far_two, far_rows, grad_down))
    grad_up = (grad_up + product(far_two, far_dense[5])).astype(BF16)
    dense_grads = after(jnp.concatenate([grad_up, grad_down], axis=1), far_grads)
    far_rows, dense_back_far, dense_grads = lax.optimization_barrier(
        (far_rows, dense_back_far, dense_grads)
    )
    dense_grads = scatter_sum(dense_grads)
    dense_back_far = from_far(dense_back_far)
    corner_rows = from_side(far_rows)
    side_rows = from_side(own_rows)
    far_expert = routed(far_rows, corner_rows, far_grads, from_side(far_grads))
    *far_expert, dense_back_far = lax.optimization_barrier((*far_expert, dense_back_far))
    far_back = chip_sum(far_expert, 2).astype(BF16)
    own_rows, far_back = lax.optimization_barrier((own_rows, far_back))
    near_expert = routed(own_rows, side_rows, own_grads, side_grads)
    *near_expert, dense_grads = lax.optimization_barrier((*near_expert, dense_grads))

    def picked(rows):
        return lax.dot_general(
            own_slots, rows, (((0,), (0,)), ((), ())), preferred_element_type=F32
        )

    expert_back = (chip_sum(near_expert, 2) + from_far(far_back).astype(F32)).astype(BF16)
    far_expert_out = chip_sum(far_expert, 0, expert_back).astype(BF16)
    dense_out_far = chip_sum(far_dense, 0, expert_back).astype(BF16)
    dense_back = chip_sum(near_dense, 2, far_back) + dense_back_far.astype(F32)

    grad_normed_two = dense_back + picked(sent(expert_back))
    dense_out = chip_sum(near_dense, 0, expert_back)
    expert_out = chip_sum(near_expert, 0, expert_back) + from_far(far_expert_out).astype(F32)
    expert_out = after(expert_out.astype(BF16), grad_normed_two)

    near_active, far_active, near_pre, far_pre, far_expert_out = lax.optimization_barrier(
        (near_expert[4], far_expert[4], near_expert[5], far_expert[5], far_expert_out)
    )
    near_tokens = jnp.concatenate([own_rows, side_rows], axis=0)
    far_tokens = jnp.concatenate([far_rows, corner_rows], axis=0)
    grad_ex_up = weight_grads(near_tokens, far_tokens, near_pre, far_pre)[None]
    grad_ex_down = weight_grads(near_active, far_active, near_expert[6], far_expert[6])[None]

    gain_two = jnp.sum(grad_normed_two * scaled_two, axis=0)
    grad_residual = cotangent.astype(F32) + norm_back(
        grad_normed_two, ln_mlp, scaled_two, inverse_two
    )
    grad_branch = grad_residual.astype(BF16)
    grad_branch_far = from_far(grad_branch)
    grad_branch_side = from_side(grad_branch)

    def into_heads(*rows):
        grads = [jnp.einsum("gd,cd->gc", part, w_out, preferred_element_type=F32) for part in rows]
        return jnp.stack(grads).astype(BF16)

    near_heads = into_heads(grad_branch, grad_branch_side)
    out_rows = sent(expert_out)
    flat = (2 * tok_dev, heads_width)
    near_branch = jnp.concatenate([grad_branch, grad_branch_side], axis=0)
    grad_w_out = product(near_branch, near_out.reshape(flat))
    grad_branch_far, near_heads, grad_w_out, grad_ex_up, grad_ex_down, _, dense_out_far, dense_out = (
        lax.optimization_barrier(
            (
                grad_branch_far,
                near_heads,
                grad_w_out,
                grad_ex_up,
                grad_ex_down,
                expert_out,
                dense_out_far,
                dense_out,
            )
        )
    )
    grad_branch_corner = from_side(grad_branch_far)
    far_heads = into_heads(grad_branch_far, grad_branch_corner)
    dense_out_far = from_far(dense_out_far)
    head_grads = near_dense[7] + far_dense[7] + near_expert[7] + far_expert[7]
    small = jnp.concatenate([head_grads[: experts + 2], gain_two[None]], axis=0)

    def pair_back(pair, near_grads, far_grads):
        return attention_backward(
            leaves, pair, near_qkv, far_qkv, near_grads, far_grads, near_out, far_out, logs
        )

    def pair_weights(pair):
        lanes = slice(pair * PAIR, (pair + 1) * PAIR)
        return jnp.concatenate([w_qkv[part, :, lanes] for part in range(3)], axis=1)

    def total(values):
        return functools.reduce(jnp.add, values)

    pairs = heads_width // PAIR
    near_results, far_results = [None] * pairs, [None] * pairs
    near_results[0], far_results[0] = pair_back(0, near_heads, far_heads)
    far_branch = jnp.concatenate([grad_branch_far, grad_branch_corner], axis=0)
    grad_w_out = grad_w_out + product(far_branch, far_out.reshape(flat))
    small_columns = -(-small.shape[0] // LANES) * LANES
    small_block = jnp.pad(small, ((0, small_columns - small.shape[0]), (0, 0))).T
    branch_grads = jnp.concatenate([grad_w_out.astype(BF16), small_block.astype(BF16)], axis=1)
    near_results[0], far_results[0], out_rows, dense_out_far, branch_grads, near_heads = (
        lax.optimization_barrier(
            (near_results[0], far_results[0], out_rows, dense_out_far, branch_grads, near_heads)
        )
    )
    branch_grads = strips_sent(branch_grads)
    for pair in range(1, pairs):
        near_results[pair], far_results[pair] = pair_back(pair, near_heads, far_heads)
    near_results, far_results, branch_grads = lax.optimization_barrier(
        (near_results, far_results, branch_grads)
    )

    def normed_part(results, quarter):
        return total([dot_nt(results[pair][quarter], pair_weights(pair)) for pair in range(pairs)])

    def qkv_weights(pair, *others):
        near_rows = near_results[pair].reshape(2 * tok_dev, 3 * PAIR)
        far_rows = far_results[pair].reshape(2 * tok_dev, 3 * PAIR)
        near_rows = after(near_rows, *others)
        return weight_grads(near_one, far_one, near_rows, far_rows).astype(BF16)

    corner_part = normed_part(far_results, 1).astype(BF16)
    from_corner = from_side(corner_part).astype(F32)
    first_grads = qkv_weights(0, corner_part)
    far_results, first_grads = lax.optimization_barrier((far_results, first_grads))
    qkv_grads = [strips_sent(first_grads)]
    far_sum = (normed_part(far_results, 0) + from_corner).astype(BF16)
    near_results, far_results, out_rows, far_sum = lax.optimization_barrier(
        (near_results, far_results, out_rows, far_sum)
    )
    near_sum = plus_side(normed_part(near_results, 0), normed_part(near_results, 1))
    out = (residual + dense_out + dense_out_far.astype(F32) + picked(out_rows)).astype(BF16)

    scaled_far = normed_far.astype(F32) / ln_attn
    gain_one = jnp.sum(
        near_sum * scaled_one + far_sum.astype(F32) * scaled_far, axis=0, keepdims=True
    )
    gain_one = sum_over(gain_one, "expert")
    last_grads = [qkv_weights(pair, far_sum) for pair in range(1, pairs)]
    qkv_grads += [strips_sent(grads) for grads in last_grads]
    far_arrived, gain_one, dense_grads, *_ = lax.optimization_barrier(
        (from_far(far_sum), gain_one, dense_grads, *last_grads)
    )
    grad_normed_one = near_sum + far_arrived.astype(F32)
    grad_ln_attn = sum_over(gain_one, "tensor")[0]
    branch_grads = strips_total(after(branch_grads, gain_one))
    small = sum_over(branch_grads[:, heads_width:], "tensor")
    qkv_grads = jnp.stack(
        [strips_total(grads).reshape(-1, 3, PAIR) for grads in qkv_grads], axis=2
    )
    grad_tokens = grad_residual + norm_back(grad_normed_one, ln_attn, scaled_one, inverse_one)

    strip = qkv_grads.shape[0]
    return (
        out,
        grad_tokens,
        grad_ln_attn,
        qkv_grads.reshape(strip, 3, heads_width).transpose(1, 0, 2),
        branch_grads[:, :heads_width].T,
        small[:, experts + 2],
        dense_grads[:, :hidden].astype(F32),
        dense_grads[:, hidden:].T.astype(F32),
        small[:, :experts],
        small[:, experts : experts + 2],
        grad_ex_up,
        grad_ex_down,
    )


def solution(mesh):
    return jax.shard_map(
        per_device,
        mesh=mesh,
        in_specs=(
            P(("expert", "tensor"), None),
            P(("expert", "tensor"), None),
            P("expert", None),
            P("expert", None),
            P(),
            P(None, None, "tensor"),
            P("tensor", None),
            P(),
            P(None, "tensor"),
            P("tensor", None),
            P(),
            P(),
            P("expert", None, "tensor"),
            P("expert", "tensor", None),
        ),
        out_specs=(
            P(("expert", "tensor"), None),
            P(("expert", "tensor"), None),
            P(),
            P(None, "expert", "tensor"),
            P("tensor", "expert"),
            P("expert"),
            P("expert", "tensor"),
            P("tensor", "expert"),
            P("expert", None),
            P("expert", None),
            P("expert", None, "tensor"),
            P("expert", "tensor", None),
        ),
        check_vma=False,
    )
```

```python
import functools

import jax
import jax.numpy as jnp
from jax import lax
from jax.experimental import pallas as pl
from jax.experimental.layout import Layout, with_layout_constraint
from jax.experimental.pallas import tpu as pltpu
from jax.sharding import PartitionSpec as P

HEAD_DIM = 64
TRUNK = 1024
SEG = 128
SEGS = 13
TREE_LEN = 2560
BRANCHES = 4
FAMILY = 3 * SEG
TEAM = 2 * FAMILY
TEAMS = BRANCHES // 2
QROWS = 256
COVER = 8
PAIR = 2 * HEAD_DIM
NEGATIVE_FILL = -1e30
F32 = jnp.float32
BF16 = jnp.bfloat16
EPSILON = 1e-05


def dot_nn(a, b):
    return lax.dot_general(a, b, (((1,), (0,)), ((), ())), preferred_element_type=F32)


def dot_nt(a, b):
    return lax.dot_general(a, b, (((1,), (1,)), ((), ())), preferred_element_type=F32)


def head_lanes(rows, head):
    lane = lax.broadcasted_iota(jnp.int32, rows.shape, 1)
    return jnp.where(lane // HEAD_DIM == head, rows, jnp.zeros_like(rows))


def causal(scores):
    key = lax.broadcasted_iota(jnp.int32, scores.shape, 0)
    query = lax.broadcasted_iota(jnp.int32, scores.shape, 1)
    return jnp.where(key <= query, scores, NEGATIVE_FILL)


def family_rows(leaves_ref, branch):
    def start(segment):
        return pl.multiple_of(TRUNK + (segment - 1) * SEG, SEG)

    return [start(branch + 1), start(leaves_ref[2 * branch]), start(leaves_ref[2 * branch + 1])]


def transpose_into(target_ref, source_ref, part):
    for first in range(0, TREE_LEN, 512):
        piece = source_ref[part, pl.ds(first, 512), :].astype(F32)
        target_ref[:, pl.ds(first, 512)] = piece.T.astype(BF16)


def widen(piece, first, width, fill):
    parts = []
    if first:
        parts.append(jnp.full((piece.shape[0], first), fill, piece.dtype))
    parts.append(piece)
    rest = width - first - piece.shape[1]
    if rest:
        parts.append(jnp.full((piece.shape[0], rest), fill, piece.dtype))
    return parts[0] if len(parts) == 1 else jnp.concatenate(parts, axis=1)


def trunk_groups(block):
    first = block * QROWS
    groups = [(0, first, 0, QROWS, None)] if first else []
    return groups + [(first, QROWS, 0, QROWS, "causal")]


def team_rows(leaves_ref, team):
    return family_rows(leaves_ref, 2 * team) + family_rows(leaves_ref, 2 * team + 1)


def team_groups(starts):
    groups = [(0, TRUNK, 0, TEAM, None)]
    for first in range(0, TEAM, FAMILY):
        at = first // SEG
        groups.append((starts[at], SEG, first, first + FAMILY, "branch"))
        for leaf in (1, 2):
            begin = first + leaf * SEG
            groups.append((starts[at + leaf], SEG, begin, begin + SEG, "causal"))
    return groups


def masked_scores(keys, queries, rule):
    scores = dot_nt(keys, queries)
    if rule == "causal":
        return causal(scores)
    if rule == "branch":
        return jnp.concatenate([causal(scores[:, :SEG]), scores[:, SEG:]], axis=1)
    return scores


def forward_block(qkv_ref, values_t_ref, queries, groups):
    width = queries.shape[0]
    outs, logs = [], []
    for head in range(2):
        own = head_lanes(queries, head)
        all_scores = [
            masked_scores(qkv_ref[1, pl.ds(start, size), :], own[first:last], rule)
            for start, size, first, last, rule in groups
        ]
        top = functools.reduce(
            jnp.maximum,
            [
                widen(jnp.max(s, axis=0, keepdims=True), first, width, NEGATIVE_FILL)
                for s, (_, _, first, last, _) in zip(all_scores, groups)
            ],
        )
        total, output = None, None
        for s, (start, size, first, last, _) in zip(all_scores, groups):
            weights = jnp.exp(s - top[:, first:last])
            part = widen(jnp.sum(weights, axis=0, keepdims=True), first, width, 0.0)
            values_t = values_t_ref[pl.ds(head * HEAD_DIM, HEAD_DIM), pl.ds(start, size)]
            mixed = widen(dot_nn(values_t, weights.astype(BF16)), first, width, 0.0)
            total = part if total is None else total + part
            output = mixed if output is None else output + mixed
        outs.append(output / total)
        logs.append(top + jnp.log(total))
    return jnp.concatenate(outs, axis=0).T.astype(BF16), jnp.concatenate(logs, axis=0)


def scaled_queries(qkv_ref, starts, size):
    rows = [qkv_ref[0, pl.ds(start, size), :] for start in starts]
    rows = rows[0] if len(rows) == 1 else jnp.concatenate(rows, axis=0)
    return rows * jnp.asarray(HEAD_DIM ** (-0.5), BF16)


def quarter_rows(leaves_ref, offset):
    quarter = TREE_LEN // 4
    return pl.ds(pl.multiple_of((leaves_ref[2 * BRANCHES] ^ offset) * quarter, quarter), quarter)


def forward_kernel(
    leaves_ref,
    near_ref,
    far_ref,
    corner_ref,
    near_out_ref,
    far_out_ref,
    trunk_log_ref,
    family_log_ref,
    qkv_ref,
    out_ref,
    values_t_ref,
):
    for offset in range(4):
        part = near_ref[:, offset] if offset < 2 else (far_ref, corner_ref)[offset - 2][...]
        qkv_ref[:, quarter_rows(leaves_ref, offset), :] = part
    transpose_into(values_t_ref, qkv_ref, 2)
    for block in range(TRUNK // QROWS):
        first = block * QROWS
        queries = scaled_queries(qkv_ref, [first], QROWS)
        out, logs = forward_block(qkv_ref, values_t_ref, queries, trunk_groups(block))
        out_ref[pl.ds(first, QROWS), :] = out
        trunk_log_ref[0, :, pl.ds(first, QROWS)] = logs

    def one_team(team, carry):
        starts = team_rows(leaves_ref, team)
        queries = scaled_queries(qkv_ref, starts, SEG)
        out, logs = forward_block(qkv_ref, values_t_ref, queries, team_groups(starts))
        for place, start in enumerate(starts):
            out_ref[pl.ds(start, SEG), :] = out[place * SEG : (place + 1) * SEG]
        family_log_ref[0, team] = logs
        return carry

    lax.fori_loop(0, TEAMS, one_team, 0)
    for offset in range(4):
        half_ref = near_out_ref if offset < 2 else far_out_ref
        half_ref[offset % 2] = out_ref[quarter_rows(leaves_ref, offset), :]


def lanes_spec(parts):
    quarter = TREE_LEN // 4
    return pl.BlockSpec((parts, quarter, PAIR), lambda p, leaves: (0, 0, p))


def attention_cost(products, cover):
    visited = (TRUNK * (TRUNK + QROWS) // 2 + BRANCHES * FAMILY * (TRUNK + SEG)) // cover
    return pl.CostEstimate(
        flops=2 * products * 4 * visited * 2 * PAIR,
        transcendentals=4 * visited,
        bytes_accessed=8 * TREE_LEN * 4 * HEAD_DIM * 2 // cover,
    )


def attention_forward(leaves, near, far, corner):
    width = near.shape[3]
    quarter = TREE_LEN // 4
    pairs = width // PAIR
    return pl.pallas_call(
        forward_kernel,
        grid_spec=pltpu.PrefetchScalarGridSpec(
            num_scalar_prefetch=1,
            grid=(pairs,),
            in_specs=[
                pl.BlockSpec((3, 2, quarter, PAIR), lambda p, leaves: (0, 0, 0, p)),
                lanes_spec(3),
                lanes_spec(3),
            ],
            out_specs=[
                lanes_spec(2),
                lanes_spec(2),
                pl.BlockSpec((1, 2, TRUNK), lambda p, leaves: (p, 0, 0)),
                pl.BlockSpec((1, TEAMS, 2, TEAM), lambda p, leaves: (p, 0, 0, 0)),
            ],
            scratch_shapes=[
                pltpu.VMEM((3, TREE_LEN, PAIR), BF16),
                pltpu.VMEM((TREE_LEN, PAIR), BF16),
                pltpu.VMEM((PAIR, TREE_LEN), BF16),
            ],
        ),
        out_shape=[
            jax.ShapeDtypeStruct((2, quarter, width), BF16),
            jax.ShapeDtypeStruct((2, quarter, width), BF16),
            jax.ShapeDtypeStruct((pairs, 2, TRUNK), F32),
            jax.ShapeDtypeStruct((pairs, TEAMS, 2, TEAM), F32),
        ],
        cost_estimate=attention_cost(2, COVER),
        name="tree_attention",
    )(leaves, near, far, corner)


def backward_block(qkv_ref, keys_t_ref, queries, grads, outs, logs, groups):
    products = grads.astype(F32) * outs.astype(F32)
    products_t = products.T
    key_ds = [[] for _ in groups]
    value_ws = [[] for _ in groups]
    own_q, own_g, query_grads = [], [], []
    for head in range(2):
        own = head_lanes(queries, head)
        own_grads = head_lanes(grads, head)
        own_q.append(own)
        own_g.append(own_grads)
        inner = jnp.sum(
            products_t[head * HEAD_DIM : (head + 1) * HEAD_DIM], axis=0, keepdims=True
        )
        log = logs[head : head + 1]
        query_grad = None
        for place, (start, size, first, last, rule) in enumerate(groups):
            scores = masked_scores(qkv_ref[1, pl.ds(start, size), :], own[first:last], rule)
            weights = jnp.exp(scores - log[:, first:last])
            grad_weights = dot_nt(qkv_ref[2, pl.ds(start, size), :], own_grads[first:last])
            grad_scores = (weights * (grad_weights - inner[:, first:last])).astype(BF16)
            keys_t = keys_t_ref[pl.ds(head * HEAD_DIM, HEAD_DIM), pl.ds(start, size)]
            part = widen(dot_nn(keys_t, grad_scores), first, queries.shape[0], 0.0)
            query_grad = part if query_grad is None else query_grad + part
            key_ds[place].append(grad_scores)
            value_ws[place].append(weights.astype(BF16))
        query_grads.append(query_grad)
    grad_query = (jnp.concatenate(query_grads, axis=0) * HEAD_DIM ** (-0.5)).T.astype(BF16)
    key_grads, value_grads = [], []
    for place, (start, size, first, last, rule) in enumerate(groups):
        stacked_q = jnp.concatenate([own_q[0][first:last], own_q[1][first:last]], axis=0)
        stacked_g = jnp.concatenate([own_g[0][first:last], own_g[1][first:last]], axis=0)
        key_grads.append(dot_nn(jnp.concatenate(key_ds[place], axis=1), stacked_q))
        value_grads.append(dot_nn(jnp.concatenate(value_ws[place], axis=1), stacked_g))
    return grad_query, key_grads, value_grads


def backward_kernel(
    leaves_ref,
    near_ref,
    far_ref,
    corner_ref,
    near_grads_ref,
    far_grads_ref,
    near_outs_ref,
    far_outs_ref,
    trunk_log_ref,
    family_log_ref,
    near_result_ref,
    far_result_ref,
    qkv_ref,
    grads_ref,
    outs_ref,
    result_ref,
    keys_t_ref,
    trunk_keys_ref,
    trunk_values_ref,
):
    for offset in range(4):
        rows = quarter_rows(leaves_ref, offset)
        at = offset % 2
        part = near_ref[:, at] if offset < 2 else (far_ref, corner_ref)[at][...]
        qkv_ref[:, rows, :] = part
        grads_ref[rows, :] = (near_grads_ref if offset < 2 else far_grads_ref)[at]
        outs_ref[rows, :] = (near_outs_ref if offset < 2 else far_outs_ref)[at]
    transpose_into(keys_t_ref, qkv_ref, 1)
    trunk_keys_ref[...] = jnp.zeros_like(trunk_keys_ref)
    trunk_values_ref[...] = jnp.zeros_like(trunk_values_ref)
    for block in range(TRUNK // QROWS):
        first = block * QROWS
        rows = pl.ds(first, QROWS)
        groups = trunk_groups(block)
        grad_query, key_grads, value_grads = backward_block(
            qkv_ref,
            keys_t_ref,
            scaled_queries(qkv_ref, [first], QROWS),
            grads_ref[rows, :],
            outs_ref[rows, :],
            trunk_log_ref[0, :, rows],
            groups,
        )
        result_ref[0, rows, :] = grad_query
        for (start, size, _, _, _), key_grad, value_grad in zip(groups, key_grads, value_grads):
            trunk_keys_ref[pl.ds(start, size), :] += key_grad
            trunk_values_ref[pl.ds(start, size), :] += value_grad

    def one_team(team, carry):
        starts = team_rows(leaves_ref, team)
        groups = team_groups(starts)
        grad_query, key_grads, value_grads = backward_block(
            qkv_ref,
            keys_t_ref,
            scaled_queries(qkv_ref, starts, SEG),
            jnp.concatenate([grads_ref[pl.ds(start, SEG), :] for start in starts], axis=0),
            jnp.concatenate([outs_ref[pl.ds(start, SEG), :] for start in starts], axis=0),
            family_log_ref[0, team],
            groups,
        )
        trunk_keys_ref[...] += key_grads[0]
        trunk_values_ref[...] += value_grads[0]
        for place, start in enumerate(starts):
            rows = pl.ds(start, SEG)
            result_ref[0, rows, :] = grad_query[place * SEG : (place + 1) * SEG]
            result_ref[1, rows, :] = key_grads[1 + place].astype(BF16)
            result_ref[2, rows, :] = value_grads[1 + place].astype(BF16)
        return carry

    lax.fori_loop(0, TEAMS, one_team, 0)
    result_ref[1, pl.ds(0, TRUNK), :] = trunk_keys_ref[...].astype(BF16)
    result_ref[2, pl.ds(0, TRUNK), :] = trunk_values_ref[...].astype(BF16)
    for offset in range(4):
        half_ref = near_result_ref if offset < 2 else far_result_ref
        rows = quarter_rows(leaves_ref, offset)
        for part in range(3):
            half_ref[offset % 2, :, part * PAIR : (part + 1) * PAIR] = result_ref[part, rows, :]


def attention_backward(leaves, pair, qkv, near_grads, far_grads, near_outs, far_outs, logs):
    quarter = TREE_LEN // 4
    rows = pl.BlockSpec((2, quarter, PAIR), lambda i, leaves: (0, 0, pair))
    parts = pl.BlockSpec((3, quarter, PAIR), lambda i, leaves: (0, 0, pair))
    result = pl.BlockSpec((2, quarter, 3 * PAIR), lambda i, leaves: (0, 0, 0))
    shape = jax.ShapeDtypeStruct((2, quarter, 3 * PAIR), BF16)
    return pl.pallas_call(
        backward_kernel,
        grid_spec=pltpu.PrefetchScalarGridSpec(
            num_scalar_prefetch=1,
            grid=(1,),
            in_specs=[
                pl.BlockSpec((3, 2, quarter, PAIR), lambda i, leaves: (0, 0, 0, pair)),
                parts,
                parts,
                rows,
                rows,
                rows,
                rows,
                pl.BlockSpec((1, 2, TRUNK), lambda i, leaves: (pair, 0, 0)),
                pl.BlockSpec((1, TEAMS, 2, TEAM), lambda i, leaves: (pair, 0, 0, 0)),
            ],
            out_specs=[result, result],
            scratch_shapes=[
                pltpu.VMEM((3, TREE_LEN, PAIR), BF16),
                pltpu.VMEM((TREE_LEN, PAIR), BF16),
                pltpu.VMEM((TREE_LEN, PAIR), BF16),
                pltpu.VMEM((3, TREE_LEN, PAIR), BF16),
                pltpu.VMEM((PAIR, TREE_LEN), BF16),
                pltpu.VMEM((TRUNK, PAIR), F32),
                pltpu.VMEM((TRUNK, PAIR), F32),
            ],
        ),
        out_shape=[shape, shape],
        cost_estimate=attention_cost(5, 10),
        name="tree_attention_back",
    )(leaves, *qkv, near_grads, far_grads, near_outs, far_outs, *logs)


def leaf_order(parents_row):
    first_leaf = BRANCHES + 1
    leaf_parents = parents_row[first_leaf:]
    segments = first_leaf + jnp.arange(leaf_parents.shape[0], dtype=jnp.int32)
    same = leaf_parents[:, None] == leaf_parents[None, :]
    later = segments[None, :] < segments[:, None]
    place = 2 * (leaf_parents - 1) + jnp.sum(jnp.where(same & later, 1, 0), axis=1)
    slots = jnp.arange(2 * BRANCHES, dtype=jnp.int32)
    return jnp.sum(jnp.where(slots[:, None] == place[None, :], segments[None, :], 0), axis=1)


def gates(logits, experts, expert):
    lane = lax.broadcasted_iota(jnp.int32, logits.shape, 1)
    first, second = logits[:, experts : experts + 1], logits[:, experts + 1 : experts + 2]
    top = jnp.maximum(first, second)
    first, second = jnp.exp(first - top), jnp.exp(second - top)
    total = first + second
    first, second = first / total, second / total
    if expert is None:
        return lane, first, second, None, None
    routed = jnp.where(lane < experts, logits, NEGATIVE_FILL)
    raised = jnp.exp(routed - jnp.max(routed, axis=1, keepdims=True))
    probs = raised / jnp.sum(raised, axis=1, keepdims=True)
    gate = jnp.sum(jnp.where(lane == expert, probs, 0.0), axis=1, keepdims=True)
    return lane, first, second, probs, gate


def both(own_ref, side_ref):
    return jnp.concatenate([own_ref[...], side_ref[...]], axis=0)


def split_store(own_ref, side_ref, rows):
    half = rows.shape[0] // 2
    own_ref[...] = rows[:half]
    side_ref[...] = rows[half:]


def feed_kernel(
    experts,
    routed,
    expert_ref,
    own_ref,
    side_ref,
    own_grads_ref,
    side_grads_ref,
    head_ref,
    up_ref,
    down_ref,
    own_out_ref,
    side_out_ref,
    own_back_ref,
    side_back_ref,
    active_ref,
    pre_ref,
    grad_ref,
    head_grad_ref,
):
    rows = both(own_ref, side_ref)
    grads = both(own_grads_ref, side_grads_ref).astype(F32)
    expert = expert_ref[0] if routed else None
    logits = dot_nn(rows, head_ref[...])
    lane, first, second, probs, gate = gates(logits, experts, expert)
    coef = second * gate if routed else first
    weighted = (coef * grads).astype(BF16)
    pre = dot_nn(rows, up_ref[...])
    grad_active = dot_nt(weighted, down_ref[...])
    cumulative = 0.5 + 0.5 * lax.erf(pre * 0.7071067811865476)
    slope = cumulative + pre * jnp.exp(-0.5 * pre * pre) * 0.3989422804014327
    active = (pre * cumulative).astype(BF16)
    grad_pre = (grad_active * slope).astype(BF16)
    half = rows.shape[0] // 2
    for ref, value in ((active_ref, active), (pre_ref, grad_pre), (grad_ref, weighted)):
        ref[0] = value[:half]
        ref[1] = value[half:]
    out = dot_nn(active, down_ref[...])
    split_store(own_out_ref, side_out_ref, (coef * out).astype(BF16))
    inner = jnp.sum(grads * out, axis=1, keepdims=True)
    swing = first * second * inner
    if routed:
        swing = -gate * swing
    grad_logits = jnp.where(lane == experts, swing, jnp.where(lane == experts + 1, -swing, 0.0))
    if routed:
        picked = jnp.where(lane == expert, 1.0, 0.0) - gate
        grad_logits = grad_logits + jnp.where(
            lane < experts, probs * picked * (second * inner), 0.0
        )
    back = dot_nt(grad_pre, up_ref[...]) + dot_nt(grad_logits.astype(BF16), head_ref[...])
    split_store(own_back_ref, side_back_ref, back.astype(BF16))
    head_grad = dot_nn(grad_logits.T.astype(BF16), rows)

    @pl.when(pl.program_id(0) == 0)
    def _():
        head_grad_ref[...] = jnp.zeros_like(head_grad_ref)

    head_grad_ref[...] += head_grad


def feed(own, side, own_grads, side_grads, head, up, down, experts, expert, size):
    count = own.shape[0]
    width, hidden = up.shape
    steps = count // size
    lanes = head.shape[1]
    routed = expert is not None
    pick = jnp.reshape(expert, (1,)) if routed else jnp.zeros((1,), jnp.int32)
    rows = pl.BlockSpec((size, width), lambda i, pick: (i, 0))

    def whole(shape):
        return pl.BlockSpec(shape, lambda i, pick: (0, 0), pipeline_mode=pl.Buffered(1))

    def pairs(columns):
        return pl.BlockSpec((2, size, columns), lambda i, pick: (0, i, 0))

    quarter = jax.ShapeDtypeStruct((count, width), BF16)
    *sums, active, pre, weighted, head_grad = pl.pallas_call(
        functools.partial(feed_kernel, experts, routed),
        grid_spec=pltpu.PrefetchScalarGridSpec(
            num_scalar_prefetch=1,
            grid=(steps,),
            in_specs=[
                rows,
                rows,
                rows,
                rows,
                whole((width, lanes)),
                whole((width, hidden)),
                whole((hidden, width)),
            ],
            out_specs=[
                rows,
                rows,
                rows,
                rows,
                pairs(hidden),
                pairs(hidden),
                pairs(width),
                pl.BlockSpec((lanes, width), lambda i, pick: (0, 0)),
            ],
        ),
        out_shape=[
            quarter,
            quarter,
            quarter,
            quarter,
            jax.ShapeDtypeStruct((2, count, hidden), BF16),
            jax.ShapeDtypeStruct((2, count, hidden), BF16),
            jax.ShapeDtypeStruct((2, count, width), BF16),
            jax.ShapeDtypeStruct((lanes, width), F32),
        ],
        cost_estimate=pl.CostEstimate(
            flops=16 * count * width * hidden // COVER,
            transcendentals=4 * count * hidden // COVER,
            bytes_accessed=2 * (8 * count * width + 4 * count * hidden + 2 * width * hidden) // COVER,
        ),
        compiler_params=pltpu.CompilerParams(vmem_limit_bytes=60 * 1024 * 1024),
        name="feed_routed" if routed else "feed_dense",
    )(pick, own, side, own_grads, side_grads, head, up, down)
    flat = [value.reshape(2 * count, value.shape[2]) for value in (active, pre, weighted)]
    return [*sums, *flat, head_grad]


LANES = 128
QUARTER_ROWS = 128


def norm_parts(values):
    row_mean = jnp.mean(values, axis=-1, keepdims=True)
    centred = values - row_mean
    row_var = jnp.mean(centred * centred, axis=-1, keepdims=True)
    inverse = lax.rsqrt(row_var + EPSILON)
    return (centred * inverse, inverse)


def norm_back(grad_normed, gain_vec, scaled, inverse):
    grad_scaled = grad_normed * gain_vec
    first_mean = jnp.mean(grad_scaled, axis=-1, keepdims=True)
    second = jnp.mean(grad_scaled * scaled, axis=-1, keepdims=True)
    return inverse * (grad_scaled - first_mean - scaled * second)


def after(value, *others):
    return lax.optimization_barrier((value, *others))[0]


def from_side(values):
    return lax.ppermute(values, "tensor", [(i, i ^ 1) for i in range(4)])


def from_far(values):
    return lax.ppermute(values, "tensor", [(i, i ^ 2) for i in range(4)])


def plus_side(own, side):
    return own.astype(F32) + from_side(side.astype(BF16)).astype(F32)


def sum_over(values, axis):
    count, step = lax.axis_size(axis), 1
    while step < count:
        pairs = [(i, i ^ step) for i in range(count)]
        values = values + lax.ppermute(values, axis, pairs)
        step *= 2
    return values


def exchange(blocks):
    return lax.all_to_all(blocks, "expert", split_axis=0, concat_axis=0, tiled=True)


def scatter_sum(strips):
    strips = with_layout_constraint(strips.astype(BF16), Layout(major_to_minor=(0, 1)))
    return lax.psum_scatter(strips, "expert", scatter_dimension=0, tiled=True)


def strips_sent(grads):
    return exchange(grads.reshape(lax.axis_size("expert"), -1, grads.shape[1]))


def strips_total(strips):
    return jnp.sum(strips.astype(F32), axis=0)


def slots_of(expert_ids, experts, capacity):
    rows = expert_ids.shape[0]
    chosen = expert_ids[:, None] == jnp.arange(experts, dtype=jnp.int32)[None, :]
    at = jnp.arange(rows, dtype=jnp.int32)
    before = (at[None, :] < at[:, None]).astype(BF16)
    earlier = jnp.dot(before, chosen.astype(BF16), preferred_element_type=F32)
    slot = jnp.sum(jnp.where(chosen, earlier, 0.0), axis=1).astype(jnp.int32)
    place = expert_ids * capacity + slot
    places = jnp.arange(experts * capacity, dtype=jnp.int32)
    return (places[:, None] == place[None, :]).astype(BF16)


def per_device(
    tokens,
    cotangent,
    routes,
    parents,
    ln_attn,
    w_qkv,
    w_out,
    ln_mlp,
    w_up,
    w_down,
    w_router,
    w_mix,
    ex_up,
    ex_down,
):
    tok_dev, width = tokens.shape
    mine = lax.axis_index("tensor")
    experts = w_router.shape[1]
    capacity = max(2, tok_dev * 7 // (5 * experts))
    heads_width = w_qkv.shape[2]
    hidden = w_up.shape[1]
    leaves = jnp.concatenate([leaf_order(parents[0]), mine.astype(jnp.int32)[None]])

    scaled_one, inverse_one = norm_parts(tokens.astype(F32))
    normed_own = (scaled_one * ln_attn).astype(BF16)
    normed_far = from_far(normed_own)
    near_one = jnp.concatenate([normed_own, from_side(normed_own)], axis=0)

    quarter_ids = routes[:, 0].reshape(4, tok_dev)

    def slots_at(offset):
        ids = lax.dynamic_index_in_dim(quarter_ids, mine ^ offset, 0, keepdims=False)
        return slots_of(ids, experts, capacity)

    own_slots, far_slots = slots_at(0), slots_at(2)

    def placed(slots, rows):
        return jnp.dot(slots, rows, preferred_element_type=F32).astype(BF16)

    def sent(rows):
        return exchange(rows.reshape(experts, capacity, width)).reshape(-1, width)

    own_grads = sent(placed(own_slots, cotangent))
    cotangent_side = from_side(cotangent)

    def project(rows):
        return jnp.einsum("td,sdc->stc", rows, w_qkv, preferred_element_type=F32).astype(BF16)

    lanes = -(-(experts + 2) // LANES) * LANES
    head = jnp.concatenate(
        [w_router, w_mix, jnp.zeros((width, lanes - experts - 2), BF16)], axis=1
    )
    near_qkv = project(near_one).reshape(3, 2, tok_dev, heads_width)
    cotangent_far = from_far(after(cotangent, normed_far))
    normed_far, near_qkv, head = lax.optimization_barrier((normed_far, near_qkv, head))
    normed_corner = from_side(normed_far)
    qkv = near_qkv, project(normed_far), project(normed_corner)
    near_out, far_out, *logs = attention_forward(leaves, *qkv)
    far_one = jnp.concatenate([normed_far, normed_corner], axis=0)
    far_out, own_grads, cotangent_far, cotangent_side = lax.optimization_barrier(
        (far_out, own_grads, cotangent_far, cotangent_side)
    )

    def branch_part(rows):
        return jnp.dot(rows, w_out, preferred_element_type=F32)

    far_sum = plus_side(branch_part(far_out[0]), branch_part(far_out[1])).astype(BF16)
    branch = plus_side(branch_part(near_out[0]), branch_part(near_out[1]))
    branch_far = from_far(far_sum)
    side_grads = from_side(own_grads)
    cotangent_corner = from_side(cotangent_far)
    far_placed = placed(far_slots, cotangent_far)
    branch_far, side_grads, cotangent_corner, far_placed = lax.optimization_barrier(
        (branch_far, side_grads, cotangent_corner, far_placed)
    )
    residual = tokens.astype(F32) + (branch + branch_far.astype(F32))

    scaled_two, inverse_two = norm_parts(residual)
    normed_two = (scaled_two * ln_mlp).astype(BF16)
    normed_two_far = from_far(normed_two)
    normed_two_side = from_side(normed_two)
    own_rows = sent(placed(own_slots, normed_two))

    def dense(own, side, own_cotangent, side_cotangent):
        return feed(
            own, side, own_cotangent, side_cotangent, head, w_up, w_down, experts, None, QUARTER_ROWS
        )

    def product(left, right):
        return jnp.einsum("gd,gf->df", left, right, preferred_element_type=F32)

    def weight_grads(near_left, far_left, near_right, far_right):
        return product(near_left, near_right) + product(far_left, far_right)

    near_dense = dense(normed_two, normed_two_side, cotangent, cotangent_side)
    near_two = jnp.concatenate([normed_two, normed_two_side], axis=0)
    grad_up = product(near_two, near_dense[5])
    grad_down = product(near_dense[6], near_dense[4])
    normed_two_far, grad_up, grad_down, own_rows = lax.optimization_barrier(
        (normed_two_far, grad_up, grad_down, own_rows)
    )
    far_rows = from_far(own_rows)
    far_grads = sent(after(far_placed, own_rows))
    normed_two_corner = from_side(normed_two_far)
    far_dense = list(dense(normed_two_far, normed_two_corner, cotangent_far, cotangent_corner))

    expert = lax.axis_index("expert").astype(jnp.int32)

    def routed(own, side, own_cotangent, side_cotangent):
        return feed(
            own,
            side,
            own_cotangent,
            side_cotangent,
            head,
            ex_up[0],
            ex_down[0],
            experts,
            expert,
            QUARTER_ROWS,
        )

    def chip_sum(parts, place, *others):
        return plus_side(parts[place], after(parts[place + 1], *others))

    def chip_sum(parts, place, *others):
        return plus_side(parts[place], after(parts[place + 1], *others))

    dense_back_far = chip_sum(far_dense, 2).astype(BF16)
    far_two = jnp.concatenate([normed_two_far, normed_two_corner], axis=0)
    grad_down = (grad_down + product(far_dense[6], far_dense[4])).astype(BF16)
    far_two, grad_down = lax.optimization_barrier((far_two, grad_down))
    grad_up = (grad_up + product(far_two, far_dense[5])).astype(BF16)
    dense_grads = after(jnp.concatenate([grad_up, grad_down], axis=1), far_grads)
    far_rows, dense_back_far, dense_grads = lax.optimization_barrier(
        (far_rows, dense_back_far, dense_grads)
    )
    dense_grads = scatter_sum(dense_grads)
    dense_back_far = from_far(dense_back_far)
    corner_rows = from_side(far_rows)
    side_rows = from_side(own_rows)
    far_expert = routed(far_rows, corner_rows, far_grads, from_side(far_grads))
    *far_expert, dense_back_far = lax.optimization_barrier((*far_expert, dense_back_far))
    far_back = chip_sum(far_expert, 2).astype(BF16)
    own_rows, far_back = lax.optimization_barrier((own_rows, far_back))
    near_expert = routed(own_rows, side_rows, own_grads, side_grads)
    *near_expert, dense_grads = lax.optimization_barrier((*near_expert, dense_grads))

    def picked(rows):
        return lax.dot_general(
            own_slots, rows, (((0,), (0,)), ((), ())), preferred_element_type=F32
        )

    expert_back = (chip_sum(near_expert, 2) + from_far(far_back).astype(F32)).astype(BF16)
    far_expert_out = chip_sum(far_expert, 0, expert_back).astype(BF16)
    dense_out_far = chip_sum(far_dense, 0, expert_back).astype(BF16)
    dense_back = chip_sum(near_dense, 2, far_back) + dense_back_far.astype(F32)

    grad_normed_two = dense_back + picked(sent(expert_back))
    dense_out = chip_sum(near_dense, 0, expert_back)
    expert_out = chip_sum(near_expert, 0, expert_back) + from_far(far_expert_out).astype(F32)
    expert_out = after(expert_out.astype(BF16), grad_normed_two)

    near_active, far_active, near_pre, far_pre, far_expert_out = lax.optimization_barrier(
        (near_expert[4], far_expert[4], near_expert[5], far_expert[5], far_expert_out)
    )
    near_tokens = jnp.concatenate([own_rows, side_rows], axis=0)
    far_tokens = jnp.concatenate([far_rows, corner_rows], axis=0)
    grad_ex_up = weight_grads(near_tokens, far_tokens, near_pre, far_pre)[None]
    grad_ex_down = weight_grads(near_active, far_active, near_expert[6], far_expert[6])[None]

    gain_two = jnp.sum(grad_normed_two * scaled_two, axis=0)
    grad_residual = cotangent.astype(F32) + norm_back(
        grad_normed_two, ln_mlp, scaled_two, inverse_two
    )
    grad_branch = grad_residual.astype(BF16)
    grad_branch_far = from_far(grad_branch)
    grad_branch_side = from_side(grad_branch)

    def into_heads(*rows):
        grads = [jnp.einsum("gd,cd->gc", part, w_out, preferred_element_type=F32) for part in rows]
        return jnp.stack(grads).astype(BF16)

    near_heads = into_heads(grad_branch, grad_branch_side)
    out_rows = sent(expert_out)
    flat = (2 * tok_dev, heads_width)
    near_branch = jnp.concatenate([grad_branch, grad_branch_side], axis=0)
    grad_w_out = product(near_branch, near_out.reshape(flat))
    grad_branch_far, near_heads, grad_w_out, grad_ex_up, grad_ex_down, _, dense_out_far, dense_out = (
        lax.optimization_barrier(
            (
                grad_branch_far,
                near_heads,
                grad_w_out,
                grad_ex_up,
                grad_ex_down,
                expert_out,
                dense_out_far,
                dense_out,
            )
        )
    )
    grad_branch_corner = from_side(grad_branch_far)
    far_heads = into_heads(grad_branch_far, grad_branch_corner)
    dense_out_far = from_far(dense_out_far)
    head_grads = near_dense[7] + far_dense[7] + near_expert[7] + far_expert[7]
    small = jnp.concatenate([head_grads[: experts + 2], gain_two[None]], axis=0)

    def pair_back(pair, near_grads, far_grads):
        return attention_backward(
            leaves, pair, qkv, near_grads, far_grads, near_out, far_out, logs
        )

    def pair_weights(pair):
        lanes = slice(pair * PAIR, (pair + 1) * PAIR)
        return jnp.concatenate([w_qkv[part, :, lanes] for part in range(3)], axis=1)

    def total(values):
        return functools.reduce(jnp.add, values)

    pairs = heads_width // PAIR
    near_results, far_results = [None] * pairs, [None] * pairs
    near_results[0], far_results[0] = pair_back(0, near_heads, far_heads)
    far_branch = jnp.concatenate([grad_branch_far, grad_branch_corner], axis=0)
    grad_w_out = grad_w_out + product(far_branch, far_out.reshape(flat))
    small_columns = -(-small.shape[0] // LANES) * LANES
    small_block = jnp.pad(small, ((0, small_columns - small.shape[0]), (0, 0))).T
    branch_grads = jnp.concatenate([grad_w_out.astype(BF16), small_block.astype(BF16)], axis=1)
    near_results[0], far_results[0], out_rows, dense_out_far, branch_grads, near_heads = (
        lax.optimization_barrier(
            (near_results[0], far_results[0], out_rows, dense_out_far, branch_grads, near_heads)
        )
    )
    branch_grads = strips_sent(branch_grads)
    for pair in range(1, pairs):
        near_results[pair], far_results[pair] = pair_back(pair, near_heads, far_heads)
    near_results, far_results, branch_grads = lax.optimization_barrier(
        (near_results, far_results, branch_grads)
    )

    def normed_part(results, quarter):
        return total([dot_nt(results[pair][quarter], pair_weights(pair)) for pair in range(pairs)])

    def qkv_weights(pair, *others):
        near_rows = near_results[pair].reshape(2 * tok_dev, 3 * PAIR)
        far_rows = far_results[pair].reshape(2 * tok_dev, 3 * PAIR)
        near_rows = after(near_rows, *others)
        return weight_grads(near_one, far_one, near_rows, far_rows).astype(BF16)

    corner_part = normed_part(far_results, 1).astype(BF16)
    from_corner = from_side(corner_part).astype(F32)
    first_grads = qkv_weights(0, corner_part)
    far_results, first_grads = lax.optimization_barrier((far_results, first_grads))
    qkv_grads = [strips_sent(first_grads)]
    far_sum = (normed_part(far_results, 0) + from_corner).astype(BF16)
    near_results, far_results, far_sum = lax.optimization_barrier(
        (near_results, far_results, far_sum)
    )
    last_grads = [qkv_weights(pair, far_sum) for pair in range(1, pairs)]
    out_rows, *last_grads = lax.optimization_barrier((out_rows, *last_grads))
    qkv_grads += [strips_sent(grads) for grads in last_grads]
    near_sum = plus_side(normed_part(near_results, 0), normed_part(near_results, 1))
    out = (residual + dense_out + dense_out_far.astype(F32) + picked(out_rows)).astype(BF16)

    scaled_far = normed_far.astype(F32) / ln_attn
    gain_one = jnp.sum(
        near_sum * scaled_one + far_sum.astype(F32) * scaled_far, axis=0, keepdims=True
    )
    gain_one = sum_over(gain_one, "expert")
    far_arrived, gain_one, dense_grads, *_ = lax.optimization_barrier(
        (from_far(far_sum), gain_one, dense_grads, *last_grads)
    )
    grad_normed_one = near_sum + far_arrived.astype(F32)
    grad_ln_attn = sum_over(gain_one, "tensor")[0]
    branch_grads = strips_total(after(branch_grads, gain_one))
    small = sum_over(branch_grads[:, heads_width:], "tensor")
    qkv_grads = jnp.stack(
        [strips_total(grads).reshape(-1, 3, PAIR) for grads in qkv_grads], axis=2
    )
    grad_tokens = grad_residual + norm_back(grad_normed_one, ln_attn, scaled_one, inverse_one)

    strip = qkv_grads.shape[0]
    return (
        out,
        grad_tokens,
        grad_ln_attn,
        qkv_grads.reshape(strip, 3, heads_width).transpose(1, 0, 2),
        branch_grads[:, :heads_width].T,
        small[:, experts + 2],
        dense_grads[:, :hidden].astype(F32),
        dense_grads[:, hidden:].T.astype(F32),
        small[:, :experts],
        small[:, experts : experts + 2],
        grad_ex_up,
        grad_ex_down,
    )


def solution(mesh):
    return jax.shard_map(
        per_device,
        mesh=mesh,
        in_specs=(
            P(("expert", "tensor"), None),
            P(("expert", "tensor"), None),
            P("expert", None),
            P("expert", None),
            P(),
            P(None, None, "tensor"),
            P("tensor", None),
            P(),
            P(None, "tensor"),
            P("tensor", None),
            P(),
            P(),
            P("expert", None, "tensor"),
            P("expert", "tensor", None),
        ),
        out_specs=(
            P(("expert", "tensor"), None),
            P(("expert", "tensor"), None),
            P(),
            P(None, "expert", "tensor"),
            P("tensor", "expert"),
            P("expert"),
            P("expert", "tensor"),
            P("tensor", "expert"),
            P("expert", None),
            P("expert", None),
            P("expert", None, "tensor"),
            P("expert", "tensor", None),
        ),
        check_vma=False,
    )
```

```python
import functools

import jax
import jax.numpy as jnp
from jax import lax
from jax.experimental import pallas as pl
from jax.experimental.layout import Layout, with_layout_constraint
from jax.experimental.pallas import tpu as pltpu
from jax.sharding import PartitionSpec as P

HEAD_DIM = 64
TRUNK = 1024
SEG = 128
SEGS = 13
TREE_LEN = 2560
BRANCHES = 4
FAMILY = 3 * SEG
TEAM = 2 * FAMILY
TEAMS = BRANCHES // 2
QROWS = 256
COVER = 8
PAIR = 2 * HEAD_DIM
NEGATIVE_FILL = -1e30
F32 = jnp.float32
BF16 = jnp.bfloat16
EPSILON = 1e-05


def dot_nn(a, b):
    return lax.dot_general(a, b, (((1,), (0,)), ((), ())), preferred_element_type=F32)


def dot_nt(a, b):
    return lax.dot_general(a, b, (((1,), (1,)), ((), ())), preferred_element_type=F32)


def head_lanes(rows, head):
    lane = lax.broadcasted_iota(jnp.int32, rows.shape, 1)
    return jnp.where(lane // HEAD_DIM == head, rows, jnp.zeros_like(rows))


def causal(scores):
    key = lax.broadcasted_iota(jnp.int32, scores.shape, 0)
    query = lax.broadcasted_iota(jnp.int32, scores.shape, 1)
    return jnp.where(key <= query, scores, NEGATIVE_FILL)


def family_rows(leaves_ref, branch):
    def start(segment):
        return pl.multiple_of(TRUNK + (segment - 1) * SEG, SEG)

    return [start(branch + 1), start(leaves_ref[2 * branch]), start(leaves_ref[2 * branch + 1])]


def transpose_into(target_ref, source_ref, part):
    for first in range(0, TREE_LEN, 512):
        piece = source_ref[part, pl.ds(first, 512), :].astype(F32)
        target_ref[:, pl.ds(first, 512)] = piece.T.astype(BF16)


def widen(piece, first, width, fill):
    parts = []
    if first:
        parts.append(jnp.full((piece.shape[0], first), fill, piece.dtype))
    parts.append(piece)
    rest = width - first - piece.shape[1]
    if rest:
        parts.append(jnp.full((piece.shape[0], rest), fill, piece.dtype))
    return parts[0] if len(parts) == 1 else jnp.concatenate(parts, axis=1)


def trunk_groups(block):
    first = block * QROWS
    groups = [(0, first, 0, QROWS, None)] if first else []
    return groups + [(first, QROWS, 0, QROWS, "causal")]


def team_rows(leaves_ref, team):
    return family_rows(leaves_ref, 2 * team) + family_rows(leaves_ref, 2 * team + 1)


def team_groups(starts):
    groups = [(0, TRUNK, 0, TEAM, None)]
    for first in range(0, TEAM, FAMILY):
        at = first // SEG
        groups.append((starts[at], SEG, first, first + FAMILY, "branch"))
        for leaf in (1, 2):
            begin = first + leaf * SEG
            groups.append((starts[at + leaf], SEG, begin, begin + SEG, "causal"))
    return groups


def masked_scores(keys, queries, rule):
    scores = dot_nt(keys, queries)
    if rule == "causal":
        return causal(scores)
    if rule == "branch":
        return jnp.concatenate([causal(scores[:, :SEG]), scores[:, SEG:]], axis=1)
    return scores


def forward_block(qkv_ref, values_t_ref, queries, groups):
    width = queries.shape[0]
    outs, logs = [], []
    for head in range(2):
        own = head_lanes(queries, head)
        all_scores = [
            masked_scores(qkv_ref[1, pl.ds(start, size), :], own[first:last], rule)
            for start, size, first, last, rule in groups
        ]
        top = functools.reduce(
            jnp.maximum,
            [
                widen(jnp.max(s, axis=0, keepdims=True), first, width, NEGATIVE_FILL)
                for s, (_, _, first, last, _) in zip(all_scores, groups)
            ],
        )
        total, output = None, None
        for s, (start, size, first, last, _) in zip(all_scores, groups):
            weights = jnp.exp(s - top[:, first:last])
            part = widen(jnp.sum(weights, axis=0, keepdims=True), first, width, 0.0)
            values_t = values_t_ref[pl.ds(head * HEAD_DIM, HEAD_DIM), pl.ds(start, size)]
            mixed = widen(dot_nn(values_t, weights.astype(BF16)), first, width, 0.0)
            total = part if total is None else total + part
            output = mixed if output is None else output + mixed
        outs.append(output / total)
        logs.append(top + jnp.log(total))
    return jnp.concatenate(outs, axis=0).T.astype(BF16), jnp.concatenate(logs, axis=0)


def scaled_queries(qkv_ref, starts, size):
    rows = [qkv_ref[0, pl.ds(start, size), :] for start in starts]
    rows = rows[0] if len(rows) == 1 else jnp.concatenate(rows, axis=0)
    return rows * jnp.asarray(HEAD_DIM ** (-0.5), BF16)


def quarter_rows(leaves_ref, offset):
    quarter = TREE_LEN // 4
    return pl.ds(pl.multiple_of((leaves_ref[2 * BRANCHES] ^ offset) * quarter, quarter), quarter)


def forward_kernel(
    leaves_ref,
    near_ref,
    far_ref,
    near_out_ref,
    far_out_ref,
    trunk_log_ref,
    family_log_ref,
    qkv_ref,
    out_ref,
    values_t_ref,
):
    for offset in range(4):
        half_ref = near_ref if offset < 2 else far_ref
        qkv_ref[:, quarter_rows(leaves_ref, offset), :] = half_ref[:, offset % 2]
    transpose_into(values_t_ref, qkv_ref, 2)
    for block in range(TRUNK // QROWS):
        first = block * QROWS
        queries = scaled_queries(qkv_ref, [first], QROWS)
        out, logs = forward_block(qkv_ref, values_t_ref, queries, trunk_groups(block))
        out_ref[pl.ds(first, QROWS), :] = out
        trunk_log_ref[0, :, pl.ds(first, QROWS)] = logs

    def one_team(team, carry):
        starts = team_rows(leaves_ref, team)
        queries = scaled_queries(qkv_ref, starts, SEG)
        out, logs = forward_block(qkv_ref, values_t_ref, queries, team_groups(starts))
        for place, start in enumerate(starts):
            out_ref[pl.ds(start, SEG), :] = out[place * SEG : (place + 1) * SEG]
        family_log_ref[0, team] = logs
        return carry

    lax.fori_loop(0, TEAMS, one_team, 0)
    for offset in range(4):
        half_ref = near_out_ref if offset < 2 else far_out_ref
        half_ref[offset % 2] = out_ref[quarter_rows(leaves_ref, offset), :]


def halves_spec(parts):
    quarter = TREE_LEN // 4
    if parts == 1:
        return pl.BlockSpec((2, quarter, PAIR), lambda p, leaves: (0, 0, p))
    return pl.BlockSpec((parts, 2, quarter, PAIR), lambda p, leaves: (0, 0, 0, p))


def attention_cost(products, cover):
    visited = (TRUNK * (TRUNK + QROWS) // 2 + BRANCHES * FAMILY * (TRUNK + SEG)) // cover
    return pl.CostEstimate(
        flops=2 * products * 4 * visited * 2 * PAIR,
        transcendentals=4 * visited,
        bytes_accessed=8 * TREE_LEN * 4 * HEAD_DIM * 2 // cover,
    )


def attention_forward(leaves, near, far):
    width = near.shape[3]
    quarter = TREE_LEN // 4
    pairs = width // PAIR
    return pl.pallas_call(
        forward_kernel,
        grid_spec=pltpu.PrefetchScalarGridSpec(
            num_scalar_prefetch=1,
            grid=(pairs,),
            in_specs=[halves_spec(3), halves_spec(3)],
            out_specs=[
                halves_spec(1),
                halves_spec(1),
                pl.BlockSpec((1, 2, TRUNK), lambda p, leaves: (p, 0, 0)),
                pl.BlockSpec((1, TEAMS, 2, TEAM), lambda p, leaves: (p, 0, 0, 0)),
            ],
            scratch_shapes=[
                pltpu.VMEM((3, TREE_LEN, PAIR), BF16),
                pltpu.VMEM((TREE_LEN, PAIR), BF16),
                pltpu.VMEM((PAIR, TREE_LEN), BF16),
            ],
        ),
        out_shape=[
            jax.ShapeDtypeStruct((2, quarter, width), BF16),
            jax.ShapeDtypeStruct((2, quarter, width), BF16),
            jax.ShapeDtypeStruct((pairs, 2, TRUNK), F32),
            jax.ShapeDtypeStruct((pairs, TEAMS, 2, TEAM), F32),
        ],
        cost_estimate=attention_cost(2, COVER),
        name="tree_attention",
    )(leaves, near, far)


def backward_block(qkv_ref, keys_t_ref, queries, grads, outs, logs, groups):
    products = grads.astype(F32) * outs.astype(F32)
    products_t = products.T
    key_ds = [[] for _ in groups]
    value_ws = [[] for _ in groups]
    own_q, own_g, query_grads = [], [], []
    for head in range(2):
        own = head_lanes(queries, head)
        own_grads = head_lanes(grads, head)
        own_q.append(own)
        own_g.append(own_grads)
        inner = jnp.sum(
            products_t[head * HEAD_DIM : (head + 1) * HEAD_DIM], axis=0, keepdims=True
        )
        log = logs[head : head + 1]
        query_grad = None
        for place, (start, size, first, last, rule) in enumerate(groups):
            scores = masked_scores(qkv_ref[1, pl.ds(start, size), :], own[first:last], rule)
            weights = jnp.exp(scores - log[:, first:last])
            grad_weights = dot_nt(qkv_ref[2, pl.ds(start, size), :], own_grads[first:last])
            grad_scores = (weights * (grad_weights - inner[:, first:last])).astype(BF16)
            keys_t = keys_t_ref[pl.ds(head * HEAD_DIM, HEAD_DIM), pl.ds(start, size)]
            part = widen(dot_nn(keys_t, grad_scores), first, queries.shape[0], 0.0)
            query_grad = part if query_grad is None else query_grad + part
            key_ds[place].append(grad_scores)
            value_ws[place].append(weights.astype(BF16))
        query_grads.append(query_grad)
    grad_query = (jnp.concatenate(query_grads, axis=0) * HEAD_DIM ** (-0.5)).T.astype(BF16)
    key_grads, value_grads = [], []
    for place, (start, size, first, last, rule) in enumerate(groups):
        stacked_q = jnp.concatenate([own_q[0][first:last], own_q[1][first:last]], axis=0)
        stacked_g = jnp.concatenate([own_g[0][first:last], own_g[1][first:last]], axis=0)
        key_grads.append(dot_nn(jnp.concatenate(key_ds[place], axis=1), stacked_q))
        value_grads.append(dot_nn(jnp.concatenate(value_ws[place], axis=1), stacked_g))
    return grad_query, key_grads, value_grads


def backward_kernel(
    leaves_ref,
    near_ref,
    far_ref,
    near_grads_ref,
    far_grads_ref,
    near_outs_ref,
    far_outs_ref,
    trunk_log_ref,
    family_log_ref,
    near_result_ref,
    far_result_ref,
    qkv_ref,
    grads_ref,
    outs_ref,
    result_ref,
    keys_t_ref,
    trunk_keys_ref,
    trunk_values_ref,
):
    for offset in range(4):
        rows = quarter_rows(leaves_ref, offset)
        at = offset % 2
        qkv_ref[:, rows, :] = (near_ref if offset < 2 else far_ref)[:, at]
        grads_ref[rows, :] = (near_grads_ref if offset < 2 else far_grads_ref)[at]
        outs_ref[rows, :] = (near_outs_ref if offset < 2 else far_outs_ref)[at]
    transpose_into(keys_t_ref, qkv_ref, 1)
    trunk_keys_ref[...] = jnp.zeros_like(trunk_keys_ref)
    trunk_values_ref[...] = jnp.zeros_like(trunk_values_ref)
    for block in range(TRUNK // QROWS):
        first = block * QROWS
        rows = pl.ds(first, QROWS)
        groups = trunk_groups(block)
        grad_query, key_grads, value_grads = backward_block(
            qkv_ref,
            keys_t_ref,
            scaled_queries(qkv_ref, [first], QROWS),
            grads_ref[rows, :],
            outs_ref[rows, :],
            trunk_log_ref[0, :, rows],
            groups,
        )
        result_ref[0, rows, :] = grad_query
        for (start, size, _, _, _), key_grad, value_grad in zip(groups, key_grads, value_grads):
            trunk_keys_ref[pl.ds(start, size), :] += key_grad
            trunk_values_ref[pl.ds(start, size), :] += value_grad

    def one_team(team, carry):
        starts = team_rows(leaves_ref, team)
        groups = team_groups(starts)
        grad_query, key_grads, value_grads = backward_block(
            qkv_ref,
            keys_t_ref,
            scaled_queries(qkv_ref, starts, SEG),
            jnp.concatenate([grads_ref[pl.ds(start, SEG), :] for start in starts], axis=0),
            jnp.concatenate([outs_ref[pl.ds(start, SEG), :] for start in starts], axis=0),
            family_log_ref[0, team],
            groups,
        )
        trunk_keys_ref[...] += key_grads[0]
        trunk_values_ref[...] += value_grads[0]
        for place, start in enumerate(starts):
            rows = pl.ds(start, SEG)
            result_ref[0, rows, :] = grad_query[place * SEG : (place + 1) * SEG]
            result_ref[1, rows, :] = key_grads[1 + place].astype(BF16)
            result_ref[2, rows, :] = value_grads[1 + place].astype(BF16)
        return carry

    lax.fori_loop(0, TEAMS, one_team, 0)
    result_ref[1, pl.ds(0, TRUNK), :] = trunk_keys_ref[...].astype(BF16)
    result_ref[2, pl.ds(0, TRUNK), :] = trunk_values_ref[...].astype(BF16)
    for offset in range(4):
        half_ref = near_result_ref if offset < 2 else far_result_ref
        rows = quarter_rows(leaves_ref, offset)
        for part in range(3):
            half_ref[offset % 2, :, part * PAIR : (part + 1) * PAIR] = result_ref[part, rows, :]


def attention_backward(leaves, pair, near, far, near_grads, far_grads, near_outs, far_outs, logs):
    quarter = TREE_LEN // 4
    rows = pl.BlockSpec((2, quarter, PAIR), lambda i, leaves: (0, 0, pair))
    parts = pl.BlockSpec((3, 2, quarter, PAIR), lambda i, leaves: (0, 0, 0, pair))
    result = pl.BlockSpec((2, quarter, 3 * PAIR), lambda i, leaves: (0, 0, 0))
    shape = jax.ShapeDtypeStruct((2, quarter, 3 * PAIR), BF16)
    return pl.pallas_call(
        backward_kernel,
        grid_spec=pltpu.PrefetchScalarGridSpec(
            num_scalar_prefetch=1,
            grid=(1,),
            in_specs=[
                parts,
                parts,
                rows,
                rows,
                rows,
                rows,
                pl.BlockSpec((1, 2, TRUNK), lambda i, leaves: (pair, 0, 0)),
                pl.BlockSpec((1, TEAMS, 2, TEAM), lambda i, leaves: (pair, 0, 0, 0)),
            ],
            out_specs=[result, result],
            scratch_shapes=[
                pltpu.VMEM((3, TREE_LEN, PAIR), BF16),
                pltpu.VMEM((TREE_LEN, PAIR), BF16),
                pltpu.VMEM((TREE_LEN, PAIR), BF16),
                pltpu.VMEM((3, TREE_LEN, PAIR), BF16),
                pltpu.VMEM((PAIR, TREE_LEN), BF16),
                pltpu.VMEM((TRUNK, PAIR), F32),
                pltpu.VMEM((TRUNK, PAIR), F32),
            ],
        ),
        out_shape=[shape, shape],
        cost_estimate=attention_cost(5, 10),
        name="tree_attention_back",
    )(leaves, near, far, near_grads, far_grads, near_outs, far_outs, *logs)


def leaf_order(parents_row):
    first_leaf = BRANCHES + 1
    leaf_parents = parents_row[first_leaf:]
    segments = first_leaf + jnp.arange(leaf_parents.shape[0], dtype=jnp.int32)
    same = leaf_parents[:, None] == leaf_parents[None, :]
    later = segments[None, :] < segments[:, None]
    place = 2 * (leaf_parents - 1) + jnp.sum(jnp.where(same & later, 1, 0), axis=1)
    slots = jnp.arange(2 * BRANCHES, dtype=jnp.int32)
    return jnp.sum(jnp.where(slots[:, None] == place[None, :], segments[None, :], 0), axis=1)


def gates(logits, experts, expert):
    lane = lax.broadcasted_iota(jnp.int32, logits.shape, 1)
    first, second = logits[:, experts : experts + 1], logits[:, experts + 1 : experts + 2]
    top = jnp.maximum(first, second)
    first, second = jnp.exp(first - top), jnp.exp(second - top)
    total = first + second
    first, second = first / total, second / total
    if expert is None:
        return lane, first, second, None, None
    routed = jnp.where(lane < experts, logits, NEGATIVE_FILL)
    raised = jnp.exp(routed - jnp.max(routed, axis=1, keepdims=True))
    probs = raised / jnp.sum(raised, axis=1, keepdims=True)
    gate = jnp.sum(jnp.where(lane == expert, probs, 0.0), axis=1, keepdims=True)
    return lane, first, second, probs, gate


def both(own_ref, side_ref):
    return jnp.concatenate([own_ref[...], side_ref[...]], axis=0)


def split_store(own_ref, side_ref, rows):
    half = rows.shape[0] // 2
    own_ref[...] = rows[:half]
    side_ref[...] = rows[half:]


def feed_kernel(
    experts,
    routed,
    expert_ref,
    own_ref,
    side_ref,
    own_grads_ref,
    side_grads_ref,
    head_ref,
    up_ref,
    down_ref,
    own_out_ref,
    side_out_ref,
    own_back_ref,
    side_back_ref,
    active_ref,
    pre_ref,
    grad_ref,
    head_grad_ref,
):
    rows = both(own_ref, side_ref)
    grads = both(own_grads_ref, side_grads_ref).astype(F32)
    expert = expert_ref[0] if routed else None
    logits = dot_nn(rows, head_ref[...])
    lane, first, second, probs, gate = gates(logits, experts, expert)
    coef = second * gate if routed else first
    weighted = (coef * grads).astype(BF16)
    pre = dot_nn(rows, up_ref[...])
    grad_active = dot_nt(weighted, down_ref[...])
    cumulative = 0.5 + 0.5 * lax.erf(pre * 0.7071067811865476)
    slope = cumulative + pre * jnp.exp(-0.5 * pre * pre) * 0.3989422804014327
    active = (pre * cumulative).astype(BF16)
    grad_pre = (grad_active * slope).astype(BF16)
    half = rows.shape[0] // 2
    for ref, value in ((active_ref, active), (pre_ref, grad_pre), (grad_ref, weighted)):
        ref[0] = value[:half]
        ref[1] = value[half:]
    out = dot_nn(active, down_ref[...])
    split_store(own_out_ref, side_out_ref, (coef * out).astype(BF16))
    inner = jnp.sum(grads * out, axis=1, keepdims=True)
    swing = first * second * inner
    if routed:
        swing = -gate * swing
    grad_logits = jnp.where(lane == experts, swing, jnp.where(lane == experts + 1, -swing, 0.0))
    if routed:
        picked = jnp.where(lane == expert, 1.0, 0.0) - gate
        grad_logits = grad_logits + jnp.where(
            lane < experts, probs * picked * (second * inner), 0.0
        )
    back = dot_nt(grad_pre, up_ref[...]) + dot_nt(grad_logits.astype(BF16), head_ref[...])
    split_store(own_back_ref, side_back_ref, back.astype(BF16))
    head_grad = dot_nn(grad_logits.T.astype(BF16), rows)

    @pl.when(pl.program_id(0) == 0)
    def _():
        head_grad_ref[...] = jnp.zeros_like(head_grad_ref)

    head_grad_ref[...] += head_grad


def feed(own, side, own_grads, side_grads, head, up, down, experts, expert, size):
    count = own.shape[0]
    width, hidden = up.shape
    steps = count // size
    lanes = head.shape[1]
    routed = expert is not None
    pick = jnp.reshape(expert, (1,)) if routed else jnp.zeros((1,), jnp.int32)
    rows = pl.BlockSpec((size, width), lambda i, pick: (i, 0))

    def whole(shape):
        return pl.BlockSpec(shape, lambda i, pick: (0, 0), pipeline_mode=pl.Buffered(1))

    def pairs(columns):
        return pl.BlockSpec((2, size, columns), lambda i, pick: (0, i, 0))

    quarter = jax.ShapeDtypeStruct((count, width), BF16)
    *sums, active, pre, weighted, head_grad = pl.pallas_call(
        functools.partial(feed_kernel, experts, routed),
        grid_spec=pltpu.PrefetchScalarGridSpec(
            num_scalar_prefetch=1,
            grid=(steps,),
            in_specs=[
                rows,
                rows,
                rows,
                rows,
                whole((width, lanes)),
                whole((width, hidden)),
                whole((hidden, width)),
            ],
            out_specs=[
                rows,
                rows,
                rows,
                rows,
                pairs(hidden),
                pairs(hidden),
                pairs(width),
                pl.BlockSpec((lanes, width), lambda i, pick: (0, 0)),
            ],
        ),
        out_shape=[
            quarter,
            quarter,
            quarter,
            quarter,
            jax.ShapeDtypeStruct((2, count, hidden), BF16),
            jax.ShapeDtypeStruct((2, count, hidden), BF16),
            jax.ShapeDtypeStruct((2, count, width), BF16),
            jax.ShapeDtypeStruct((lanes, width), F32),
        ],
        cost_estimate=pl.CostEstimate(
            flops=16 * count * width * hidden // COVER,
            transcendentals=4 * count * hidden // COVER,
            bytes_accessed=2 * (8 * count * width + 4 * count * hidden + 2 * width * hidden) // COVER,
        ),
        compiler_params=pltpu.CompilerParams(vmem_limit_bytes=60 * 1024 * 1024),
        name="feed_routed" if routed else "feed_dense",
    )(pick, own, side, own_grads, side_grads, head, up, down)
    flat = [value.reshape(2 * count, value.shape[2]) for value in (active, pre, weighted)]
    return [*sums, *flat, head_grad]


LANES = 128
QUARTER_ROWS = 128


def norm_parts(values):
    row_mean = jnp.mean(values, axis=-1, keepdims=True)
    centred = values - row_mean
    row_var = jnp.mean(centred * centred, axis=-1, keepdims=True)
    inverse = lax.rsqrt(row_var + EPSILON)
    return (centred * inverse, inverse)


def norm_back(grad_normed, gain_vec, scaled, inverse):
    grad_scaled = grad_normed * gain_vec
    first_mean = jnp.mean(grad_scaled, axis=-1, keepdims=True)
    second = jnp.mean(grad_scaled * scaled, axis=-1, keepdims=True)
    return inverse * (grad_scaled - first_mean - scaled * second)


def after(value, *others):
    return lax.optimization_barrier((value, *others))[0]


def from_side(values):
    return lax.ppermute(values, "tensor", [(i, i ^ 1) for i in range(4)])


def from_far(values):
    return lax.ppermute(values, "tensor", [(i, i ^ 2) for i in range(4)])


def plus_side(own, side):
    return own.astype(F32) + from_side(side.astype(BF16)).astype(F32)


def sum_over(values, axis):
    count, step = lax.axis_size(axis), 1
    while step < count:
        pairs = [(i, i ^ step) for i in range(count)]
        values = values + lax.ppermute(values, axis, pairs)
        step *= 2
    return values


def exchange(blocks):
    return lax.all_to_all(blocks, "expert", split_axis=0, concat_axis=0, tiled=True)


def scatter_sum(strips):
    strips = with_layout_constraint(strips.astype(BF16), Layout(major_to_minor=(0, 1)))
    return lax.psum_scatter(strips, "expert", scatter_dimension=0, tiled=True)


def strips_sent(grads):
    return exchange(grads.reshape(lax.axis_size("expert"), -1, grads.shape[1]))


def strips_total(strips):
    return jnp.sum(strips.astype(F32), axis=0)


def slots_of(expert_ids, experts, capacity):
    rows = expert_ids.shape[0]
    chosen = expert_ids[:, None] == jnp.arange(experts, dtype=jnp.int32)[None, :]
    at = jnp.arange(rows, dtype=jnp.int32)
    before = (at[None, :] < at[:, None]).astype(BF16)
    earlier = jnp.dot(before, chosen.astype(BF16), preferred_element_type=F32)
    slot = jnp.sum(jnp.where(chosen, earlier, 0.0), axis=1).astype(jnp.int32)
    place = expert_ids * capacity + slot
    places = jnp.arange(experts * capacity, dtype=jnp.int32)
    return (places[:, None] == place[None, :]).astype(BF16)


def per_device(
    tokens,
    cotangent,
    routes,
    parents,
    ln_attn,
    w_qkv,
    w_out,
    ln_mlp,
    w_up,
    w_down,
    w_router,
    w_mix,
    ex_up,
    ex_down,
):
    tok_dev, width = tokens.shape
    mine = lax.axis_index("tensor")
    experts = w_router.shape[1]
    capacity = max(2, tok_dev * 7 // (5 * experts))
    heads_width = w_qkv.shape[2]
    hidden = w_up.shape[1]
    leaves = jnp.concatenate([leaf_order(parents[0]), mine.astype(jnp.int32)[None]])

    scaled_one, inverse_one = norm_parts(tokens.astype(F32))
    normed_own = (scaled_one * ln_attn).astype(BF16)
    normed_far = from_far(normed_own)
    near_one = jnp.concatenate([normed_own, from_side(normed_own)], axis=0)

    quarter_ids = routes[:, 0].reshape(4, tok_dev)

    def slots_at(offset):
        ids = lax.dynamic_index_in_dim(quarter_ids, mine ^ offset, 0, keepdims=False)
        return slots_of(ids, experts, capacity)

    own_slots, far_slots = slots_at(0), slots_at(2)

    def placed(slots, rows):
        return jnp.dot(slots, rows, preferred_element_type=F32).astype(BF16)

    def sent(rows):
        return exchange(rows.reshape(experts, capacity, width)).reshape(-1, width)

    own_grads = sent(placed(own_slots, cotangent))
    cotangent_side = from_side(cotangent)

    def project(rows):
        qkv = jnp.einsum("td,sdc->stc", rows, w_qkv, preferred_element_type=F32)
        return qkv.astype(BF16).reshape(3, 2, tok_dev, heads_width)

    lanes = -(-(experts + 2) // LANES) * LANES
    head = jnp.concatenate(
        [w_router, w_mix, jnp.zeros((width, lanes - experts - 2), BF16)], axis=1
    )
    near_qkv = project(near_one)
    cotangent_far = from_far(after(cotangent, normed_far))
    normed_far, near_qkv, head = lax.optimization_barrier((normed_far, near_qkv, head))
    far_one = jnp.concatenate([normed_far, from_side(normed_far)], axis=0)
    far_qkv = project(far_one)
    near_out, far_out, *logs = attention_forward(leaves, near_qkv, far_qkv)
    far_out, own_grads, cotangent_far, cotangent_side = lax.optimization_barrier(
        (far_out, own_grads, cotangent_far, cotangent_side)
    )

    def branch_part(rows):
        return jnp.dot(rows, w_out, preferred_element_type=F32)

    far_sum = plus_side(branch_part(far_out[0]), branch_part(far_out[1])).astype(BF16)
    branch = plus_side(branch_part(near_out[0]), branch_part(near_out[1]))
    branch_far = from_far(far_sum)
    side_grads = from_side(own_grads)
    cotangent_corner = from_side(cotangent_far)
    far_placed = placed(far_slots, cotangent_far)
    branch_far, side_grads, cotangent_corner, far_placed = lax.optimization_barrier(
        (branch_far, side_grads, cotangent_corner, far_placed)
    )
    residual = tokens.astype(F32) + (branch + branch_far.astype(F32))

    scaled_two, inverse_two = norm_parts(residual)
    normed_two = (scaled_two * ln_mlp).astype(BF16)
    normed_two_far = from_far(normed_two)
    normed_two_side = from_side(normed_two)
    own_rows = sent(placed(own_slots, normed_two))

    def dense(own, side, own_cotangent, side_cotangent):
        return feed(
            own, side, own_cotangent, side_cotangent, head, w_up, w_down, experts, None, QUARTER_ROWS
        )

    def product(left, right):
        return jnp.einsum("gd,gf->df", left, right, preferred_element_type=F32)

    def weight_grads(near_left, far_left, near_right, far_right):
        return product(near_left, near_right) + product(far_left, far_right)

    near_dense = dense(normed_two, normed_two_side, cotangent, cotangent_side)
    near_two = jnp.concatenate([normed_two, normed_two_side], axis=0)
    grad_up = product(near_two, near_dense[5])
    grad_down = product(near_dense[6], near_dense[4])
    normed_two_far, grad_up, grad_down, own_rows = lax.optimization_barrier(
        (normed_two_far, grad_up, grad_down, own_rows)
    )
    far_rows = from_far(own_rows)
    far_grads = sent(after(far_placed, own_rows))
    normed_two_corner = from_side(normed_two_far)
    far_dense = list(dense(normed_two_far, normed_two_corner, cotangent_far, cotangent_corner))

    expert = lax.axis_index("expert").astype(jnp.int32)

    def routed(own, side, own_cotangent, side_cotangent):
        return feed(
            own,
            side,
            own_cotangent,
            side_cotangent,
            head,
            ex_up[0],
            ex_down[0],
            experts,
            expert,
            QUARTER_ROWS,
        )

    def chip_sum(parts, place, *others):
        return plus_side(parts[place], after(parts[place + 1], *others))

    def chip_sum(parts, place, *others):
        return plus_side(parts[place], after(parts[place + 1], *others))

    dense_back_far = chip_sum(far_dense, 2).astype(BF16)
    far_two = jnp.concatenate([normed_two_far, normed_two_corner], axis=0)
    grad_down = (grad_down + product(far_dense[6], far_dense[4])).astype(BF16)
    far_two, grad_down = lax.optimization_barrier((far_two, grad_down))
    grad_up = (grad_up + product(far_two, far_dense[5])).astype(BF16)
    dense_grads = after(jnp.concatenate([grad_up, grad_down], axis=1), far_grads)
    far_rows, dense_back_far, dense_grads = lax.optimization_barrier(
        (far_rows, dense_back_far, dense_grads)
    )
    dense_grads = scatter_sum(dense_grads)
    dense_back_far = from_far(dense_back_far)
    corner_rows = from_side(far_rows)
    side_rows = from_side(own_rows)
    far_expert = routed(far_rows, corner_rows, far_grads, from_side(far_grads))
    *far_expert, dense_back_far = lax.optimization_barrier((*far_expert, dense_back_far))
    far_back = chip_sum(far_expert, 2).astype(BF16)
    own_rows, far_back = lax.optimization_barrier((own_rows, far_back))
    near_expert = routed(own_rows, side_rows, own_grads, side_grads)
    *near_expert, dense_grads = lax.optimization_barrier((*near_expert, dense_grads))

    def picked(rows):
        return lax.dot_general(
            own_slots, rows, (((0,), (0,)), ((), ())), preferred_element_type=F32
        )

    expert_back = (chip_sum(near_expert, 2) + from_far(far_back).astype(F32)).astype(BF16)
    far_expert_out = chip_sum(far_expert, 0, expert_back).astype(BF16)
    dense_out_far = chip_sum(far_dense, 0, expert_back).astype(BF16)
    dense_back = chip_sum(near_dense, 2, far_back) + dense_back_far.astype(F32)

    grad_normed_two = dense_back + picked(sent(expert_back))
    dense_out = chip_sum(near_dense, 0, expert_back)
    expert_out = chip_sum(near_expert, 0, expert_back) + from_far(far_expert_out).astype(F32)
    expert_out = after(expert_out.astype(BF16), grad_normed_two)

    near_active, far_active, near_pre, far_pre, far_expert_out = lax.optimization_barrier(
        (near_expert[4], far_expert[4], near_expert[5], far_expert[5], far_expert_out)
    )
    near_tokens = jnp.concatenate([own_rows, side_rows], axis=0)
    far_tokens = jnp.concatenate([far_rows, corner_rows], axis=0)
    grad_ex_up = weight_grads(near_tokens, far_tokens, near_pre, far_pre)[None]
    grad_ex_down = weight_grads(near_active, far_active, near_expert[6], far_expert[6])[None]

    gain_two = jnp.sum(grad_normed_two * scaled_two, axis=0)
    grad_residual = cotangent.astype(F32) + norm_back(
        grad_normed_two, ln_mlp, scaled_two, inverse_two
    )
    grad_branch = grad_residual.astype(BF16)
    grad_branch_far = from_far(grad_branch)
    grad_branch_side = from_side(grad_branch)

    def into_heads(*rows):
        grads = [jnp.einsum("gd,cd->gc", part, w_out, preferred_element_type=F32) for part in rows]
        return jnp.stack(grads).astype(BF16)

    near_heads = into_heads(grad_branch, grad_branch_side)
    out_rows = sent(expert_out)
    flat = (2 * tok_dev, heads_width)
    near_branch = jnp.concatenate([grad_branch, grad_branch_side], axis=0)
    grad_w_out = product(near_branch, near_out.reshape(flat))
    grad_branch_far, near_heads, grad_w_out, grad_ex_up, grad_ex_down, _, dense_out_far, dense_out = (
        lax.optimization_barrier(
            (
                grad_branch_far,
                near_heads,
                grad_w_out,
                grad_ex_up,
                grad_ex_down,
                expert_out,
                dense_out_far,
                dense_out,
            )
        )
    )
    grad_branch_corner = from_side(grad_branch_far)
    far_heads = into_heads(grad_branch_far, grad_branch_corner)
    dense_out_far = from_far(dense_out_far)
    head_grads = near_dense[7] + far_dense[7] + near_expert[7] + far_expert[7]
    small = jnp.concatenate([head_grads[: experts + 2], gain_two[None]], axis=0)

    def pair_back(pair, near_grads, far_grads):
        return attention_backward(
            leaves, pair, near_qkv, far_qkv, near_grads, far_grads, near_out, far_out, logs
        )

    def pair_weights(pair):
        lanes = slice(pair * PAIR, (pair + 1) * PAIR)
        return jnp.concatenate([w_qkv[part, :, lanes] for part in range(3)], axis=1)

    def total(values):
        return functools.reduce(jnp.add, values)

    pairs = heads_width // PAIR
    near_results, far_results = [None] * pairs, [None] * pairs
    near_results[0], far_results[0] = pair_back(0, near_heads, far_heads)
    far_branch = jnp.concatenate([grad_branch_far, grad_branch_corner], axis=0)
    grad_w_out = grad_w_out + product(far_branch, far_out.reshape(flat))
    small_columns = -(-small.shape[0] // LANES) * LANES
    small_block = jnp.pad(small, ((0, small_columns - small.shape[0]), (0, 0))).T
    branch_grads = jnp.concatenate([grad_w_out.astype(BF16), small_block.astype(BF16)], axis=1)
    near_results[0], far_results[0], out_rows, dense_out_far, branch_grads, near_heads = (
        lax.optimization_barrier(
            (near_results[0], far_results[0], out_rows, dense_out_far, branch_grads, near_heads)
        )
    )
    branch_grads = strips_sent(branch_grads)
    for pair in range(1, pairs):
        near_results[pair], far_results[pair] = pair_back(pair, near_heads, far_heads)
    near_results, far_results, branch_grads = lax.optimization_barrier(
        (near_results, far_results, branch_grads)
    )

    def normed_part(results, quarter):
        return total([dot_nt(results[pair][quarter], pair_weights(pair)) for pair in range(pairs)])

    def qkv_weights(pair, *others):
        near_rows = near_results[pair].reshape(2 * tok_dev, 3 * PAIR)
        far_rows = far_results[pair].reshape(2 * tok_dev, 3 * PAIR)
        near_rows = after(near_rows, *others)
        return weight_grads(near_one, far_one, near_rows, far_rows).astype(BF16)

    corner_part = normed_part(far_results, 1).astype(BF16)
    from_corner = from_side(corner_part).astype(F32)
    first_grads = qkv_weights(0, corner_part)
    far_results, first_grads = lax.optimization_barrier((far_results, first_grads))
    qkv_grads = [strips_sent(first_grads)]
    far_sum = (normed_part(far_results, 0) + from_corner).astype(BF16)
    near_results, far_results, out_rows, far_sum = lax.optimization_barrier(
        (near_results, far_results, out_rows, far_sum)
    )
    near_sum = plus_side(normed_part(near_results, 0), normed_part(near_results, 1))

    scaled_far = normed_far.astype(F32) / ln_attn
    gain_one = jnp.sum(
        near_sum * scaled_one + far_sum.astype(F32) * scaled_far, axis=0, keepdims=True
    )
    gain_one = sum_over(gain_one, "expert")
    out_rows = after(out_rows, gain_one)
    out = (residual + dense_out + dense_out_far.astype(F32) + picked(out_rows)).astype(BF16)
    last_grads = [qkv_weights(pair, far_sum) for pair in range(1, pairs)]
    qkv_grads += [strips_sent(grads) for grads in last_grads]
    far_arrived, gain_one, dense_grads, *_ = lax.optimization_barrier(
        (from_far(far_sum), gain_one, dense_grads, *last_grads)
    )
    grad_normed_one = near_sum + far_arrived.astype(F32)
    grad_ln_attn = sum_over(gain_one, "tensor")[0]
    branch_grads = strips_total(after(branch_grads, gain_one))
    small = sum_over(branch_grads[:, heads_width:], "tensor")
    qkv_grads = jnp.stack(
        [strips_total(grads).reshape(-1, 3, PAIR) for grads in qkv_grads], axis=2
    )
    grad_tokens = grad_residual + norm_back(grad_normed_one, ln_attn, scaled_one, inverse_one)

    strip = qkv_grads.shape[0]
    return (
        out,
        grad_tokens,
        grad_ln_attn,
        qkv_grads.reshape(strip, 3, heads_width).transpose(1, 0, 2),
        branch_grads[:, :heads_width].T,
        small[:, experts + 2],
        dense_grads[:, :hidden].astype(F32),
        dense_grads[:, hidden:].T.astype(F32),
        small[:, :experts],
        small[:, experts : experts + 2],
        grad_ex_up,
        grad_ex_down,
    )


def solution(mesh):
    return jax.shard_map(
        per_device,
        mesh=mesh,
        in_specs=(
            P(("expert", "tensor"), None),
            P(("expert", "tensor"), None),
            P("expert", None),
            P("expert", None),
            P(),
            P(None, None, "tensor"),
            P("tensor", None),
            P(),
            P(None, "tensor"),
            P("tensor", None),
            P(),
            P(),
            P("expert", None, "tensor"),
            P("expert", "tensor", None),
        ),
        out_specs=(
            P(("expert", "tensor"), None),
            P(("expert", "tensor"), None),
            P(),
            P(None, "expert", "tensor"),
            P("tensor", "expert"),
            P("expert"),
            P("expert", "tensor"),
            P("tensor", "expert"),
            P("expert", None),
            P("expert", None),
            P("expert", None, "tensor"),
            P("expert", "tensor", None),
        ),
        check_vma=False,
    )
```

```python
import functools

import jax
import jax.numpy as jnp
from jax import lax
from jax.experimental import pallas as pl
from jax.experimental.layout import Layout, with_layout_constraint
from jax.experimental.pallas import tpu as pltpu
from jax.sharding import PartitionSpec as P

HEAD_DIM = 64
TRUNK = 1024
SEG = 128
SEGS = 13
TREE_LEN = 2560
BRANCHES = 4
FAMILY = 3 * SEG
TEAM = 2 * FAMILY
TEAMS = BRANCHES // 2
QROWS = 256
COVER = 8
PAIR = 2 * HEAD_DIM
NEGATIVE_FILL = -1e30
F32 = jnp.float32
BF16 = jnp.bfloat16
EPSILON = 1e-05


def dot_nn(a, b):
    return lax.dot_general(a, b, (((1,), (0,)), ((), ())), preferred_element_type=F32)


def dot_nt(a, b):
    return lax.dot_general(a, b, (((1,), (1,)), ((), ())), preferred_element_type=F32)


def head_lanes(rows, head):
    lane = lax.broadcasted_iota(jnp.int32, rows.shape, 1)
    return jnp.where(lane // HEAD_DIM == head, rows, jnp.zeros_like(rows))


def causal(scores):
    key = lax.broadcasted_iota(jnp.int32, scores.shape, 0)
    query = lax.broadcasted_iota(jnp.int32, scores.shape, 1)
    return jnp.where(key <= query, scores, NEGATIVE_FILL)


def family_rows(leaves_ref, branch):
    def start(segment):
        return pl.multiple_of(TRUNK + (segment - 1) * SEG, SEG)

    return [start(branch + 1), start(leaves_ref[2 * branch]), start(leaves_ref[2 * branch + 1])]


def transpose_into(target_ref, source_ref, part):
    for first in range(0, TREE_LEN, 512):
        piece = source_ref[part, pl.ds(first, 512), :].astype(F32)
        target_ref[:, pl.ds(first, 512)] = piece.T.astype(BF16)


def widen(piece, first, width, fill):
    parts = []
    if first:
        parts.append(jnp.full((piece.shape[0], first), fill, piece.dtype))
    parts.append(piece)
    rest = width - first - piece.shape[1]
    if rest:
        parts.append(jnp.full((piece.shape[0], rest), fill, piece.dtype))
    return parts[0] if len(parts) == 1 else jnp.concatenate(parts, axis=1)


def trunk_groups(block):
    first = block * QROWS
    groups = [(0, first, 0, QROWS, None)] if first else []
    return groups + [(first, QROWS, 0, QROWS, "causal")]


def team_rows(leaves_ref, team):
    return family_rows(leaves_ref, 2 * team) + family_rows(leaves_ref, 2 * team + 1)


def team_groups(starts):
    groups = [(0, TRUNK, 0, TEAM, None)]
    for first in range(0, TEAM, FAMILY):
        at = first // SEG
        groups.append((starts[at], SEG, first, first + FAMILY, "branch"))
        for leaf in (1, 2):
            begin = first + leaf * SEG
            groups.append((starts[at + leaf], SEG, begin, begin + SEG, "causal"))
    return groups


def masked_scores(keys, queries, rule):
    scores = dot_nt(keys, queries)
    if rule == "causal":
        return causal(scores)
    if rule == "branch":
        return jnp.concatenate([causal(scores[:, :SEG]), scores[:, SEG:]], axis=1)
    return scores


def forward_block(qkv_ref, values_t_ref, queries, groups):
    width = queries.shape[0]
    outs, logs = [], []
    for head in range(2):
        own = head_lanes(queries, head)
        all_scores = [
            masked_scores(qkv_ref[1, pl.ds(start, size), :], own[first:last], rule)
            for start, size, first, last, rule in groups
        ]
        top = functools.reduce(
            jnp.maximum,
            [
                widen(jnp.max(s, axis=0, keepdims=True), first, width, NEGATIVE_FILL)
                for s, (_, _, first, last, _) in zip(all_scores, groups)
            ],
        )
        total, output = None, None
        for s, (start, size, first, last, _) in zip(all_scores, groups):
            weights = jnp.exp(s - top[:, first:last])
            part = widen(jnp.sum(weights, axis=0, keepdims=True), first, width, 0.0)
            values_t = values_t_ref[pl.ds(head * HEAD_DIM, HEAD_DIM), pl.ds(start, size)]
            mixed = widen(dot_nn(values_t, weights.astype(BF16)), first, width, 0.0)
            total = part if total is None else total + part
            output = mixed if output is None else output + mixed
        outs.append(output / total)
        logs.append(top + jnp.log(total))
    return jnp.concatenate(outs, axis=0).T.astype(BF16), jnp.concatenate(logs, axis=0)


def scaled_queries(qkv_ref, starts, size):
    rows = [qkv_ref[0, pl.ds(start, size), :] for start in starts]
    rows = rows[0] if len(rows) == 1 else jnp.concatenate(rows, axis=0)
    return rows * jnp.asarray(HEAD_DIM ** (-0.5), BF16)


def quarter_rows(leaves_ref, offset):
    quarter = TREE_LEN // 4
    return pl.ds(pl.multiple_of((leaves_ref[2 * BRANCHES] ^ offset) * quarter, quarter), quarter)


def forward_kernel(
    leaves_ref,
    near_ref,
    far_ref,
    near_out_ref,
    far_out_ref,
    trunk_log_ref,
    family_log_ref,
    qkv_ref,
    out_ref,
    values_t_ref,
):
    for offset in range(4):
        half_ref = near_ref if offset < 2 else far_ref
        qkv_ref[:, quarter_rows(leaves_ref, offset), :] = half_ref[:, offset % 2]
    transpose_into(values_t_ref, qkv_ref, 2)
    for block in range(TRUNK // QROWS):
        first = block * QROWS
        queries = scaled_queries(qkv_ref, [first], QROWS)
        out, logs = forward_block(qkv_ref, values_t_ref, queries, trunk_groups(block))
        out_ref[pl.ds(first, QROWS), :] = out
        trunk_log_ref[0, :, pl.ds(first, QROWS)] = logs

    def one_team(team, carry):
        starts = team_rows(leaves_ref, team)
        queries = scaled_queries(qkv_ref, starts, SEG)
        out, logs = forward_block(qkv_ref, values_t_ref, queries, team_groups(starts))
        for place, start in enumerate(starts):
            out_ref[pl.ds(start, SEG), :] = out[place * SEG : (place + 1) * SEG]
        family_log_ref[0, team] = logs
        return carry

    lax.fori_loop(0, TEAMS, one_team, 0)
    for offset in range(4):
        half_ref = near_out_ref if offset < 2 else far_out_ref
        half_ref[offset % 2] = out_ref[quarter_rows(leaves_ref, offset), :]


def halves_spec(parts):
    quarter = TREE_LEN // 4
    if parts == 1:
        return pl.BlockSpec((2, quarter, PAIR), lambda p, leaves: (0, 0, p))
    return pl.BlockSpec((parts, 2, quarter, PAIR), lambda p, leaves: (0, 0, 0, p))


def attention_cost(products, cover):
    visited = (TRUNK * (TRUNK + QROWS) // 2 + BRANCHES * FAMILY * (TRUNK + SEG)) // cover
    return pl.CostEstimate(
        flops=2 * products * 4 * visited * 2 * PAIR,
        transcendentals=4 * visited,
        bytes_accessed=8 * TREE_LEN * 4 * HEAD_DIM * 2 // cover,
    )


def attention_forward(leaves, near, far):
    width = near.shape[3]
    quarter = TREE_LEN // 4
    pairs = width // PAIR
    return pl.pallas_call(
        forward_kernel,
        grid_spec=pltpu.PrefetchScalarGridSpec(
            num_scalar_prefetch=1,
            grid=(pairs,),
            in_specs=[halves_spec(3), halves_spec(3)],
            out_specs=[
                halves_spec(1),
                halves_spec(1),
                pl.BlockSpec((1, 2, TRUNK), lambda p, leaves: (p, 0, 0)),
                pl.BlockSpec((1, TEAMS, 2, TEAM), lambda p, leaves: (p, 0, 0, 0)),
            ],
            scratch_shapes=[
                pltpu.VMEM((3, TREE_LEN, PAIR), BF16),
                pltpu.VMEM((TREE_LEN, PAIR), BF16),
                pltpu.VMEM((PAIR, TREE_LEN), BF16),
            ],
        ),
        out_shape=[
            jax.ShapeDtypeStruct((2, quarter, width), BF16),
            jax.ShapeDtypeStruct((2, quarter, width), BF16),
            jax.ShapeDtypeStruct((pairs, 2, TRUNK), F32),
            jax.ShapeDtypeStruct((pairs, TEAMS, 2, TEAM), F32),
        ],
        cost_estimate=attention_cost(2, COVER),
        name="tree_attention",
    )(leaves, near, far)


def backward_block(qkv_ref, keys_t_ref, queries, grads, outs, logs, groups):
    products = grads.astype(F32) * outs.astype(F32)
    products_t = products.T
    key_ds = [[] for _ in groups]
    value_ws = [[] for _ in groups]
    own_q, own_g, query_grads = [], [], []
    for head in range(2):
        own = head_lanes(queries, head)
        own_grads = head_lanes(grads, head)
        own_q.append(own)
        own_g.append(own_grads)
        inner = jnp.sum(
            products_t[head * HEAD_DIM : (head + 1) * HEAD_DIM], axis=0, keepdims=True
        )
        log = logs[head : head + 1]
        query_grad = None
        for place, (start, size, first, last, rule) in enumerate(groups):
            scores = masked_scores(qkv_ref[1, pl.ds(start, size), :], own[first:last], rule)
            weights = jnp.exp(scores - log[:, first:last])
            grad_weights = dot_nt(qkv_ref[2, pl.ds(start, size), :], own_grads[first:last])
            grad_scores = (weights * (grad_weights - inner[:, first:last])).astype(BF16)
            keys_t = keys_t_ref[pl.ds(head * HEAD_DIM, HEAD_DIM), pl.ds(start, size)]
            part = widen(dot_nn(keys_t, grad_scores), first, queries.shape[0], 0.0)
            query_grad = part if query_grad is None else query_grad + part
            key_ds[place].append(grad_scores)
            value_ws[place].append(weights.astype(BF16))
        query_grads.append(query_grad)
    grad_query = (jnp.concatenate(query_grads, axis=0) * HEAD_DIM ** (-0.5)).T.astype(BF16)
    key_grads, value_grads = [], []
    for place, (start, size, first, last, rule) in enumerate(groups):
        stacked_q = jnp.concatenate([own_q[0][first:last], own_q[1][first:last]], axis=0)
        stacked_g = jnp.concatenate([own_g[0][first:last], own_g[1][first:last]], axis=0)
        key_grads.append(dot_nn(jnp.concatenate(key_ds[place], axis=1), stacked_q))
        value_grads.append(dot_nn(jnp.concatenate(value_ws[place], axis=1), stacked_g))
    return grad_query, key_grads, value_grads


def backward_kernel(
    leaves_ref,
    near_ref,
    far_ref,
    near_grads_ref,
    far_grads_ref,
    near_outs_ref,
    far_outs_ref,
    trunk_log_ref,
    family_log_ref,
    near_result_ref,
    far_result_ref,
    qkv_ref,
    grads_ref,
    outs_ref,
    result_ref,
    keys_t_ref,
    trunk_keys_ref,
    trunk_values_ref,
):
    for offset in range(4):
        rows = quarter_rows(leaves_ref, offset)
        at = offset % 2
        qkv_ref[:, rows, :] = (near_ref if offset < 2 else far_ref)[:, at]
        grads_ref[rows, :] = (near_grads_ref if offset < 2 else far_grads_ref)[at]
        outs_ref[rows, :] = (near_outs_ref if offset < 2 else far_outs_ref)[at]
    transpose_into(keys_t_ref, qkv_ref, 1)
    trunk_keys_ref[...] = jnp.zeros_like(trunk_keys_ref)
    trunk_values_ref[...] = jnp.zeros_like(trunk_values_ref)
    for block in range(TRUNK // QROWS):
        first = block * QROWS
        rows = pl.ds(first, QROWS)
        groups = trunk_groups(block)
        grad_query, key_grads, value_grads = backward_block(
            qkv_ref,
            keys_t_ref,
            scaled_queries(qkv_ref, [first], QROWS),
            grads_ref[rows, :],
            outs_ref[rows, :],
            trunk_log_ref[0, :, rows],
            groups,
        )
        result_ref[0, rows, :] = grad_query
        for (start, size, _, _, _), key_grad, value_grad in zip(groups, key_grads, value_grads):
            trunk_keys_ref[pl.ds(start, size), :] += key_grad
            trunk_values_ref[pl.ds(start, size), :] += value_grad

    def one_team(team, carry):
        starts = team_rows(leaves_ref, team)
        groups = team_groups(starts)
        grad_query, key_grads, value_grads = backward_block(
            qkv_ref,
            keys_t_ref,
            scaled_queries(qkv_ref, starts, SEG),
            jnp.concatenate([grads_ref[pl.ds(start, SEG), :] for start in starts], axis=0),
            jnp.concatenate([outs_ref[pl.ds(start, SEG), :] for start in starts], axis=0),
            family_log_ref[0, team],
            groups,
        )
        trunk_keys_ref[...] += key_grads[0]
        trunk_values_ref[...] += value_grads[0]
        for place, start in enumerate(starts):
            rows = pl.ds(start, SEG)
            result_ref[0, rows, :] = grad_query[place * SEG : (place + 1) * SEG]
            result_ref[1, rows, :] = key_grads[1 + place].astype(BF16)
            result_ref[2, rows, :] = value_grads[1 + place].astype(BF16)
        return carry

    lax.fori_loop(0, TEAMS, one_team, 0)
    result_ref[1, pl.ds(0, TRUNK), :] = trunk_keys_ref[...].astype(BF16)
    result_ref[2, pl.ds(0, TRUNK), :] = trunk_values_ref[...].astype(BF16)
    for offset in range(4):
        half_ref = near_result_ref if offset < 2 else far_result_ref
        rows = quarter_rows(leaves_ref, offset)
        for part in range(3):
            half_ref[offset % 2, :, part * PAIR : (part + 1) * PAIR] = result_ref[part, rows, :]


def attention_backward(leaves, pair, near, far, near_grads, far_grads, near_outs, far_outs, logs):
    quarter = TREE_LEN // 4
    rows = pl.BlockSpec((2, quarter, PAIR), lambda i, leaves: (0, 0, pair))
    parts = pl.BlockSpec((3, 2, quarter, PAIR), lambda i, leaves: (0, 0, 0, pair))
    result = pl.BlockSpec((2, quarter, 3 * PAIR), lambda i, leaves: (0, 0, 0))
    shape = jax.ShapeDtypeStruct((2, quarter, 3 * PAIR), BF16)
    return pl.pallas_call(
        backward_kernel,
        grid_spec=pltpu.PrefetchScalarGridSpec(
            num_scalar_prefetch=1,
            grid=(1,),
            in_specs=[
                parts,
                parts,
                rows,
                rows,
                rows,
                rows,
                pl.BlockSpec((1, 2, TRUNK), lambda i, leaves: (pair, 0, 0)),
                pl.BlockSpec((1, TEAMS, 2, TEAM), lambda i, leaves: (pair, 0, 0, 0)),
            ],
            out_specs=[result, result],
            scratch_shapes=[
                pltpu.VMEM((3, TREE_LEN, PAIR), BF16),
                pltpu.VMEM((TREE_LEN, PAIR), BF16),
                pltpu.VMEM((TREE_LEN, PAIR), BF16),
                pltpu.VMEM((3, TREE_LEN, PAIR), BF16),
                pltpu.VMEM((PAIR, TREE_LEN), BF16),
                pltpu.VMEM((TRUNK, PAIR), F32),
                pltpu.VMEM((TRUNK, PAIR), F32),
            ],
        ),
        out_shape=[shape, shape],
        cost_estimate=attention_cost(5, 10),
        name="tree_attention_back",
    )(leaves, near, far, near_grads, far_grads, near_outs, far_outs, *logs)


def leaf_order(parents_row):
    first_leaf = BRANCHES + 1
    leaf_parents = parents_row[first_leaf:]
    segments = first_leaf + jnp.arange(leaf_parents.shape[0], dtype=jnp.int32)
    same = leaf_parents[:, None] == leaf_parents[None, :]
    later = segments[None, :] < segments[:, None]
    place = 2 * (leaf_parents - 1) + jnp.sum(jnp.where(same & later, 1, 0), axis=1)
    slots = jnp.arange(2 * BRANCHES, dtype=jnp.int32)
    return jnp.sum(jnp.where(slots[:, None] == place[None, :], segments[None, :], 0), axis=1)


def gates(logits, experts, expert):
    lane = lax.broadcasted_iota(jnp.int32, logits.shape, 1)
    first, second = logits[:, experts : experts + 1], logits[:, experts + 1 : experts + 2]
    top = jnp.maximum(first, second)
    first, second = jnp.exp(first - top), jnp.exp(second - top)
    total = first + second
    first, second = first / total, second / total
    if expert is None:
        return lane, first, second, None, None
    routed = jnp.where(lane < experts, logits, NEGATIVE_FILL)
    raised = jnp.exp(routed - jnp.max(routed, axis=1, keepdims=True))
    probs = raised / jnp.sum(raised, axis=1, keepdims=True)
    gate = jnp.sum(jnp.where(lane == expert, probs, 0.0), axis=1, keepdims=True)
    return lane, first, second, probs, gate


def both(own_ref, side_ref):
    return jnp.concatenate([own_ref[...], side_ref[...]], axis=0)


def split_store(own_ref, side_ref, rows):
    half = rows.shape[0] // 2
    own_ref[...] = rows[:half]
    side_ref[...] = rows[half:]


def feed_kernel(
    experts,
    routed,
    expert_ref,
    own_ref,
    side_ref,
    own_grads_ref,
    side_grads_ref,
    head_ref,
    up_ref,
    down_ref,
    own_out_ref,
    side_out_ref,
    own_back_ref,
    side_back_ref,
    active_ref,
    pre_ref,
    grad_ref,
    head_grad_ref,
):
    rows = both(own_ref, side_ref)
    grads = both(own_grads_ref, side_grads_ref).astype(F32)
    expert = expert_ref[0] if routed else None
    logits = dot_nn(rows, head_ref[...])
    lane, first, second, probs, gate = gates(logits, experts, expert)
    coef = second * gate if routed else first
    weighted = (coef * grads).astype(BF16)
    pre = dot_nn(rows, up_ref[...])
    grad_active = dot_nt(weighted, down_ref[...])
    cumulative = 0.5 + 0.5 * lax.erf(pre * 0.7071067811865476)
    slope = cumulative + pre * jnp.exp(-0.5 * pre * pre) * 0.3989422804014327
    active = (pre * cumulative).astype(BF16)
    grad_pre = (grad_active * slope).astype(BF16)
    half = rows.shape[0] // 2
    for ref, value in ((active_ref, active), (pre_ref, grad_pre), (grad_ref, weighted)):
        ref[0] = value[:half]
        ref[1] = value[half:]
    out = dot_nn(active, down_ref[...])
    split_store(own_out_ref, side_out_ref, (coef * out).astype(BF16))
    inner = jnp.sum(grads * out, axis=1, keepdims=True)
    swing = first * second * inner
    if routed:
        swing = -gate * swing
    grad_logits = jnp.where(lane == experts, swing, jnp.where(lane == experts + 1, -swing, 0.0))
    if routed:
        picked = jnp.where(lane == expert, 1.0, 0.0) - gate
        grad_logits = grad_logits + jnp.where(
            lane < experts, probs * picked * (second * inner), 0.0
        )
    back = dot_nt(grad_pre, up_ref[...]) + dot_nt(grad_logits.astype(BF16), head_ref[...])
    split_store(own_back_ref, side_back_ref, back.astype(BF16))
    head_grad = dot_nn(grad_logits.T.astype(BF16), rows)

    @pl.when(pl.program_id(0) == 0)
    def _():
        head_grad_ref[...] = jnp.zeros_like(head_grad_ref)

    head_grad_ref[...] += head_grad


def feed(own, side, own_grads, side_grads, head, up, down, experts, expert, size):
    count = own.shape[0]
    width, hidden = up.shape
    steps = count // size
    lanes = head.shape[1]
    routed = expert is not None
    pick = jnp.reshape(expert, (1,)) if routed else jnp.zeros((1,), jnp.int32)
    rows = pl.BlockSpec((size, width), lambda i, pick: (i, 0))

    def whole(shape):
        return pl.BlockSpec(shape, lambda i, pick: (0, 0), pipeline_mode=pl.Buffered(1))

    def pairs(columns):
        return pl.BlockSpec((2, size, columns), lambda i, pick: (0, i, 0))

    quarter = jax.ShapeDtypeStruct((count, width), BF16)
    *sums, active, pre, weighted, head_grad = pl.pallas_call(
        functools.partial(feed_kernel, experts, routed),
        grid_spec=pltpu.PrefetchScalarGridSpec(
            num_scalar_prefetch=1,
            grid=(steps,),
            in_specs=[
                rows,
                rows,
                rows,
                rows,
                whole((width, lanes)),
                whole((width, hidden)),
                whole((hidden, width)),
            ],
            out_specs=[
                rows,
                rows,
                rows,
                rows,
                pairs(hidden),
                pairs(hidden),
                pairs(width),
                pl.BlockSpec((lanes, width), lambda i, pick: (0, 0)),
            ],
        ),
        out_shape=[
            quarter,
            quarter,
            quarter,
            quarter,
            jax.ShapeDtypeStruct((2, count, hidden), BF16),
            jax.ShapeDtypeStruct((2, count, hidden), BF16),
            jax.ShapeDtypeStruct((2, count, width), BF16),
            jax.ShapeDtypeStruct((lanes, width), F32),
        ],
        cost_estimate=pl.CostEstimate(
            flops=16 * count * width * hidden // COVER,
            transcendentals=4 * count * hidden // COVER,
            bytes_accessed=2 * (8 * count * width + 4 * count * hidden + 2 * width * hidden) // COVER,
        ),
        compiler_params=pltpu.CompilerParams(vmem_limit_bytes=60 * 1024 * 1024),
        name="feed_routed" if routed else "feed_dense",
    )(pick, own, side, own_grads, side_grads, head, up, down)
    flat = [value.reshape(2 * count, value.shape[2]) for value in (active, pre, weighted)]
    return [*sums, *flat, head_grad]


LANES = 128
QUARTER_ROWS = 128


def norm_parts(values):
    row_mean = jnp.mean(values, axis=-1, keepdims=True)
    centred = values - row_mean
    row_var = jnp.mean(centred * centred, axis=-1, keepdims=True)
    inverse = lax.rsqrt(row_var + EPSILON)
    return (centred * inverse, inverse)


def norm_back(grad_normed, gain_vec, scaled, inverse):
    grad_scaled = grad_normed * gain_vec
    first_mean = jnp.mean(grad_scaled, axis=-1, keepdims=True)
    second = jnp.mean(grad_scaled * scaled, axis=-1, keepdims=True)
    return inverse * (grad_scaled - first_mean - scaled * second)


def after(value, *others):
    return lax.optimization_barrier((value, *others))[0]


def from_side(values):
    return lax.ppermute(values, "tensor", [(i, i ^ 1) for i in range(4)])


def from_far(values):
    return lax.ppermute(values, "tensor", [(i, i ^ 2) for i in range(4)])


def plus_side(own, side):
    return own.astype(F32) + from_side(side.astype(BF16)).astype(F32)


def sum_over(values, axis):
    count, step = lax.axis_size(axis), 1
    while step < count:
        pairs = [(i, i ^ step) for i in range(count)]
        values = values + lax.ppermute(values, axis, pairs)
        step *= 2
    return values


def exchange(blocks):
    return lax.all_to_all(blocks, "expert", split_axis=0, concat_axis=0, tiled=True)


def scatter_sum(strips):
    strips = with_layout_constraint(strips.astype(BF16), Layout(major_to_minor=(0, 1)))
    return lax.psum_scatter(strips, "expert", scatter_dimension=0, tiled=True)


def strips_sent(grads):
    return exchange(grads.reshape(lax.axis_size("expert"), -1, grads.shape[1]))


def strips_total(strips):
    return jnp.sum(strips.astype(F32), axis=0)


def slots_of(expert_ids, experts, capacity):
    rows = expert_ids.shape[0]
    chosen = expert_ids[:, None] == jnp.arange(experts, dtype=jnp.int32)[None, :]
    at = jnp.arange(rows, dtype=jnp.int32)
    before = (at[None, :] < at[:, None]).astype(BF16)
    earlier = jnp.dot(before, chosen.astype(BF16), preferred_element_type=F32)
    slot = jnp.sum(jnp.where(chosen, earlier, 0.0), axis=1).astype(jnp.int32)
    place = expert_ids * capacity + slot
    places = jnp.arange(experts * capacity, dtype=jnp.int32)
    return (places[:, None] == place[None, :]).astype(BF16)


def per_device(
    tokens,
    cotangent,
    routes,
    parents,
    ln_attn,
    w_qkv,
    w_out,
    ln_mlp,
    w_up,
    w_down,
    w_router,
    w_mix,
    ex_up,
    ex_down,
):
    tok_dev, width = tokens.shape
    mine = lax.axis_index("tensor")
    experts = w_router.shape[1]
    capacity = max(2, tok_dev * 7 // (5 * experts))
    heads_width = w_qkv.shape[2]
    hidden = w_up.shape[1]
    leaves = jnp.concatenate([leaf_order(parents[0]), mine.astype(jnp.int32)[None]])

    scaled_one, inverse_one = norm_parts(tokens.astype(F32))
    normed_own = (scaled_one * ln_attn).astype(BF16)
    normed_far = from_far(normed_own)
    near_one = jnp.concatenate([normed_own, from_side(normed_own)], axis=0)

    quarter_ids = routes[:, 0].reshape(4, tok_dev)

    def slots_at(offset):
        ids = lax.dynamic_index_in_dim(quarter_ids, mine ^ offset, 0, keepdims=False)
        return slots_of(ids, experts, capacity)

    own_slots, far_slots = slots_at(0), slots_at(2)

    def placed(slots, rows):
        return jnp.dot(slots, rows, preferred_element_type=F32).astype(BF16)

    def sent(rows):
        return exchange(rows.reshape(experts, capacity, width)).reshape(-1, width)

    own_grads = sent(placed(own_slots, cotangent))
    cotangent_side = from_side(cotangent)

    def project(rows):
        qkv = jnp.einsum("td,sdc->stc", rows, w_qkv, preferred_element_type=F32)
        return qkv.astype(BF16).reshape(3, 2, tok_dev, heads_width)

    lanes = -(-(experts + 2) // LANES) * LANES
    head = jnp.concatenate(
        [w_router, w_mix, jnp.zeros((width, lanes - experts - 2), BF16)], axis=1
    )
    near_qkv = project(near_one)
    cotangent_far = from_far(after(cotangent, normed_far))
    normed_far, near_qkv, head = lax.optimization_barrier((normed_far, near_qkv, head))
    far_one = jnp.concatenate([normed_far, from_side(normed_far)], axis=0)
    far_qkv = project(far_one)
    near_out, far_out, *logs = attention_forward(leaves, near_qkv, far_qkv)
    far_out, own_grads, cotangent_far, cotangent_side = lax.optimization_barrier(
        (far_out, own_grads, cotangent_far, cotangent_side)
    )

    def branch_part(rows):
        return jnp.dot(rows, w_out, preferred_element_type=F32)

    far_sum = plus_side(branch_part(far_out[0]), branch_part(far_out[1])).astype(BF16)
    branch = plus_side(branch_part(near_out[0]), branch_part(near_out[1]))
    branch_far = from_far(far_sum)
    side_grads = from_side(own_grads)
    cotangent_corner = from_side(cotangent_far)
    far_placed = placed(far_slots, cotangent_far)
    branch_far, side_grads, cotangent_corner, far_placed = lax.optimization_barrier(
        (branch_far, side_grads, cotangent_corner, far_placed)
    )
    residual = tokens.astype(F32) + (branch + branch_far.astype(F32))

    scaled_two, inverse_two = norm_parts(residual)
    normed_two = (scaled_two * ln_mlp).astype(BF16)
    normed_two_far = from_far(normed_two)
    normed_two_side = from_side(normed_two)
    own_rows = sent(placed(own_slots, normed_two))

    def dense(own, side, own_cotangent, side_cotangent):
        return feed(
            own, side, own_cotangent, side_cotangent, head, w_up, w_down, experts, None, QUARTER_ROWS
        )

    def product(left, right):
        return jnp.einsum("gd,gf->df", left, right, preferred_element_type=F32)

    def weight_grads(near_left, far_left, near_right, far_right):
        return product(near_left, near_right) + product(far_left, far_right)

    near_dense = dense(normed_two, normed_two_side, cotangent, cotangent_side)
    near_two = jnp.concatenate([normed_two, normed_two_side], axis=0)
    grad_up = product(near_two, near_dense[5])
    grad_down = product(near_dense[6], near_dense[4])
    normed_two_far, grad_up, grad_down, own_rows = lax.optimization_barrier(
        (normed_two_far, grad_up, grad_down, own_rows)
    )
    far_rows = from_far(own_rows)
    far_grads = sent(after(far_placed, own_rows))
    normed_two_corner = from_side(normed_two_far)
    far_dense = list(dense(normed_two_far, normed_two_corner, cotangent_far, cotangent_corner))

    expert = lax.axis_index("expert").astype(jnp.int32)

    def routed(own, side, own_cotangent, side_cotangent):
        return feed(
            own,
            side,
            own_cotangent,
            side_cotangent,
            head,
            ex_up[0],
            ex_down[0],
            experts,
            expert,
            QUARTER_ROWS,
        )

    def chip_sum(parts, place, *others):
        return plus_side(parts[place], after(parts[place + 1], *others))

    def chip_sum(parts, place, *others):
        return plus_side(parts[place], after(parts[place + 1], *others))

    dense_back_far = chip_sum(far_dense, 2).astype(BF16)
    far_two = jnp.concatenate([normed_two_far, normed_two_corner], axis=0)
    grad_down = (grad_down + product(far_dense[6], far_dense[4])).astype(BF16)
    far_two, grad_down = lax.optimization_barrier((far_two, grad_down))
    grad_up = (grad_up + product(far_two, far_dense[5])).astype(BF16)
    dense_grads = after(jnp.concatenate([grad_up, grad_down], axis=1), far_grads)
    corner_rows = from_side(far_rows)
    far_rows, dense_back_far, dense_grads = lax.optimization_barrier(
        (far_rows, dense_back_far, dense_grads)
    )
    dense_grads = scatter_sum(dense_grads)
    dense_back_far = from_far(dense_back_far)
    side_rows = from_side(own_rows)
    far_expert = routed(far_rows, corner_rows, far_grads, from_side(far_grads))
    *far_expert, dense_back_far = lax.optimization_barrier((*far_expert, dense_back_far))
    far_back = chip_sum(far_expert, 2).astype(BF16)
    own_rows, far_back = lax.optimization_barrier((own_rows, far_back))
    near_expert = routed(own_rows, side_rows, own_grads, side_grads)
    *near_expert, dense_grads = lax.optimization_barrier((*near_expert, dense_grads))

    def picked(rows):
        return lax.dot_general(
            own_slots, rows, (((0,), (0,)), ((), ())), preferred_element_type=F32
        )

    expert_back = (chip_sum(near_expert, 2) + from_far(far_back).astype(F32)).astype(BF16)
    far_expert_out = chip_sum(far_expert, 0, expert_back).astype(BF16)
    dense_out_far = chip_sum(far_dense, 0, expert_back).astype(BF16)
    dense_back = chip_sum(near_dense, 2, far_back) + dense_back_far.astype(F32)

    grad_normed_two = dense_back + picked(sent(expert_back))
    dense_out = chip_sum(near_dense, 0, expert_back)
    expert_out = chip_sum(near_expert, 0, expert_back) + from_far(far_expert_out).astype(F32)
    expert_out = after(expert_out.astype(BF16), grad_normed_two)

    near_active, far_active, near_pre, far_pre, far_expert_out = lax.optimization_barrier(
        (near_expert[4], far_expert[4], near_expert[5], far_expert[5], far_expert_out)
    )
    near_tokens = jnp.concatenate([own_rows, side_rows], axis=0)
    far_tokens = jnp.concatenate([far_rows, corner_rows], axis=0)
    grad_ex_up = weight_grads(near_tokens, far_tokens, near_pre, far_pre)[None]
    grad_ex_down = weight_grads(near_active, far_active, near_expert[6], far_expert[6])[None]

    gain_two = jnp.sum(grad_normed_two * scaled_two, axis=0)
    grad_residual = cotangent.astype(F32) + norm_back(
        grad_normed_two, ln_mlp, scaled_two, inverse_two
    )
    grad_branch = grad_residual.astype(BF16)
    grad_branch_far = from_far(grad_branch)
    grad_branch_side = from_side(grad_branch)

    def into_heads(*rows):
        grads = [jnp.einsum("gd,cd->gc", part, w_out, preferred_element_type=F32) for part in rows]
        return jnp.stack(grads).astype(BF16)

    near_heads = into_heads(grad_branch, grad_branch_side)
    out_rows = sent(expert_out)
    flat = (2 * tok_dev, heads_width)
    near_branch = jnp.concatenate([grad_branch, grad_branch_side], axis=0)
    grad_w_out = product(near_branch, near_out.reshape(flat))
    grad_branch_far, near_heads, grad_w_out, grad_ex_up, grad_ex_down, _, dense_out_far, dense_out = (
        lax.optimization_barrier(
            (
                grad_branch_far,
                near_heads,
                grad_w_out,
                grad_ex_up,
                grad_ex_down,
                expert_out,
                dense_out_far,
                dense_out,
            )
        )
    )
    grad_branch_corner = from_side(grad_branch_far)
    far_heads = into_heads(grad_branch_far, grad_branch_corner)
    dense_out_far = from_far(dense_out_far)
    head_grads = near_dense[7] + far_dense[7] + near_expert[7] + far_expert[7]
    small = jnp.concatenate([head_grads[: experts + 2], gain_two[None]], axis=0)

    def pair_back(pair, near_grads, far_grads):
        return attention_backward(
            leaves, pair, near_qkv, far_qkv, near_grads, far_grads, near_out, far_out, logs
        )

    def pair_weights(pair):
        lanes = slice(pair * PAIR, (pair + 1) * PAIR)
        return jnp.concatenate([w_qkv[part, :, lanes] for part in range(3)], axis=1)

    def total(values):
        return functools.reduce(jnp.add, values)

    pairs = heads_width // PAIR
    near_results, far_results = [None] * pairs, [None] * pairs
    near_results[0], far_results[0] = pair_back(0, near_heads, far_heads)
    far_branch = jnp.concatenate([grad_branch_far, grad_branch_corner], axis=0)
    grad_w_out = grad_w_out + product(far_branch, far_out.reshape(flat))
    small_columns = -(-small.shape[0] // LANES) * LANES
    small_block = jnp.pad(small, ((0, small_columns - small.shape[0]), (0, 0))).T
    branch_grads = jnp.concatenate([grad_w_out.astype(BF16), small_block.astype(BF16)], axis=1)
    near_results[0], far_results[0], out_rows, dense_out_far, branch_grads, near_heads = (
        lax.optimization_barrier(
            (near_results[0], far_results[0], out_rows, dense_out_far, branch_grads, near_heads)
        )
    )
    branch_grads = strips_sent(branch_grads)
    for pair in range(1, pairs):
        near_results[pair], far_results[pair] = pair_back(pair, near_heads, far_heads)
    near_results, far_results, branch_grads = lax.optimization_barrier(
        (near_results, far_results, branch_grads)
    )

    def normed_part(results, quarter):
        return total([dot_nt(results[pair][quarter], pair_weights(pair)) for pair in range(pairs)])

    def qkv_weights(pair, *others):
        near_rows = near_results[pair].reshape(2 * tok_dev, 3 * PAIR)
        far_rows = far_results[pair].reshape(2 * tok_dev, 3 * PAIR)
        near_rows = after(near_rows, *others)
        return weight_grads(near_one, far_one, near_rows, far_rows).astype(BF16)

    corner_part = normed_part(far_results, 1).astype(BF16)
    from_corner = from_side(corner_part).astype(F32)
    first_grads = qkv_weights(0, corner_part)
    far_results, first_grads = lax.optimization_barrier((far_results, first_grads))
    qkv_grads = [strips_sent(first_grads)]
    far_sum = (normed_part(far_results, 0) + from_corner).astype(BF16)
    near_results, far_results, out_rows, far_sum, branch_grads = lax.optimization_barrier(
        (near_results, far_results, out_rows, far_sum, branch_grads)
    )
    near_sum = plus_side(normed_part(near_results, 0), normed_part(near_results, 1))

    scaled_far = normed_far.astype(F32) / ln_attn
    gain_one = jnp.sum(
        near_sum * scaled_one + far_sum.astype(F32) * scaled_far, axis=0, keepdims=True
    )
    gain_one = sum_over(gain_one, "expert")
    out_rows = after(out_rows, gain_one)
    out = (residual + dense_out + dense_out_far.astype(F32) + picked(out_rows)).astype(BF16)
    last_grads = [qkv_weights(pair, far_sum) for pair in range(1, pairs)]
    qkv_grads += [strips_sent(grads) for grads in last_grads]
    branch_grads = strips_total(branch_grads)
    small = sum_over(branch_grads[:, heads_width:], "tensor")
    far_arrived, gain_one, dense_grads, small, *_ = lax.optimization_barrier(
        (from_far(far_sum), gain_one, dense_grads, small, *last_grads)
    )
    grad_normed_one = near_sum + far_arrived.astype(F32)
    grad_ln_attn = sum_over(gain_one, "tensor")[0]
    qkv_grads = jnp.stack(
        [strips_total(grads).reshape(-1, 3, PAIR) for grads in qkv_grads], axis=2
    )
    grad_tokens = grad_residual + norm_back(grad_normed_one, ln_attn, scaled_one, inverse_one)

    strip = qkv_grads.shape[0]
    return (
        out,
        grad_tokens,
        grad_ln_attn,
        qkv_grads.reshape(strip, 3, heads_width).transpose(1, 0, 2),
        branch_grads[:, :heads_width].T,
        small[:, experts + 2],
        dense_grads[:, :hidden].astype(F32),
        dense_grads[:, hidden:].T.astype(F32),
        small[:, :experts],
        small[:, experts : experts + 2],
        grad_ex_up,
        grad_ex_down,
    )


def solution(mesh):
    return jax.shard_map(
        per_device,
        mesh=mesh,
        in_specs=(
            P(("expert", "tensor"), None),
            P(("expert", "tensor"), None),
            P("expert", None),
            P("expert", None),
            P(),
            P(None, None, "tensor"),
            P("tensor", None),
            P(),
            P(None, "tensor"),
            P("tensor", None),
            P(),
            P(),
            P("expert", None, "tensor"),
            P("expert", "tensor", None),
        ),
        out_specs=(
            P(("expert", "tensor"), None),
            P(("expert", "tensor"), None),
            P(),
            P(None, "expert", "tensor"),
            P("tensor", "expert"),
            P("expert"),
            P("expert", "tensor"),
            P("tensor", "expert"),
            P("expert", None),
            P("expert", None),
            P("expert", None, "tensor"),
            P("expert", "tensor", None),
        ),
        check_vma=False,
    )
```

```python
import functools

import jax
import jax.numpy as jnp
from jax import lax
from jax.experimental import pallas as pl
from jax.experimental.layout import Layout, with_layout_constraint
from jax.experimental.pallas import tpu as pltpu
from jax.sharding import PartitionSpec as P

HEAD_DIM = 64
TRUNK = 1024
SEG = 128
SEGS = 13
TREE_LEN = 2560
BRANCHES = 4
FAMILY = 3 * SEG
TEAM = 2 * FAMILY
TEAMS = BRANCHES // 2
QROWS = 256
COVER = 8
PAIR = 2 * HEAD_DIM
NEGATIVE_FILL = -1e30
F32 = jnp.float32
BF16 = jnp.bfloat16
EPSILON = 1e-05


def dot_nn(a, b):
    return lax.dot_general(a, b, (((1,), (0,)), ((), ())), preferred_element_type=F32)


def dot_nt(a, b):
    return lax.dot_general(a, b, (((1,), (1,)), ((), ())), preferred_element_type=F32)


def head_lanes(rows, head):
    lane = lax.broadcasted_iota(jnp.int32, rows.shape, 1)
    return jnp.where(lane // HEAD_DIM == head, rows, jnp.zeros_like(rows))


def causal(scores):
    key = lax.broadcasted_iota(jnp.int32, scores.shape, 0)
    query = lax.broadcasted_iota(jnp.int32, scores.shape, 1)
    return jnp.where(key <= query, scores, NEGATIVE_FILL)


def family_rows(leaves_ref, branch):
    def start(segment):
        return pl.multiple_of(TRUNK + (segment - 1) * SEG, SEG)

    return [start(branch + 1), start(leaves_ref[2 * branch]), start(leaves_ref[2 * branch + 1])]


def transpose_into(target_ref, source_ref, part):
    for first in range(0, TREE_LEN, 512):
        piece = source_ref[part, pl.ds(first, 512), :].astype(F32)
        target_ref[:, pl.ds(first, 512)] = piece.T.astype(BF16)


def widen(piece, first, width, fill):
    parts = []
    if first:
        parts.append(jnp.full((piece.shape[0], first), fill, piece.dtype))
    parts.append(piece)
    rest = width - first - piece.shape[1]
    if rest:
        parts.append(jnp.full((piece.shape[0], rest), fill, piece.dtype))
    return parts[0] if len(parts) == 1 else jnp.concatenate(parts, axis=1)


def trunk_groups(block):
    first = block * QROWS
    groups = [(0, first, 0, QROWS, None)] if first else []
    return groups + [(first, QROWS, 0, QROWS, "causal")]


def team_rows(leaves_ref, team):
    return family_rows(leaves_ref, 2 * team) + family_rows(leaves_ref, 2 * team + 1)


def team_groups(starts):
    groups = [(0, TRUNK, 0, TEAM, None)]
    for first in range(0, TEAM, FAMILY):
        at = first // SEG
        groups.append((starts[at], SEG, first, first + FAMILY, "branch"))
        for leaf in (1, 2):
            begin = first + leaf * SEG
            groups.append((starts[at + leaf], SEG, begin, begin + SEG, "causal"))
    return groups


def masked_scores(keys, queries, rule):
    scores = dot_nt(keys, queries)
    if rule == "causal":
        return causal(scores)
    if rule == "branch":
        return jnp.concatenate([causal(scores[:, :SEG]), scores[:, SEG:]], axis=1)
    return scores


def forward_block(qkv_ref, values_t_ref, queries, groups):
    width = queries.shape[0]
    outs, logs = [], []
    for head in range(2):
        own = head_lanes(queries, head)
        all_scores = [
            masked_scores(qkv_ref[1, pl.ds(start, size), :], own[first:last], rule)
            for start, size, first, last, rule in groups
        ]
        top = functools.reduce(
            jnp.maximum,
            [
                widen(jnp.max(s, axis=0, keepdims=True), first, width, NEGATIVE_FILL)
                for s, (_, _, first, last, _) in zip(all_scores, groups)
            ],
        )
        total, output = None, None
        for s, (start, size, first, last, _) in zip(all_scores, groups):
            weights = jnp.exp(s - top[:, first:last])
            part = widen(jnp.sum(weights, axis=0, keepdims=True), first, width, 0.0)
            values_t = values_t_ref[pl.ds(head * HEAD_DIM, HEAD_DIM), pl.ds(start, size)]
            mixed = widen(dot_nn(values_t, weights.astype(BF16)), first, width, 0.0)
            total = part if total is None else total + part
            output = mixed if output is None else output + mixed
        outs.append(output / total)
        logs.append(top + jnp.log(total))
    return jnp.concatenate(outs, axis=0).T.astype(BF16), jnp.concatenate(logs, axis=0)


def scaled_queries(qkv_ref, starts, size):
    rows = [qkv_ref[0, pl.ds(start, size), :] for start in starts]
    rows = rows[0] if len(rows) == 1 else jnp.concatenate(rows, axis=0)
    return rows * jnp.asarray(HEAD_DIM ** (-0.5), BF16)


def quarter_rows(leaves_ref, offset):
    quarter = TREE_LEN // 4
    return pl.ds(pl.multiple_of((leaves_ref[2 * BRANCHES] ^ offset) * quarter, quarter), quarter)


def forward_kernel(
    leaves_ref,
    near_ref,
    far_ref,
    near_out_ref,
    far_out_ref,
    trunk_log_ref,
    family_log_ref,
    qkv_ref,
    out_ref,
    values_t_ref,
):
    for offset in range(4):
        half_ref = near_ref if offset < 2 else far_ref
        qkv_ref[:, quarter_rows(leaves_ref, offset), :] = half_ref[:, offset % 2]
    transpose_into(values_t_ref, qkv_ref, 2)
    for block in range(TRUNK // QROWS):
        first = block * QROWS
        queries = scaled_queries(qkv_ref, [first], QROWS)
        out, logs = forward_block(qkv_ref, values_t_ref, queries, trunk_groups(block))
        out_ref[pl.ds(first, QROWS), :] = out
        trunk_log_ref[0, :, pl.ds(first, QROWS)] = logs

    def one_team(team, carry):
        starts = team_rows(leaves_ref, team)
        queries = scaled_queries(qkv_ref, starts, SEG)
        out, logs = forward_block(qkv_ref, values_t_ref, queries, team_groups(starts))
        for place, start in enumerate(starts):
            out_ref[pl.ds(start, SEG), :] = out[place * SEG : (place + 1) * SEG]
        family_log_ref[0, team] = logs
        return carry

    lax.fori_loop(0, TEAMS, one_team, 0)
    for offset in range(4):
        half_ref = near_out_ref if offset < 2 else far_out_ref
        half_ref[offset % 2] = out_ref[quarter_rows(leaves_ref, offset), :]


def halves_spec(parts):
    quarter = TREE_LEN // 4
    if parts == 1:
        return pl.BlockSpec((2, quarter, PAIR), lambda p, leaves: (0, 0, p))
    return pl.BlockSpec((parts, 2, quarter, PAIR), lambda p, leaves: (0, 0, 0, p))


def attention_cost(products, cover):
    visited = (TRUNK * (TRUNK + QROWS) // 2 + BRANCHES * FAMILY * (TRUNK + SEG)) // cover
    return pl.CostEstimate(
        flops=2 * products * 4 * visited * 2 * PAIR,
        transcendentals=4 * visited,
        bytes_accessed=8 * TREE_LEN * 4 * HEAD_DIM * 2 // cover,
    )


def attention_forward(leaves, near, far):
    width = near.shape[3]
    quarter = TREE_LEN // 4
    pairs = width // PAIR
    return pl.pallas_call(
        forward_kernel,
        grid_spec=pltpu.PrefetchScalarGridSpec(
            num_scalar_prefetch=1,
            grid=(pairs,),
            in_specs=[halves_spec(3), halves_spec(3)],
            out_specs=[
                halves_spec(1),
                halves_spec(1),
                pl.BlockSpec((1, 2, TRUNK), lambda p, leaves: (p, 0, 0)),
                pl.BlockSpec((1, TEAMS, 2, TEAM), lambda p, leaves: (p, 0, 0, 0)),
            ],
            scratch_shapes=[
                pltpu.VMEM((3, TREE_LEN, PAIR), BF16),
                pltpu.VMEM((TREE_LEN, PAIR), BF16),
                pltpu.VMEM((PAIR, TREE_LEN), BF16),
            ],
        ),
        out_shape=[
            jax.ShapeDtypeStruct((2, quarter, width), BF16),
            jax.ShapeDtypeStruct((2, quarter, width), BF16),
            jax.ShapeDtypeStruct((pairs, 2, TRUNK), F32),
            jax.ShapeDtypeStruct((pairs, TEAMS, 2, TEAM), F32),
        ],
        cost_estimate=attention_cost(2, COVER),
        name="tree_attention",
    )(leaves, near, far)


def backward_block(qkv_ref, keys_t_ref, queries, grads, outs, logs, groups):
    products = grads.astype(F32) * outs.astype(F32)
    products_t = products.T
    key_ds = [[] for _ in groups]
    value_ws = [[] for _ in groups]
    own_q, own_g, query_grads = [], [], []
    for head in range(2):
        own = head_lanes(queries, head)
        own_grads = head_lanes(grads, head)
        own_q.append(own)
        own_g.append(own_grads)
        inner = jnp.sum(
            products_t[head * HEAD_DIM : (head + 1) * HEAD_DIM], axis=0, keepdims=True
        )
        log = logs[head : head + 1]
        query_grad = None
        for place, (start, size, first, last, rule) in enumerate(groups):
            scores = masked_scores(qkv_ref[1, pl.ds(start, size), :], own[first:last], rule)
            weights = jnp.exp(scores - log[:, first:last])
            grad_weights = dot_nt(qkv_ref[2, pl.ds(start, size), :], own_grads[first:last])
            grad_scores = (weights * (grad_weights - inner[:, first:last])).astype(BF16)
            keys_t = keys_t_ref[pl.ds(head * HEAD_DIM, HEAD_DIM), pl.ds(start, size)]
            part = widen(dot_nn(keys_t, grad_scores), first, queries.shape[0], 0.0)
            query_grad = part if query_grad is None else query_grad + part
            key_ds[place].append(grad_scores)
            value_ws[place].append(weights.astype(BF16))
        query_grads.append(query_grad)
    grad_query = (jnp.concatenate(query_grads, axis=0) * HEAD_DIM ** (-0.5)).T.astype(BF16)
    key_grads, value_grads = [], []
    for place, (start, size, first, last, rule) in enumerate(groups):
        stacked_q = jnp.concatenate([own_q[0][first:last], own_q[1][first:last]], axis=0)
        stacked_g = jnp.concatenate([own_g[0][first:last], own_g[1][first:last]], axis=0)
        key_grads.append(dot_nn(jnp.concatenate(key_ds[place], axis=1), stacked_q))
        value_grads.append(dot_nn(jnp.concatenate(value_ws[place], axis=1), stacked_g))
    return grad_query, key_grads, value_grads


def backward_kernel(
    leaves_ref,
    near_ref,
    far_ref,
    near_grads_ref,
    far_grads_ref,
    near_outs_ref,
    far_outs_ref,
    trunk_log_ref,
    family_log_ref,
    near_result_ref,
    far_result_ref,
    qkv_ref,
    grads_ref,
    outs_ref,
    result_ref,
    keys_t_ref,
    trunk_keys_ref,
    trunk_values_ref,
):
    for offset in range(4):
        rows = quarter_rows(leaves_ref, offset)
        at = offset % 2
        qkv_ref[:, rows, :] = (near_ref if offset < 2 else far_ref)[:, at]
        grads_ref[rows, :] = (near_grads_ref if offset < 2 else far_grads_ref)[at]
        outs_ref[rows, :] = (near_outs_ref if offset < 2 else far_outs_ref)[at]
    transpose_into(keys_t_ref, qkv_ref, 1)
    trunk_keys_ref[...] = jnp.zeros_like(trunk_keys_ref)
    trunk_values_ref[...] = jnp.zeros_like(trunk_values_ref)
    for block in range(TRUNK // QROWS):
        first = block * QROWS
        rows = pl.ds(first, QROWS)
        groups = trunk_groups(block)
        grad_query, key_grads, value_grads = backward_block(
            qkv_ref,
            keys_t_ref,
            scaled_queries(qkv_ref, [first], QROWS),
            grads_ref[rows, :],
            outs_ref[rows, :],
            trunk_log_ref[0, :, rows],
            groups,
        )
        result_ref[0, rows, :] = grad_query
        for (start, size, _, _, _), key_grad, value_grad in zip(groups, key_grads, value_grads):
            trunk_keys_ref[pl.ds(start, size), :] += key_grad
            trunk_values_ref[pl.ds(start, size), :] += value_grad

    def one_team(team, carry):
        starts = team_rows(leaves_ref, team)
        groups = team_groups(starts)
        grad_query, key_grads, value_grads = backward_block(
            qkv_ref,
            keys_t_ref,
            scaled_queries(qkv_ref, starts, SEG),
            jnp.concatenate([grads_ref[pl.ds(start, SEG), :] for start in starts], axis=0),
            jnp.concatenate([outs_ref[pl.ds(start, SEG), :] for start in starts], axis=0),
            family_log_ref[0, team],
            groups,
        )
        trunk_keys_ref[...] += key_grads[0]
        trunk_values_ref[...] += value_grads[0]
        for place, start in enumerate(starts):
            rows = pl.ds(start, SEG)
            result_ref[0, rows, :] = grad_query[place * SEG : (place + 1) * SEG]
            result_ref[1, rows, :] = key_grads[1 + place].astype(BF16)
            result_ref[2, rows, :] = value_grads[1 + place].astype(BF16)
        return carry

    lax.fori_loop(0, TEAMS, one_team, 0)
    result_ref[1, pl.ds(0, TRUNK), :] = trunk_keys_ref[...].astype(BF16)
    result_ref[2, pl.ds(0, TRUNK), :] = trunk_values_ref[...].astype(BF16)
    for offset in range(4):
        half_ref = near_result_ref if offset < 2 else far_result_ref
        rows = quarter_rows(leaves_ref, offset)
        for part in range(3):
            half_ref[offset % 2, :, part * PAIR : (part + 1) * PAIR] = result_ref[part, rows, :]


def attention_backward(leaves, pair, near, far, near_grads, far_grads, near_outs, far_outs, logs):
    quarter = TREE_LEN // 4
    rows = pl.BlockSpec((2, quarter, PAIR), lambda i, leaves: (0, 0, pair))
    parts = pl.BlockSpec((3, 2, quarter, PAIR), lambda i, leaves: (0, 0, 0, pair))
    result = pl.BlockSpec((2, quarter, 3 * PAIR), lambda i, leaves: (0, 0, 0))
    shape = jax.ShapeDtypeStruct((2, quarter, 3 * PAIR), BF16)
    return pl.pallas_call(
        backward_kernel,
        grid_spec=pltpu.PrefetchScalarGridSpec(
            num_scalar_prefetch=1,
            grid=(1,),
            in_specs=[
                parts,
                parts,
                rows,
                rows,
                rows,
                rows,
                pl.BlockSpec((1, 2, TRUNK), lambda i, leaves: (pair, 0, 0)),
                pl.BlockSpec((1, TEAMS, 2, TEAM), lambda i, leaves: (pair, 0, 0, 0)),
            ],
            out_specs=[result, result],
            scratch_shapes=[
                pltpu.VMEM((3, TREE_LEN, PAIR), BF16),
                pltpu.VMEM((TREE_LEN, PAIR), BF16),
                pltpu.VMEM((TREE_LEN, PAIR), BF16),
                pltpu.VMEM((3, TREE_LEN, PAIR), BF16),
                pltpu.VMEM((PAIR, TREE_LEN), BF16),
                pltpu.VMEM((TRUNK, PAIR), F32),
                pltpu.VMEM((TRUNK, PAIR), F32),
            ],
        ),
        out_shape=[shape, shape],
        cost_estimate=attention_cost(5, 10),
        name="tree_attention_back",
    )(leaves, near, far, near_grads, far_grads, near_outs, far_outs, *logs)


def leaf_order(parents_row):
    first_leaf = BRANCHES + 1
    leaf_parents = parents_row[first_leaf:]
    segments = first_leaf + jnp.arange(leaf_parents.shape[0], dtype=jnp.int32)
    same = leaf_parents[:, None] == leaf_parents[None, :]
    later = segments[None, :] < segments[:, None]
    place = 2 * (leaf_parents - 1) + jnp.sum(jnp.where(same & later, 1, 0), axis=1)
    slots = jnp.arange(2 * BRANCHES, dtype=jnp.int32)
    return jnp.sum(jnp.where(slots[:, None] == place[None, :], segments[None, :], 0), axis=1)


def gates(logits, experts, expert):
    lane = lax.broadcasted_iota(jnp.int32, logits.shape, 1)
    first, second = logits[:, experts : experts + 1], logits[:, experts + 1 : experts + 2]
    top = jnp.maximum(first, second)
    first, second = jnp.exp(first - top), jnp.exp(second - top)
    total = first + second
    first, second = first / total, second / total
    if expert is None:
        return lane, first, second, None, None
    routed = jnp.where(lane < experts, logits, NEGATIVE_FILL)
    raised = jnp.exp(routed - jnp.max(routed, axis=1, keepdims=True))
    probs = raised / jnp.sum(raised, axis=1, keepdims=True)
    gate = jnp.sum(jnp.where(lane == expert, probs, 0.0), axis=1, keepdims=True)
    return lane, first, second, probs, gate


def both(own_ref, side_ref):
    return jnp.concatenate([own_ref[...], side_ref[...]], axis=0)


def split_store(own_ref, side_ref, rows):
    half = rows.shape[0] // 2
    own_ref[...] = rows[:half]
    side_ref[...] = rows[half:]


def feed_kernel(
    experts,
    routed,
    expert_ref,
    own_ref,
    side_ref,
    own_grads_ref,
    side_grads_ref,
    head_ref,
    up_ref,
    down_ref,
    own_out_ref,
    side_out_ref,
    own_back_ref,
    side_back_ref,
    active_ref,
    pre_ref,
    grad_ref,
    head_grad_ref,
):
    rows = both(own_ref, side_ref)
    grads = both(own_grads_ref, side_grads_ref).astype(F32)
    expert = expert_ref[0] if routed else None
    logits = dot_nn(rows, head_ref[...])
    lane, first, second, probs, gate = gates(logits, experts, expert)
    coef = second * gate if routed else first
    weighted = (coef * grads).astype(BF16)
    pre = dot_nn(rows, up_ref[...])
    grad_active = dot_nt(weighted, down_ref[...])
    cumulative = 0.5 + 0.5 * lax.erf(pre * 0.7071067811865476)
    slope = cumulative + pre * jnp.exp(-0.5 * pre * pre) * 0.3989422804014327
    active = (pre * cumulative).astype(BF16)
    grad_pre = (grad_active * slope).astype(BF16)
    half = rows.shape[0] // 2
    for ref, value in ((active_ref, active), (pre_ref, grad_pre), (grad_ref, weighted)):
        ref[0] = value[:half]
        ref[1] = value[half:]
    out = dot_nn(active, down_ref[...])
    split_store(own_out_ref, side_out_ref, (coef * out).astype(BF16))
    inner = jnp.sum(grads * out, axis=1, keepdims=True)
    swing = first * second * inner
    if routed:
        swing = -gate * swing
    grad_logits = jnp.where(lane == experts, swing, jnp.where(lane == experts + 1, -swing, 0.0))
    if routed:
        picked = jnp.where(lane == expert, 1.0, 0.0) - gate
        grad_logits = grad_logits + jnp.where(
            lane < experts, probs * picked * (second * inner), 0.0
        )
    back = dot_nt(grad_pre, up_ref[...]) + dot_nt(grad_logits.astype(BF16), head_ref[...])
    split_store(own_back_ref, side_back_ref, back.astype(BF16))
    head_grad = dot_nn(grad_logits.T.astype(BF16), rows)

    @pl.when(pl.program_id(0) == 0)
    def _():
        head_grad_ref[...] = jnp.zeros_like(head_grad_ref)

    head_grad_ref[...] += head_grad


def feed(own, side, own_grads, side_grads, head, up, down, experts, expert, size):
    count = own.shape[0]
    width, hidden = up.shape
    steps = count // size
    lanes = head.shape[1]
    routed = expert is not None
    pick = jnp.reshape(expert, (1,)) if routed else jnp.zeros((1,), jnp.int32)
    rows = pl.BlockSpec((size, width), lambda i, pick: (i, 0))

    def whole(shape):
        return pl.BlockSpec(shape, lambda i, pick: (0, 0), pipeline_mode=pl.Buffered(1))

    def pairs(columns):
        return pl.BlockSpec((2, size, columns), lambda i, pick: (0, i, 0))

    quarter = jax.ShapeDtypeStruct((count, width), BF16)
    *sums, active, pre, weighted, head_grad = pl.pallas_call(
        functools.partial(feed_kernel, experts, routed),
        grid_spec=pltpu.PrefetchScalarGridSpec(
            num_scalar_prefetch=1,
            grid=(steps,),
            in_specs=[
                rows,
                rows,
                rows,
                rows,
                whole((width, lanes)),
                whole((width, hidden)),
                whole((hidden, width)),
            ],
            out_specs=[
                rows,
                rows,
                rows,
                rows,
                pairs(hidden),
                pairs(hidden),
                pairs(width),
                pl.BlockSpec((lanes, width), lambda i, pick: (0, 0)),
            ],
        ),
        out_shape=[
            quarter,
            quarter,
            quarter,
            quarter,
            jax.ShapeDtypeStruct((2, count, hidden), BF16),
            jax.ShapeDtypeStruct((2, count, hidden), BF16),
            jax.ShapeDtypeStruct((2, count, width), BF16),
            jax.ShapeDtypeStruct((lanes, width), F32),
        ],
        cost_estimate=pl.CostEstimate(
            flops=16 * count * width * hidden // COVER,
            transcendentals=4 * count * hidden // COVER,
            bytes_accessed=2 * (8 * count * width + 4 * count * hidden + 2 * width * hidden) // COVER,
        ),
        compiler_params=pltpu.CompilerParams(vmem_limit_bytes=60 * 1024 * 1024),
        name="feed_routed" if routed else "feed_dense",
    )(pick, own, side, own_grads, side_grads, head, up, down)
    flat = [value.reshape(2 * count, value.shape[2]) for value in (active, pre, weighted)]
    return [*sums, *flat, head_grad]


LANES = 128
QUARTER_ROWS = 128


def norm_parts(values):
    row_mean = jnp.mean(values, axis=-1, keepdims=True)
    centred = values - row_mean
    row_var = jnp.mean(centred * centred, axis=-1, keepdims=True)
    inverse = lax.rsqrt(row_var + EPSILON)
    return (centred * inverse, inverse)


def norm_kernel(rows_ref, gain_ref, out_ref):
    scaled, _ = norm_parts(rows_ref[...].astype(F32))
    out_ref[...] = (scaled * gain_ref[...]).astype(BF16)


def normed_rows(rows, gain_vec):
    count, width = rows.shape
    block = pl.BlockSpec((QUARTER_ROWS, width), lambda i: (i, 0))
    return pl.pallas_call(
        norm_kernel,
        grid=(count // QUARTER_ROWS,),
        in_specs=[block, pl.BlockSpec((1, width), lambda i: (0, 0))],
        out_specs=block,
        out_shape=jax.ShapeDtypeStruct((count, width), BF16),
        name="row_norm",
    )(rows, gain_vec[None])


def norm_back(grad_normed, gain_vec, scaled, inverse):
    grad_scaled = grad_normed * gain_vec
    first_mean = jnp.mean(grad_scaled, axis=-1, keepdims=True)
    second = jnp.mean(grad_scaled * scaled, axis=-1, keepdims=True)
    return inverse * (grad_scaled - first_mean - scaled * second)


def after(value, *others):
    return lax.optimization_barrier((value, *others))[0]


def from_side(values):
    return lax.ppermute(values, "tensor", [(i, i ^ 1) for i in range(4)])


def from_far(values):
    return lax.ppermute(values, "tensor", [(i, i ^ 2) for i in range(4)])


def plus_side(own, side):
    return own.astype(F32) + from_side(side.astype(BF16)).astype(F32)


def sum_over(values, axis):
    count, step = lax.axis_size(axis), 1
    while step < count:
        pairs = [(i, i ^ step) for i in range(count)]
        values = values + lax.ppermute(values, axis, pairs)
        step *= 2
    return values


def exchange(blocks):
    return lax.all_to_all(blocks, "expert", split_axis=0, concat_axis=0, tiled=True)


def scatter_sum(strips):
    strips = with_layout_constraint(strips.astype(BF16), Layout(major_to_minor=(0, 1)))
    return lax.psum_scatter(strips, "expert", scatter_dimension=0, tiled=True)


def strips_sent(grads):
    return exchange(grads.reshape(lax.axis_size("expert"), -1, grads.shape[1]))


def strips_total(strips):
    return jnp.sum(strips.astype(F32), axis=0)


def slots_of(expert_ids, experts, capacity):
    rows = expert_ids.shape[0]
    chosen = expert_ids[:, None] == jnp.arange(experts, dtype=jnp.int32)[None, :]
    at = jnp.arange(rows, dtype=jnp.int32)
    before = (at[None, :] < at[:, None]).astype(BF16)
    earlier = jnp.dot(before, chosen.astype(BF16), preferred_element_type=F32)
    slot = jnp.sum(jnp.where(chosen, earlier, 0.0), axis=1).astype(jnp.int32)
    place = expert_ids * capacity + slot
    places = jnp.arange(experts * capacity, dtype=jnp.int32)
    return (places[:, None] == place[None, :]).astype(BF16)


def per_device(
    tokens,
    cotangent,
    routes,
    parents,
    ln_attn,
    w_qkv,
    w_out,
    ln_mlp,
    w_up,
    w_down,
    w_router,
    w_mix,
    ex_up,
    ex_down,
):
    tok_dev, width = tokens.shape
    mine = lax.axis_index("tensor")
    experts = w_router.shape[1]
    capacity = max(2, tok_dev * 7 // (5 * experts))
    heads_width = w_qkv.shape[2]
    hidden = w_up.shape[1]
    leaves = jnp.concatenate([leaf_order(parents[0]), mine.astype(jnp.int32)[None]])

    scaled_one, inverse_one = norm_parts(tokens.astype(F32))
    normed_own = normed_rows(tokens, ln_attn)
    normed_far = from_far(normed_own)
    near_one = jnp.concatenate([normed_own, from_side(normed_own)], axis=0)

    quarter_ids = routes[:, 0].reshape(4, tok_dev)

    def slots_at(offset):
        ids = lax.dynamic_index_in_dim(quarter_ids, mine ^ offset, 0, keepdims=False)
        return slots_of(ids, experts, capacity)

    own_slots, far_slots = slots_at(0), slots_at(2)

    def placed(slots, rows):
        return jnp.dot(slots, rows, preferred_element_type=F32).astype(BF16)

    def sent(rows):
        return exchange(rows.reshape(experts, capacity, width)).reshape(-1, width)

    own_grads = sent(placed(own_slots, cotangent))
    cotangent_side = from_side(cotangent)

    def project(rows):
        qkv = jnp.einsum("td,sdc->stc", rows, w_qkv, preferred_element_type=F32)
        return qkv.astype(BF16).reshape(3, 2, tok_dev, heads_width)

    lanes = -(-(experts + 2) // LANES) * LANES
    head = jnp.concatenate(
        [w_router, w_mix, jnp.zeros((width, lanes - experts - 2), BF16)], axis=1
    )
    near_qkv = project(near_one)
    cotangent_far = from_far(after(cotangent, normed_far))
    normed_far, near_qkv, head = lax.optimization_barrier((normed_far, near_qkv, head))
    far_one = jnp.concatenate([normed_far, from_side(normed_far)], axis=0)
    far_qkv = project(far_one)
    near_out, far_out, *logs = attention_forward(leaves, near_qkv, far_qkv)
    far_out, own_grads, cotangent_far, cotangent_side = lax.optimization_barrier(
        (far_out, own_grads, cotangent_far, cotangent_side)
    )

    def branch_part(rows):
        return jnp.dot(rows, w_out, preferred_element_type=F32)

    far_sum = plus_side(branch_part(far_out[0]), branch_part(far_out[1])).astype(BF16)
    branch = plus_side(branch_part(near_out[0]), branch_part(near_out[1]))
    branch_far = from_far(far_sum)
    side_grads = from_side(own_grads)
    cotangent_corner = from_side(cotangent_far)
    far_placed = placed(far_slots, cotangent_far)
    branch_far, side_grads, cotangent_corner, far_placed = lax.optimization_barrier(
        (branch_far, side_grads, cotangent_corner, far_placed)
    )
    residual = tokens.astype(F32) + (branch + branch_far.astype(F32))

    scaled_two, inverse_two = norm_parts(residual)
    normed_two = (scaled_two * ln_mlp).astype(BF16)
    normed_two_far = from_far(normed_two)
    normed_two_side = from_side(normed_two)
    own_rows = sent(placed(own_slots, normed_two))

    def dense(own, side, own_cotangent, side_cotangent):
        return feed(
            own, side, own_cotangent, side_cotangent, head, w_up, w_down, experts, None, QUARTER_ROWS
        )

    def product(left, right):
        return jnp.einsum("gd,gf->df", left, right, preferred_element_type=F32)

    def weight_grads(near_left, far_left, near_right, far_right):
        return product(near_left, near_right) + product(far_left, far_right)

    near_dense = dense(normed_two, normed_two_side, cotangent, cotangent_side)
    near_two = jnp.concatenate([normed_two, normed_two_side], axis=0)
    grad_up = product(near_two, near_dense[5])
    grad_down = product(near_dense[6], near_dense[4])
    normed_two_far, grad_up, grad_down, own_rows = lax.optimization_barrier(
        (normed_two_far, grad_up, grad_down, own_rows)
    )
    far_rows = from_far(own_rows)
    far_grads = sent(after(far_placed, own_rows))
    normed_two_corner = from_side(normed_two_far)
    far_dense = list(dense(normed_two_far, normed_two_corner, cotangent_far, cotangent_corner))

    expert = lax.axis_index("expert").astype(jnp.int32)

    def routed(own, side, own_cotangent, side_cotangent):
        return feed(
            own,
            side,
            own_cotangent,
            side_cotangent,
            head,
            ex_up[0],
            ex_down[0],
            experts,
            expert,
            QUARTER_ROWS,
        )

    def chip_sum(parts, place, *others):
        return plus_side(parts[place], after(parts[place + 1], *others))

    def chip_sum(parts, place, *others):
        return plus_side(parts[place], after(parts[place + 1], *others))

    dense_back_far = chip_sum(far_dense, 2).astype(BF16)
    far_two = jnp.concatenate([normed_two_far, normed_two_corner], axis=0)
    grad_down = (grad_down + product(far_dense[6], far_dense[4])).astype(BF16)
    far_two, grad_down = lax.optimization_barrier((far_two, grad_down))
    grad_up = (grad_up + product(far_two, far_dense[5])).astype(BF16)
    dense_grads = after(jnp.concatenate([grad_up, grad_down], axis=1), far_grads)
    far_rows, dense_back_far, dense_grads = lax.optimization_barrier(
        (far_rows, dense_back_far, dense_grads)
    )
    dense_grads = scatter_sum(dense_grads)
    dense_back_far = from_far(dense_back_far)
    corner_rows = from_side(far_rows)
    side_rows = from_side(own_rows)
    far_expert = routed(far_rows, corner_rows, far_grads, from_side(far_grads))
    *far_expert, dense_back_far = lax.optimization_barrier((*far_expert, dense_back_far))
    far_back = chip_sum(far_expert, 2).astype(BF16)
    own_rows, far_back = lax.optimization_barrier((own_rows, far_back))
    near_expert = routed(own_rows, side_rows, own_grads, side_grads)
    *near_expert, dense_grads = lax.optimization_barrier((*near_expert, dense_grads))

    def picked(rows):
        return lax.dot_general(
            own_slots, rows, (((0,), (0,)), ((), ())), preferred_element_type=F32
        )

    expert_back = (chip_sum(near_expert, 2) + from_far(far_back).astype(F32)).astype(BF16)
    far_expert_out = chip_sum(far_expert, 0, expert_back).astype(BF16)
    dense_out_far = chip_sum(far_dense, 0, expert_back).astype(BF16)
    dense_back = chip_sum(near_dense, 2, far_back) + dense_back_far.astype(F32)

    grad_normed_two = dense_back + picked(sent(expert_back))
    dense_out = chip_sum(near_dense, 0, expert_back)
    expert_out = chip_sum(near_expert, 0, expert_back) + from_far(far_expert_out).astype(F32)
    expert_out = after(expert_out.astype(BF16), grad_normed_two)

    near_active, far_active, near_pre, far_pre, far_expert_out = lax.optimization_barrier(
        (near_expert[4], far_expert[4], near_expert[5], far_expert[5], far_expert_out)
    )
    near_tokens = jnp.concatenate([own_rows, side_rows], axis=0)
    far_tokens = jnp.concatenate([far_rows, corner_rows], axis=0)
    grad_ex_up = weight_grads(near_tokens, far_tokens, near_pre, far_pre)[None]
    grad_ex_down = weight_grads(near_active, far_active, near_expert[6], far_expert[6])[None]

    gain_two = jnp.sum(grad_normed_two * scaled_two, axis=0)
    grad_residual = cotangent.astype(F32) + norm_back(
        grad_normed_two, ln_mlp, scaled_two, inverse_two
    )
    grad_branch = grad_residual.astype(BF16)
    grad_branch_far = from_far(grad_branch)
    grad_branch_side = from_side(grad_branch)

    def into_heads(*rows):
        grads = [jnp.einsum("gd,cd->gc", part, w_out, preferred_element_type=F32) for part in rows]
        return jnp.stack(grads).astype(BF16)

    near_heads = into_heads(grad_branch, grad_branch_side)
    out_rows = sent(expert_out)
    flat = (2 * tok_dev, heads_width)
    near_branch = jnp.concatenate([grad_branch, grad_branch_side], axis=0)
    grad_w_out = product(near_branch, near_out.reshape(flat))
    grad_branch_far, near_heads, grad_w_out, grad_ex_up, grad_ex_down, _, dense_out_far, dense_out = (
        lax.optimization_barrier(
            (
                grad_branch_far,
                near_heads,
                grad_w_out,
                grad_ex_up,
                grad_ex_down,
                expert_out,
                dense_out_far,
                dense_out,
            )
        )
    )
    grad_branch_corner = from_side(grad_branch_far)
    far_heads = into_heads(grad_branch_far, grad_branch_corner)
    dense_out_far = from_far(dense_out_far)
    head_grads = near_dense[7] + far_dense[7] + near_expert[7] + far_expert[7]
    small = jnp.concatenate([head_grads[: experts + 2], gain_two[None]], axis=0)

    def pair_back(pair, near_grads, far_grads):
        return attention_backward(
            leaves, pair, near_qkv, far_qkv, near_grads, far_grads, near_out, far_out, logs
        )

    def pair_weights(pair):
        lanes = slice(pair * PAIR, (pair + 1) * PAIR)
        return jnp.concatenate([w_qkv[part, :, lanes] for part in range(3)], axis=1)

    def total(values):
        return functools.reduce(jnp.add, values)

    pairs = heads_width // PAIR
    near_results, far_results = [None] * pairs, [None] * pairs
    near_results[0], far_results[0] = pair_back(0, near_heads, far_heads)
    far_branch = jnp.concatenate([grad_branch_far, grad_branch_corner], axis=0)
    grad_w_out = grad_w_out + product(far_branch, far_out.reshape(flat))
    small_columns = -(-small.shape[0] // LANES) * LANES
    small_block = jnp.pad(small, ((0, small_columns - small.shape[0]), (0, 0))).T
    branch_grads = jnp.concatenate([grad_w_out.astype(BF16), small_block.astype(BF16)], axis=1)
    near_results[0], far_results[0], out_rows, dense_out_far, branch_grads, near_heads = (
        lax.optimization_barrier(
            (near_results[0], far_results[0], out_rows, dense_out_far, branch_grads, near_heads)
        )
    )
    branch_grads = strips_sent(branch_grads)
    for pair in range(1, pairs):
        near_results[pair], far_results[pair] = pair_back(pair, near_heads, far_heads)
    near_results, far_results, branch_grads = lax.optimization_barrier(
        (near_results, far_results, branch_grads)
    )

    def normed_part(results, quarter):
        return total([dot_nt(results[pair][quarter], pair_weights(pair)) for pair in range(pairs)])

    def qkv_weights(pair, *others):
        near_rows = near_results[pair].reshape(2 * tok_dev, 3 * PAIR)
        far_rows = far_results[pair].reshape(2 * tok_dev, 3 * PAIR)
        near_rows = after(near_rows, *others)
        return weight_grads(near_one, far_one, near_rows, far_rows).astype(BF16)

    corner_part = normed_part(far_results, 1).astype(BF16)
    from_corner = from_side(corner_part).astype(F32)
    first_grads = qkv_weights(0, corner_part)
    far_results, first_grads = lax.optimization_barrier((far_results, first_grads))
    qkv_grads = [strips_sent(first_grads)]
    far_sum = (normed_part(far_results, 0) + from_corner).astype(BF16)
    near_results, far_results, out_rows, far_sum = lax.optimization_barrier(
        (near_results, far_results, out_rows, far_sum)
    )
    near_sum = plus_side(normed_part(near_results, 0), normed_part(near_results, 1))

    scaled_far = normed_far.astype(F32) / ln_attn
    gain_one = jnp.sum(
        near_sum * scaled_one + far_sum.astype(F32) * scaled_far, axis=0, keepdims=True
    )
    gain_one = sum_over(gain_one, "expert")
    out_rows = after(out_rows, gain_one)
    out = (residual + dense_out + dense_out_far.astype(F32) + picked(out_rows)).astype(BF16)
    last_grads = [qkv_weights(pair, far_sum) for pair in range(1, pairs)]
    qkv_grads += [strips_sent(grads) for grads in last_grads]
    far_arrived, gain_one, dense_grads, *_ = lax.optimization_barrier(
        (from_far(far_sum), gain_one, dense_grads, *last_grads)
    )
    grad_normed_one = near_sum + far_arrived.astype(F32)
    grad_ln_attn = sum_over(gain_one, "tensor")[0]
    branch_grads = strips_total(after(branch_grads, gain_one))
    small = sum_over(branch_grads[:, heads_width:], "tensor")
    qkv_grads = jnp.stack(
        [strips_total(grads).reshape(-1, 3, PAIR) for grads in qkv_grads], axis=2
    )
    grad_tokens = grad_residual + norm_back(grad_normed_one, ln_attn, scaled_one, inverse_one)

    strip = qkv_grads.shape[0]
    return (
        out,
        grad_tokens,
        grad_ln_attn,
        qkv_grads.reshape(strip, 3, heads_width).transpose(1, 0, 2),
        branch_grads[:, :heads_width].T,
        small[:, experts + 2],
        dense_grads[:, :hidden].astype(F32),
        dense_grads[:, hidden:].T.astype(F32),
        small[:, :experts],
        small[:, experts : experts + 2],
        grad_ex_up,
        grad_ex_down,
    )


def solution(mesh):
    return jax.shard_map(
        per_device,
        mesh=mesh,
        in_specs=(
            P(("expert", "tensor"), None),
            P(("expert", "tensor"), None),
            P("expert", None),
            P("expert", None),
            P(),
            P(None, None, "tensor"),
            P("tensor", None),
            P(),
            P(None, "tensor"),
            P("tensor", None),
            P(),
            P(),
            P("expert", None, "tensor"),
            P("expert", "tensor", None),
        ),
        out_specs=(
            P(("expert", "tensor"), None),
            P(("expert", "tensor"), None),
            P(),
            P(None, "expert", "tensor"),
            P("tensor", "expert"),
            P("expert"),
            P("expert", "tensor"),
            P("tensor", "expert"),
            P("expert", None),
            P("expert", None),
            P("expert", None, "tensor"),
            P("expert", "tensor", None),
        ),
        check_vma=False,
    )
```
